32 devices in a mesh: fsdp: 2 (over x), ctx: 4 (over z), tp: 4 (over y, core).
Axes of the slice: x: 2, y: 2, z: 4, core: 2. Of those that a mesh axis runs over, the one named last changes fastest.
Arguments:
- entering_activations: bfloat16 [4, 2048, 2048], P('fsdp', 'ctx'), may hold values from -6 to 6
- document_indices: int32 [4, 2048], P('fsdp'), may hold values from 0 to 10, never falling along the last dimension, each value on 1 to 800 neighbouring positions
- acceptor_matrix: bfloat16 [2048, 2048], P(('fsdp', 'ctx'), 'tp'), may hold values from -0.125 to 0.125
- lookup_matrix: bfloat16 [2048, 2048], P(('fsdp', 'ctx'), 'tp'), may hold values from -0.125 to 0.125
- payload_matrix: bfloat16 [2048, 2048], P(('fsdp', 'ctx'), 'tp'), may hold values from -0.125 to 0.125
- valve_matrix: bfloat16 [2048, 2048], P(('fsdp', 'ctx'), 'tp'), may hold values from -0.125 to 0.125
- result_matrix: bfloat16 [2048, 2048], P('tp', ('fsdp', 'ctx')), may hold values from -0.25 to 0.25
- ffn_lookup_matrix: bfloat16 [2048, 7168], P(('fsdp', 'ctx'), 'tp'), may hold values from -0.125 to 0.125
- ffn_payload_matrix: bfloat16 [7168, 2048], P('tp', ('fsdp', 'ctx')), may hold values from -0.0625 to 0.0625
- ffn_acceptor_matrix: bfloat16 [2048, 2048], P(('fsdp', 'ctx'), 'tp'), may hold values from -0.125 to 0.125
- first_standardize_scaling: float32 [2048], replicated, may hold values from 0.5 to 1.5
- first_standardize_offset: float32 [2048], replicated, may hold values from -0.8 to 0.8
- acceptor_lerp_factor: float32 [2048], replicated, may hold values from 0.05 to 0.95
- lookup_lerp_factor: float32 [2048], replicated, may hold values from 0.05 to 0.95
- payload_lerp_factor: float32 [2048], replicated, may hold values from 0.05 to 0.95
- valve_lerp_factor: float32 [2048], replicated, may hold values from 0.05 to 0.95
- token_fading: float32 [2048], replicated, may hold values from 0.9 to 0.9998
- diagonal_reward: float32 [2048], replicated, may hold values from -2 to 2
- subspace_standardize_scaling: float32 [2048], replicated, may hold values from 0.5 to 1.5
- subspace_standardize_offset: float32 [2048], replicated, may hold values from -0.8 to 0.8
- second_standardize_scaling: float32 [2048], replicated, may hold values from 0.5 to 1.5
- second_standardize_offset: float32 [2048], replicated, may hold values from -0.8 to 0.8
- ffn_lookup_lerp: float32 [2048], replicated, may hold values from 0.05 to 0.95
- ffn_acceptor_lerp: float32 [2048], replicated, may hold values from 0.05 to 0.95
- upstream_derivative: bfloat16 [4, 2048, 2048], P('fsdp', 'ctx', 'tp'), may hold values from -6 to 6
Outputs:
- result: bfloat16 [4, 2048, 2048], P('fsdp', 'ctx', 'tp')
- grad_inputs: float32 [4, 2048, 2048], P('fsdp', 'ctx')
- grad_time_recept: float32 [2048, 2048], P(('fsdp', 'ctx'), 'tp')
- grad_time_key: float32 [2048, 2048], P(('fsdp', 'ctx'), 'tp')
- grad_time_value: float32 [2048, 2048], P(('fsdp', 'ctx'), 'tp')
- grad_time_gate: float32 [2048, 2048], P(('fsdp', 'ctx'), 'tp')
- grad_time_output: float32 [2048, 2048], P('tp', ('fsdp', 'ctx'))
- grad_chan_key: float32 [2048, 7168], P(('fsdp', 'ctx'), 'tp')
- grad_chan_value: float32 [7168, 2048], P('tp', ('fsdp', 'ctx'))
- grad_chan_recept: float32 [2048, 2048], P(('fsdp', 'ctx'), 'tp')
- grad_first_gain: float32 [2048], P(('fsdp', 'ctx'))
- grad_first_bias: float32 [2048], P(('fsdp', 'ctx'))
- grad_mix_recept: float32 [2048], P(('fsdp', 'ctx'))
- grad_mix_key: float32 [2048], P(('fsdp', 'ctx'))
- grad_mix_value: float32 [2048], P(('fsdp', 'ctx'))
- grad_mix_gate: float32 [2048], P(('fsdp', 'ctx'))
- grad_time_decay: float32 [2048], P(('fsdp', 'ctx'))
- grad_time_bonus: float32 [2048], P(('fsdp', 'ctx'))
- grad_group_gain: float32 [2048], P(('fsdp', 'ctx'))
- grad_group_bias: float32 [2048], P(('fsdp', 'ctx'))
- grad_second_gain: float32 [2048], P(('fsdp', 'ctx'))
- grad_second_bias: float32 [2048], P(('fsdp', 'ctx'))
- grad_shift_key: float32 [2048], P(('fsdp', 'ctx'))
- grad_shift_recept: float32 [2048], P(('fsdp', 'ctx'))
The draws below stay inside these ranges and needn't reach their ends.
Inputs may be any that keep to these rules, and one draw needn't show every extreme that they name: `document_indices`: segment numbers never fall along a sequence; each document has 1 to min(800, 2048) positions.
All inputs are finite; a program needn't handle non-finite values.
Results may differ from the reference program's by a relative error of at most 0.029.
Values may be sent and summed in bfloat16 or wider, within the bound.
A program may use at most 320 MiB of HBM per device.

```python
import math
from functools import partial
import jax
import jax.numpy as jnp
import numpy as np
from jax import lax

EMBED_DIMENSION = 2048
TIMEMIX_COUNT = 32
SUBSPACE_SIZE = 64
FF = 7168
BLOCK = 64
DOC_MOST = 800
LEN = 2048
SEQS = 4


def draw_token_fading(key, part):
    rate = jnp.exp(jax.random.uniform(key, (EMBED_DIMENSION,), jnp.float32, minval=math.log(0.0005), maxval=math.log(0.1)))
    return (1.0 - rate).astype(jnp.float32)


def levels(own_key, shape, cuts, smallest, high):
    factor_of, own = 1.0, jax.random.fold_in(own_key, 6)
    for axis_at, parts in cuts:
        steps = jnp.exp(jax.random.uniform(jax.random.fold_in(own, axis_at), (parts,), jnp.float32, smallest / len(cuts), high / len(cuts)))
        factor_of = factor_of * jnp.repeat(steps, shape[axis_at] // parts).reshape([-1 if axis == axis_at else 1 for axis in range(len(shape))])
    return factor_of


def split_up(count, total, most, skew):
    weights = [(1 << 20) // math.isqrt(grade ** skew) + 1 for grade in range(2, count + 1)]
    spare, given = total - most - (count - 1), [1] * (count - 1)
    while spare > 0:
        candidates = [i for i in range(count - 1) if given[i] < most]
        pool, budget = sum([weights[i] for i in candidates]), spare
        for i in candidates:
            addition = min(most - given[i], max(1, budget * weights[i] // pool), spare)
            given[i] = given[i] + addition
            spare = spare - addition
    return np.array([most] + given)


def ragged(rng, count, total, most, slope):
    if count == 2:
        one = jax.random.randint(rng, (), max(1, total - most), min(most, total - 1) + 1)
        return jnp.stack([one, total - one])
    sizes = jnp.asarray(split_up(count, total, most, slope), jnp.int32)
    twos = (count - 1) // 2
    giver, receiver = sizes[1:1 + 2 * twos:2], sizes[2:2 + 2 * twos:2]
    room = jnp.minimum(giver - 1, most - receiver)
    passed = jax.random.randint(jax.random.fold_in(rng, 1), (twos,), 0, 1 << 20) % (room + 1)
    sizes = sizes.at[1:1 + 2 * twos:2].set(giver - passed).at[2:2 + 2 * twos:2].set(receiver + passed)
    return sizes[jax.random.permutation(jax.random.fold_in(rng, 2), count)]


def centred(stream_key, extent, spread, limit, pieces=(), kind=jnp.bfloat16):
    values = spread * jax.random.normal(stream_key, extent, jnp.float32)
    if pieces:
        values = values * levels(stream_key, extent, pieces, -0.22, 0.18)
    return jnp.clip(values, -limit, limit).astype(kind)


def setup_inputs(seed: int = 0) -> dict:
    splits = jax.random.split(jax.random.key(seed), 26)
    return {
        "entering_activations": centred(splits[0], (SEQS, LEN, EMBED_DIMENSION), 1.0, 6.0, ((0, 2), (1, 4))),
        "document_indices": jax.vmap(lambda own: jnp.searchsorted(jnp.cumsum(ragged(own, 4 * LEN // DOC_MOST + 1, LEN, min(DOC_MOST, LEN), 2)), jnp.arange(LEN), side="right"))(jax.random.split(splits[1], SEQS)).reshape((SEQS, LEN)).astype(jnp.int32),
        "acceptor_matrix": centred(splits[2], (EMBED_DIMENSION, EMBED_DIMENSION), EMBED_DIMENSION ** -0.5, 0.125, ((0, 8), (1, 4))),
        "lookup_matrix": centred(splits[3], (EMBED_DIMENSION, EMBED_DIMENSION), EMBED_DIMENSION ** -0.5, 0.125, ((0, 8), (1, 4))),
        "payload_matrix": centred(splits[4], (EMBED_DIMENSION, EMBED_DIMENSION), EMBED_DIMENSION ** -0.5, 0.125, ((0, 8), (1, 4))),
        "valve_matrix": centred(splits[5], (EMBED_DIMENSION, EMBED_DIMENSION), EMBED_DIMENSION ** -0.5, 0.125, ((0, 8), (1, 4))),
        "result_matrix": centred(splits[6], (EMBED_DIMENSION, EMBED_DIMENSION), (EMBED_DIMENSION // 4) ** -0.5, 0.25, ((0, 4), (1, 8))),
        "ffn_lookup_matrix": centred(splits[7], (EMBED_DIMENSION, FF), EMBED_DIMENSION ** -0.5, 0.125, ((0, 8), (1, 4))),
        "ffn_payload_matrix": centred(splits[8], (FF, EMBED_DIMENSION), FF ** -0.5, 0.0625, ((0, 4), (1, 8))),
        "ffn_acceptor_matrix": centred(splits[9], (EMBED_DIMENSION, EMBED_DIMENSION), EMBED_DIMENSION ** -0.5, 0.125, ((0, 8), (1, 4))),
        "first_standardize_scaling": jnp.clip(1.0 + 0.1 * jax.random.normal(splits[10], (EMBED_DIMENSION,), jnp.float32), 0.5, 1.5),
        "first_standardize_offset": centred(splits[11], (EMBED_DIMENSION,), 0.2, 0.8, (), jnp.float32),
        "acceptor_lerp_factor": jnp.clip(jax.random.uniform(splits[12], (EMBED_DIMENSION,), jnp.float32, 0.05, 0.95), 0.05, 0.95),
        "lookup_lerp_factor": jnp.clip(jax.random.uniform(splits[13], (EMBED_DIMENSION,), jnp.float32, 0.05, 0.95), 0.05, 0.95),
        "payload_lerp_factor": jnp.clip(jax.random.uniform(splits[14], (EMBED_DIMENSION,), jnp.float32, 0.05, 0.95), 0.05, 0.95),
        "valve_lerp_factor": jnp.clip(jax.random.uniform(splits[15], (EMBED_DIMENSION,), jnp.float32, 0.05, 0.95), 0.05, 0.95),
        "token_fading": draw_token_fading(jax.random.fold_in(splits[25], 71), 0),
        "diagonal_reward": centred(splits[17], (EMBED_DIMENSION,), 0.5, 2.0, (), jnp.float32),
        "subspace_standardize_scaling": jnp.clip(1.0 + 0.1 * jax.random.normal(splits[18], (EMBED_DIMENSION,), jnp.float32), 0.5, 1.5),
        "subspace_standardize_offset": centred(splits[19], (EMBED_DIMENSION,), 0.2, 0.8, (), jnp.float32),
        "second_standardize_scaling": jnp.clip(1.0 + 0.1 * jax.random.normal(splits[20], (EMBED_DIMENSION,), jnp.float32), 0.5, 1.5),
        "second_standardize_offset": centred(splits[21], (EMBED_DIMENSION,), 0.2, 0.8, (), jnp.float32),
        "ffn_lookup_lerp": jnp.clip(jax.random.uniform(splits[22], (EMBED_DIMENSION,), jnp.float32, 0.05, 0.95), 0.05, 0.95),
        "ffn_acceptor_lerp": jnp.clip(jax.random.uniform(splits[23], (EMBED_DIMENSION,), jnp.float32, 0.05, 0.95), 0.05, 0.95),
        "upstream_derivative": centred(splits[24], (SEQS, LEN, EMBED_DIMENSION), 1.0, 6.0, ((0, 2), (1, 4), (2, 4))),
    }


HIGH = lax.Precision.HIGHEST
EPS = 1e-05
GROUP_EPS = 4.0

@jax.custom_vjp
def low(v):
    return lax.optimization_barrier(v.astype(jnp.bfloat16)).astype(jnp.float32)

@jax.custom_vjp
def low_back(v):
    return v

def low_keep(v):
    return (low(v), None)

def low_pass(kept, grad):
    return (grad,)

def back_keep(v):
    return (v, None)

def back_low(kept, grad):
    return (low(grad),)
low.defvjp(low_keep, low_pass)
low_back.defvjp(back_keep, back_low)

def product(left, right):
    return jnp.dot(left, right, precision=HIGH, preferred_element_type=jnp.float32)

def fading_payload_tile(fading_exponent, reward_addend, memory_matrix_kept, fragment_collection):
    acceptor_entries, lookup_share, payload_share, seg_block, seg_start = fragment_collection
    length = acceptor_entries.shape[0]
    offsets = jnp.arange(length, dtype=jnp.float32)[:, None, None]
    rising = jnp.exp(offsets * fading_exponent)
    falling = jnp.exp(-(offsets + 1.0) * fading_exponent)
    closing = jnp.exp((float(length) - 1.0 - offsets) * fading_exponent)
    query_dec = acceptor_entries * rising
    key_dec = lookup_share * falling
    scores = jnp.einsum('thi,shi->hts', query_dec, key_dec, precision=HIGH)
    later_mask = jnp.arange(length, dtype=jnp.int32)[:, None] > jnp.arange(length, dtype=jnp.int32)[None, :]
    same_doc = seg_block[:, None] == seg_block[None, :]
    coefficient_collection = jnp.where(later_mask & same_doc, scores, jnp.zeros_like(scores))
    immediate_addend = lax.optimization_barrier(jnp.sum(acceptor_entries * reward_addend * lookup_share, axis=-1, keepdims=True))
    live_mask = (seg_block == seg_start).astype(jnp.float32)[:, None, None]
    result = jnp.einsum('hts,shj->thj', coefficient_collection, payload_share, precision=HIGH) + immediate_addend * payload_share
    result = result + live_mask * jnp.einsum('thi,hij->thj', query_dec, memory_matrix_kept, precision=HIGH)
    ending = (seg_block == seg_block[-1]).astype(jnp.float32)[:, None, None]
    key_end = lookup_share * closing * ending
    carried = jnp.exp(float(length) * fading_exponent) * live_mask[-1]
    new_state = carried[:, :, None] * memory_matrix_kept + jnp.einsum('shi,shj->hij', key_end, payload_share, precision=HIGH)
    return (new_state, result)

def fading_payload_sweeper(acceptor_entries, lookup_share, payload_share, fading_coefficients, reward_coefficients, memory_matrix_kept, document_sweeper, document_begins):
    length = acceptor_entries.shape[0]
    blocks = length // BLOCK
    fading_exponent = jnp.log(fading_coefficients)

    def to_blocks(array):
        return array.reshape((blocks, BLOCK) + array.shape[1:])
    seg_blocks = document_sweeper.reshape(blocks, BLOCK)
    seg_starts = jnp.concatenate([document_begins.astype(jnp.int32), seg_blocks[:-1, -1].astype(jnp.int32)])
    scan_update = jax.checkpoint(partial(fading_payload_tile, fading_exponent, reward_coefficients))
    final_memory_matrix, block_outs = lax.scan(scan_update, memory_matrix_kept, (to_blocks(acceptor_entries), to_blocks(lookup_share), to_blocks(payload_share), seg_blocks, seg_starts))
    return (block_outs.reshape(acceptor_entries.shape), final_memory_matrix)

def layer_norm(values, gain, bias_term, epsilon):
    average = lax.optimization_barrier(jnp.mean(values, -1, keepdims=True))
    centered = values - average
    variance = lax.optimization_barrier(jnp.mean(centered * centered, -1, keepdims=True))
    return centered * lax.rsqrt(variance + epsilon) * gain + bias_term

def forward_one(row_input, learnable_collection, document_labels):
    acceptor_matrix, lookup_matrix, payload_matrix, valve_matrix, result_matrix, ffn_lookup_matrix, ffn_payload_matrix, ffn_acceptor_matrix, first_standardize_scaling, first_standardize_offset, acceptor_lerp_factor, lookup_lerp_factor, payload_lerp_factor, valve_lerp_factor, token_fading, diagonal_reward, subspace_standardize_scaling, subspace_standardize_offset, second_standardize_scaling, second_standardize_offset, ffn_lookup_lerp, ffn_acceptor_lerp = learnable_collection
    document_labels = document_labels.astype(jnp.int32)
    document_begins = jnp.full((1,), -1, jnp.int32)
    seg_before = jnp.concatenate([document_begins, document_labels[:-1]])
    keep_mask = (document_labels == seg_before).astype(jnp.float32)[:, None]
    zero_row = jnp.zeros((1, EMBED_DIMENSION), jnp.float32)
    normed = layer_norm(row_input, first_standardize_scaling, first_standardize_offset, EPS)
    previous = jnp.concatenate([zero_row, normed[:-1]], axis=0) * keep_mask
    delta = normed - previous
    acceptor_vector = low(low_back(product(low(previous + acceptor_lerp_factor * delta), acceptor_matrix)))
    lookup_vector = low(low_back(product(low(previous + lookup_lerp_factor * delta), lookup_matrix)))
    payload_vector = low(low_back(product(low(previous + payload_lerp_factor * delta), payload_matrix)))
    gate_pre = low_back(product(low(previous + valve_lerp_factor * delta), valve_matrix))
    gate_act = jax.nn.silu(gate_pre)
    subspace_dimensions = (LEN, TIMEMIX_COUNT, SUBSPACE_SIZE)
    initial_memory_matrix = jnp.zeros((TIMEMIX_COUNT, SUBSPACE_SIZE, SUBSPACE_SIZE), jnp.float32)
    timemix_result, final_memory_matrix = fading_payload_sweeper(acceptor_vector.reshape(subspace_dimensions), lookup_vector.reshape(subspace_dimensions), payload_vector.reshape(subspace_dimensions), token_fading.reshape(TIMEMIX_COUNT, SUBSPACE_SIZE), diagonal_reward.reshape(TIMEMIX_COUNT, SUBSPACE_SIZE), initial_memory_matrix, document_labels, document_begins)
    grouped = layer_norm(timemix_result, subspace_standardize_scaling.reshape(TIMEMIX_COUNT, SUBSPACE_SIZE), subspace_standardize_offset.reshape(TIMEMIX_COUNT, SUBSPACE_SIZE), GROUP_EPS)
    joined = low(grouped.reshape(LEN, EMBED_DIMENSION) * gate_act)
    mixed_out = low_back(product(joined, result_matrix))
    middle = row_input + mixed_out
    normed_two = layer_norm(middle, second_standardize_scaling, second_standardize_offset, EPS)
    previous_two = jnp.concatenate([zero_row, normed_two[:-1]], axis=0) * keep_mask
    delta_two = normed_two - previous_two
    key_pre = low_back(product(low(previous_two + ffn_lookup_lerp * delta_two), ffn_lookup_matrix))
    hidden = low(jnp.square(jax.nn.relu(key_pre)))
    chan_out = low_back(product(hidden, ffn_payload_matrix))
    rec_gate = jax.nn.sigmoid(low_back(product(low(previous_two + ffn_acceptor_lerp * delta_two), ffn_acceptor_matrix)))
    return middle + rec_gate * chan_out

def reference(entering_activations, document_indices, acceptor_matrix, lookup_matrix, payload_matrix, valve_matrix, result_matrix, ffn_lookup_matrix, ffn_payload_matrix, ffn_acceptor_matrix, first_standardize_scaling, first_standardize_offset, acceptor_lerp_factor, lookup_lerp_factor, payload_lerp_factor, valve_lerp_factor, token_fading, diagonal_reward, subspace_standardize_scaling, subspace_standardize_offset, second_standardize_scaling, second_standardize_offset, ffn_lookup_lerp, ffn_acceptor_lerp, upstream_derivative):
    everything = (acceptor_matrix, lookup_matrix, payload_matrix, valve_matrix, result_matrix, ffn_lookup_matrix, ffn_payload_matrix, ffn_acceptor_matrix, first_standardize_scaling, first_standardize_offset, acceptor_lerp_factor, lookup_lerp_factor, payload_lerp_factor, valve_lerp_factor, token_fading, diagonal_reward, subspace_standardize_scaling, subspace_standardize_offset, second_standardize_scaling, second_standardize_offset, ffn_lookup_lerp, ffn_acceptor_lerp)
    learnable_collection = tuple((item.astype(jnp.float32) for item in everything))

    def one_sequence(totals, fragment_collection):
        row_input, document_labels, row_cot = fragment_collection

        def closed(row_in, param_list):
            return forward_one(row_in, param_list, document_labels)
        output, backward = jax.vjp(closed, row_input, learnable_collection)
        grad_row, grad_params = backward(row_cot)
        totals = tuple((left + right.astype(jnp.float32) for left, right in zip(totals, grad_params)))
        return (totals, (output.astype(jnp.bfloat16), grad_row.astype(jnp.float32)))
    zeros = tuple((jnp.zeros(item.shape, jnp.float32) for item in learnable_collection))
    totals, outputs = lax.scan(one_sequence, zeros, (entering_activations.astype(jnp.float32), document_indices.astype(jnp.int32), upstream_derivative.astype(jnp.float32)))
    result, grad_inputs = outputs
    return (result, grad_inputs, totals[0], totals[1], totals[2], totals[3], totals[4], totals[5], totals[6], totals[7], totals[8], totals[9], totals[10], totals[11], totals[12], totals[13], totals[14], totals[15], totals[16], totals[17], totals[18], totals[19], totals[20], totals[21])
```

```python
from functools import partial

import jax
import jax.numpy as jnp
from jax import lax
from jax.sharding import PartitionSpec as P

SUBSPACE_SIZE = 64
BLOCK = 64


HIGH = lax.Precision.HIGHEST
EPS = 1e-05
GROUP_EPS = 4.0


def shifted(x, axis, by):
    count = lax.axis_size(axis)
    pairs = [(i, i + by) for i in range(count) if 0 <= i + by < count]
    return lax.ppermute(x, axis, pairs)


def earlier_shift(x, axis, by):
    count = lax.axis_size(axis)
    return lax.ppermute(x, axis, [(i, i + by) for i in range(count) if 0 <= i + by < count])


def carried(mult, sums, axis, toward):
    count = lax.axis_size(axis)
    low = (mult.astype(jnp.bfloat16), sums.astype(jnp.bfloat16))
    arrived = [
        jax.tree.map(lambda part: earlier_shift(part, axis, toward * by), low)
        for by in range(1, count)
    ]
    state = jnp.zeros_like(sums)
    for far_mult, far_sums in reversed(arrived):
        state = far_mult.astype(jnp.float32)[..., None] * state + far_sums.astype(jnp.float32)
    return state


def partner(x, bit):
    count = lax.axis_size("tp")
    return lax.ppermute(x, "tp", [(i, i ^ bit) for i in range(count)])


def halves(x, axis, bit):
    size = x.shape[axis] // 2
    mine = (lax.axis_index("tp") // bit) % 2
    return (
        lax.dynamic_slice_in_dim(x, mine * size, size, axis),
        lax.dynamic_slice_in_dim(x, (1 - mine) * size, size, axis),
    )


def add_low(left, right):
    return (left.astype(jnp.float32) + right.astype(jnp.float32)).astype(jnp.bfloat16)


def ordered(mine, other, axis, bit):
    first = (lax.axis_index("tp") // bit) % 2 == 0
    return jnp.where(
        first,
        jnp.concatenate([mine, other], axis),
        jnp.concatenate([other, mine], axis),
    )


def tp_sum(x):
    mine, other = halves(x, 0, 1)
    part = add_low(mine, partner(other, 1))
    bit = 2
    while bit < lax.axis_size("tp"):
        part = add_low(part, partner(part, bit))
        bit *= 2
    return ordered(part, partner(part, 1), 0, 1)


def whole_sum(x, axes):
    for axis in axes:
        count = lax.axis_size(axis)
        bit = 1
        while bit < count:
            x = x + lax.ppermute(x, axis, [(i, i ^ bit) for i in range(count)])
            bit *= 2
    return x


def tp_scatter(x):
    count, place = lax.axis_size("tp"), lax.axis_index("tp")
    width = x.shape[1] // count
    parts = [
        lax.dynamic_slice_in_dim(x, (place ^ relative) * width, width, 1)
        for relative in range(count)
    ]
    bit = 1
    while bit < count:
        for relative in reversed(range(count)):
            if relative & bit and relative & (bit - 1) == 0:
                arrived = partner(parts[relative], bit)
                parts[relative ^ bit] = add_low(parts[relative ^ bit], arrived)
        bit *= 2
    return parts[0]


def tp_gather(x):
    count, place = lax.axis_size("tp"), lax.axis_index("tp")
    width = x.shape[1]
    parts = {0: x}
    bit = count // 2
    while bit:
        parts.update({relative ^ bit: partner(part, bit) for relative, part in parts.items()})
        bit //= 2
    whole = jnp.zeros((x.shape[0], width * count), x.dtype)
    for relative, part in parts.items():
        whole = lax.dynamic_update_slice_in_dim(whole, part, (place ^ relative) * width, 1)
    return whole


def after(value, *earlier):
    return lax.optimization_barrier((value,) + earlier)


def matmul(left, right):
    return jnp.dot(left, right, preferred_element_type=jnp.float32)


def matmul_tn(left, right):
    return lax.dot_general(
        left, right, (((0,), (0,)), ((), ())), preferred_element_type=jnp.float32
    )


def matmul_nt(left, right):
    return lax.dot_general(
        left, right, (((1,), (1,)), ((), ())), preferred_element_type=jnp.float32
    )


def fading_payload_tile(fading_exponent, reward_addend, memory_matrix_kept, fragment_collection):
    acceptor_entries, lookup_share, payload_share, seg_block, seg_start = fragment_collection
    length = acceptor_entries.shape[0]
    offsets = jnp.arange(length, dtype=jnp.float32)[:, None, None]
    rising = jnp.exp(offsets * fading_exponent)
    falling = jnp.exp(-(offsets + 1.0) * fading_exponent)
    closing = jnp.exp((float(length) - 1.0 - offsets) * fading_exponent)
    query_dec = acceptor_entries * rising
    key_dec = lookup_share * falling
    scores = jnp.einsum("thi,shi->hts", query_dec, key_dec, precision=HIGH)
    later_mask = (
        jnp.arange(length, dtype=jnp.int32)[:, None] > jnp.arange(length, dtype=jnp.int32)[None, :]
    )
    same_doc = seg_block[:, None] == seg_block[None, :]
    coefficient_collection = jnp.where(later_mask & same_doc, scores, jnp.zeros_like(scores))
    immediate_addend = jnp.sum(
        acceptor_entries * reward_addend * lookup_share, axis=-1, keepdims=True
    )
    live_mask = (seg_block == seg_start).astype(jnp.float32)[:, None, None]
    result = (
        jnp.einsum("hts,shj->thj", coefficient_collection, payload_share, precision=HIGH)
        + immediate_addend * payload_share
    )
    result = result + live_mask * jnp.einsum(
        "thi,hij->thj", query_dec, memory_matrix_kept, precision=HIGH
    )
    ending = (seg_block == seg_block[-1]).astype(jnp.float32)[:, None, None]
    key_end = lookup_share * closing * ending
    carried = jnp.exp(float(length) * fading_exponent) * live_mask[-1]
    new_state = carried[:, :, None] * memory_matrix_kept + jnp.einsum(
        "shi,shj->hij", key_end, payload_share, precision=HIGH
    )
    return (new_state, result)


def fading_payload_sweeper(
    acceptor_entries,
    lookup_share,
    payload_share,
    fading_coefficients,
    reward_coefficients,
    memory_matrix_kept,
    document_sweeper,
    document_begins,
):
    length = acceptor_entries.shape[0]
    blocks = length // BLOCK
    fading_exponent = jnp.log(fading_coefficients)

    def to_blocks(array):
        return array.reshape((blocks, BLOCK) + array.shape[1:])

    seg_blocks = document_sweeper.reshape(blocks, BLOCK)
    seg_starts = jnp.concatenate([document_begins, seg_blocks[:-1, -1]])
    scan_update = jax.checkpoint(partial(fading_payload_tile, fading_exponent, reward_coefficients))
    final_memory_matrix, block_outs = lax.scan(
        scan_update,
        memory_matrix_kept,
        (
            to_blocks(acceptor_entries),
            to_blocks(lookup_share),
            to_blocks(payload_share),
            seg_blocks,
            seg_starts,
        ),
    )
    return (block_outs.reshape(acceptor_entries.shape), final_memory_matrix)


def weighted_value_piece(
    segment_present,
    document_begins,
    acceptor_entries,
    lookup_share,
    payload_share,
    decay_quantity,
    reward_amount,
    incoming_state,
):
    mapped_function = jax.vmap(fading_payload_sweeper, in_axes=(0, 0, 0, None, None, 0, 0, 0))
    return mapped_function(
        acceptor_entries,
        lookup_share,
        payload_share,
        decay_quantity,
        reward_amount,
        incoming_state,
        segment_present,
        document_begins,
    )


def layer_norm(values, gain, bias_term):
    centered = values - jnp.mean(values, -1, keepdims=True)
    inverse = lax.rsqrt(jnp.mean(centered * centered, -1, keepdims=True) + EPS)
    unit_vals = centered * inverse
    return (unit_vals * gain + bias_term, unit_vals, inverse)


def norm_back(d_out, gain, unit_vals, inverse):
    scaled = d_out * gain
    d_in = inverse * (
        scaled
        - jnp.mean(scaled, -1, keepdims=True)
        - unit_vals * jnp.mean(scaled * unit_vals, -1, keepdims=True)
    )
    return (d_in, jnp.sum(d_out * unit_vals, axis=(0, 1)), jnp.sum(d_out, axis=(0, 1)))


def sharding_spec(vector, embedding_extent, start):
    return lax.dynamic_update_slice_in_dim(
        jnp.zeros((embedding_extent,), jnp.float32), vector.reshape(-1), start, 0
    )


def per_device(
    entering_activations,
    document_indices,
    acceptor_matrix,
    lookup_matrix,
    payload_matrix,
    valve_matrix,
    result_matrix,
    ffn_lookup_matrix,
    ffn_payload_matrix,
    ffn_acceptor_matrix,
    first_standardize_scaling,
    first_standardize_offset,
    acceptor_lerp_factor,
    lookup_lerp_factor,
    payload_lerp_factor,
    valve_lerp_factor,
    token_fading,
    diagonal_reward,
    subspace_standardize_scaling,
    subspace_standardize_offset,
    second_standardize_scaling,
    second_standardize_offset,
    ffn_lookup_lerp,
    ffn_acceptor_lerp,
    upstream_derivative,
):
    seqs_here, piece_len, embedding_extent = entering_activations.shape
    token_count = seqs_here * piece_len
    tp_count = lax.axis_size("tp")
    fourth_extent = embedding_extent // tp_count
    heads_here = fourth_extent // SUBSPACE_SIZE
    sharded_layout = lax.axis_index("tp") * fourth_extent
    ctx_place = lax.axis_index("ctx") * piece_len
    padded_seg = jnp.concatenate(
        [jnp.full((seqs_here, 1), -1, jnp.int32), document_indices], axis=1
    )
    segment_present = lax.dynamic_slice_in_dim(document_indices, ctx_place, piece_len, 1)
    seg_before = lax.dynamic_slice_in_dim(padded_seg, ctx_place, piece_len, 1)
    document_begins = seg_before[:, :1]
    keep_mask = (segment_present == seg_before).astype(jnp.float32)[:, :, None]
    owners = ("fsdp", "ctx")
    w_time = lax.all_gather(
        jnp.concatenate(
            [acceptor_matrix, lookup_matrix, payload_matrix, valve_matrix, result_matrix.T], axis=1
        ),
        owners,
        axis=0,
        tiled=True,
    )
    w_chan = lax.all_gather(
        jnp.concatenate([ffn_acceptor_matrix, ffn_lookup_matrix, ffn_payload_matrix.T], axis=1),
        owners,
        axis=0,
        tiled=True,
    )
    units = ffn_lookup_matrix.shape[1]
    w_recept, w_key, w_value, w_gate, w_output_t = (
        w_time[:, at * fourth_extent : (at + 1) * fourth_extent] for at in range(5)
    )
    w_chanrecept = w_chan[:, :fourth_extent]
    w_chankey = w_chan[:, fourth_extent : fourth_extent + units]
    w_chanvalue_t = w_chan[:, fourth_extent + units :]
    residual = entering_activations.astype(jnp.float32)
    normed, unit_one, inv_one = layer_norm(
        residual, first_standardize_scaling, first_standardize_offset
    )
    edge_one = shifted(normed[:, -1], "ctx", 1)
    prev_one = jnp.concatenate([edge_one[:, None], normed[:, :-1]], axis=1) * keep_mask
    delta_one = normed - prev_one
    mix_list = (acceptor_lerp_factor, lookup_lerp_factor, payload_lerp_factor, valve_lerp_factor)
    mixed_in = [
        (prev_one + mixer * delta_one).astype(jnp.bfloat16).reshape(token_count, embedding_extent)
        for mixer in mix_list
    ]
    recept_low = matmul(mixed_in[0], w_recept).astype(jnp.bfloat16)
    key_low = matmul(mixed_in[1], w_key).astype(jnp.bfloat16)
    value_low = matmul(mixed_in[2], w_value).astype(jnp.bfloat16)
    gate_pre = matmul(mixed_in[3], w_gate)
    gate_act = jax.nn.silu(gate_pre)
    split_shape = (seqs_here, piece_len, heads_here, SUBSPACE_SIZE)
    recept_f = recept_low.astype(jnp.float32).reshape(split_shape)
    key_f = key_low.astype(jnp.float32).reshape(split_shape)
    value_f = value_low.astype(jnp.float32).reshape(split_shape)
    decay_quantity = lax.dynamic_slice_in_dim(
        token_fading, sharded_layout, fourth_extent, 0
    ).reshape(heads_here, SUBSPACE_SIZE)
    reward_amount = lax.dynamic_slice_in_dim(
        diagonal_reward, sharded_layout, fourth_extent, 0
    ).reshape(heads_here, SUBSPACE_SIZE)
    ggain_q = lax.dynamic_slice_in_dim(
        subspace_standardize_scaling, sharded_layout, fourth_extent, 0
    ).reshape(heads_here, SUBSPACE_SIZE)
    gbias_q = lax.dynamic_slice_in_dim(
        subspace_standardize_offset, sharded_layout, fourth_extent, 0
    ).reshape(heads_here, SUBSPACE_SIZE)
    fading_exponent = jnp.log(decay_quantity)
    offsets = jnp.arange(piece_len, dtype=jnp.float32)[:, None, None]
    closing = jnp.exp((float(piece_len) - 1.0 - offsets) * fading_exponent)
    rising = jnp.exp(offsets * fading_exponent)
    ending = (segment_present == segment_present[:, -1:]).astype(jnp.float32)[:, :, None, None]
    carry_sums = jnp.einsum("bshi,bshj->bhij", key_f * closing * ending, value_f, precision=HIGH)
    alive_mask = (segment_present[:, -1] == document_begins[:, 0]).astype(jnp.float32)[
        :, None, None
    ]
    carry_mult = jnp.exp(float(piece_len) * fading_exponent) * alive_mask
    incoming = carried(carry_mult, carry_sums, "ctx", 1)
    wkv_out, weighted_value_backward = jax.vjp(
        partial(weighted_value_piece, segment_present, document_begins),
        recept_f,
        key_f,
        value_f,
        decay_quantity,
        reward_amount,
        incoming,
    )
    timemix_result = wkv_out[0]
    centered = timemix_result - jnp.mean(timemix_result, -1, keepdims=True)
    inv_group = lax.rsqrt(jnp.mean(centered * centered, -1, keepdims=True) + GROUP_EPS)
    unit_group = centered * inv_group
    grouped = (unit_group * ggain_q + gbias_q).reshape(token_count, fourth_extent)
    joined_low = (grouped * gate_act).astype(jnp.bfloat16)
    mixed_out = tp_sum(matmul_nt(joined_low, w_output_t).astype(jnp.bfloat16)).astype(jnp.float32)
    middle = residual + mixed_out.reshape(seqs_here, piece_len, embedding_extent)
    normed_two, unit_two, inv_two = layer_norm(
        middle, second_standardize_scaling, second_standardize_offset
    )
    edge_two = shifted(normed_two[:, -1], "ctx", 1)
    prev_two = jnp.concatenate([edge_two[:, None], normed_two[:, :-1]], axis=1) * keep_mask
    delta_two = normed_two - prev_two
    key_in = (
        (prev_two + ffn_lookup_lerp * delta_two)
        .astype(jnp.bfloat16)
        .reshape(token_count, embedding_extent)
    )
    rec_in = (
        (prev_two + ffn_acceptor_lerp * delta_two)
        .astype(jnp.bfloat16)
        .reshape(token_count, embedding_extent)
    )
    rec_gate = jax.nn.sigmoid(matmul(rec_in, w_chanrecept))
    d_result = upstream_derivative.astype(jnp.float32).reshape(token_count, fourth_extent)
    d_chan = (d_result * rec_gate).astype(jnp.bfloat16)
    d_chan_full = tp_gather(d_chan)
    key_pre = matmul(key_in, w_chankey)
    hidden = jnp.square(jax.nn.relu(key_pre)).astype(jnp.bfloat16)
    grad_chanvalue = matmul_tn(hidden, d_chan_full).astype(jnp.bfloat16)
    g_chanvalue = lax.psum_scatter(grad_chanvalue, owners, scatter_dimension=1, tiled=True)
    hidden, grad_chanvalue = after(hidden, grad_chanvalue)
    chan_sum = tp_scatter(matmul_nt(hidden, w_chanvalue_t).astype(jnp.bfloat16)).astype(jnp.float32)
    middle_q = lax.dynamic_slice_in_dim(
        middle.reshape(token_count, embedding_extent), sharded_layout, fourth_extent, 1
    )
    result = (
        (middle_q + rec_gate * chan_sum)
        .astype(jnp.bfloat16)
        .reshape(seqs_here, piece_len, fourth_extent)
    )
    d_rec_pre = (d_result * chan_sum * rec_gate * (1.0 - rec_gate)).astype(jnp.bfloat16)
    d_hidden = matmul(d_chan_full, w_chanvalue_t)
    d_key_pre = (d_hidden * 2.0 * jax.nn.relu(key_pre)).astype(jnp.bfloat16)
    grad_chankey = matmul_tn(key_in, d_key_pre)
    grad_chanrecept = matmul_tn(rec_in, d_rec_pre)
    full_shape = (seqs_here, piece_len, embedding_extent)
    d_key_in = matmul_nt(d_key_pre, w_chankey).reshape(full_shape)
    d_rec_in = matmul_nt(d_rec_pre, w_chanrecept).reshape(full_shape)
    d_norm_two = d_key_in * ffn_lookup_lerp + d_rec_in * ffn_acceptor_lerp
    d_prev_two = (
        d_key_in * (1.0 - ffn_lookup_lerp) + d_rec_in * (1.0 - ffn_acceptor_lerp)
    ) * keep_mask
    back_two = shifted(d_prev_two[:, 0], "ctx", -1)
    d_norm_two = d_norm_two + jnp.concatenate([d_prev_two[:, 1:], back_two[:, None]], axis=1)
    d_middle_part, g_second_gain, g_second_bias = norm_back(
        d_norm_two, second_standardize_scaling, unit_two, inv_two
    )
    chan_small_part = jnp.stack(
        [
            g_second_gain,
            g_second_bias,
            jnp.sum(d_key_in * delta_two, axis=(0, 1)),
            jnp.sum(d_rec_in * delta_two, axis=(0, 1)),
        ]
    )
    flat_part = d_middle_part.reshape(token_count, embedding_extent)
    own_cols = lax.dynamic_slice_in_dim(flat_part, sharded_layout, fourth_extent, 1) + d_result
    flat_part = lax.dynamic_update_slice_in_dim(flat_part, own_cols, sharded_layout, 1)
    d_mixed = tp_sum(flat_part.astype(jnp.bfloat16))
    grad_output_t = matmul_tn(d_mixed, joined_low)
    grads_chan = jnp.concatenate(
        [item.astype(jnp.bfloat16) for item in (grad_output_t, grad_chanrecept, grad_chankey)],
        axis=1,
    )
    d_mixed, grads_chan, g_chanvalue = after(d_mixed, grads_chan, g_chanvalue)
    d_middle = d_mixed.astype(jnp.float32)
    g_chan = lax.psum_scatter(grads_chan, owners, scatter_dimension=0, tiled=True)
    d_joined = matmul(d_mixed, w_output_t)
    d_gate_act = d_joined * grouped
    d_grouped = (d_joined * gate_act).reshape(split_shape)
    attention_gradient, g_ggain, g_gbias = norm_back(d_grouped, ggain_q, unit_group, inv_group)
    gate_sig = jax.nn.sigmoid(gate_pre)
    d_gate_pre = (d_gate_act * gate_sig * (1.0 + gate_pre * (1.0 - gate_sig))).astype(jnp.bfloat16)
    live_mask = (segment_present == document_begins).astype(jnp.float32)[:, :, None, None]
    local_grad = jnp.einsum(
        "bthi,bthj->bhij", recept_f * rising * live_mask, attention_gradient, precision=HIGH
    )
    outgoing_state = carried(carry_mult, local_grad, "ctx", -1)
    (
        receptance_gradient,
        key_gradient,
        value_gradient,
        decay_gradient,
        reward_derivative,
        discarded_state,
    ) = weighted_value_backward((attention_gradient, outgoing_state))
    d_lows = [
        item.astype(jnp.bfloat16).reshape(token_count, fourth_extent)
        for item in (receptance_gradient, key_gradient, value_gradient)
    ] + [d_gate_pre]
    weights_time = (w_recept, w_key, w_value, w_gate)
    grads_time = jnp.concatenate(
        [
            matmul_tn(mixed, grad_low).astype(jnp.bfloat16)
            for mixed, grad_low in zip(mixed_in, d_lows)
        ],
        axis=1,
    )
    *d_lows, grads_time, g_chan = after(d_lows[0], *d_lows[1:], grads_time, g_chan)
    g_time = lax.psum_scatter(grads_time, owners, scatter_dimension=0, tiled=True)
    d_mix_ins = [
        matmul_nt(grad_low, weight).reshape(full_shape)
        for grad_low, weight in zip(d_lows, weights_time)
    ]
    d_norm_one = sum((grad_in * mixer for grad_in, mixer in zip(d_mix_ins, mix_list)))
    d_prev_one = (
        sum((grad_in * (1.0 - mixer) for grad_in, mixer in zip(d_mix_ins, mix_list))) * keep_mask
    )
    back_one = shifted(d_prev_one[:, 0], "ctx", -1)
    d_norm_one = d_norm_one + jnp.concatenate([d_prev_one[:, 1:], back_one[:, None]], axis=1)
    d_input_part, g_first_gain, g_first_bias = norm_back(
        d_norm_one, first_standardize_scaling, unit_one, inv_one
    )
    time_small_part = jnp.stack(
        [g_first_gain, g_first_bias]
        + [jnp.sum(grad_in * delta_one, axis=(0, 1)) for grad_in in d_mix_ins]
        + [
            sharding_spec(decay_gradient, embedding_extent, sharded_layout),
            sharding_spec(reward_derivative, embedding_extent, sharded_layout),
            sharding_spec(g_ggain, embedding_extent, sharded_layout),
            sharding_spec(g_gbias, embedding_extent, sharded_layout),
        ]
    )
    small_sum = whole_sum(
        jnp.concatenate([time_small_part, chan_small_part], axis=0), ("tp", "fsdp", "ctx")
    )
    owned = embedding_extent // (lax.axis_size("fsdp") * lax.axis_size("ctx"))
    small_owned = lax.dynamic_slice_in_dim(
        small_sum, (lax.axis_index("fsdp") * lax.axis_size("ctx") + lax.axis_index("ctx")) * owned, owned, 1
    )
    d_input_sum = tp_sum(
        d_input_part.reshape(token_count, embedding_extent).astype(jnp.bfloat16)
    ).astype(jnp.float32)
    grad_inputs = (d_middle + d_input_sum).reshape(full_shape)
    g_chanvalue = g_chanvalue.astype(jnp.float32)
    g_chan = g_chan.astype(jnp.float32)
    g_time = g_time.astype(jnp.float32)
    g_recept, g_key, g_value, g_gate = (
        g_time[:, at * fourth_extent : (at + 1) * fourth_extent] for at in range(4)
    )
    g_output = g_chan[:, :fourth_extent].T
    g_chanrecept = g_chan[:, fourth_extent : 2 * fourth_extent]
    g_chankey = g_chan[:, 2 * fourth_extent :]
    return (
        result,
        grad_inputs,
        g_recept,
        g_key,
        g_value,
        g_gate,
        g_output,
        g_chankey,
        g_chanvalue,
        g_chanrecept,
        small_owned[0],
        small_owned[1],
        small_owned[2],
        small_owned[3],
        small_owned[4],
        small_owned[5],
        small_owned[6],
        small_owned[7],
        small_owned[8],
        small_owned[9],
        small_owned[10],
        small_owned[11],
        small_owned[12],
        small_owned[13],
    )


def solution(mesh):
    return jax.shard_map(
        per_device,
        mesh=mesh,
        in_specs=(
            P("fsdp", "ctx", None),
            P("fsdp", None),
            P(("fsdp", "ctx"), "tp"),
            P(("fsdp", "ctx"), "tp"),
            P(("fsdp", "ctx"), "tp"),
            P(("fsdp", "ctx"), "tp"),
            P("tp", ("fsdp", "ctx")),
            P(("fsdp", "ctx"), "tp"),
            P("tp", ("fsdp", "ctx")),
            P(("fsdp", "ctx"), "tp"),
            P(),
            P(),
            P(),
            P(),
            P(),
            P(),
            P(),
            P(),
            P(),
            P(),
            P(),
            P(),
            P(),
            P(),
            P("fsdp", "ctx", "tp"),
        ),
        out_specs=(
            P("fsdp", "ctx", "tp"),
            P("fsdp", "ctx", None),
            P(("fsdp", "ctx"), "tp"),
            P(("fsdp", "ctx"), "tp"),
            P(("fsdp", "ctx"), "tp"),
            P(("fsdp", "ctx"), "tp"),
            P("tp", ("fsdp", "ctx")),
            P(("fsdp", "ctx"), "tp"),
            P("tp", ("fsdp", "ctx")),
            P(("fsdp", "ctx"), "tp"),
            P(("fsdp", "ctx")),
            P(("fsdp", "ctx")),
            P(("fsdp", "ctx")),
            P(("fsdp", "ctx")),
            P(("fsdp", "ctx")),
            P(("fsdp", "ctx")),
            P(("fsdp", "ctx")),
            P(("fsdp", "ctx")),
            P(("fsdp", "ctx")),
            P(("fsdp", "ctx")),
            P(("fsdp", "ctx")),
            P(("fsdp", "ctx")),
            P(("fsdp", "ctx")),
            P(("fsdp", "ctx")),
        ),
        check_vma=False,
    )
```

```python
from functools import partial

import jax
import jax.numpy as jnp
from jax import lax
from jax.experimental import pallas as pl
from jax.experimental.pallas import tpu as pltpu
from jax.sharding import PartitionSpec as P

SUBSPACE_SIZE = 64
PAIR = 128
GROUP = 16
TILE = 256


EPS = 1e-05
GROUP_EPS = 4.0


def shifted(x, axis, by):
    count = lax.axis_size(axis)
    pairs = [(i, i + by) for i in range(count) if 0 <= i + by < count]
    return lax.ppermute(x, axis, pairs)


def earlier_shift(x, axis, by):
    count = lax.axis_size(axis)
    return lax.ppermute(x, axis, [(i, i + by) for i in range(count) if 0 <= i + by < count])


def carried(mult, sums, axis, toward):
    count = lax.axis_size(axis)
    low = (mult.astype(jnp.bfloat16), sums.astype(jnp.bfloat16))
    arrived = [
        jax.tree.map(lambda part: earlier_shift(part, axis, toward * by), low)
        for by in range(1, count)
    ]
    state = jnp.zeros_like(sums)
    for far_mult, far_sums in reversed(arrived):
        state = far_mult.astype(jnp.float32) * state + far_sums.astype(jnp.float32)
    return state


def partner(x, bit):
    count = lax.axis_size("tp")
    return lax.ppermute(x, "tp", [(i, i ^ bit) for i in range(count)])


def halves(x, axis, bit):
    size = x.shape[axis] // 2
    mine = (lax.axis_index("tp") // bit) % 2
    return (
        lax.dynamic_slice_in_dim(x, mine * size, size, axis),
        lax.dynamic_slice_in_dim(x, (1 - mine) * size, size, axis),
    )


def add_low(left, right):
    return (left.astype(jnp.float32) + right.astype(jnp.float32)).astype(jnp.bfloat16)


def ordered(mine, other, axis, bit):
    first = (lax.axis_index("tp") // bit) % 2 == 0
    return jnp.where(
        first,
        jnp.concatenate([mine, other], axis),
        jnp.concatenate([other, mine], axis),
    )


def tp_sum(x):
    mine, other = halves(x, 0, 1)
    part = add_low(mine, partner(other, 1))
    bit = 2
    while bit < lax.axis_size("tp"):
        part = add_low(part, partner(part, bit))
        bit *= 2
    return ordered(part, partner(part, 1), 0, 1)


def whole_sum(x, axes):
    for axis in axes:
        count = lax.axis_size(axis)
        bit = 1
        while bit < count:
            x = x + lax.ppermute(x, axis, [(i, i ^ bit) for i in range(count)])
            bit *= 2
    return x


def tp_scatter(x):
    count, place = lax.axis_size("tp"), lax.axis_index("tp")
    width = x.shape[1] // count
    parts = [
        lax.dynamic_slice_in_dim(x, (place ^ relative) * width, width, 1)
        for relative in range(count)
    ]
    bit = 1
    while bit < count:
        for relative in reversed(range(count)):
            if relative & bit and relative & (bit - 1) == 0:
                arrived = partner(parts[relative], bit)
                parts[relative ^ bit] = add_low(parts[relative ^ bit], arrived)
        bit *= 2
    return parts[0]


def tp_gather(x):
    count, place = lax.axis_size("tp"), lax.axis_index("tp")
    width = x.shape[1]
    parts = {0: x}
    bit = count // 2
    while bit:
        parts.update({relative ^ bit: partner(part, bit) for relative, part in parts.items()})
        bit //= 2
    whole = jnp.zeros((x.shape[0], width * count), x.dtype)
    for relative, part in parts.items():
        whole = lax.dynamic_update_slice_in_dim(whole, part, (place ^ relative) * width, 1)
    return whole


def after(value, *earlier):
    return lax.optimization_barrier((value,) + earlier)


def matmul(left, right):
    return jnp.dot(left, right, preferred_element_type=jnp.float32)


def matmul_tn(left, right):
    return lax.dot_general(
        left, right, (((0,), (0,)), ((), ())), preferred_element_type=jnp.float32
    )


def matmul_nt(left, right):
    return lax.dot_general(
        left, right, (((1,), (1,)), ((), ())), preferred_element_type=jnp.float32
    )


def dot_nn(left, right):
    return lax.dot_general(
        left, right, (((1,), (0,)), ((), ())), preferred_element_type=jnp.float32
    )


def lanes_of(shape):
    return lax.broadcasted_iota(jnp.int32, shape, len(shape) - 1)


def low_head(shape):
    return lanes_of(shape) < SUBSPACE_SIZE


def head_sum(x):
    first = low_head(x.shape)
    low = jnp.sum(jnp.where(first, x, 0.0), -1, keepdims=True)
    high = jnp.sum(jnp.where(first, 0.0, x), -1, keepdims=True)
    return jnp.where(first, low, high)


def fold_pair(both):
    return jnp.where(
        low_head((SUBSPACE_SIZE, PAIR)), both[:SUBSPACE_SIZE], both[SUBSPACE_SIZE:]
    )


def spread_pair(folded):
    first = low_head((SUBSPACE_SIZE, PAIR))
    return jnp.concatenate(
        [jnp.where(first, folded, 0.0), jnp.where(first, 0.0, folded)], axis=0
    ).astype(jnp.bfloat16)


def head_parts(x):
    first = low_head(x.shape)
    zero = jnp.zeros_like(x)
    return jnp.where(first, x, zero), jnp.where(first, zero, x)


def places(length):
    return lax.broadcasted_iota(jnp.int32, (length, PAIR), 0).astype(jnp.float32)


def carry_kernel(k_ref, v_ref, log_ref, cols_ref, out_ref):
    length = k_ref.shape[0]
    closing = jnp.exp((length - 1.0 - places(length)) * log_ref[...])
    ending = cols_ref[:, 2:3]
    k_end = (k_ref[...].astype(jnp.float32) * closing * ending).astype(jnp.bfloat16)
    out_ref[0, 0] = fold_pair(matmul_tn(v_ref[...], k_end))


def group_norm(attend):
    centered = attend - head_sum(attend) * (1.0 / SUBSPACE_SIZE)
    inverse = lax.rsqrt(head_sum(centered * centered) * (1.0 / SUBSPACE_SIZE) + GROUP_EPS)
    return centered * inverse, inverse


def mix_kernel(
    r_ref, k_ref, v_ref, gate_ref, log_ref, rows_ref, cols_ref, seg_ref, state_ref,
    joined_ref, attend_ref,
):
    length = r_ref.shape[0]
    at = places(length)
    log = log_ref[...]
    r = r_ref[...].astype(jnp.float32)
    k = k_ref[...].astype(jnp.float32)
    v = v_ref[...]
    q_low = (r * jnp.exp(at * log)).astype(jnp.bfloat16)
    k_low = (k * jnp.exp(-(at + 1.0) * log)).astype(jnp.bfloat16)
    state = spread_pair(state_ref[0, 0])
    bonus = head_sum(r * rows_ref[0:1, :] * k)
    base = bonus * v.astype(jnp.float32) + cols_ref[:, 1:2] * matmul_nt(q_low, state)
    step = min(length, TILE)
    for top in range(0, length, step):
        reach = top + step
        rows = slice(top, reach)
        keep = pair_mask(cols_ref[rows, 0:1], seg_ref[0, :, :reach], top, step, reach)
        parts = []
        for q_part in head_parts(q_low[rows]):
            scores = matmul_nt(q_part, k_low[:reach])
            scores = jnp.where(keep, scores, 0.0).astype(jnp.bfloat16)
            parts.append(dot_nn(scores, v[:reach]))
        attend = base[rows] + jnp.where(low_head(parts[0].shape), parts[0], parts[1])
        unit, _ = group_norm(attend)
        grouped = unit * rows_ref[1:2, :] + rows_ref[2:3, :]
        gate = gate_ref[rows, :]
        attend_ref[rows, :] = attend
        joined_ref[rows, :] = (grouped * (gate * jax.nn.sigmoid(gate))).astype(jnp.bfloat16)


def pair_mask(seg_col, seg_row, top, count, reach):
    later = lax.broadcasted_iota(jnp.int32, (count, reach), 0) + top
    return (seg_col == seg_row) & (later > lanes_of((count, reach)))


def pair_mask_t(seg_col, seg_row, top, count, start):
    width = seg_row.shape[1]
    earlier = lax.broadcasted_iota(jnp.int32, (count, width), 0) + top
    return (seg_col == seg_row) & (lanes_of((count, width)) + start > earlier)


def gate_back_kernel(
    dj_ref, attend_ref, gate_ref, r_ref, log_ref, rows_ref, cols_ref,
    dgate_ref, dattend_ref, state_ref, small_ref,
):
    length = r_ref.shape[0]
    d_joined = dj_ref[...]
    gate = gate_ref[...]
    unit, inverse = group_norm(attend_ref[...])
    gain = rows_ref[1:2, :]
    grouped = unit * gain + rows_ref[2:3, :]
    sig = jax.nn.sigmoid(gate)
    dgate_ref[...] = (d_joined * grouped * sig * (1.0 + gate * (1.0 - sig))).astype(jnp.bfloat16)
    d_grouped = d_joined * gate * sig
    sums = [
        jnp.sum(d_grouped * unit, axis=0, keepdims=True),
        jnp.sum(d_grouped, axis=0, keepdims=True),
    ]
    scaled = d_grouped * gain
    share = 1.0 / SUBSPACE_SIZE
    d_attend = (
        inverse * (scaled - head_sum(scaled) * share - unit * (head_sum(scaled * unit) * share))
    ).astype(jnp.bfloat16)
    dattend_ref[...] = d_attend
    rising = jnp.exp(places(length) * log_ref[...])
    q_live = (r_ref[...].astype(jnp.float32) * rising * cols_ref[:, 1:2]).astype(jnp.bfloat16)
    state_ref[0, 0] = fold_pair(matmul_tn(d_attend, q_live))
    collect(small_ref, sums)


def collect(small_ref, sums):
    pad = jnp.zeros((small_ref.shape[0] - len(sums), sums[0].shape[1]), jnp.float32)
    total = jnp.concatenate(sums + [pad], axis=0)

    @pl.when(pl.program_id(1) == 0)
    def _():
        small_ref[...] = total

    @pl.when(pl.program_id(1) > 0)
    def _():
        small_ref[...] += total


def mix_back_kernel(
    r_ref, k_ref, v_ref, da_ref, log_ref, rows_ref, cols_ref, seg_ref, state_ref, gstate_ref,
    mult_ref, dr_ref, dk_ref, dv_ref, small_ref,
):
    length = r_ref.shape[0]
    at = places(length)
    log = log_ref[...]
    reward = rows_ref[0:1, :]
    r = r_ref[...].astype(jnp.float32)
    k = k_ref[...].astype(jnp.float32)
    v = v_ref[...]
    da = da_ref[...]
    rising = jnp.exp(at * log)
    falling = jnp.exp(-(at + 1.0) * log)
    closing = jnp.exp((length - 1.0 - at) * log) * cols_ref[:, 2:3]
    q_low = (r * rising).astype(jnp.bfloat16)
    k_low = (k * falling).astype(jnp.bfloat16)
    k_end = (k * closing).astype(jnp.bfloat16)
    state, gstate = state_ref[0, 0], gstate_ref[0, 0]
    state_low, gstate_low = spread_pair(state), spread_pair(gstate)
    v_f, da_f = v.astype(jnp.float32), da.astype(jnp.float32)
    dot_va = head_sum(v_f * da_f)
    dk_end = dot_nn(v, gstate_low)
    dq_base = cols_ref[:, 1:2] * dot_nn(da, state_low)
    dv_base = head_sum(r * reward * k) * da_f + matmul_nt(k_end, gstate_low)
    q_f, k_f = q_low.astype(jnp.float32), k_low.astype(jnp.float32)
    d_log = jnp.sum((length - 1.0 - at) * k_end.astype(jnp.float32) * dk_end, 0, keepdims=True)
    d_log += length * mult_ref[0, 0] * jnp.sum(
        state.astype(jnp.bfloat16).astype(jnp.float32)
        * gstate.astype(jnp.bfloat16).astype(jnp.float32),
        0,
        keepdims=True,
    )
    step = min(length, TILE)
    for top in range(0, length, step):
        rows = slice(top, top + step)
        reach = top + step
        keep = pair_mask(cols_ref[rows, 0:1], seg_ref[0, :, :reach], top, step, reach)
        dq = []
        for da_part in head_parts(da[rows]):
            pull = jnp.where(keep, matmul_nt(da_part, v[:reach]), 0.0).astype(jnp.bfloat16)
            dq.append(dot_nn(pull, k_low[:reach]))
        first = low_head(dq[0].shape)
        dq = jnp.where(first, dq[0], dq[1]) + dq_base[rows]
        d_log += jnp.sum(at[rows] * q_f[rows] * dq, 0, keepdims=True)
        dr_ref[rows, :] = (dq * rising[rows] + reward * k[rows] * dot_va[rows]).astype(jnp.bfloat16)
        keep = pair_mask_t(cols_ref[rows, 0:1], seg_ref[0, :, top:], top, step, top)
        dk, dv = [], []
        for v_part, k_part in zip(head_parts(v[rows]), head_parts(k_low[rows])):
            pull = jnp.where(keep, matmul_nt(v_part, da[top:]), 0.0).astype(jnp.bfloat16)
            dk.append(dot_nn(pull, q_low[top:]))
            scores = jnp.where(keep, matmul_nt(k_part, q_low[top:]), 0.0).astype(jnp.bfloat16)
            dv.append(dot_nn(scores, da[top:]))
        dk = jnp.where(first, dk[0], dk[1])
        d_log -= jnp.sum((at[rows] + 1.0) * k_f[rows] * dk, 0, keepdims=True)
        dk_ref[rows, :] = (
            dk * falling[rows]
            + dk_end[rows] * closing[rows]
            + reward * r[rows] * dot_va[rows]
        ).astype(jnp.bfloat16)
        dv_ref[rows, :] = (jnp.where(first, dv[0], dv[1]) + dv_base[rows]).astype(jnp.bfloat16)
    collect(small_ref, [d_log * jnp.exp(-log), jnp.sum(r * k * dot_va, 0, keepdims=True)])


def pair_call(kernel, seqs, length, width, operands, outs, name, flops):
    pairs = width // PAIR
    specs = {
        "wide": pl.BlockSpec((length, PAIR), lambda p, s: (s, p)),
        "vector": pl.BlockSpec((1, PAIR), lambda p, s: (0, p)),
        "vectors": pl.BlockSpec((8, PAIR), lambda p, s: (0, p)),
        "cols": pl.BlockSpec((length, 4), lambda p, s: (s, 0)),
        "row": pl.BlockSpec((1, 1, length), lambda p, s: (s, 0, 0)),
        "state": pl.BlockSpec((1, 1, SUBSPACE_SIZE, PAIR), lambda p, s: (s, p, 0, 0)),
        "mult": pl.BlockSpec((1, 1, 1, PAIR), lambda p, s: (s, p, 0, 0)),
    }
    shapes = {
        "wide": (seqs * length, width),
        "vectors": (8, width),
        "state": (seqs, pairs, SUBSPACE_SIZE, PAIR),
    }
    kinds, arrays = zip(*operands)
    size = sum(array.size * array.dtype.itemsize for array in arrays)
    return pl.pallas_call(
        kernel,
        grid=(pairs, seqs),
        in_specs=[specs[kind] for kind in kinds],
        out_specs=[specs[kind] for kind, _ in outs],
        out_shape=[jax.ShapeDtypeStruct(shapes[kind], dtype) for kind, dtype in outs],
        cost_estimate=pl.CostEstimate(flops=flops, bytes_accessed=2 * size, transcendentals=0),
        name=name,
    )(*arrays)


def norm_rows(x, gain, bias_term):
    centered = x - jnp.mean(x, -1, keepdims=True)
    inverse = lax.rsqrt(jnp.mean(centered * centered, -1, keepdims=True) + EPS)
    unit = centered * inverse
    return unit * gain + bias_term, unit, inverse


def total_rows(refs, rows):
    total = refs[0][rows, :].astype(jnp.float32)
    for ref in refs[1:]:
        total = total + ref[rows, :].astype(jnp.float32)
    return total


def blend_kernel(parts, mixes, per_seq, *refs):
    x_refs, refs = refs[:parts], refs[parts:]
    keep_ref, edge_ref, norm_ref, mix_ref = refs[:4]
    outs, before = refs[4 : 4 + mixes], refs[4 + mixes]
    rows = x_refs[0].shape[0]

    @pl.when(pl.program_id(0) % per_seq == 0)
    def _():
        before[...] = jnp.broadcast_to(edge_ref[0], before.shape)

    def group(g, _):
        place = pl.ds(pl.multiple_of(g * GROUP, GROUP), GROUP)
        normed, _, _ = norm_rows(total_rows(x_refs, place), norm_ref[0:1, :], norm_ref[1:2, :])
        top = lax.broadcasted_iota(jnp.int32, normed.shape, 0) == 0
        previous = jnp.where(top, before[0:1, :], pltpu.roll(normed, 1, 0)) * keep_ref[place, 0:1]
        before[0:1, :] = normed[GROUP - 1 :, :]
        delta = normed - previous
        for at, out in enumerate(outs):
            out[place, :] = (previous + mix_ref[at : at + 1, :] * delta).astype(jnp.bfloat16)
        return 0

    lax.fori_loop(0, rows // GROUP, group, 0)


def blend(xs, keep, edge, norm, mixers, piece, name):
    tokens, width = xs[0].shape
    rows = min(piece, 256)
    mixes = mixers.shape[0]
    per_seq = piece // rows
    wide = pl.BlockSpec((rows, width), lambda i: (i, 0))
    return pl.pallas_call(
        partial(blend_kernel, len(xs), mixes, per_seq),
        grid=(tokens // rows,),
        in_specs=[wide] * len(xs)
        + [
            pl.BlockSpec((rows, 1), lambda i: (i, 0)),
            pl.BlockSpec((1, 1, width), lambda i: (i // per_seq, 0, 0)),
            pl.BlockSpec((2, width), lambda i: (0, 0)),
            pl.BlockSpec((mixes, width), lambda i: (0, 0)),
        ],
        out_specs=[wide] * mixes,
        out_shape=[jax.ShapeDtypeStruct((tokens, width), jnp.bfloat16)] * mixes,
        scratch_shapes=[pltpu.VMEM((8, width), jnp.float32)],
        cost_estimate=pl.CostEstimate(
            flops=20 * tokens * width,
            bytes_accessed=2 * tokens * width * (len(xs) + mixes),
            transcendentals=0,
        ),
        name=name,
    )(*xs, keep, edge, norm, mixers)


def blend_back_kernel(parts, mixes, per_seq, own, *refs):
    x_refs, refs = refs[:parts], refs[parts:]
    halo_refs, refs = refs[:parts], refs[parts:]
    grad_refs, refs = refs[:mixes], refs[mixes:]
    weight_refs, refs = refs[:mixes], refs[mixes:]
    keep_ref, edge_ref, back_ref, norm_ref, mix_ref = refs[:5]
    refs = refs[5:]
    own_refs, refs = refs[: 2 * own], refs[2 * own :]
    out_ref, small_ref, d_scr, unit_scr, inv_scr, sums, after_row = refs
    rows, width = x_refs[0].shape
    tiles = pl.num_programs(0)
    tile = tiles - 1 - pl.program_id(0)
    gain, bias_term = norm_ref[0:1, :], norm_ref[1:2, :]

    @pl.when(pl.program_id(0) == 0)
    def _():
        sums[...] = jnp.zeros_like(sums)

    @pl.when(tile % per_seq == per_seq - 1)
    def _():
        after_row[...] = jnp.broadcast_to(back_ref[0], after_row.shape)

    for at in range(mixes):
        d_scr[at] = matmul_nt(grad_refs[at][...], weight_refs[at][...])

    halo, _, _ = norm_rows(total_rows(halo_refs, slice(None)), gain, bias_term)
    first = jnp.where(tile % per_seq == 0, edge_ref[0], halo[GROUP - 1 :, :])

    def unit_group(g, _):
        place = pl.ds(pl.multiple_of(g * GROUP, GROUP), GROUP)
        _, unit, inverse = norm_rows(total_rows(x_refs, place), gain, bias_term)
        unit_scr[place, :] = unit
        inv_scr[place, :] = jnp.broadcast_to(inverse, (GROUP, inv_scr.shape[1]))
        return 0

    groups = rows // GROUP
    lax.fori_loop(0, groups, unit_group, 0)

    def group(step, _):
        g = groups - 1 - step
        start = pl.multiple_of(g * GROUP, GROUP)
        place = pl.ds(start, GROUP)
        unit = unit_scr[place, :]
        inverse = inv_scr[place, 0:1]
        keep = keep_ref[place, 0:1]
        normed = unit * gain + bias_term
        before_at = pl.multiple_of(jnp.maximum(start - 8, 0), 8)
        inside = unit_scr[pl.ds(before_at, 8), :][7:8, :] * gain + bias_term
        before = jnp.where(g == 0, first, inside)
        place_in = lax.broadcasted_iota(jnp.int32, normed.shape, 0)
        delta = normed - jnp.where(place_in == 0, before, pltpu.roll(normed, 1, 0)) * keep
        d_norm = jnp.zeros_like(normed)
        d_all = jnp.zeros_like(normed)
        for at in range(mixes):
            d_in = d_scr[at, place, :]
            d_norm = d_norm + d_in * mix_ref[at : at + 1, :]
            d_all = d_all + d_in
            product = d_in * delta
            sums[2 + at] += product[:8] + product[8:]
        d_prev = (d_all - d_norm) * keep
        d_next = jnp.where(
            place_in == GROUP - 1, after_row[0:1, :], pltpu.roll(d_prev, GROUP - 1, 0)
        )
        after_row[0:1, :] = d_prev[0:1, :]
        d_norm = d_norm + d_next
        product = d_norm * unit
        sums[0] += product[:8] + product[8:]
        sums[1] += d_norm[:8] + d_norm[8:]
        scaled = d_norm * gain
        d_in = inverse * (
            scaled
            - jnp.mean(scaled, -1, keepdims=True)
            - unit * jnp.mean(scaled * unit, -1, keepdims=True)
        )
        if own:
            extra = own_refs[0][place, :].astype(jnp.float32)
            extra = jnp.concatenate([extra] * (width // extra.shape[1]), axis=1)
            d_in = d_in + extra * own_refs[1][...]
        out_ref[place, :] = d_in.astype(jnp.bfloat16)
        return 0

    lax.fori_loop(0, groups, group, 0)

    @pl.when(pl.program_id(0) == tiles - 1)
    def _():
        for at in range(2 + mixes):
            small_ref[at : at + 1, :] = jnp.sum(sums[at], 0, keepdims=True)


def blend_back(xs, grads, weights, keep, edge, back, norm, mixers, piece, own, name):
    tokens, width = xs[0].shape
    rows = min(piece, 128)
    mixes = mixers.shape[0]
    per_seq = piece // rows
    tiles = tokens // rows

    def reverse(i):
        return tiles - 1 - i

    def halo_at(i):
        return (jnp.maximum(reverse(i) * (rows // GROUP) - 1, 0), 0)

    wide = pl.BlockSpec((rows, width), lambda i: (reverse(i), 0))
    per = pl.BlockSpec((1, 1, width), lambda i: (reverse(i) // per_seq, 0, 0))
    weight_specs, weight_arrays = [], []
    for (array, at), grad in zip(weights, grads):
        weight_specs.append(
            pl.BlockSpec(
                (width, grad.shape[1]), partial(lambda at, i: (0, at), at),
                pipeline_mode=pl.Buffered(1),
            )
        )
        weight_arrays.append(array)
    return pl.pallas_call(
        partial(blend_back_kernel, len(xs), mixes, per_seq, int(own is not None)),
        grid=(tiles,),
        in_specs=[wide] * len(xs)
        + [pl.BlockSpec((GROUP, width), halo_at)] * len(xs)
        + [pl.BlockSpec((rows, grad.shape[1]), lambda i: (reverse(i), 0)) for grad in grads]
        + weight_specs
        + [
            pl.BlockSpec((rows, 1), lambda i: (reverse(i), 0)),
            per,
            per,
            pl.BlockSpec((2, width), lambda i: (0, 0)),
            pl.BlockSpec((mixes, width), lambda i: (0, 0)),
        ]
        + (
            [
                pl.BlockSpec((rows, own[0].shape[1]), lambda i: (reverse(i), 0)),
                pl.BlockSpec((1, width), lambda i: (0, 0)),
            ]
            if own is not None
            else []
        ),
        out_specs=[wide, pl.BlockSpec((8, width), lambda i: (0, 0))],
        out_shape=[
            jax.ShapeDtypeStruct((tokens, width), jnp.bfloat16),
            jax.ShapeDtypeStruct((8, width), jnp.float32),
        ],
        scratch_shapes=[
            pltpu.VMEM((mixes, rows, width), jnp.float32),
            pltpu.VMEM((rows, width), jnp.float32),
            pltpu.VMEM((rows, PAIR), jnp.float32),
            pltpu.VMEM((2 + mixes, 8, width), jnp.float32),
            pltpu.VMEM((8, width), jnp.float32),
        ],
        cost_estimate=pl.CostEstimate(
            flops=2 * tokens * width * sum(grad.shape[1] for grad in grads),
            bytes_accessed=2 * tokens * width * 4,
            transcendentals=0,
        ),
        name=name,
    )(*xs, *xs, *grads, *weight_arrays, keep, edge, back, norm, mixers, *(own or ()))


def per_device(
    entering_activations,
    document_indices,
    acceptor_matrix,
    lookup_matrix,
    payload_matrix,
    valve_matrix,
    result_matrix,
    ffn_lookup_matrix,
    ffn_payload_matrix,
    ffn_acceptor_matrix,
    first_standardize_scaling,
    first_standardize_offset,
    acceptor_lerp_factor,
    lookup_lerp_factor,
    payload_lerp_factor,
    valve_lerp_factor,
    token_fading,
    diagonal_reward,
    subspace_standardize_scaling,
    subspace_standardize_offset,
    second_standardize_scaling,
    second_standardize_offset,
    ffn_lookup_lerp,
    ffn_acceptor_lerp,
    upstream_derivative,
):
    seqs_here, piece_len, embedding_extent = entering_activations.shape
    token_count = seqs_here * piece_len
    tp_count = lax.axis_size("tp")
    fourth_extent = embedding_extent // tp_count
    sharded_layout = lax.axis_index("tp") * fourth_extent
    ctx_place = lax.axis_index("ctx") * piece_len
    padded_seg = jnp.concatenate(
        [jnp.full((seqs_here, 1), -1, jnp.int32), document_indices], axis=1
    )
    segment_present = lax.dynamic_slice_in_dim(document_indices, ctx_place, piece_len, 1)
    seg_before = lax.dynamic_slice_in_dim(padded_seg, ctx_place, piece_len, 1)
    document_begins = seg_before[:, :1]
    pairs_here = fourth_extent // PAIR
    same_mask = segment_present == seg_before
    live_mask = segment_present == document_begins
    ending_mask = segment_present == segment_present[:, -1:]
    cols = jnp.stack([segment_present, live_mask, ending_mask, same_mask], axis=-1)
    cols = cols.astype(jnp.float32).reshape(token_count, 4)
    keep = same_mask.astype(jnp.float32).reshape(token_count, 1)
    keep_first = same_mask[:, :1].astype(jnp.float32)
    seg_row = segment_present.astype(jnp.float32)[:, None, :]
    owners = ("fsdp", "ctx")
    w_time = lax.all_gather(
        jnp.concatenate(
            [acceptor_matrix, lookup_matrix, payload_matrix, valve_matrix, result_matrix.T], axis=1
        ),
        owners,
        axis=0,
        tiled=True,
    )
    w_chan = lax.all_gather(
        jnp.concatenate([ffn_lookup_matrix, ffn_payload_matrix.T, ffn_acceptor_matrix], axis=1),
        owners,
        axis=0,
        tiled=True,
    )
    units = ffn_lookup_matrix.shape[1]
    w_recept, w_key, w_value, w_gate, w_output_t = (
        w_time[:, at * fourth_extent : (at + 1) * fourth_extent] for at in range(5)
    )
    w_chankey = w_chan[:, :units]
    w_chanvalue_t = w_chan[:, units : 2 * units]
    w_chanrecept = w_chan[:, 2 * units :]
    x_low = entering_activations.reshape(token_count, embedding_extent)
    norm_one = jnp.stack([first_standardize_scaling, first_standardize_offset])
    norm_two = jnp.stack([second_standardize_scaling, second_standardize_offset])
    mix_one = jnp.stack(
        [acceptor_lerp_factor, lookup_lerp_factor, payload_lerp_factor, valve_lerp_factor]
    )
    mix_two = jnp.stack([ffn_lookup_lerp, ffn_acceptor_lerp])

    def edge_from(last_rows, norm):
        last, _, _ = norm_rows(last_rows, norm[0], norm[1])
        return shifted(last, "ctx", 1)[:, None]

    def back_from(grads, weights, mixers):
        first = jnp.zeros((seqs_here, embedding_extent), jnp.float32)
        for at, (grad_low, weight) in enumerate(zip(grads, weights)):
            rows = grad_low.reshape(seqs_here, piece_len, -1)[:, 0]
            first = first + matmul_nt(rows, weight) * (1.0 - mixers[at])
        return shifted(first * keep_first, "ctx", -1)[:, None]

    edge_one = edge_from(entering_activations[:, -1].astype(jnp.float32), norm_one)
    mixed_in = blend((x_low,), keep, edge_one, norm_one, mix_one, piece_len, "blend_one")
    key_low = matmul(mixed_in[1], w_key).astype(jnp.bfloat16)
    value_low = matmul(mixed_in[2], w_value).astype(jnp.bfloat16)

    def own_share(vector):
        return lax.dynamic_slice_in_dim(vector, sharded_layout, fourth_extent, 0)[None]

    log_row = jnp.log(own_share(token_fading))
    vectors = jnp.concatenate(
        [own_share(diagonal_reward), own_share(subspace_standardize_scaling)]
        + [own_share(subspace_standardize_offset)] * 6
    )
    call = partial(pair_call, seqs=seqs_here, length=piece_len, width=fourth_extent)
    square = 2 * token_count * piece_len * fourth_extent
    (carry_sums,) = call(
        carry_kernel,
        operands=[("wide", key_low), ("wide", value_low), ("vector", log_row), ("cols", cols)],
        outs=[("state", jnp.float32)],
        name="carry",
        flops=square // 8,
    )
    alive_mask = (live_mask[:, -1]).astype(jnp.float32)[:, None, None, None]
    carry_mult = alive_mask * jnp.exp(float(piece_len) * log_row).reshape(1, pairs_here, 1, PAIR)
    incoming = carried(carry_mult, carry_sums, "ctx", 1)
    recept_low = matmul(mixed_in[0], w_recept).astype(jnp.bfloat16)
    gate_pre = matmul(mixed_in[3], w_gate)
    joined_low, attend = call(
        mix_kernel,
        operands=[
            ("wide", recept_low),
            ("wide", key_low),
            ("wide", value_low),
            ("wide", gate_pre),
            ("vector", log_row),
            ("vectors", vectors),
            ("cols", cols),
            ("row", seg_row),
            ("state", incoming),
        ],
        outs=[("wide", jnp.bfloat16), ("wide", jnp.float32)],
        name="mix",
        flops=2 * square,
    )
    mixed_out = tp_sum(matmul_nt(joined_low, w_output_t).astype(jnp.bfloat16))
    last_rows = entering_activations[:, -1].astype(jnp.float32) + mixed_out.reshape(
        seqs_here, piece_len, embedding_extent
    )[:, -1].astype(jnp.float32)
    edge_two = edge_from(last_rows, norm_two)
    key_in, rec_in = blend(
        (x_low, mixed_out), keep, edge_two, norm_two, mix_two, piece_len, "blend_two"
    )
    rec_gate = jax.nn.sigmoid(matmul(rec_in, w_chanrecept))
    d_result_low = upstream_derivative.reshape(token_count, fourth_extent)
    d_result = d_result_low.astype(jnp.float32)
    d_chan = (d_result * rec_gate).astype(jnp.bfloat16)
    d_chan_full = tp_gather(d_chan)
    key_pre = matmul(key_in, w_chankey)
    hidden = jnp.square(jax.nn.relu(key_pre)).astype(jnp.bfloat16)
    grad_chanvalue = matmul_tn(hidden, d_chan_full).astype(jnp.bfloat16)
    g_chanvalue = lax.psum_scatter(grad_chanvalue, owners, scatter_dimension=1, tiled=True)
    hidden, grad_chanvalue = after(hidden, grad_chanvalue)
    chan_sum = tp_scatter(matmul_nt(hidden, w_chanvalue_t).astype(jnp.bfloat16)).astype(jnp.float32)
    middle_q = lax.dynamic_slice_in_dim(x_low, sharded_layout, fourth_extent, 1).astype(
        jnp.float32
    ) + lax.dynamic_slice_in_dim(mixed_out, sharded_layout, fourth_extent, 1).astype(jnp.float32)
    result = (
        (middle_q + rec_gate * chan_sum)
        .astype(jnp.bfloat16)
        .reshape(seqs_here, piece_len, fourth_extent)
    )
    d_rec_pre = (d_result * chan_sum * rec_gate * (1.0 - rec_gate)).astype(jnp.bfloat16)
    d_hidden = matmul(d_chan_full, w_chanvalue_t)
    d_key_pre = (d_hidden * 2.0 * jax.nn.relu(key_pre)).astype(jnp.bfloat16)
    grad_chankey = matmul_tn(key_in, d_key_pre)
    grad_chanrecept = matmul_tn(rec_in, d_rec_pre)
    full_shape = (seqs_here, piece_len, embedding_extent)
    own_mask = (jnp.arange(embedding_extent) // fourth_extent == lax.axis_index("tp")).astype(
        jnp.float32
    )[None]
    d_middle_part, chan_small = blend_back(
        (x_low, mixed_out),
        (d_key_pre, d_rec_pre),
        ((w_chan, 0), (w_chan, 2 * units // fourth_extent)),
        keep,
        edge_two,
        back_from((d_key_pre, d_rec_pre), (w_chankey, w_chanrecept), mix_two),
        norm_two,
        mix_two,
        piece_len,
        (d_result_low, own_mask),
        "blend_two_back",
    )
    d_mixed = tp_sum(d_middle_part)
    grad_output_t = matmul_tn(d_mixed, joined_low)
    grads_chan = jnp.concatenate(
        [item.astype(jnp.bfloat16) for item in (grad_output_t, grad_chanrecept, grad_chankey)],
        axis=1,
    )
    d_mixed, grads_chan, g_chanvalue = after(d_mixed, grads_chan, g_chanvalue)
    g_chan = lax.psum_scatter(grads_chan, owners, scatter_dimension=0, tiled=True)
    d_joined = matmul(d_mixed, w_output_t)
    d_gate_pre, d_attend, local_grad, group_small = call(
        gate_back_kernel,
        operands=[
            ("wide", d_joined),
            ("wide", attend),
            ("wide", gate_pre),
            ("wide", recept_low),
            ("vector", log_row),
            ("vectors", vectors),
            ("cols", cols),
        ],
        outs=[
            ("wide", jnp.bfloat16),
            ("wide", jnp.bfloat16),
            ("state", jnp.float32),
            ("vectors", jnp.float32),
        ],
        name="gate_back",
        flops=square // 8,
    )
    outgoing_state = carried(carry_mult, local_grad, "ctx", -1)
    d_recept, d_key, d_value, state_small = call(
        mix_back_kernel,
        operands=[
            ("wide", recept_low),
            ("wide", key_low),
            ("wide", value_low),
            ("wide", d_attend),
            ("vector", log_row),
            ("vectors", vectors),
            ("cols", cols),
            ("row", seg_row),
            ("state", incoming),
            ("state", outgoing_state),
            ("mult", carry_mult),
        ],
        outs=[("wide", jnp.bfloat16)] * 3 + [("vectors", jnp.float32)],
        name="mix_back",
        flops=6 * square,
    )
    d_lows = [d_recept, d_key, d_value, d_gate_pre]
    weights_time = (w_recept, w_key, w_value, w_gate)
    grads_time = jnp.concatenate(
        [
            matmul_tn(mixed, grad_low).astype(jnp.bfloat16)
            for mixed, grad_low in zip(mixed_in, d_lows)
        ],
        axis=1,
    )
    *d_lows, grads_time, g_chan = after(d_lows[0], *d_lows[1:], grads_time, g_chan)
    g_time = lax.psum_scatter(grads_time, owners, scatter_dimension=0, tiled=True)
    d_input_part, time_small = blend_back(
        (x_low,),
        d_lows,
        [(w_time, at) for at in range(4)],
        keep,
        edge_one,
        back_from(d_lows, weights_time, mix_one),
        norm_one,
        mix_one,
        piece_len,
        None,
        "blend_one_back",
    )
    head_small = jnp.concatenate([state_small[:2], group_small[:2]])
    head_small = lax.dynamic_update_slice_in_dim(
        jnp.zeros((4, embedding_extent), jnp.float32), head_small, sharded_layout, 1
    )
    small_sum = whole_sum(
        jnp.concatenate([time_small[:6], head_small, chan_small[:4]], axis=0),
        ("tp", "fsdp", "ctx"),
    )
    owned = embedding_extent // (lax.axis_size("fsdp") * lax.axis_size("ctx"))
    small_owned = lax.dynamic_slice_in_dim(
        small_sum,
        (lax.axis_index("fsdp") * lax.axis_size("ctx") + lax.axis_index("ctx")) * owned,
        owned,
        1,
    )
    d_input_sum = tp_sum(d_input_part)
    grad_inputs = (d_mixed.astype(jnp.float32) + d_input_sum.astype(jnp.float32)).reshape(
        full_shape
    )
    g_chanvalue = g_chanvalue.astype(jnp.float32)
    g_chan = g_chan.astype(jnp.float32)
    g_time = g_time.astype(jnp.float32)
    g_recept, g_key, g_value, g_gate = (
        g_time[:, at * fourth_extent : (at + 1) * fourth_extent] for at in range(4)
    )
    g_output = g_chan[:, :fourth_extent].T
    g_chanrecept = g_chan[:, fourth_extent : 2 * fourth_extent]
    g_chankey = g_chan[:, 2 * fourth_extent :]
    return (
        result,
        grad_inputs,
        g_recept,
        g_key,
        g_value,
        g_gate,
        g_output,
        g_chankey,
        g_chanvalue,
        g_chanrecept,
    ) + tuple(small_owned[at] for at in range(14))


def solution(mesh):
    return jax.shard_map(
        per_device,
        mesh=mesh,
        in_specs=(
            P("fsdp", "ctx", None),
            P("fsdp", None),
            P(("fsdp", "ctx"), "tp"),
            P(("fsdp", "ctx"), "tp"),
            P(("fsdp", "ctx"), "tp"),
            P(("fsdp", "ctx"), "tp"),
            P("tp", ("fsdp", "ctx")),
            P(("fsdp", "ctx"), "tp"),
            P("tp", ("fsdp", "ctx")),
            P(("fsdp", "ctx"), "tp"),
            P(),
            P(),
            P(),
            P(),
            P(),
            P(),
            P(),
            P(),
            P(),
            P(),
            P(),
            P(),
            P(),
            P(),
            P("fsdp", "ctx", "tp"),
        ),
        out_specs=(
            P("fsdp", "ctx", "tp"),
            P("fsdp", "ctx", None),
            P(("fsdp", "ctx"), "tp"),
            P(("fsdp", "ctx"), "tp"),
            P(("fsdp", "ctx"), "tp"),
            P(("fsdp", "ctx"), "tp"),
            P("tp", ("fsdp", "ctx")),
            P(("fsdp", "ctx"), "tp"),
            P("tp", ("fsdp", "ctx")),
            P(("fsdp", "ctx"), "tp"),
            P(("fsdp", "ctx")),
            P(("fsdp", "ctx")),
            P(("fsdp", "ctx")),
            P(("fsdp", "ctx")),
            P(("fsdp", "ctx")),
            P(("fsdp", "ctx")),
            P(("fsdp", "ctx")),
            P(("fsdp", "ctx")),
            P(("fsdp", "ctx")),
            P(("fsdp", "ctx")),
            P(("fsdp", "ctx")),
            P(("fsdp", "ctx")),
            P(("fsdp", "ctx")),
            P(("fsdp", "ctx")),
        ),
        check_vma=False,
    )
```

```python
from functools import partial

import jax
import jax.numpy as jnp
from jax import lax
from jax.experimental import pallas as pl
from jax.experimental.pallas import tpu as pltpu
from jax.sharding import PartitionSpec as P

SUBSPACE_SIZE = 64
PAIR = 128
GROUP = 16
HALO = 8
SPAN = 64
TILE = 256


EPS = 1e-05
GROUP_EPS = 4.0


def shifted(x, axis, by):
    count = lax.axis_size(axis)
    pairs = [(i, i + by) for i in range(count) if 0 <= i + by < count]
    return lax.ppermute(x, axis, pairs)


def earlier_shift(x, axis, by):
    count = lax.axis_size(axis)
    return lax.ppermute(x, axis, [(i, i + by) for i in range(count) if 0 <= i + by < count])


def carried(mult, sums, axis, toward):
    count = lax.axis_size(axis)
    low = (mult.astype(jnp.bfloat16), sums.astype(jnp.bfloat16))
    arrived = [
        jax.tree.map(lambda part: earlier_shift(part, axis, toward * by), low)
        for by in range(1, count)
    ]
    state = jnp.zeros_like(sums)
    for far_mult, far_sums in reversed(arrived):
        state = far_mult.astype(jnp.float32) * state + far_sums.astype(jnp.float32)
    return state


def partner(x, bit):
    count = lax.axis_size("tp")
    return lax.ppermute(x, "tp", [(i, i ^ bit) for i in range(count)])


def halves(x, axis, bit):
    size = x.shape[axis] // 2
    mine = (lax.axis_index("tp") // bit) % 2
    return (
        lax.dynamic_slice_in_dim(x, mine * size, size, axis),
        lax.dynamic_slice_in_dim(x, (1 - mine) * size, size, axis),
    )


def add_low(left, right):
    return (left.astype(jnp.float32) + right.astype(jnp.float32)).astype(jnp.bfloat16)


def ordered(mine, other, axis, bit):
    first = (lax.axis_index("tp") // bit) % 2 == 0
    return jnp.where(
        first,
        jnp.concatenate([mine, other], axis),
        jnp.concatenate([other, mine], axis),
    )


def after(value, *earlier):
    return lax.optimization_barrier((value,) + earlier)


def tp_sum(x, work=None):
    mine, other = halves(x, 0, 1)
    part = add_low(mine, partner(other, 1))
    made = work(part) if work else None
    bit = 2
    while bit < lax.axis_size("tp"):
        arrived = partner(part, bit)
        if work and bit == 2:
            part = after(part, made)[0]
        part = add_low(part, arrived)
        bit *= 2
    whole = ordered(part, partner(part, 1), 0, 1)
    return (whole, made) if work else whole


def axis_bits(axis):
    bits, bit = [], 1
    while bit < lax.axis_size(axis):
        bits.append((axis, bit))
        bit *= 2
    return bits


def swap(x, axis, bit):
    return lax.ppermute(x, axis, [(i, i ^ bit) for i in range(lax.axis_size(axis))])


def owner_scatter_steps(x):
    fsdp_bits, ctx_bits = axis_bits("fsdp"), axis_bits("ctx")
    dims = list(reversed(fsdp_bits)) + list(reversed(ctx_bits))
    rows = x.shape[0] // 2 ** len(dims)
    part = x.reshape(*([2] * len(dims)), rows, x.shape[1])
    for axis, bit in fsdp_bits + ctx_bits:
        dim = dims.index((axis, bit))
        dims.pop(dim)
        mine = (lax.axis_index(axis) // bit) % 2
        own = lax.dynamic_index_in_dim(part, mine, dim, False)
        arrived = swap(lax.dynamic_index_in_dim(part, 1 - mine, dim, False), axis, bit)
        part = add_low(own, arrived)
        part = yield part
    yield None


def whole_sum(x, axes):
    for axis in axes:
        count = lax.axis_size(axis)
        bit = 1
        while bit < count:
            x = x + lax.ppermute(x, axis, [(i, i ^ bit) for i in range(count)])
            bit *= 2
    return x


def tp_scatter(x):
    count, place = lax.axis_size("tp"), lax.axis_index("tp")
    width = x.shape[1] // count
    parts = [
        lax.dynamic_slice_in_dim(x, (place ^ relative) * width, width, 1)
        for relative in range(count)
    ]
    bit = 1
    while bit < count:
        for relative in reversed(range(count)):
            if relative & bit and relative & (bit - 1) == 0:
                arrived = partner(parts[relative], bit)
                parts[relative ^ bit] = add_low(parts[relative ^ bit], arrived)
        bit *= 2
    return parts[0]


def tp_gather(x):
    count, place = lax.axis_size("tp"), lax.axis_index("tp")
    width = x.shape[1]
    parts = {0: x}
    bit = count // 2
    while bit:
        parts.update({relative ^ bit: partner(part, bit) for relative, part in parts.items()})
        bit //= 2
    whole = jnp.zeros((x.shape[0], width * count), x.dtype)
    for relative, part in parts.items():
        whole = lax.dynamic_update_slice_in_dim(whole, part, (place ^ relative) * width, 1)
    return whole


def matmul(left, right):
    return jnp.dot(left, right, preferred_element_type=jnp.float32)


def matmul_tn(left, right):
    return lax.dot_general(
        left, right, (((0,), (0,)), ((), ())), preferred_element_type=jnp.float32
    )


def matmul_nt(left, right):
    return lax.dot_general(
        left, right, (((1,), (1,)), ((), ())), preferred_element_type=jnp.float32
    )


def dot_nn(left, right):
    return lax.dot_general(
        left, right, (((1,), (0,)), ((), ())), preferred_element_type=jnp.float32
    )


def lanes_of(shape):
    return lax.broadcasted_iota(jnp.int32, shape, len(shape) - 1)


def low_head(shape):
    return lanes_of(shape) < SUBSPACE_SIZE


def head_sum(x):
    first = low_head(x.shape)
    low = jnp.sum(jnp.where(first, x, 0.0), -1, keepdims=True)
    high = jnp.sum(jnp.where(first, 0.0, x), -1, keepdims=True)
    return jnp.where(first, low, high)


def fold_pair(both):
    return jnp.where(
        low_head((SUBSPACE_SIZE, PAIR)), both[:SUBSPACE_SIZE], both[SUBSPACE_SIZE:]
    )


def spread_pair(folded):
    first = low_head((SUBSPACE_SIZE, PAIR))
    return jnp.concatenate(
        [jnp.where(first, folded, 0.0), jnp.where(first, 0.0, folded)], axis=0
    ).astype(jnp.bfloat16)


def head_parts(x):
    first = low_head(x.shape)
    zero = jnp.zeros_like(x)
    return jnp.where(first, x, zero), jnp.where(first, zero, x)


def places(length):
    return lax.broadcasted_iota(jnp.int32, (length, PAIR), 0).astype(jnp.float32)


def carry_kernel(k_ref, v_ref, log_ref, cols_ref, out_ref):
    length = k_ref.shape[0]
    closing = jnp.exp((length - 1.0 - places(length)) * log_ref[...])
    ending = cols_ref[:, 2:3]
    k_end = (k_ref[...].astype(jnp.float32) * closing * ending).astype(jnp.bfloat16)
    out_ref[0, 0] = fold_pair(matmul_tn(v_ref[...], k_end))


def group_norm(attend):
    centered = attend - head_sum(attend) * (1.0 / SUBSPACE_SIZE)
    inverse = lax.rsqrt(head_sum(centered * centered) * (1.0 / SUBSPACE_SIZE) + GROUP_EPS)
    return centered * inverse, inverse


def mix_kernel(
    r_ref, k_ref, v_ref, gate_ref, log_ref, rows_ref, cols_ref, seg_ref, state_ref,
    joined_ref, attend_ref,
):
    length = r_ref.shape[0]
    at = places(length)
    log = log_ref[...]
    r = r_ref[...].astype(jnp.float32)
    k = k_ref[...].astype(jnp.float32)
    v = v_ref[...]
    q_low = (r * jnp.exp(at * log)).astype(jnp.bfloat16)
    k_low = (k * jnp.exp(-(at + 1.0) * log)).astype(jnp.bfloat16)
    state = spread_pair(state_ref[0, 0])
    bonus = head_sum(r * rows_ref[0:1, :] * k)
    base = bonus * v.astype(jnp.float32) + cols_ref[:, 1:2] * matmul_nt(q_low, state)
    step = min(length, TILE)
    for top in range(0, length, step):
        reach = top + step
        rows = slice(top, reach)
        keep = pair_mask(cols_ref[rows, 0:1], seg_ref[0, :, :reach], top, step, reach)
        parts = []
        for q_part in head_parts(q_low[rows]):
            scores = matmul_nt(q_part, k_low[:reach])
            scores = jnp.where(keep, scores, 0.0).astype(jnp.bfloat16)
            parts.append(dot_nn(scores, v[:reach]))
        attend = base[rows] + jnp.where(low_head(parts[0].shape), parts[0], parts[1])
        unit, _ = group_norm(attend)
        grouped = unit * rows_ref[1:2, :] + rows_ref[2:3, :]
        gate = gate_ref[rows, :]
        attend_ref[rows, :] = attend
        joined_ref[rows, :] = (grouped * (gate * jax.nn.sigmoid(gate))).astype(jnp.bfloat16)


def pair_mask(seg_col, seg_row, top, count, reach):
    later = lax.broadcasted_iota(jnp.int32, (count, reach), 0) + top
    return (seg_col == seg_row) & (later > lanes_of((count, reach)))


def pair_mask_t(seg_col, seg_row, top, count, start):
    width = seg_row.shape[1]
    earlier = lax.broadcasted_iota(jnp.int32, (count, width), 0) + top
    return (seg_col == seg_row) & (lanes_of((count, width)) + start > earlier)


def gate_back_kernel(
    dj_ref, attend_ref, gate_ref, r_ref, log_ref, rows_ref, cols_ref,
    dgate_ref, dattend_ref, state_ref, small_ref,
):
    length = r_ref.shape[0]
    d_joined = dj_ref[...]
    gate = gate_ref[...]
    unit, inverse = group_norm(attend_ref[...])
    gain = rows_ref[1:2, :]
    grouped = unit * gain + rows_ref[2:3, :]
    sig = jax.nn.sigmoid(gate)
    dgate_ref[...] = (d_joined * grouped * sig * (1.0 + gate * (1.0 - sig))).astype(jnp.bfloat16)
    d_grouped = d_joined * gate * sig
    sums = [
        jnp.sum(d_grouped * unit, axis=0, keepdims=True),
        jnp.sum(d_grouped, axis=0, keepdims=True),
    ]
    scaled = d_grouped * gain
    share = 1.0 / SUBSPACE_SIZE
    d_attend = (
        inverse * (scaled - head_sum(scaled) * share - unit * (head_sum(scaled * unit) * share))
    ).astype(jnp.bfloat16)
    dattend_ref[...] = d_attend
    rising = jnp.exp(places(length) * log_ref[...])
    q_live = (r_ref[...].astype(jnp.float32) * rising * cols_ref[:, 1:2]).astype(jnp.bfloat16)
    state_ref[0, 0] = fold_pair(matmul_tn(d_attend, q_live))
    collect(small_ref, sums)


def collect(small_ref, sums):
    pad = jnp.zeros((small_ref.shape[0] - len(sums), sums[0].shape[1]), jnp.float32)
    total = jnp.concatenate(sums + [pad], axis=0)

    @pl.when(pl.program_id(1) == 0)
    def _():
        small_ref[...] = total

    @pl.when(pl.program_id(1) > 0)
    def _():
        small_ref[...] += total


def mix_back_kernel(
    r_ref, k_ref, v_ref, da_ref, log_ref, rows_ref, cols_ref, seg_ref, state_ref, gstate_ref,
    mult_ref, dr_ref, dk_ref, dv_ref, small_ref,
):
    length = r_ref.shape[0]
    at = places(length)
    log = log_ref[...]
    reward = rows_ref[0:1, :]
    r = r_ref[...].astype(jnp.float32)
    k = k_ref[...].astype(jnp.float32)
    v = v_ref[...]
    da = da_ref[...]
    rising = jnp.exp(at * log)
    falling = jnp.exp(-(at + 1.0) * log)
    closing = jnp.exp((length - 1.0 - at) * log) * cols_ref[:, 2:3]
    q_low = (r * rising).astype(jnp.bfloat16)
    k_low = (k * falling).astype(jnp.bfloat16)
    k_end = (k * closing).astype(jnp.bfloat16)
    state, gstate = state_ref[0, 0], gstate_ref[0, 0]
    state_low, gstate_low = spread_pair(state), spread_pair(gstate)
    v_f, da_f = v.astype(jnp.float32), da.astype(jnp.float32)
    dot_va = head_sum(v_f * da_f)
    dk_end = dot_nn(v, gstate_low)
    dq_base = cols_ref[:, 1:2] * dot_nn(da, state_low)
    dv_base = head_sum(r * reward * k) * da_f + matmul_nt(k_end, gstate_low)
    q_f, k_f = q_low.astype(jnp.float32), k_low.astype(jnp.float32)
    d_log = jnp.sum((length - 1.0 - at) * k_end.astype(jnp.float32) * dk_end, 0, keepdims=True)
    d_log += length * mult_ref[0, 0] * jnp.sum(
        state.astype(jnp.bfloat16).astype(jnp.float32)
        * gstate.astype(jnp.bfloat16).astype(jnp.float32),
        0,
        keepdims=True,
    )
    step = min(length, TILE)
    for top in range(0, length, step):
        rows = slice(top, top + step)
        reach = top + step
        keep = pair_mask(cols_ref[rows, 0:1], seg_ref[0, :, :reach], top, step, reach)
        dq = []
        for da_part in head_parts(da[rows]):
            pull = jnp.where(keep, matmul_nt(da_part, v[:reach]), 0.0).astype(jnp.bfloat16)
            dq.append(dot_nn(pull, k_low[:reach]))
        first = low_head(dq[0].shape)
        dq = jnp.where(first, dq[0], dq[1]) + dq_base[rows]
        d_log += jnp.sum(at[rows] * q_f[rows] * dq, 0, keepdims=True)
        dr_ref[rows, :] = (dq * rising[rows] + reward * k[rows] * dot_va[rows]).astype(jnp.bfloat16)
        keep = pair_mask_t(cols_ref[rows, 0:1], seg_ref[0, :, top:], top, step, top)
        dk, dv = [], []
        for v_part, k_part in zip(head_parts(v[rows]), head_parts(k_low[rows])):
            pull = jnp.where(keep, matmul_nt(v_part, da[top:]), 0.0).astype(jnp.bfloat16)
            dk.append(dot_nn(pull, q_low[top:]))
            scores = jnp.where(keep, matmul_nt(k_part, q_low[top:]), 0.0).astype(jnp.bfloat16)
            dv.append(dot_nn(scores, da[top:]))
        dk = jnp.where(first, dk[0], dk[1])
        d_log -= jnp.sum((at[rows] + 1.0) * k_f[rows] * dk, 0, keepdims=True)
        dk_ref[rows, :] = (
            dk * falling[rows]
            + dk_end[rows] * closing[rows]
            + reward * r[rows] * dot_va[rows]
        ).astype(jnp.bfloat16)
        dv_ref[rows, :] = (jnp.where(first, dv[0], dv[1]) + dv_base[rows]).astype(jnp.bfloat16)
    collect(small_ref, [d_log * jnp.exp(-log), jnp.sum(r * k * dot_va, 0, keepdims=True)])


def pair_call(kernel, seqs, length, width, operands, outs, name, flops):
    pairs = width // PAIR
    specs = {
        "wide": pl.BlockSpec((length, PAIR), lambda p, s: (s, p)),
        "vector": pl.BlockSpec((1, PAIR), lambda p, s: (0, p)),
        "vectors": pl.BlockSpec((8, PAIR), lambda p, s: (0, p)),
        "cols": pl.BlockSpec((length, 4), lambda p, s: (s, 0)),
        "row": pl.BlockSpec((1, 1, length), lambda p, s: (s, 0, 0)),
        "state": pl.BlockSpec((1, 1, SUBSPACE_SIZE, PAIR), lambda p, s: (s, p, 0, 0)),
        "mult": pl.BlockSpec((1, 1, 1, PAIR), lambda p, s: (s, p, 0, 0)),
    }
    shapes = {
        "wide": (seqs * length, width),
        "vectors": (8, width),
        "state": (seqs, pairs, SUBSPACE_SIZE, PAIR),
    }
    kinds, arrays = zip(*operands)
    size = sum(array.size * array.dtype.itemsize for array in arrays)
    return pl.pallas_call(
        kernel,
        grid=(pairs, seqs),
        in_specs=[specs[kind] for kind in kinds],
        out_specs=[specs[kind] for kind, _ in outs],
        out_shape=[jax.ShapeDtypeStruct(shapes[kind], dtype) for kind, dtype in outs],
        cost_estimate=pl.CostEstimate(flops=flops, bytes_accessed=2 * size, transcendentals=0),
        name=name,
    )(*arrays)


def unit_rows(x):
    centered = x - jnp.mean(x, -1, keepdims=True)
    return centered * lax.rsqrt(jnp.mean(centered * centered, -1, keepdims=True) + EPS)


def total_at(refs, rows, lanes):
    total = refs[0][rows, lanes].astype(jnp.float32)
    for ref in refs[1:]:
        total = total + ref[rows, lanes].astype(jnp.float32)
    return total


def lane_loop(width, body):
    def step(at, _):
        body(pl.ds(pl.multiple_of(at * PAIR, PAIR), PAIR))
        return 0

    lax.fori_loop(0, width // PAIR, step, 0)


def row_blocks(rows):
    return [slice(top, min(top + SPAN, rows)) for top in range(0, rows, SPAN)]


def unit_into(refs, unit_scr, rows, width):
    inverses = []
    for block in row_blocks(rows):
        inside = slice(block.start + HALO, block.stop + HALO)
        zero = jnp.zeros((block.stop - block.start, PAIR), jnp.float32)

        def load(at, total):
            lanes = pl.ds(pl.multiple_of(at * PAIR, PAIR), PAIR)
            value = total_at(refs, block, lanes)
            unit_scr[inside, lanes] = value
            return total + value

        total = lax.fori_loop(0, width // PAIR, load, zero, unroll=4)
        mean = jnp.sum(total, -1, keepdims=True) * (1.0 / width)

        def square(at, total):
            lanes = pl.ds(pl.multiple_of(at * PAIR, PAIR), PAIR)
            value = unit_scr[inside, lanes] - mean
            return total + value * value

        total = lax.fori_loop(0, width // PAIR, square, zero, unroll=4)
        inverse = lax.rsqrt(jnp.sum(total, -1, keepdims=True) * (1.0 / width) + EPS)

        def scale(at, _):
            lanes = pl.ds(pl.multiple_of(at * PAIR, PAIR), PAIR)
            unit_scr[inside, lanes] = (unit_scr[inside, lanes] - mean) * inverse
            return 0

        lax.fori_loop(0, width // PAIR, scale, 0, unroll=4)
        inverses.append(inverse)
    return inverses


def blend_kernel(parts, mixes, per_seq, *refs):
    x_refs, refs = refs[:parts], refs[parts:]
    keep_ref, edge_ref, norm_ref, mix_ref = refs[:4]
    outs, unit_scr = refs[4 : 4 + mixes], refs[4 + mixes]
    rows, width = x_refs[0].shape

    @pl.when(pl.program_id(0) % per_seq == 0)
    def _():
        unit_scr[HALO - 1 : HALO, :] = edge_ref[0]

    unit_into(x_refs, unit_scr, rows, width)

    def lane_block(lanes):
        gain, bias_term = norm_ref[0:1, lanes], norm_ref[1:2, lanes]
        mixers = [mix_ref[at : at + 1, lanes] for at in range(mixes)]
        for block in row_blocks(rows):
            normed = unit_scr[block.start + HALO : block.stop + HALO, lanes] * gain + bias_term
            before = pltpu.roll(unit_scr[block.start : block.stop + HALO, lanes], 1, 0)[HALO:]
            previous = (before * gain + bias_term) * keep_ref[block, 0:1]
            delta = normed - previous
            for mixer, out in zip(mixers, outs):
                out[block, lanes] = (previous + mixer * delta).astype(jnp.bfloat16)

    lane_loop(width, lane_block)
    unit_scr[HALO - 1 : HALO, :] = unit_scr[rows + HALO - 1 : rows + HALO, :]


def blend(xs, keep, edge, norm, mixers, piece, name):
    tokens, width = xs[0].shape
    rows = min(piece, 256)
    mixes = mixers.shape[0]
    per_seq = piece // rows
    wide = pl.BlockSpec((rows, width), lambda i: (i, 0))
    return pl.pallas_call(
        partial(blend_kernel, len(xs), mixes, per_seq),
        grid=(tokens // rows,),
        in_specs=[wide] * len(xs)
        + [
            pl.BlockSpec((rows, 1), lambda i: (i, 0)),
            pl.BlockSpec((1, 1, width), lambda i: (i // per_seq, 0, 0)),
            pl.BlockSpec((2, width), lambda i: (0, 0)),
            pl.BlockSpec((mixes, width), lambda i: (0, 0)),
        ],
        out_specs=[wide] * mixes,
        out_shape=[jax.ShapeDtypeStruct((tokens, width), jnp.bfloat16)] * mixes,
        scratch_shapes=[pltpu.VMEM((rows + HALO, width), jnp.float32)],
        cost_estimate=pl.CostEstimate(
            flops=20 * tokens * width,
            bytes_accessed=2 * tokens * width * (len(xs) + mixes),
            transcendentals=0,
        ),
        name=name,
    )(*xs, keep, edge, norm, mixers)


def blend_back_kernel(parts, mixes, per_seq, own, *refs):
    x_refs, refs = refs[:parts], refs[parts:]
    halo_refs, refs = refs[:parts], refs[parts:]
    grad_refs, refs = refs[:mixes], refs[mixes:]
    weight_refs, refs = refs[:mixes], refs[mixes:]
    keep_ref, edge_ref, back_ref, norm_ref, mix_ref = refs[:5]
    refs = refs[5:]
    own_refs, refs = refs[: 2 * own], refs[2 * own :]
    out_ref, small_ref, d_scr, unit_scr, prev_scr, row_scr, sums = refs
    rows, width = x_refs[0].shape
    tiles = pl.num_programs(0)
    tile = tiles - 1 - pl.program_id(0)

    @pl.when(pl.program_id(0) == 0)
    def _():
        sums[...] = jnp.zeros_like(sums)

    @pl.when(tile % per_seq == per_seq - 1)
    def _():
        prev_scr[rows : rows + 1, :] = back_ref[0]

    @pl.when(tile % per_seq < per_seq - 1)
    def _():
        prev_scr[rows : rows + 1, :] = prev_scr[0:1, :]

    for at in range(mixes):
        d_scr[at] = matmul_nt(grad_refs[at][...], weight_refs[at][...])

    halo = unit_rows(total_at(halo_refs, slice(None), slice(None)))[GROUP - 1 :, :]
    unit_scr[HALO - 1 : HALO, :] = jnp.where(tile % per_seq == 0, edge_ref[0], halo)
    inverses = unit_into(x_refs, unit_scr, rows, width)
    row_scr[...] = jnp.zeros_like(row_scr)

    def gather(at, value):
        total = value[0:8]
        for top in range(8, value.shape[0], 8):
            total = total + value[top : top + 8]
        return total

    def first_pass(lanes):
        gain, bias_term = norm_ref[0:1, lanes], norm_ref[1:2, lanes]
        mixers = [mix_ref[at : at + 1, lanes] for at in range(mixes)]
        totals = [jnp.zeros((8, PAIR), jnp.float32)] * mixes
        for block in row_blocks(rows):
            keep = keep_ref[block, 0:1]
            normed = unit_scr[block.start + HALO : block.stop + HALO, lanes] * gain + bias_term
            before = pltpu.roll(unit_scr[block.start : block.stop + HALO, lanes], 1, 0)[HALO:]
            delta = normed - (before * gain + bias_term) * keep
            d_norm, d_all = None, None
            for at in range(mixes):
                d_in = d_scr[at, block, lanes]
                totals[at] = totals[at] + gather(at, d_in * delta)
                share = d_in * mixers[at]
                d_norm = share if d_norm is None else d_norm + share
                d_all = d_in if d_all is None else d_all + d_in
            prev_scr[block, lanes] = (d_all - d_norm) * keep
            d_scr[0, block, lanes] = d_norm
        for at in range(mixes):
            sums[2 + at, :, lanes] += totals[at]

    lane_loop(width, first_pass)

    def second_pass(lanes):
        gain = norm_ref[0:1, lanes]
        totals = [jnp.zeros((8, PAIR), jnp.float32)] * 2
        for block in row_blocks(rows):
            size = block.stop - block.start
            later = pltpu.roll(
                prev_scr[block.start : block.stop + HALO, lanes], size + HALO - 1, 0
            )[:size]
            d_norm = d_scr[0, block, lanes] + later
            unit = unit_scr[block.start + HALO : block.stop + HALO, lanes]
            product = d_norm * unit
            totals[0] = totals[0] + gather(0, product)
            totals[1] = totals[1] + gather(1, d_norm)
            d_scr[0, block, lanes] = d_norm * gain
            row_scr[0, block, :] += d_norm * gain
            row_scr[1, block, :] += product * gain
        for at in range(2):
            sums[at, :, lanes] += totals[at]

    lane_loop(width, second_pass)
    means, tilts = [], []
    for block in row_blocks(rows):
        means.append(jnp.sum(row_scr[0, block, :], -1, keepdims=True) * (1.0 / width))
        tilts.append(jnp.sum(row_scr[1, block, :], -1, keepdims=True) * (1.0 / width))
    blocks = list(zip(row_blocks(rows), inverses, means, tilts))

    def last_pass(start, lanes):
        for block, inverse, mean, tilt in blocks:
            unit = unit_scr[block.start + HALO : block.stop + HALO, lanes]
            value = inverse * (d_scr[0, block, lanes] - mean - unit * tilt)
            if own:
                extra = own_refs[0][block, start].astype(jnp.float32)
                value = value + extra * own_refs[1][0:1, lanes]
            out_ref[block, lanes] = value.astype(jnp.bfloat16)

    def last_step(at, _):
        lanes = pl.ds(pl.multiple_of(at * PAIR, PAIR), PAIR)
        inner = None
        if own:
            count = own_refs[0].shape[1] // PAIR
            inner = pl.ds(pl.multiple_of((at % count) * PAIR, PAIR), PAIR)
        last_pass(inner, lanes)
        return 0

    lax.fori_loop(0, width // PAIR, last_step, 0)

    @pl.when(pl.program_id(0) == tiles - 1)
    def _():
        for at in range(2 + mixes):
            small_ref[at : at + 1, :] = jnp.sum(sums[at], 0, keepdims=True)


def blend_back(xs, grads, weights, keep, edge, back, norm, mixers, piece, own, name):
    tokens, width = xs[0].shape
    rows = min(piece, 256)
    mixes = mixers.shape[0]
    per_seq = piece // rows
    tiles = tokens // rows

    def reverse(i):
        return tiles - 1 - i

    def halo_at(i):
        return (jnp.maximum(reverse(i) * (rows // GROUP) - 1, 0), 0)

    wide = pl.BlockSpec((rows, width), lambda i: (reverse(i), 0))
    per = pl.BlockSpec((1, 1, width), lambda i: (reverse(i) // per_seq, 0, 0))
    weight_specs, weight_arrays = [], []
    for (array, at), grad in zip(weights, grads):
        weight_specs.append(
            pl.BlockSpec(
                (width, grad.shape[1]), partial(lambda at, i: (0, at), at),
                pipeline_mode=pl.Buffered(1),
            )
        )
        weight_arrays.append(array)
    return pl.pallas_call(
        partial(blend_back_kernel, len(xs), mixes, per_seq, int(own is not None)),
        grid=(tiles,),
        in_specs=[wide] * len(xs)
        + [pl.BlockSpec((GROUP, width), halo_at)] * len(xs)
        + [pl.BlockSpec((rows, grad.shape[1]), lambda i: (reverse(i), 0)) for grad in grads]
        + weight_specs
        + [
            pl.BlockSpec((rows, 1), lambda i: (reverse(i), 0)),
            per,
            per,
            pl.BlockSpec((2, width), lambda i: (0, 0)),
            pl.BlockSpec((mixes, width), lambda i: (0, 0)),
        ]
        + (
            [
                pl.BlockSpec((rows, own[0].shape[1]), lambda i: (reverse(i), 0)),
                pl.BlockSpec((1, width), lambda i: (0, 0)),
            ]
            if own is not None
            else []
        ),
        out_specs=[wide, pl.BlockSpec((8, width), lambda i: (0, 0))],
        out_shape=[
            jax.ShapeDtypeStruct((tokens, width), jnp.bfloat16),
            jax.ShapeDtypeStruct((8, width), jnp.float32),
        ],
        scratch_shapes=[
            pltpu.VMEM((mixes, rows, width), jnp.float32),
            pltpu.VMEM((rows + HALO, width), jnp.float32),
            pltpu.VMEM((rows + HALO, width), jnp.float32),
            pltpu.VMEM((2, rows, PAIR), jnp.float32),
            pltpu.VMEM((2 + mixes, 8, width), jnp.float32),
        ],
        cost_estimate=pl.CostEstimate(
            flops=2 * tokens * width * sum(grad.shape[1] for grad in grads),
            bytes_accessed=2 * tokens * width * 4,
            transcendentals=0,
        ),
        name=name,
    )(*xs, *xs, *grads, *weight_arrays, keep, edge, back, norm, mixers, *(own or ()))


def per_device(
    entering_activations,
    document_indices,
    acceptor_matrix,
    lookup_matrix,
    payload_matrix,
    valve_matrix,
    result_matrix,
    ffn_lookup_matrix,
    ffn_payload_matrix,
    ffn_acceptor_matrix,
    first_standardize_scaling,
    first_standardize_offset,
    acceptor_lerp_factor,
    lookup_lerp_factor,
    payload_lerp_factor,
    valve_lerp_factor,
    token_fading,
    diagonal_reward,
    subspace_standardize_scaling,
    subspace_standardize_offset,
    second_standardize_scaling,
    second_standardize_offset,
    ffn_lookup_lerp,
    ffn_acceptor_lerp,
    upstream_derivative,
):
    seqs_here, piece_len, embedding_extent = entering_activations.shape
    token_count = seqs_here * piece_len
    tp_count = lax.axis_size("tp")
    fourth_extent = embedding_extent // tp_count
    sharded_layout = lax.axis_index("tp") * fourth_extent
    ctx_place = lax.axis_index("ctx") * piece_len
    padded_seg = jnp.concatenate(
        [jnp.full((seqs_here, 1), -1, jnp.int32), document_indices], axis=1
    )
    segment_present = lax.dynamic_slice_in_dim(document_indices, ctx_place, piece_len, 1)
    seg_before = lax.dynamic_slice_in_dim(padded_seg, ctx_place, piece_len, 1)
    document_begins = seg_before[:, :1]
    pairs_here = fourth_extent // PAIR
    same_mask = segment_present == seg_before
    live_mask = segment_present == document_begins
    ending_mask = segment_present == segment_present[:, -1:]
    cols = jnp.stack([segment_present, live_mask, ending_mask, same_mask], axis=-1)
    cols = cols.astype(jnp.float32).reshape(token_count, 4)
    keep = same_mask.astype(jnp.float32).reshape(token_count, 1)
    keep_first = same_mask[:, :1].astype(jnp.float32)
    seg_row = segment_present.astype(jnp.float32)[:, None, :]
    owners = ("fsdp", "ctx")
    w_time = lax.all_gather(
        jnp.concatenate(
            [acceptor_matrix, lookup_matrix, payload_matrix, valve_matrix, result_matrix.T], axis=1
        ),
        owners,
        axis=0,
        tiled=True,
    )
    w_chan = lax.all_gather(
        jnp.concatenate([ffn_lookup_matrix, ffn_acceptor_matrix], axis=1),
        owners,
        axis=0,
        tiled=True,
    )
    units = ffn_lookup_matrix.shape[1]
    w_recept, w_key, w_value, w_gate, w_output_t = (
        w_time[:, at * fourth_extent : (at + 1) * fourth_extent] for at in range(5)
    )
    w_chankey = w_chan[:, :units]
    w_chanrecept = w_chan[:, units:]
    w_chanvalue_t = lax.all_gather(ffn_payload_matrix.T, owners, axis=0, tiled=True)
    x_low = entering_activations.reshape(token_count, embedding_extent)
    norm_one = jnp.stack([first_standardize_scaling, first_standardize_offset])
    norm_two = jnp.stack([second_standardize_scaling, second_standardize_offset])
    mix_one = jnp.stack(
        [acceptor_lerp_factor, lookup_lerp_factor, payload_lerp_factor, valve_lerp_factor]
    )
    mix_two = jnp.stack([ffn_lookup_lerp, ffn_acceptor_lerp])

    def edge_from(last_rows):
        return shifted(unit_rows(last_rows), "ctx", 1)[:, None]

    def back_from(grads, weights, mixers):
        first = jnp.zeros((seqs_here, embedding_extent), jnp.float32)
        for at, (grad_low, weight) in enumerate(zip(grads, weights)):
            rows = grad_low.reshape(seqs_here, piece_len, -1)[:, 0]
            first = first + matmul_nt(rows, weight) * (1.0 - mixers[at])
        return shifted(first * keep_first, "ctx", -1)[:, None]

    edge_one = edge_from(entering_activations[:, -1].astype(jnp.float32))
    mixed_in = blend((x_low,), keep, edge_one, norm_one, mix_one, piece_len, "blend_one")
    key_low = matmul(mixed_in[1], w_key).astype(jnp.bfloat16)
    value_low = matmul(mixed_in[2], w_value).astype(jnp.bfloat16)

    def own_share(vector):
        return lax.dynamic_slice_in_dim(vector, sharded_layout, fourth_extent, 0)[None]

    log_row = jnp.log(own_share(token_fading))
    vectors = jnp.concatenate(
        [own_share(diagonal_reward), own_share(subspace_standardize_scaling)]
        + [own_share(subspace_standardize_offset)] * 6
    )
    call = partial(pair_call, seqs=seqs_here, length=piece_len, width=fourth_extent)
    square = 2 * token_count * piece_len * fourth_extent
    (carry_sums,) = call(
        carry_kernel,
        operands=[("wide", key_low), ("wide", value_low), ("vector", log_row), ("cols", cols)],
        outs=[("state", jnp.float32)],
        name="carry",
        flops=square // 8,
    )
    alive_mask = (live_mask[:, -1]).astype(jnp.float32)[:, None, None, None]
    carry_mult = alive_mask * jnp.exp(float(piece_len) * log_row).reshape(1, pairs_here, 1, PAIR)
    incoming = carried(carry_mult, carry_sums, "ctx", 1)
    recept_low = matmul(mixed_in[0], w_recept).astype(jnp.bfloat16)
    gate_pre = matmul(mixed_in[3], w_gate)
    joined_low, attend = call(
        mix_kernel,
        operands=[
            ("wide", recept_low),
            ("wide", key_low),
            ("wide", value_low),
            ("wide", gate_pre),
            ("vector", log_row),
            ("vectors", vectors),
            ("cols", cols),
            ("row", seg_row),
            ("state", incoming),
        ],
        outs=[("wide", jnp.bfloat16), ("wide", jnp.float32)],
        name="mix",
        flops=2 * square,
    )
    mixed_out = tp_sum(matmul_nt(joined_low, w_output_t).astype(jnp.bfloat16))
    last_rows = entering_activations[:, -1].astype(jnp.float32) + mixed_out.reshape(
        seqs_here, piece_len, embedding_extent
    )[:, -1].astype(jnp.float32)
    edge_two = edge_from(last_rows)
    key_in, rec_in = blend(
        (x_low, mixed_out), keep, edge_two, norm_two, mix_two, piece_len, "blend_two"
    )
    rec_gate = jax.nn.sigmoid(matmul(rec_in, w_chanrecept))
    d_result_low = upstream_derivative.reshape(token_count, fourth_extent)
    d_result = d_result_low.astype(jnp.float32)
    d_chan = (d_result * rec_gate).astype(jnp.bfloat16)
    d_chan_full = tp_gather(d_chan)
    key_pre = matmul(key_in, w_chankey)
    hidden = jnp.square(jax.nn.relu(key_pre)).astype(jnp.bfloat16)
    grad_chanvalue = matmul_tn(hidden, d_chan_full).astype(jnp.bfloat16)
    g_chanvalue = lax.psum_scatter(grad_chanvalue, owners, scatter_dimension=1, tiled=True)
    hidden, grad_chanvalue = after(hidden, grad_chanvalue)
    chan_sum = tp_scatter(matmul_nt(hidden, w_chanvalue_t).astype(jnp.bfloat16)).astype(jnp.float32)
    middle_q = lax.dynamic_slice_in_dim(x_low, sharded_layout, fourth_extent, 1).astype(
        jnp.float32
    ) + lax.dynamic_slice_in_dim(mixed_out, sharded_layout, fourth_extent, 1).astype(jnp.float32)
    result = (
        (middle_q + rec_gate * chan_sum)
        .astype(jnp.bfloat16)
        .reshape(seqs_here, piece_len, fourth_extent)
    )
    d_rec_pre = (d_result * chan_sum * rec_gate * (1.0 - rec_gate)).astype(jnp.bfloat16)
    d_hidden = matmul(d_chan_full, w_chanvalue_t)
    d_key_pre = (d_hidden * 2.0 * jax.nn.relu(key_pre)).astype(jnp.bfloat16)
    full_shape = (seqs_here, piece_len, embedding_extent)
    own_mask = (jnp.arange(embedding_extent) // fourth_extent == lax.axis_index("tp")).astype(
        jnp.float32
    )[None]
    d_middle_part, chan_small = blend_back(
        (x_low, mixed_out),
        (d_key_pre, d_rec_pre),
        ((w_chan, 0), (w_chanrecept, 0)),
        keep,
        edge_two,
        back_from((d_key_pre, d_rec_pre), (w_chankey, w_chanrecept), mix_two),
        norm_two,
        mix_two,
        piece_len,
        (d_result_low, own_mask),
        "blend_two_back",
    )

    def chan_grads(token):
        d_key_late, d_rec_late, _ = after(d_key_pre, d_rec_pre, token)
        return jnp.concatenate(
            [
                matmul_tn(key_in, d_key_late).astype(jnp.bfloat16),
                matmul_tn(rec_in, d_rec_late).astype(jnp.bfloat16),
            ],
            axis=1,
        )

    d_mixed, grads_chan = tp_sum(d_middle_part, chan_grads)
    d_mixed, grads_chan, g_chanvalue = after(d_mixed, grads_chan, g_chanvalue)
    g_chan = lax.psum_scatter(grads_chan, owners, scatter_dimension=0, tiled=True)
    grad_output_t = matmul_tn(d_mixed, joined_low).astype(jnp.bfloat16)
    d_joined = matmul(d_mixed, w_output_t)
    d_gate_pre, d_attend, local_grad, group_small = call(
        gate_back_kernel,
        operands=[
            ("wide", d_joined),
            ("wide", attend),
            ("wide", gate_pre),
            ("wide", recept_low),
            ("vector", log_row),
            ("vectors", vectors),
            ("cols", cols),
        ],
        outs=[
            ("wide", jnp.bfloat16),
            ("wide", jnp.bfloat16),
            ("state", jnp.float32),
            ("vectors", jnp.float32),
        ],
        name="gate_back",
        flops=square // 8,
    )
    grads_early = jnp.concatenate(
        [grad_output_t, matmul_tn(mixed_in[3], d_gate_pre).astype(jnp.bfloat16)], axis=1
    )
    early = owner_scatter_steps(grads_early)
    g_early = next(early)
    outgoing_state = carried(carry_mult, local_grad, "ctx", -1)
    d_recept, d_key, d_value, state_small = call(
        mix_back_kernel,
        operands=[
            ("wide", recept_low),
            ("wide", key_low),
            ("wide", value_low),
            ("wide", d_attend),
            ("vector", log_row),
            ("vectors", vectors),
            ("cols", cols),
            ("row", seg_row),
            ("state", incoming),
            ("state", outgoing_state),
            ("mult", carry_mult),
        ],
        outs=[("wide", jnp.bfloat16)] * 3 + [("vectors", jnp.float32)],
        name="mix_back",
        flops=6 * square,
    )
    early_steps = len(axis_bits("fsdp")) + len(axis_bits("ctx"))
    d_recept, d_key, d_value, g_early = after(d_recept, d_key, d_value, g_early)
    for _ in range(early_steps - 2):
        g_early = early.send(g_early)
    d_lows = [d_recept, d_key, d_value, d_gate_pre]
    weights_time = (w_recept, w_key, w_value, w_gate)
    grads_time = jnp.concatenate(
        [
            matmul_tn(mixed, grad_low).astype(jnp.bfloat16)
            for mixed, grad_low in zip(mixed_in, d_lows[:3])
        ],
        axis=1,
    )
    *d_lows, _, g_early = after(d_lows[0], *d_lows[1:], grads_time, g_early)
    g_early = early.send(g_early)
    g_time = lax.psum_scatter(grads_time, owners, scatter_dimension=0, tiled=True)
    d_input_part, time_small = blend_back(
        (x_low,),
        d_lows,
        [(w_time, at) for at in range(4)],
        keep,
        edge_one,
        back_from(d_lows, weights_time, mix_one),
        norm_one,
        mix_one,
        piece_len,
        None,
        "blend_one_back",
    )
    d_input_part, g_early, g_chan = after(d_input_part, g_early, g_chan)
    head_small = jnp.concatenate([state_small[:2], group_small[:2]])
    head_small = lax.dynamic_update_slice_in_dim(
        jnp.zeros((4, embedding_extent), jnp.float32), head_small, sharded_layout, 1
    )
    small_sum = whole_sum(
        jnp.concatenate([time_small[:6], head_small, chan_small[:4]], axis=0),
        ("tp", "fsdp", "ctx"),
    )
    owned = embedding_extent // (lax.axis_size("fsdp") * lax.axis_size("ctx"))
    small_owned = lax.dynamic_slice_in_dim(
        small_sum,
        (lax.axis_index("fsdp") * lax.axis_size("ctx") + lax.axis_index("ctx")) * owned,
        owned,
        1,
    )
    d_input_sum = tp_sum(d_input_part)
    grad_inputs = (d_mixed.astype(jnp.float32) + d_input_sum.astype(jnp.float32)).reshape(
        full_shape
    )
    g_chanvalue = g_chanvalue.astype(jnp.float32)
    g_chan = g_chan.astype(jnp.float32)
    g_time = g_time.astype(jnp.float32)
    g_early = g_early.astype(jnp.float32)
    g_recept, g_key, g_value = (
        g_time[:, at * fourth_extent : (at + 1) * fourth_extent] for at in range(3)
    )
    g_output = g_early[:, :fourth_extent].T
    g_gate = g_early[:, fourth_extent:]
    g_chankey = g_chan[:, :units]
    g_chanrecept = g_chan[:, units:]
    return (
        result,
        grad_inputs,
        g_recept,
        g_key,
        g_value,
        g_gate,
        g_output,
        g_chankey,
        g_chanvalue,
        g_chanrecept,
    ) + tuple(small_owned[at] for at in range(14))


def solution(mesh):
    return jax.shard_map(
        per_device,
        mesh=mesh,
        in_specs=(
            P("fsdp", "ctx", None),
            P("fsdp", None),
            P(("fsdp", "ctx"), "tp"),
            P(("fsdp", "ctx"), "tp"),
            P(("fsdp", "ctx"), "tp"),
            P(("fsdp", "ctx"), "tp"),
            P("tp", ("fsdp", "ctx")),
            P(("fsdp", "ctx"), "tp"),
            P("tp", ("fsdp", "ctx")),
            P(("fsdp", "ctx"), "tp"),
            P(),
            P(),
            P(),
            P(),
            P(),
            P(),
            P(),
            P(),
            P(),
            P(),
            P(),
            P(),
            P(),
            P(),
            P("fsdp", "ctx", "tp"),
        ),
        out_specs=(
            P("fsdp", "ctx", "tp"),
            P("fsdp", "ctx", None),
            P(("fsdp", "ctx"), "tp"),
            P(("fsdp", "ctx"), "tp"),
            P(("fsdp", "ctx"), "tp"),
            P(("fsdp", "ctx"), "tp"),
            P("tp", ("fsdp", "ctx")),
            P(("fsdp", "ctx"), "tp"),
            P("tp", ("fsdp", "ctx")),
            P(("fsdp", "ctx"), "tp"),
            P(("fsdp", "ctx")),
            P(("fsdp", "ctx")),
            P(("fsdp", "ctx")),
            P(("fsdp", "ctx")),
            P(("fsdp", "ctx")),
            P(("fsdp", "ctx")),
            P(("fsdp", "ctx")),
            P(("fsdp", "ctx")),
            P(("fsdp", "ctx")),
            P(("fsdp", "ctx")),
            P(("fsdp", "ctx")),
            P(("fsdp", "ctx")),
            P(("fsdp", "ctx")),
            P(("fsdp", "ctx")),
        ),
        check_vma=False,
    )
```

```python
from functools import partial

import jax
import jax.numpy as jnp
from jax import lax
from jax.experimental import pallas as pl
from jax.experimental.pallas import tpu as pltpu
from jax.sharding import PartitionSpec as P

SUBSPACE_SIZE = 64
PAIR = 128
GROUP = 16
HALO = 8
SPAN = 64
TILE = 256


EPS = 1e-05
GROUP_EPS = 4.0


def shifted(x, axis, by):
    count = lax.axis_size(axis)
    pairs = [(i, i + by) for i in range(count) if 0 <= i + by < count]
    return lax.ppermute(x, axis, pairs)


def earlier_shift(x, axis, by):
    count = lax.axis_size(axis)
    return lax.ppermute(x, axis, [(i, i + by) for i in range(count) if 0 <= i + by < count])


def carried(mult, sums, axis, toward):
    count = lax.axis_size(axis)
    low = (mult.astype(jnp.bfloat16), sums.astype(jnp.bfloat16))
    arrived = [
        jax.tree.map(lambda part: earlier_shift(part, axis, toward * by), low)
        for by in range(1, count)
    ]
    state = jnp.zeros_like(sums)
    for far_mult, far_sums in reversed(arrived):
        state = far_mult.astype(jnp.float32) * state + far_sums.astype(jnp.float32)
    return state


def partner(x, bit):
    count = lax.axis_size("tp")
    return lax.ppermute(x, "tp", [(i, i ^ bit) for i in range(count)])


def halves(x, axis, bit):
    size = x.shape[axis] // 2
    mine = (lax.axis_index("tp") // bit) % 2
    return (
        lax.dynamic_slice_in_dim(x, mine * size, size, axis),
        lax.dynamic_slice_in_dim(x, (1 - mine) * size, size, axis),
    )


def add_low(left, right):
    return (left.astype(jnp.float32) + right.astype(jnp.float32)).astype(jnp.bfloat16)


def ordered(mine, other, axis, bit):
    first = (lax.axis_index("tp") // bit) % 2 == 0
    return jnp.where(
        first,
        jnp.concatenate([mine, other], axis),
        jnp.concatenate([other, mine], axis),
    )


def after(value, *earlier):
    return lax.optimization_barrier((value,) + earlier)


def tp_sum(x, work=None):
    mine, other = halves(x, 0, 1)
    part = add_low(mine, partner(other, 1))
    made = work(part) if work else None
    bit = 2
    while bit < lax.axis_size("tp"):
        arrived = partner(part, bit)
        if work and bit == 2:
            part = after(part, made)[0]
        part = add_low(part, arrived)
        bit *= 2
    whole = ordered(part, partner(part, 1), 0, 1)
    return (whole, made) if work else whole


def axis_bits(axis):
    bits, bit = [], 1
    while bit < lax.axis_size(axis):
        bits.append((axis, bit))
        bit *= 2
    return bits


def swap(x, axis, bit):
    return lax.ppermute(x, axis, [(i, i ^ bit) for i in range(lax.axis_size(axis))])


def owner_scatter_steps(x):
    fsdp_bits, ctx_bits = axis_bits("fsdp"), axis_bits("ctx")
    dims = list(reversed(fsdp_bits)) + list(reversed(ctx_bits))
    rows = x.shape[0] // 2 ** len(dims)
    part = x.reshape(*([2] * len(dims)), rows, x.shape[1])
    for axis, bit in fsdp_bits + ctx_bits:
        dim = dims.index((axis, bit))
        dims.pop(dim)
        mine = (lax.axis_index(axis) // bit) % 2
        own = lax.dynamic_index_in_dim(part, mine, dim, False)
        arrived = swap(lax.dynamic_index_in_dim(part, 1 - mine, dim, False), axis, bit)
        part = add_low(own, arrived)
        part = yield part
    yield None


def whole_sum(x, axes):
    for axis in axes:
        count = lax.axis_size(axis)
        bit = 1
        while bit < count:
            x = x + lax.ppermute(x, axis, [(i, i ^ bit) for i in range(count)])
            bit *= 2
    return x


def tp_scatter(x):
    count, place = lax.axis_size("tp"), lax.axis_index("tp")
    width = x.shape[1] // count
    parts = [
        lax.dynamic_slice_in_dim(x, (place ^ relative) * width, width, 1)
        for relative in range(count)
    ]
    bit = 1
    while bit < count:
        for relative in reversed(range(count)):
            if relative & bit and relative & (bit - 1) == 0:
                arrived = partner(parts[relative], bit)
                parts[relative ^ bit] = add_low(parts[relative ^ bit], arrived)
        bit *= 2
    return parts[0]


def tp_gather(x):
    count, place = lax.axis_size("tp"), lax.axis_index("tp")
    width = x.shape[1]
    parts = {0: x}
    bit = count // 2
    while bit:
        parts.update({relative ^ bit: partner(part, bit) for relative, part in parts.items()})
        bit //= 2
    whole = jnp.zeros((x.shape[0], width * count), x.dtype)
    for relative, part in parts.items():
        whole = lax.dynamic_update_slice_in_dim(whole, part, (place ^ relative) * width, 1)
    return whole


def matmul(left, right):
    return jnp.dot(left, right, preferred_element_type=jnp.float32)


def matmul_tn(left, right):
    return lax.dot_general(
        left, right, (((0,), (0,)), ((), ())), preferred_element_type=jnp.float32
    )


def matmul_nt(left, right):
    return lax.dot_general(
        left, right, (((1,), (1,)), ((), ())), preferred_element_type=jnp.float32
    )


def dot_nn(left, right):
    return lax.dot_general(
        left, right, (((1,), (0,)), ((), ())), preferred_element_type=jnp.float32
    )


def lanes_of(shape):
    return lax.broadcasted_iota(jnp.int32, shape, len(shape) - 1)


def low_head(shape):
    return lanes_of(shape) < SUBSPACE_SIZE


def head_sum(x):
    first = low_head(x.shape)
    low = jnp.sum(jnp.where(first, x, 0.0), -1, keepdims=True)
    high = jnp.sum(jnp.where(first, 0.0, x), -1, keepdims=True)
    return jnp.where(first, low, high)


def fold_pair(both):
    return jnp.where(
        low_head((SUBSPACE_SIZE, PAIR)), both[:SUBSPACE_SIZE], both[SUBSPACE_SIZE:]
    )


def spread_pair(folded):
    first = low_head((SUBSPACE_SIZE, PAIR))
    return jnp.concatenate(
        [jnp.where(first, folded, 0.0), jnp.where(first, 0.0, folded)], axis=0
    ).astype(jnp.bfloat16)


def head_parts(x):
    first = low_head(x.shape)
    zero = jnp.zeros_like(x)
    return jnp.where(first, x, zero), jnp.where(first, zero, x)


def places(length):
    return lax.broadcasted_iota(jnp.int32, (length, PAIR), 0).astype(jnp.float32)


def carry_kernel(k_ref, v_ref, log_ref, cols_ref, out_ref):
    length = k_ref.shape[0]
    closing = jnp.exp((length - 1.0 - places(length)) * log_ref[...])
    ending = cols_ref[:, 2:3]
    k_end = (k_ref[...].astype(jnp.float32) * closing * ending).astype(jnp.bfloat16)
    out_ref[0, 0] = fold_pair(matmul_tn(v_ref[...], k_end))


def group_norm(attend):
    centered = attend - head_sum(attend) * (1.0 / SUBSPACE_SIZE)
    inverse = lax.rsqrt(head_sum(centered * centered) * (1.0 / SUBSPACE_SIZE) + GROUP_EPS)
    return centered * inverse, inverse


def mix_kernel(
    r_ref, k_ref, v_ref, gate_ref, log_ref, rows_ref, cols_ref, seg_ref, state_ref,
    joined_ref, attend_ref,
):
    length = r_ref.shape[0]
    at = places(length)
    log = log_ref[...]
    r = r_ref[...].astype(jnp.float32)
    k = k_ref[...].astype(jnp.float32)
    v = v_ref[...]
    q_low = (r * jnp.exp(at * log)).astype(jnp.bfloat16)
    k_low = (k * jnp.exp(-(at + 1.0) * log)).astype(jnp.bfloat16)
    state = spread_pair(state_ref[0, 0])
    bonus = head_sum(r * rows_ref[0:1, :] * k)
    base = bonus * v.astype(jnp.float32) + cols_ref[:, 1:2] * matmul_nt(q_low, state)
    step = min(length, TILE)
    for top in range(0, length, step):
        reach = top + step
        rows = slice(top, reach)
        keep = pair_mask(cols_ref[rows, 0:1], seg_ref[0, :, :reach], top, step, reach)
        parts = []
        for q_part in head_parts(q_low[rows]):
            scores = matmul_nt(q_part, k_low[:reach])
            scores = jnp.where(keep, scores, 0.0).astype(jnp.bfloat16)
            parts.append(dot_nn(scores, v[:reach]))
        attend = base[rows] + jnp.where(low_head(parts[0].shape), parts[0], parts[1])
        unit, _ = group_norm(attend)
        grouped = unit * rows_ref[1:2, :] + rows_ref[2:3, :]
        gate = gate_ref[rows, :]
        attend_ref[rows, :] = attend
        joined_ref[rows, :] = (grouped * (gate * jax.nn.sigmoid(gate))).astype(jnp.bfloat16)


def pair_mask(seg_col, seg_row, top, count, reach):
    later = lax.broadcasted_iota(jnp.int32, (count, reach), 0) + top
    return (seg_col == seg_row) & (later > lanes_of((count, reach)))


def pair_mask_t(seg_col, seg_row, top, count, start):
    width = seg_row.shape[1]
    earlier = lax.broadcasted_iota(jnp.int32, (count, width), 0) + top
    return (seg_col == seg_row) & (lanes_of((count, width)) + start > earlier)


def gate_back_kernel(
    dj_ref, attend_ref, gate_ref, r_ref, log_ref, rows_ref, cols_ref,
    dgate_ref, dattend_ref, state_ref, small_ref,
):
    length = r_ref.shape[0]
    d_joined = dj_ref[...]
    gate = gate_ref[...]
    unit, inverse = group_norm(attend_ref[...])
    gain = rows_ref[1:2, :]
    grouped = unit * gain + rows_ref[2:3, :]
    sig = jax.nn.sigmoid(gate)
    dgate_ref[...] = (d_joined * grouped * sig * (1.0 + gate * (1.0 - sig))).astype(jnp.bfloat16)
    d_grouped = d_joined * gate * sig
    sums = [
        jnp.sum(d_grouped * unit, axis=0, keepdims=True),
        jnp.sum(d_grouped, axis=0, keepdims=True),
    ]
    scaled = d_grouped * gain
    share = 1.0 / SUBSPACE_SIZE
    d_attend = (
        inverse * (scaled - head_sum(scaled) * share - unit * (head_sum(scaled * unit) * share))
    ).astype(jnp.bfloat16)
    dattend_ref[...] = d_attend
    rising = jnp.exp(places(length) * log_ref[...])
    q_live = (r_ref[...].astype(jnp.float32) * rising * cols_ref[:, 1:2]).astype(jnp.bfloat16)
    state_ref[0, 0] = fold_pair(matmul_tn(d_attend, q_live))
    collect(small_ref, sums)


def collect(small_ref, sums):
    pad = jnp.zeros((small_ref.shape[0] - len(sums), sums[0].shape[1]), jnp.float32)
    total = jnp.concatenate(sums + [pad], axis=0)

    @pl.when(pl.program_id(1) == 0)
    def _():
        small_ref[...] = total

    @pl.when(pl.program_id(1) > 0)
    def _():
        small_ref[...] += total


def mix_back_kernel(
    r_ref, k_ref, v_ref, da_ref, log_ref, rows_ref, cols_ref, seg_ref, state_ref, gstate_ref,
    mult_ref, dr_ref, dk_ref, dv_ref, small_ref,
):
    length = r_ref.shape[0]
    at = places(length)
    log = log_ref[...]
    reward = rows_ref[0:1, :]
    r = r_ref[...].astype(jnp.float32)
    k = k_ref[...].astype(jnp.float32)
    v = v_ref[...]
    da = da_ref[...]
    rising = jnp.exp(at * log)
    falling = jnp.exp(-(at + 1.0) * log)
    closing = jnp.exp((length - 1.0 - at) * log) * cols_ref[:, 2:3]
    q_low = (r * rising).astype(jnp.bfloat16)
    k_low = (k * falling).astype(jnp.bfloat16)
    k_end = (k * closing).astype(jnp.bfloat16)
    state, gstate = state_ref[0, 0], gstate_ref[0, 0]
    state_low, gstate_low = spread_pair(state), spread_pair(gstate)
    v_f, da_f = v.astype(jnp.float32), da.astype(jnp.float32)
    dot_va = head_sum(v_f * da_f)
    dk_end = dot_nn(v, gstate_low)
    dq_base = cols_ref[:, 1:2] * dot_nn(da, state_low)
    dv_base = head_sum(r * reward * k) * da_f + matmul_nt(k_end, gstate_low)
    q_f, k_f = q_low.astype(jnp.float32), k_low.astype(jnp.float32)
    d_log = jnp.sum((length - 1.0 - at) * k_end.astype(jnp.float32) * dk_end, 0, keepdims=True)
    d_log += length * mult_ref[0, 0] * jnp.sum(
        state.astype(jnp.bfloat16).astype(jnp.float32)
        * gstate.astype(jnp.bfloat16).astype(jnp.float32),
        0,
        keepdims=True,
    )
    step = min(length, TILE)
    for top in range(0, length, step):
        rows = slice(top, top + step)
        reach = top + step
        keep = pair_mask(cols_ref[rows, 0:1], seg_ref[0, :, :reach], top, step, reach)
        dq = []
        for da_part in head_parts(da[rows]):
            pull = jnp.where(keep, matmul_nt(da_part, v[:reach]), 0.0).astype(jnp.bfloat16)
            dq.append(dot_nn(pull, k_low[:reach]))
        first = low_head(dq[0].shape)
        dq = jnp.where(first, dq[0], dq[1]) + dq_base[rows]
        d_log += jnp.sum(at[rows] * q_f[rows] * dq, 0, keepdims=True)
        dr_ref[rows, :] = (dq * rising[rows] + reward * k[rows] * dot_va[rows]).astype(jnp.bfloat16)
        keep = pair_mask_t(cols_ref[rows, 0:1], seg_ref[0, :, top:], top, step, top)
        dk, dv = [], []
        for v_part, k_part in zip(head_parts(v[rows]), head_parts(k_low[rows])):
            pull = jnp.where(keep, matmul_nt(v_part, da[top:]), 0.0).astype(jnp.bfloat16)
            dk.append(dot_nn(pull, q_low[top:]))
            scores = jnp.where(keep, matmul_nt(k_part, q_low[top:]), 0.0).astype(jnp.bfloat16)
            dv.append(dot_nn(scores, da[top:]))
        dk = jnp.where(first, dk[0], dk[1])
        d_log -= jnp.sum((at[rows] + 1.0) * k_f[rows] * dk, 0, keepdims=True)
        dk_ref[rows, :] = (
            dk * falling[rows]
            + dk_end[rows] * closing[rows]
            + reward * r[rows] * dot_va[rows]
        ).astype(jnp.bfloat16)
        dv_ref[rows, :] = (jnp.where(first, dv[0], dv[1]) + dv_base[rows]).astype(jnp.bfloat16)
    collect(small_ref, [d_log * jnp.exp(-log), jnp.sum(r * k * dot_va, 0, keepdims=True)])


def pair_call(kernel, seqs, length, width, operands, outs, name, flops):
    pairs = width // PAIR
    specs = {
        "wide": pl.BlockSpec((length, PAIR), lambda p, s: (s, p)),
        "vector": pl.BlockSpec((1, PAIR), lambda p, s: (0, p)),
        "vectors": pl.BlockSpec((8, PAIR), lambda p, s: (0, p)),
        "cols": pl.BlockSpec((length, 4), lambda p, s: (s, 0)),
        "row": pl.BlockSpec((1, 1, length), lambda p, s: (s, 0, 0)),
        "state": pl.BlockSpec((1, 1, SUBSPACE_SIZE, PAIR), lambda p, s: (s, p, 0, 0)),
        "mult": pl.BlockSpec((1, 1, 1, PAIR), lambda p, s: (s, p, 0, 0)),
    }
    shapes = {
        "wide": (seqs * length, width),
        "vectors": (8, width),
        "state": (seqs, pairs, SUBSPACE_SIZE, PAIR),
    }
    kinds, arrays = zip(*operands)
    size = sum(array.size * array.dtype.itemsize for array in arrays)
    return pl.pallas_call(
        kernel,
        grid=(pairs, seqs),
        in_specs=[specs[kind] for kind in kinds],
        out_specs=[specs[kind] for kind, _ in outs],
        out_shape=[jax.ShapeDtypeStruct(shapes[kind], dtype) for kind, dtype in outs],
        cost_estimate=pl.CostEstimate(flops=flops, bytes_accessed=2 * size, transcendentals=0),
        name=name,
    )(*arrays)


def unit_rows(x):
    centered = x - jnp.mean(x, -1, keepdims=True)
    return centered * lax.rsqrt(jnp.mean(centered * centered, -1, keepdims=True) + EPS)


def total_at(refs, rows, lanes):
    total = refs[0][rows, lanes].astype(jnp.float32)
    for ref in refs[1:]:
        total = total + ref[rows, lanes].astype(jnp.float32)
    return total


def lane_loop(width, body):
    def step(at, _):
        body(pl.ds(pl.multiple_of(at * PAIR, PAIR), PAIR))
        return 0

    lax.fori_loop(0, width // PAIR, step, 0)


def row_blocks(rows):
    return [slice(top, min(top + SPAN, rows)) for top in range(0, rows, SPAN)]


def unit_into(refs, unit_scr, rows, width):
    inverses = []
    for block in row_blocks(rows):
        inside = slice(block.start + HALO, block.stop + HALO)
        zero = jnp.zeros((block.stop - block.start, PAIR), jnp.float32)

        def load(at, total):
            lanes = pl.ds(pl.multiple_of(at * PAIR, PAIR), PAIR)
            value = total_at(refs, block, lanes)
            unit_scr[inside, lanes] = value
            return total + value

        total = lax.fori_loop(0, width // PAIR, load, zero, unroll=4)
        mean = jnp.sum(total, -1, keepdims=True) * (1.0 / width)

        def square(at, total):
            lanes = pl.ds(pl.multiple_of(at * PAIR, PAIR), PAIR)
            value = unit_scr[inside, lanes] - mean
            return total + value * value

        total = lax.fori_loop(0, width // PAIR, square, zero, unroll=4)
        inverse = lax.rsqrt(jnp.sum(total, -1, keepdims=True) * (1.0 / width) + EPS)

        def scale(at, _):
            lanes = pl.ds(pl.multiple_of(at * PAIR, PAIR), PAIR)
            unit_scr[inside, lanes] = (unit_scr[inside, lanes] - mean) * inverse
            return 0

        lax.fori_loop(0, width // PAIR, scale, 0, unroll=4)
        inverses.append(inverse)
    return inverses


def blend_kernel(parts, mixes, per_seq, *refs):
    x_refs, refs = refs[:parts], refs[parts:]
    keep_ref, edge_ref, norm_ref, mix_ref = refs[:4]
    outs, unit_scr = refs[4 : 4 + mixes], refs[4 + mixes]
    rows, width = x_refs[0].shape

    @pl.when(pl.program_id(0) % per_seq == 0)
    def _():
        unit_scr[HALO - 1 : HALO, :] = edge_ref[0]

    unit_into(x_refs, unit_scr, rows, width)

    def lane_block(lanes):
        gain, bias_term = norm_ref[0:1, lanes], norm_ref[1:2, lanes]
        mixers = [mix_ref[at : at + 1, lanes] for at in range(mixes)]
        for block in row_blocks(rows):
            normed = unit_scr[block.start + HALO : block.stop + HALO, lanes] * gain + bias_term
            before = pltpu.roll(unit_scr[block.start : block.stop + HALO, lanes], 1, 0)[HALO:]
            previous = (before * gain + bias_term) * keep_ref[block, 0:1]
            delta = normed - previous
            for mixer, out in zip(mixers, outs):
                out[block, lanes] = (previous + mixer * delta).astype(jnp.bfloat16)

    lane_loop(width, lane_block)
    unit_scr[HALO - 1 : HALO, :] = unit_scr[rows + HALO - 1 : rows + HALO, :]


def blend(xs, keep, edge, norm, mixers, piece, name):
    tokens, width = xs[0].shape
    rows = min(piece, 256)
    mixes = mixers.shape[0]
    per_seq = piece // rows
    wide = pl.BlockSpec((rows, width), lambda i: (i, 0))
    return pl.pallas_call(
        partial(blend_kernel, len(xs), mixes, per_seq),
        grid=(tokens // rows,),
        in_specs=[wide] * len(xs)
        + [
            pl.BlockSpec((rows, 1), lambda i: (i, 0)),
            pl.BlockSpec((1, 1, width), lambda i: (i // per_seq, 0, 0)),
            pl.BlockSpec((2, width), lambda i: (0, 0)),
            pl.BlockSpec((mixes, width), lambda i: (0, 0)),
        ],
        out_specs=[wide] * mixes,
        out_shape=[jax.ShapeDtypeStruct((tokens, width), jnp.bfloat16)] * mixes,
        scratch_shapes=[pltpu.VMEM((rows + HALO, width), jnp.float32)],
        cost_estimate=pl.CostEstimate(
            flops=20 * tokens * width,
            bytes_accessed=2 * tokens * width * (len(xs) + mixes),
            transcendentals=0,
        ),
        name=name,
    )(*xs, keep, edge, norm, mixers)


def blend_back_kernel(parts, mixes, per_seq, own, *refs):
    x_refs, refs = refs[:parts], refs[parts:]
    halo_refs, refs = refs[:parts], refs[parts:]
    grad_refs, refs = refs[:mixes], refs[mixes:]
    weight_refs, refs = refs[:mixes], refs[mixes:]
    keep_ref, edge_ref, back_ref, norm_ref, mix_ref = refs[:5]
    refs = refs[5:]
    own_refs, refs = refs[: 2 * own], refs[2 * own :]
    out_ref, small_ref, d_scr, unit_scr, prev_scr, row_scr, sums = refs
    rows, width = x_refs[0].shape
    tiles = pl.num_programs(0)
    tile = tiles - 1 - pl.program_id(0)

    @pl.when(pl.program_id(0) == 0)
    def _():
        sums[...] = jnp.zeros_like(sums)

    @pl.when(tile % per_seq == per_seq - 1)
    def _():
        prev_scr[rows : rows + 1, :] = back_ref[0]

    @pl.when(tile % per_seq < per_seq - 1)
    def _():
        prev_scr[rows : rows + 1, :] = prev_scr[0:1, :]

    for at in range(mixes):
        d_scr[at] = matmul_nt(grad_refs[at][...], weight_refs[at][...])

    halo = unit_rows(total_at(halo_refs, slice(None), slice(None)))[GROUP - 1 :, :]
    unit_scr[HALO - 1 : HALO, :] = jnp.where(tile % per_seq == 0, edge_ref[0], halo)
    inverses = unit_into(x_refs, unit_scr, rows, width)
    row_scr[...] = jnp.zeros_like(row_scr)

    def gather(at, value):
        total = value[0:8]
        for top in range(8, value.shape[0], 8):
            total = total + value[top : top + 8]
        return total

    def first_pass(lanes):
        gain, bias_term = norm_ref[0:1, lanes], norm_ref[1:2, lanes]
        mixers = [mix_ref[at : at + 1, lanes] for at in range(mixes)]
        totals = [jnp.zeros((8, PAIR), jnp.float32)] * mixes
        for block in row_blocks(rows):
            keep = keep_ref[block, 0:1]
            normed = unit_scr[block.start + HALO : block.stop + HALO, lanes] * gain + bias_term
            before = pltpu.roll(unit_scr[block.start : block.stop + HALO, lanes], 1, 0)[HALO:]
            delta = normed - (before * gain + bias_term) * keep
            d_norm, d_all = None, None
            for at in range(mixes):
                d_in = d_scr[at, block, lanes]
                totals[at] = totals[at] + gather(at, d_in * delta)
                share = d_in * mixers[at]
                d_norm = share if d_norm is None else d_norm + share
                d_all = d_in if d_all is None else d_all + d_in
            prev_scr[block, lanes] = (d_all - d_norm) * keep
            d_scr[0, block, lanes] = d_norm
        for at in range(mixes):
            sums[2 + at, :, lanes] += totals[at]

    lane_loop(width, first_pass)

    def second_pass(lanes):
        gain = norm_ref[0:1, lanes]
        totals = [jnp.zeros((8, PAIR), jnp.float32)] * 2
        for block in row_blocks(rows):
            size = block.stop - block.start
            later = pltpu.roll(
                prev_scr[block.start : block.stop + HALO, lanes], size + HALO - 1, 0
            )[:size]
            d_norm = d_scr[0, block, lanes] + later
            unit = unit_scr[block.start + HALO : block.stop + HALO, lanes]
            product = d_norm * unit
            totals[0] = totals[0] + gather(0, product)
            totals[1] = totals[1] + gather(1, d_norm)
            d_scr[0, block, lanes] = d_norm * gain
            row_scr[0, block, :] += d_norm * gain
            row_scr[1, block, :] += product * gain
        for at in range(2):
            sums[at, :, lanes] += totals[at]

    lane_loop(width, second_pass)
    means, tilts = [], []
    for block in row_blocks(rows):
        means.append(jnp.sum(row_scr[0, block, :], -1, keepdims=True) * (1.0 / width))
        tilts.append(jnp.sum(row_scr[1, block, :], -1, keepdims=True) * (1.0 / width))
    blocks = list(zip(row_blocks(rows), inverses, means, tilts))

    def last_pass(start, lanes):
        for block, inverse, mean, tilt in blocks:
            unit = unit_scr[block.start + HALO : block.stop + HALO, lanes]
            value = inverse * (d_scr[0, block, lanes] - mean - unit * tilt)
            if own:
                extra = own_refs[0][block, start].astype(jnp.float32)
                value = value + extra * own_refs[1][0:1, lanes]
            out_ref[block, lanes] = value.astype(jnp.bfloat16)

    def last_step(at, _):
        lanes = pl.ds(pl.multiple_of(at * PAIR, PAIR), PAIR)
        inner = None
        if own:
            count = own_refs[0].shape[1] // PAIR
            inner = pl.ds(pl.multiple_of((at % count) * PAIR, PAIR), PAIR)
        last_pass(inner, lanes)
        return 0

    lax.fori_loop(0, width // PAIR, last_step, 0)

    @pl.when(pl.program_id(0) == tiles - 1)
    def _():
        for at in range(2 + mixes):
            small_ref[at : at + 1, :] = jnp.sum(sums[at], 0, keepdims=True)


def blend_back(xs, grads, weights, keep, edge, back, norm, mixers, piece, own, name):
    tokens, width = xs[0].shape
    rows = min(piece, 256)
    mixes = mixers.shape[0]
    per_seq = piece // rows
    tiles = tokens // rows

    def reverse(i):
        return tiles - 1 - i

    def halo_at(i):
        return (jnp.maximum(reverse(i) * (rows // GROUP) - 1, 0), 0)

    wide = pl.BlockSpec((rows, width), lambda i: (reverse(i), 0))
    per = pl.BlockSpec((1, 1, width), lambda i: (reverse(i) // per_seq, 0, 0))
    weight_specs, weight_arrays = [], []
    for (array, at), grad in zip(weights, grads):
        weight_specs.append(
            pl.BlockSpec(
                (width, grad.shape[1]), partial(lambda at, i: (0, at), at),
                pipeline_mode=pl.Buffered(1),
            )
        )
        weight_arrays.append(array)
    return pl.pallas_call(
        partial(blend_back_kernel, len(xs), mixes, per_seq, int(own is not None)),
        grid=(tiles,),
        in_specs=[wide] * len(xs)
        + [pl.BlockSpec((GROUP, width), halo_at)] * len(xs)
        + [pl.BlockSpec((rows, grad.shape[1]), lambda i: (reverse(i), 0)) for grad in grads]
        + weight_specs
        + [
            pl.BlockSpec((rows, 1), lambda i: (reverse(i), 0)),
            per,
            per,
            pl.BlockSpec((2, width), lambda i: (0, 0)),
            pl.BlockSpec((mixes, width), lambda i: (0, 0)),
        ]
        + (
            [
                pl.BlockSpec((rows, own[0].shape[1]), lambda i: (reverse(i), 0)),
                pl.BlockSpec((1, width), lambda i: (0, 0)),
            ]
            if own is not None
            else []
        ),
        out_specs=[wide, pl.BlockSpec((8, width), lambda i: (0, 0))],
        out_shape=[
            jax.ShapeDtypeStruct((tokens, width), jnp.bfloat16),
            jax.ShapeDtypeStruct((8, width), jnp.float32),
        ],
        scratch_shapes=[
            pltpu.VMEM((mixes, rows, width), jnp.float32),
            pltpu.VMEM((rows + HALO, width), jnp.float32),
            pltpu.VMEM((rows + HALO, width), jnp.float32),
            pltpu.VMEM((2, rows, PAIR), jnp.float32),
            pltpu.VMEM((2 + mixes, 8, width), jnp.float32),
        ],
        cost_estimate=pl.CostEstimate(
            flops=2 * tokens * width * sum(grad.shape[1] for grad in grads),
            bytes_accessed=2 * tokens * width * 4,
            transcendentals=0,
        ),
        name=name,
    )(*xs, *xs, *grads, *weight_arrays, keep, edge, back, norm, mixers, *(own or ()))


def per_device(
    entering_activations,
    document_indices,
    acceptor_matrix,
    lookup_matrix,
    payload_matrix,
    valve_matrix,
    result_matrix,
    ffn_lookup_matrix,
    ffn_payload_matrix,
    ffn_acceptor_matrix,
    first_standardize_scaling,
    first_standardize_offset,
    acceptor_lerp_factor,
    lookup_lerp_factor,
    payload_lerp_factor,
    valve_lerp_factor,
    token_fading,
    diagonal_reward,
    subspace_standardize_scaling,
    subspace_standardize_offset,
    second_standardize_scaling,
    second_standardize_offset,
    ffn_lookup_lerp,
    ffn_acceptor_lerp,
    upstream_derivative,
):
    seqs_here, piece_len, embedding_extent = entering_activations.shape
    token_count = seqs_here * piece_len
    tp_count = lax.axis_size("tp")
    fourth_extent = embedding_extent // tp_count
    sharded_layout = lax.axis_index("tp") * fourth_extent
    ctx_place = lax.axis_index("ctx") * piece_len
    padded_seg = jnp.concatenate(
        [jnp.full((seqs_here, 1), -1, jnp.int32), document_indices], axis=1
    )
    segment_present = lax.dynamic_slice_in_dim(document_indices, ctx_place, piece_len, 1)
    seg_before = lax.dynamic_slice_in_dim(padded_seg, ctx_place, piece_len, 1)
    document_begins = seg_before[:, :1]
    pairs_here = fourth_extent // PAIR
    same_mask = segment_present == seg_before
    live_mask = segment_present == document_begins
    ending_mask = segment_present == segment_present[:, -1:]
    cols = jnp.stack([segment_present, live_mask, ending_mask, same_mask], axis=-1)
    cols = cols.astype(jnp.float32).reshape(token_count, 4)
    keep = same_mask.astype(jnp.float32).reshape(token_count, 1)
    keep_first = same_mask[:, :1].astype(jnp.float32)
    seg_row = segment_present.astype(jnp.float32)[:, None, :]
    owners = ("fsdp", "ctx")
    w_time = lax.all_gather(
        jnp.concatenate(
            [acceptor_matrix, lookup_matrix, payload_matrix, valve_matrix, result_matrix.T], axis=1
        ),
        owners,
        axis=0,
        tiled=True,
    )
    w_chan = lax.all_gather(
        jnp.concatenate([ffn_lookup_matrix, ffn_acceptor_matrix], axis=1),
        owners,
        axis=0,
        tiled=True,
    )
    units = ffn_lookup_matrix.shape[1]
    w_recept, w_key, w_value, w_gate, w_output_t = (
        w_time[:, at * fourth_extent : (at + 1) * fourth_extent] for at in range(5)
    )
    w_chankey = w_chan[:, :units]
    w_chanrecept = w_chan[:, units:]
    w_chanvalue_t = lax.all_gather(ffn_payload_matrix.T, owners, axis=0, tiled=True)
    x_low = entering_activations.reshape(token_count, embedding_extent)
    norm_one = jnp.stack([first_standardize_scaling, first_standardize_offset])
    norm_two = jnp.stack([second_standardize_scaling, second_standardize_offset])
    mix_one = jnp.stack(
        [acceptor_lerp_factor, lookup_lerp_factor, payload_lerp_factor, valve_lerp_factor]
    )
    mix_two = jnp.stack([ffn_lookup_lerp, ffn_acceptor_lerp])

    def edge_from(last_rows):
        return shifted(unit_rows(last_rows), "ctx", 1)[:, None]

    def back_from(grads, weights, mixers):
        first = jnp.zeros((seqs_here, embedding_extent), jnp.float32)
        for at, (grad_low, weight) in enumerate(zip(grads, weights)):
            rows = grad_low.reshape(seqs_here, piece_len, -1)[:, 0]
            first = first + matmul_nt(rows, weight) * (1.0 - mixers[at])
        return shifted(first * keep_first, "ctx", -1)[:, None]

    edge_one = edge_from(entering_activations[:, -1].astype(jnp.float32))
    mixed_in = blend((x_low,), keep, edge_one, norm_one, mix_one, piece_len, "blend_one")
    key_low = matmul(mixed_in[1], w_key).astype(jnp.bfloat16)
    value_low = matmul(mixed_in[2], w_value).astype(jnp.bfloat16)

    def own_share(vector):
        return lax.dynamic_slice_in_dim(vector, sharded_layout, fourth_extent, 0)[None]

    log_row = jnp.log(own_share(token_fading))
    vectors = jnp.concatenate(
        [own_share(diagonal_reward), own_share(subspace_standardize_scaling)]
        + [own_share(subspace_standardize_offset)] * 6
    )
    call = partial(pair_call, seqs=seqs_here, length=piece_len, width=fourth_extent)
    square = 2 * token_count * piece_len * fourth_extent
    (carry_sums,) = call(
        carry_kernel,
        operands=[("wide", key_low), ("wide", value_low), ("vector", log_row), ("cols", cols)],
        outs=[("state", jnp.float32)],
        name="carry",
        flops=square // 8,
    )
    alive_mask = (live_mask[:, -1]).astype(jnp.float32)[:, None, None, None]
    carry_mult = alive_mask * jnp.exp(float(piece_len) * log_row).reshape(1, pairs_here, 1, PAIR)
    incoming = carried(carry_mult, carry_sums, "ctx", 1)
    recept_low = matmul(mixed_in[0], w_recept).astype(jnp.bfloat16)
    gate_pre = matmul(mixed_in[3], w_gate)
    joined_low, attend = call(
        mix_kernel,
        operands=[
            ("wide", recept_low),
            ("wide", key_low),
            ("wide", value_low),
            ("wide", gate_pre),
            ("vector", log_row),
            ("vectors", vectors),
            ("cols", cols),
            ("row", seg_row),
            ("state", incoming),
        ],
        outs=[("wide", jnp.bfloat16), ("wide", jnp.float32)],
        name="mix",
        flops=2 * square,
    )
    mixed_out = tp_sum(matmul_nt(joined_low, w_output_t).astype(jnp.bfloat16))
    last_rows = entering_activations[:, -1].astype(jnp.float32) + mixed_out.reshape(
        seqs_here, piece_len, embedding_extent
    )[:, -1].astype(jnp.float32)
    edge_two = edge_from(last_rows)
    key_in, rec_in = blend(
        (x_low, mixed_out), keep, edge_two, norm_two, mix_two, piece_len, "blend_two"
    )
    rec_gate = jax.nn.sigmoid(matmul(rec_in, w_chanrecept))
    d_result_low = upstream_derivative.reshape(token_count, fourth_extent)
    d_result = d_result_low.astype(jnp.float32)
    d_chan = (d_result * rec_gate).astype(jnp.bfloat16)
    d_chan_full = tp_gather(d_chan)
    key_pre = matmul(key_in, w_chankey)
    hidden = jnp.square(jax.nn.relu(key_pre)).astype(jnp.bfloat16)
    grad_chanvalue = matmul_tn(d_chan_full, hidden).astype(jnp.bfloat16)
    steps_f, steps_c = len(axis_bits("fsdp")), len(axis_bits("ctx"))
    value_steps = owner_scatter_steps(grad_chanvalue)
    g_chanvalue = next(value_steps)
    hidden, grad_chanvalue = after(hidden, grad_chanvalue)
    chan_sum = tp_scatter(matmul_nt(hidden, w_chanvalue_t).astype(jnp.bfloat16)).astype(jnp.float32)
    middle_q = lax.dynamic_slice_in_dim(x_low, sharded_layout, fourth_extent, 1).astype(
        jnp.float32
    ) + lax.dynamic_slice_in_dim(mixed_out, sharded_layout, fourth_extent, 1).astype(jnp.float32)
    result = (
        (middle_q + rec_gate * chan_sum)
        .astype(jnp.bfloat16)
        .reshape(seqs_here, piece_len, fourth_extent)
    )
    d_rec_pre = (d_result * chan_sum * rec_gate * (1.0 - rec_gate)).astype(jnp.bfloat16)
    d_hidden = matmul(d_chan_full, w_chanvalue_t)
    d_key_pre = (d_hidden * 2.0 * jax.nn.relu(key_pre)).astype(jnp.bfloat16)
    d_key_pre, g_chanvalue = after(d_key_pre, g_chanvalue)
    for _ in range(steps_f + steps_c - 2):
        g_chanvalue = value_steps.send(g_chanvalue)
    full_shape = (seqs_here, piece_len, embedding_extent)
    own_mask = (jnp.arange(embedding_extent) // fourth_extent == lax.axis_index("tp")).astype(
        jnp.float32
    )[None]
    d_middle_part, chan_small = blend_back(
        (x_low, mixed_out),
        (d_key_pre, d_rec_pre),
        ((w_chan, 0), (w_chanrecept, 0)),
        keep,
        edge_two,
        back_from((d_key_pre, d_rec_pre), (w_chankey, w_chanrecept), mix_two),
        norm_two,
        mix_two,
        piece_len,
        (d_result_low, own_mask),
        "blend_two_back",
    )

    def chan_grads(token):
        d_key_late, d_rec_late, _ = after(d_key_pre, d_rec_pre, token)
        return jnp.concatenate(
            [
                matmul_tn(key_in, d_key_late).astype(jnp.bfloat16),
                matmul_tn(rec_in, d_rec_late).astype(jnp.bfloat16),
            ],
            axis=1,
        )

    d_middle_part, g_chanvalue = after(d_middle_part, g_chanvalue)
    g_chanvalue = value_steps.send(g_chanvalue)
    d_mixed, grads_chan = tp_sum(d_middle_part, chan_grads)
    d_mixed, grads_chan = after(d_mixed, grads_chan)
    g_chan = lax.psum_scatter(grads_chan, owners, scatter_dimension=0, tiled=True)
    grad_output_t = matmul_tn(d_mixed, joined_low).astype(jnp.bfloat16)
    d_joined = matmul(d_mixed, w_output_t)
    d_gate_pre, d_attend, local_grad, group_small = call(
        gate_back_kernel,
        operands=[
            ("wide", d_joined),
            ("wide", attend),
            ("wide", gate_pre),
            ("wide", recept_low),
            ("vector", log_row),
            ("vectors", vectors),
            ("cols", cols),
        ],
        outs=[
            ("wide", jnp.bfloat16),
            ("wide", jnp.bfloat16),
            ("state", jnp.float32),
            ("vectors", jnp.float32),
        ],
        name="gate_back",
        flops=square // 8,
    )
    grads_early = jnp.concatenate(
        [grad_output_t, matmul_tn(mixed_in[3], d_gate_pre).astype(jnp.bfloat16)], axis=1
    )
    early = owner_scatter_steps(grads_early)
    g_early = next(early)
    outgoing_state = carried(carry_mult, local_grad, "ctx", -1)
    d_recept, d_key, d_value, state_small = call(
        mix_back_kernel,
        operands=[
            ("wide", recept_low),
            ("wide", key_low),
            ("wide", value_low),
            ("wide", d_attend),
            ("vector", log_row),
            ("vectors", vectors),
            ("cols", cols),
            ("row", seg_row),
            ("state", incoming),
            ("state", outgoing_state),
            ("mult", carry_mult),
        ],
        outs=[("wide", jnp.bfloat16)] * 3 + [("vectors", jnp.float32)],
        name="mix_back",
        flops=6 * square,
    )
    d_recept, d_key, d_value, g_early = after(d_recept, d_key, d_value, g_early)
    for _ in range(steps_f + steps_c - 2):
        g_early = early.send(g_early)
    d_lows = [d_recept, d_key, d_value, d_gate_pre]
    weights_time = (w_recept, w_key, w_value, w_gate)
    grads_time = jnp.concatenate(
        [
            matmul_tn(mixed, grad_low).astype(jnp.bfloat16)
            for mixed, grad_low in zip(mixed_in, d_lows[:3])
        ],
        axis=1,
    )
    *d_lows, _ = after(d_lows[0], *d_lows[1:], grads_time)
    g_time = lax.psum_scatter(grads_time, owners, scatter_dimension=0, tiled=True)
    d_input_part, time_small = blend_back(
        (x_low,),
        d_lows,
        [(w_time, at) for at in range(4)],
        keep,
        edge_one,
        back_from(d_lows, weights_time, mix_one),
        norm_one,
        mix_one,
        piece_len,
        None,
        "blend_one_back",
    )
    d_input_part, g_early, g_chan = after(d_input_part, g_early, g_chan)
    g_early = early.send(g_early)
    head_small = jnp.concatenate([state_small[:2], group_small[:2]])
    head_small = lax.dynamic_update_slice_in_dim(
        jnp.zeros((4, embedding_extent), jnp.float32), head_small, sharded_layout, 1
    )
    small_part = jnp.concatenate([time_small[:6], head_small, chan_small[:4]], axis=0)

    def small_total(token):
        return whole_sum(after(small_part, token)[0], ("tp", "fsdp", "ctx"))

    d_input_sum, small_sum = tp_sum(d_input_part, small_total)
    owned = embedding_extent // (lax.axis_size("fsdp") * lax.axis_size("ctx"))
    small_owned = lax.dynamic_slice_in_dim(
        small_sum,
        (lax.axis_index("fsdp") * lax.axis_size("ctx") + lax.axis_index("ctx")) * owned,
        owned,
        1,
    )
    grad_inputs = (d_mixed.astype(jnp.float32) + d_input_sum.astype(jnp.float32)).reshape(
        full_shape
    )
    g_chanvalue = g_chanvalue.astype(jnp.float32).T
    g_chan = g_chan.astype(jnp.float32)
    g_time = g_time.astype(jnp.float32)
    g_early = g_early.astype(jnp.float32)
    g_recept, g_key, g_value = (
        g_time[:, at * fourth_extent : (at + 1) * fourth_extent] for at in range(3)
    )
    g_output = g_early[:, :fourth_extent].T
    g_gate = g_early[:, fourth_extent:]
    g_chankey = g_chan[:, :units]
    g_chanrecept = g_chan[:, units:]
    return (
        result,
        grad_inputs,
        g_recept,
        g_key,
        g_value,
        g_gate,
        g_output,
        g_chankey,
        g_chanvalue,
        g_chanrecept,
    ) + tuple(small_owned[at] for at in range(14))


def solution(mesh):
    return jax.shard_map(
        per_device,
        mesh=mesh,
        in_specs=(
            P("fsdp", "ctx", None),
            P("fsdp", None),
            P(("fsdp", "ctx"), "tp"),
            P(("fsdp", "ctx"), "tp"),
            P(("fsdp", "ctx"), "tp"),
            P(("fsdp", "ctx"), "tp"),
            P("tp", ("fsdp", "ctx")),
            P(("fsdp", "ctx"), "tp"),
            P("tp", ("fsdp", "ctx")),
            P(("fsdp", "ctx"), "tp"),
            P(),
            P(),
            P(),
            P(),
            P(),
            P(),
            P(),
            P(),
            P(),
            P(),
            P(),
            P(),
            P(),
            P(),
            P("fsdp", "ctx", "tp"),
        ),
        out_specs=(
            P("fsdp", "ctx", "tp"),
            P("fsdp", "ctx", None),
            P(("fsdp", "ctx"), "tp"),
            P(("fsdp", "ctx"), "tp"),
            P(("fsdp", "ctx"), "tp"),
            P(("fsdp", "ctx"), "tp"),
            P("tp", ("fsdp", "ctx")),
            P(("fsdp", "ctx"), "tp"),
            P("tp", ("fsdp", "ctx")),
            P(("fsdp", "ctx"), "tp"),
            P(("fsdp", "ctx")),
            P(("fsdp", "ctx")),
            P(("fsdp", "ctx")),
            P(("fsdp", "ctx")),
            P(("fsdp", "ctx")),
            P(("fsdp", "ctx")),
            P(("fsdp", "ctx")),
            P(("fsdp", "ctx")),
            P(("fsdp", "ctx")),
            P(("fsdp", "ctx")),
            P(("fsdp", "ctx")),
            P(("fsdp", "ctx")),
            P(("fsdp", "ctx")),
            P(("fsdp", "ctx")),
        ),
        check_vma=False,
    )
```

```python
from functools import partial

import jax
import jax.numpy as jnp
from jax import lax
from jax.experimental import pallas as pl
from jax.experimental.pallas import tpu as pltpu
from jax.sharding import PartitionSpec as P

SUBSPACE_SIZE = 64
PAIR = 128
GROUP = 16
HALO = 8
SPAN = 64
TILE = 256


EPS = 1e-05
GROUP_EPS = 4.0


def shifted(x, axis, by):
    count = lax.axis_size(axis)
    pairs = [(i, i + by) for i in range(count) if 0 <= i + by < count]
    return lax.ppermute(x, axis, pairs)


def earlier_shift(x, axis, by):
    count = lax.axis_size(axis)
    return lax.ppermute(x, axis, [(i, i + by) for i in range(count) if 0 <= i + by < count])


def carried(mult, sums, axis, toward):
    count = lax.axis_size(axis)
    low = (mult.astype(jnp.bfloat16), sums.astype(jnp.bfloat16))
    arrived = [
        jax.tree.map(lambda part: earlier_shift(part, axis, toward * by), low)
        for by in range(1, count)
    ]
    state = jnp.zeros_like(sums)
    for far_mult, far_sums in reversed(arrived):
        state = far_mult.astype(jnp.float32) * state + far_sums.astype(jnp.float32)
    return state


def partner(x, bit):
    count = lax.axis_size("tp")
    return lax.ppermute(x, "tp", [(i, i ^ bit) for i in range(count)])


def halves(x, axis, bit):
    size = x.shape[axis] // 2
    mine = (lax.axis_index("tp") // bit) % 2
    return (
        lax.dynamic_slice_in_dim(x, mine * size, size, axis),
        lax.dynamic_slice_in_dim(x, (1 - mine) * size, size, axis),
    )


def add_low(left, right):
    return (left.astype(jnp.float32) + right.astype(jnp.float32)).astype(jnp.bfloat16)


def ordered(mine, other, axis, bit):
    first = (lax.axis_index("tp") // bit) % 2 == 0
    return jnp.where(
        first,
        jnp.concatenate([mine, other], axis),
        jnp.concatenate([other, mine], axis),
    )


def after(value, *earlier):
    return lax.optimization_barrier((value,) + earlier)


def tp_sum(x, work=None):
    mine, other = halves(x, 0, 1)
    part = add_low(mine, partner(other, 1))
    made = work(part) if work else None
    bit = 2
    while bit < lax.axis_size("tp"):
        arrived = partner(part, bit)
        if work and bit == 2:
            part = after(part, made)[0]
        part = add_low(part, arrived)
        bit *= 2
    whole = ordered(part, partner(part, 1), 0, 1)
    return (whole, made) if work else whole


def axis_bits(axis):
    bits, bit = [], 1
    while bit < lax.axis_size(axis):
        bits.append((axis, bit))
        bit *= 2
    return bits


def swap(x, axis, bit):
    return lax.ppermute(x, axis, [(i, i ^ bit) for i in range(lax.axis_size(axis))])


def owner_gather(x):
    whole = x[None]
    for axis, bit in list(reversed(axis_bits("ctx"))) + axis_bits("fsdp"):
        whole = jnp.concatenate([whole, swap(whole, axis, bit)])
    ctx, fsdp = lax.axis_size("ctx"), lax.axis_size("fsdp")
    ctx_bits = [bit for _, bit in reversed(axis_bits("ctx"))]
    rows = []
    for f in range(fsdp):
        for c in range(ctx):
            far_f, far_c = lax.axis_index("fsdp") ^ f, lax.axis_index("ctx") ^ c
            at = far_f * ctx + sum(((far_c // bit) % 2) * (1 << k) for k, bit in enumerate(ctx_bits))
            rows.append(lax.dynamic_index_in_dim(whole, at, 0, False))
    return jnp.concatenate(rows)


def whole_sum(x, axes):
    for axis in axes:
        count = lax.axis_size(axis)
        bit = 1
        while bit < count:
            x = x + lax.ppermute(x, axis, [(i, i ^ bit) for i in range(count)])
            bit *= 2
    return x


def tp_scatter(x):
    count, place = lax.axis_size("tp"), lax.axis_index("tp")
    width = x.shape[1] // count
    parts = [
        lax.dynamic_slice_in_dim(x, (place ^ relative) * width, width, 1)
        for relative in range(count)
    ]
    bit = 1
    while bit < count:
        for relative in reversed(range(count)):
            if relative & bit and relative & (bit - 1) == 0:
                arrived = partner(parts[relative], bit)
                parts[relative ^ bit] = add_low(parts[relative ^ bit], arrived)
        bit *= 2
    return parts[0]


def tp_gather(x):
    count, place = lax.axis_size("tp"), lax.axis_index("tp")
    width = x.shape[1]
    parts = {0: x}
    bit = count // 2
    while bit:
        parts.update({relative ^ bit: partner(part, bit) for relative, part in parts.items()})
        bit //= 2
    whole = jnp.zeros((x.shape[0], width * count), x.dtype)
    for relative, part in parts.items():
        whole = lax.dynamic_update_slice_in_dim(whole, part, (place ^ relative) * width, 1)
    return whole


def matmul(left, right):
    return jnp.dot(left, right, preferred_element_type=jnp.float32)


def matmul_tn(left, right):
    return lax.dot_general(
        left, right, (((0,), (0,)), ((), ())), preferred_element_type=jnp.float32
    )


def matmul_nt(left, right):
    return lax.dot_general(
        left, right, (((1,), (1,)), ((), ())), preferred_element_type=jnp.float32
    )


def dot_nn(left, right):
    return lax.dot_general(
        left, right, (((1,), (0,)), ((), ())), preferred_element_type=jnp.float32
    )


def lanes_of(shape):
    return lax.broadcasted_iota(jnp.int32, shape, len(shape) - 1)


def low_head(shape):
    return lanes_of(shape) < SUBSPACE_SIZE


def head_sum(x):
    first = low_head(x.shape)
    low = jnp.sum(jnp.where(first, x, 0.0), -1, keepdims=True)
    high = jnp.sum(jnp.where(first, 0.0, x), -1, keepdims=True)
    return jnp.where(first, low, high)


def fold_pair(both):
    return jnp.where(
        low_head((SUBSPACE_SIZE, PAIR)), both[:SUBSPACE_SIZE], both[SUBSPACE_SIZE:]
    )


def spread_pair(folded):
    first = low_head((SUBSPACE_SIZE, PAIR))
    return jnp.concatenate(
        [jnp.where(first, folded, 0.0), jnp.where(first, 0.0, folded)], axis=0
    ).astype(jnp.bfloat16)


def head_parts(x):
    first = low_head(x.shape)
    zero = jnp.zeros_like(x)
    return jnp.where(first, x, zero), jnp.where(first, zero, x)


def places(length):
    return lax.broadcasted_iota(jnp.int32, (length, PAIR), 0).astype(jnp.float32)


def carry_kernel(k_ref, v_ref, log_ref, cols_ref, out_ref):
    length = k_ref.shape[0]
    closing = jnp.exp((length - 1.0 - places(length)) * log_ref[...])
    ending = cols_ref[:, 2:3]
    k_end = (k_ref[...].astype(jnp.float32) * closing * ending).astype(jnp.bfloat16)
    out_ref[0, 0] = fold_pair(matmul_tn(v_ref[...], k_end))


def group_norm(attend):
    centered = attend - head_sum(attend) * (1.0 / SUBSPACE_SIZE)
    inverse = lax.rsqrt(head_sum(centered * centered) * (1.0 / SUBSPACE_SIZE) + GROUP_EPS)
    return centered * inverse, inverse


def mix_kernel(
    r_ref, k_ref, v_ref, gate_ref, log_ref, rows_ref, cols_ref, seg_ref, state_ref,
    joined_ref, attend_ref,
):
    length = r_ref.shape[0]
    at = places(length)
    log = log_ref[...]
    r = r_ref[...].astype(jnp.float32)
    k = k_ref[...].astype(jnp.float32)
    v = v_ref[...]
    q_low = (r * jnp.exp(at * log)).astype(jnp.bfloat16)
    k_low = (k * jnp.exp(-(at + 1.0) * log)).astype(jnp.bfloat16)
    state = spread_pair(state_ref[0, 0])
    bonus = head_sum(r * rows_ref[0:1, :] * k)
    base = bonus * v.astype(jnp.float32) + cols_ref[:, 1:2] * matmul_nt(q_low, state)
    step = min(length, TILE)
    for top in range(0, length, step):
        reach = top + step
        rows = slice(top, reach)
        keep = pair_mask(cols_ref[rows, 0:1], seg_ref[0, :, :reach], top, step, reach)
        parts = []
        for q_part in head_parts(q_low[rows]):
            scores = matmul_nt(q_part, k_low[:reach])
            scores = jnp.where(keep, scores, 0.0).astype(jnp.bfloat16)
            parts.append(dot_nn(scores, v[:reach]))
        attend = base[rows] + jnp.where(low_head(parts[0].shape), parts[0], parts[1])
        unit, _ = group_norm(attend)
        grouped = unit * rows_ref[1:2, :] + rows_ref[2:3, :]
        gate = gate_ref[rows, :]
        attend_ref[rows, :] = attend
        joined_ref[rows, :] = (grouped * (gate * jax.nn.sigmoid(gate))).astype(jnp.bfloat16)


def pair_mask(seg_col, seg_row, top, count, reach):
    later = lax.broadcasted_iota(jnp.int32, (count, reach), 0) + top
    return (seg_col == seg_row) & (later > lanes_of((count, reach)))


def pair_mask_t(seg_col, seg_row, top, count, start):
    width = seg_row.shape[1]
    earlier = lax.broadcasted_iota(jnp.int32, (count, width), 0) + top
    return (seg_col == seg_row) & (lanes_of((count, width)) + start > earlier)


def gate_back_kernel(
    dj_ref, attend_ref, gate_ref, r_ref, log_ref, rows_ref, cols_ref,
    dgate_ref, dattend_ref, state_ref, small_ref,
):
    length = r_ref.shape[0]
    d_joined = dj_ref[...]
    gate = gate_ref[...]
    unit, inverse = group_norm(attend_ref[...])
    gain = rows_ref[1:2, :]
    grouped = unit * gain + rows_ref[2:3, :]
    sig = jax.nn.sigmoid(gate)
    dgate_ref[...] = (d_joined * grouped * sig * (1.0 + gate * (1.0 - sig))).astype(jnp.bfloat16)
    d_grouped = d_joined * gate * sig
    sums = [
        jnp.sum(d_grouped * unit, axis=0, keepdims=True),
        jnp.sum(d_grouped, axis=0, keepdims=True),
    ]
    scaled = d_grouped * gain
    share = 1.0 / SUBSPACE_SIZE
    d_attend = (
        inverse * (scaled - head_sum(scaled) * share - unit * (head_sum(scaled * unit) * share))
    ).astype(jnp.bfloat16)
    dattend_ref[...] = d_attend
    rising = jnp.exp(places(length) * log_ref[...])
    q_live = (r_ref[...].astype(jnp.float32) * rising * cols_ref[:, 1:2]).astype(jnp.bfloat16)
    state_ref[0, 0] = fold_pair(matmul_tn(d_attend, q_live))
    collect(small_ref, sums)


def collect(small_ref, sums):
    pad = jnp.zeros((small_ref.shape[0] - len(sums), sums[0].shape[1]), jnp.float32)
    total = jnp.concatenate(sums + [pad], axis=0)

    @pl.when(pl.program_id(1) == 0)
    def _():
        small_ref[...] = total

    @pl.when(pl.program_id(1) > 0)
    def _():
        small_ref[...] += total


def mix_back_kernel(
    r_ref, k_ref, v_ref, da_ref, log_ref, rows_ref, cols_ref, seg_ref, state_ref, gstate_ref,
    mult_ref, dr_ref, dk_ref, dv_ref, small_ref,
):
    length = r_ref.shape[0]
    at = places(length)
    log = log_ref[...]
    reward = rows_ref[0:1, :]
    r = r_ref[...].astype(jnp.float32)
    k = k_ref[...].astype(jnp.float32)
    v = v_ref[...]
    da = da_ref[...]
    rising = jnp.exp(at * log)
    falling = jnp.exp(-(at + 1.0) * log)
    closing = jnp.exp((length - 1.0 - at) * log) * cols_ref[:, 2:3]
    q_low = (r * rising).astype(jnp.bfloat16)
    k_low = (k * falling).astype(jnp.bfloat16)
    k_end = (k * closing).astype(jnp.bfloat16)
    state, gstate = state_ref[0, 0], gstate_ref[0, 0]
    state_low, gstate_low = spread_pair(state), spread_pair(gstate)
    v_f, da_f = v.astype(jnp.float32), da.astype(jnp.float32)
    dot_va = head_sum(v_f * da_f)
    dk_end = dot_nn(v, gstate_low)
    dq_base = cols_ref[:, 1:2] * dot_nn(da, state_low)
    dv_base = head_sum(r * reward * k) * da_f + matmul_nt(k_end, gstate_low)
    q_f, k_f = q_low.astype(jnp.float32), k_low.astype(jnp.float32)
    d_log = jnp.sum((length - 1.0 - at) * k_end.astype(jnp.float32) * dk_end, 0, keepdims=True)
    d_log += length * mult_ref[0, 0] * jnp.sum(
        state.astype(jnp.bfloat16).astype(jnp.float32)
        * gstate.astype(jnp.bfloat16).astype(jnp.float32),
        0,
        keepdims=True,
    )
    step = min(length, TILE)
    for top in range(0, length, step):
        rows = slice(top, top + step)
        reach = top + step
        keep = pair_mask(cols_ref[rows, 0:1], seg_ref[0, :, :reach], top, step, reach)
        dq = []
        for da_part in head_parts(da[rows]):
            pull = jnp.where(keep, matmul_nt(da_part, v[:reach]), 0.0).astype(jnp.bfloat16)
            dq.append(dot_nn(pull, k_low[:reach]))
        first = low_head(dq[0].shape)
        dq = jnp.where(first, dq[0], dq[1]) + dq_base[rows]
        d_log += jnp.sum(at[rows] * q_f[rows] * dq, 0, keepdims=True)
        dr_ref[rows, :] = (dq * rising[rows] + reward * k[rows] * dot_va[rows]).astype(jnp.bfloat16)
        keep = pair_mask_t(cols_ref[rows, 0:1], seg_ref[0, :, top:], top, step, top)
        dk, dv = [], []
        for v_part, k_part in zip(head_parts(v[rows]), head_parts(k_low[rows])):
            pull = jnp.where(keep, matmul_nt(v_part, da[top:]), 0.0).astype(jnp.bfloat16)
            dk.append(dot_nn(pull, q_low[top:]))
            scores = jnp.where(keep, matmul_nt(k_part, q_low[top:]), 0.0).astype(jnp.bfloat16)
            dv.append(dot_nn(scores, da[top:]))
        dk = jnp.where(first, dk[0], dk[1])
        d_log -= jnp.sum((at[rows] + 1.0) * k_f[rows] * dk, 0, keepdims=True)
        dk_ref[rows, :] = (
            dk * falling[rows]
            + dk_end[rows] * closing[rows]
            + reward * r[rows] * dot_va[rows]
        ).astype(jnp.bfloat16)
        dv_ref[rows, :] = (jnp.where(first, dv[0], dv[1]) + dv_base[rows]).astype(jnp.bfloat16)
    collect(small_ref, [d_log * jnp.exp(-log), jnp.sum(r * k * dot_va, 0, keepdims=True)])


def pair_call(kernel, seqs, length, width, operands, outs, name, flops):
    pairs = width // PAIR
    specs = {
        "wide": pl.BlockSpec((length, PAIR), lambda p, s: (s, p)),
        "vector": pl.BlockSpec((1, PAIR), lambda p, s: (0, p)),
        "vectors": pl.BlockSpec((8, PAIR), lambda p, s: (0, p)),
        "cols": pl.BlockSpec((length, 4), lambda p, s: (s, 0)),
        "row": pl.BlockSpec((1, 1, length), lambda p, s: (s, 0, 0)),
        "state": pl.BlockSpec((1, 1, SUBSPACE_SIZE, PAIR), lambda p, s: (s, p, 0, 0)),
        "mult": pl.BlockSpec((1, 1, 1, PAIR), lambda p, s: (s, p, 0, 0)),
    }
    shapes = {
        "wide": (seqs * length, width),
        "vectors": (8, width),
        "state": (seqs, pairs, SUBSPACE_SIZE, PAIR),
    }
    kinds, arrays = zip(*operands)
    size = sum(array.size * array.dtype.itemsize for array in arrays)
    return pl.pallas_call(
        kernel,
        grid=(pairs, seqs),
        in_specs=[specs[kind] for kind in kinds],
        out_specs=[specs[kind] for kind, _ in outs],
        out_shape=[jax.ShapeDtypeStruct(shapes[kind], dtype) for kind, dtype in outs],
        cost_estimate=pl.CostEstimate(flops=flops, bytes_accessed=2 * size, transcendentals=0),
        name=name,
    )(*arrays)


def unit_rows(x):
    centered = x - jnp.mean(x, -1, keepdims=True)
    return centered * lax.rsqrt(jnp.mean(centered * centered, -1, keepdims=True) + EPS)


def total_at(refs, rows, lanes):
    total = refs[0][rows, lanes].astype(jnp.float32)
    for ref in refs[1:]:
        total = total + ref[rows, lanes].astype(jnp.float32)
    return total


def lane_loop(width, body):
    def step(at, _):
        body(pl.ds(pl.multiple_of(at * PAIR, PAIR), PAIR))
        return 0

    lax.fori_loop(0, width // PAIR, step, 0)


def row_blocks(rows):
    return [slice(top, min(top + SPAN, rows)) for top in range(0, rows, SPAN)]


def unit_into(refs, unit_scr, rows, width):
    inverses = []
    for block in row_blocks(rows):
        inside = slice(block.start + HALO, block.stop + HALO)
        zero = jnp.zeros((block.stop - block.start, PAIR), jnp.float32)

        def load(at, total):
            lanes = pl.ds(pl.multiple_of(at * PAIR, PAIR), PAIR)
            value = total_at(refs, block, lanes)
            unit_scr[inside, lanes] = value
            return total + value

        total = lax.fori_loop(0, width // PAIR, load, zero, unroll=4)
        mean = jnp.sum(total, -1, keepdims=True) * (1.0 / width)

        def square(at, total):
            lanes = pl.ds(pl.multiple_of(at * PAIR, PAIR), PAIR)
            value = unit_scr[inside, lanes] - mean
            return total + value * value

        total = lax.fori_loop(0, width // PAIR, square, zero, unroll=4)
        inverse = lax.rsqrt(jnp.sum(total, -1, keepdims=True) * (1.0 / width) + EPS)

        def scale(at, _):
            lanes = pl.ds(pl.multiple_of(at * PAIR, PAIR), PAIR)
            unit_scr[inside, lanes] = (unit_scr[inside, lanes] - mean) * inverse
            return 0

        lax.fori_loop(0, width // PAIR, scale, 0, unroll=4)
        inverses.append(inverse)
    return inverses


def blend_kernel(parts, mixes, per_seq, *refs):
    x_refs, refs = refs[:parts], refs[parts:]
    keep_ref, edge_ref, norm_ref, mix_ref = refs[:4]
    outs, unit_scr = refs[4 : 4 + mixes], refs[4 + mixes]
    rows, width = x_refs[0].shape

    @pl.when(pl.program_id(0) % per_seq == 0)
    def _():
        unit_scr[HALO - 1 : HALO, :] = edge_ref[0]

    unit_into(x_refs, unit_scr, rows, width)

    def lane_block(lanes):
        gain, bias_term = norm_ref[0:1, lanes], norm_ref[1:2, lanes]
        mixers = [mix_ref[at : at + 1, lanes] for at in range(mixes)]
        for block in row_blocks(rows):
            normed = unit_scr[block.start + HALO : block.stop + HALO, lanes] * gain + bias_term
            before = pltpu.roll(unit_scr[block.start : block.stop + HALO, lanes], 1, 0)[HALO:]
            previous = (before * gain + bias_term) * keep_ref[block, 0:1]
            delta = normed - previous
            for mixer, out in zip(mixers, outs):
                out[block, lanes] = (previous + mixer * delta).astype(jnp.bfloat16)

    lane_loop(width, lane_block)
    unit_scr[HALO - 1 : HALO, :] = unit_scr[rows + HALO - 1 : rows + HALO, :]


def blend(xs, keep, edge, norm, mixers, piece, name):
    tokens, width = xs[0].shape
    rows = min(piece, 256)
    mixes = mixers.shape[0]
    per_seq = piece // rows
    wide = pl.BlockSpec((rows, width), lambda i: (i, 0))
    return pl.pallas_call(
        partial(blend_kernel, len(xs), mixes, per_seq),
        grid=(tokens // rows,),
        in_specs=[wide] * len(xs)
        + [
            pl.BlockSpec((rows, 1), lambda i: (i, 0)),
            pl.BlockSpec((1, 1, width), lambda i: (i // per_seq, 0, 0)),
            pl.BlockSpec((2, width), lambda i: (0, 0)),
            pl.BlockSpec((mixes, width), lambda i: (0, 0)),
        ],
        out_specs=[wide] * mixes,
        out_shape=[jax.ShapeDtypeStruct((tokens, width), jnp.bfloat16)] * mixes,
        scratch_shapes=[pltpu.VMEM((rows + HALO, width), jnp.float32)],
        cost_estimate=pl.CostEstimate(
            flops=20 * tokens * width,
            bytes_accessed=2 * tokens * width * (len(xs) + mixes),
            transcendentals=0,
        ),
        name=name,
    )(*xs, keep, edge, norm, mixers)


def blend_back_kernel(parts, mixes, per_seq, own, *refs):
    x_refs, refs = refs[:parts], refs[parts:]
    halo_refs, refs = refs[:parts], refs[parts:]
    grad_refs, refs = refs[:mixes], refs[mixes:]
    weight_refs, refs = refs[:mixes], refs[mixes:]
    keep_ref, edge_ref, back_ref, norm_ref, mix_ref = refs[:5]
    refs = refs[5:]
    own_refs, refs = refs[: 2 * own], refs[2 * own :]
    out_ref, small_ref, d_scr, unit_scr, prev_scr, row_scr, sums = refs
    rows, width = x_refs[0].shape
    tiles = pl.num_programs(0)
    tile = tiles - 1 - pl.program_id(0)

    @pl.when(pl.program_id(0) == 0)
    def _():
        sums[...] = jnp.zeros_like(sums)

    @pl.when(tile % per_seq == per_seq - 1)
    def _():
        prev_scr[rows : rows + 1, :] = back_ref[0]

    @pl.when(tile % per_seq < per_seq - 1)
    def _():
        prev_scr[rows : rows + 1, :] = prev_scr[0:1, :]

    for at in range(mixes):
        d_scr[at] = matmul_nt(grad_refs[at][...], weight_refs[at][...])

    halo = unit_rows(total_at(halo_refs, slice(None), slice(None)))[GROUP - 1 :, :]
    unit_scr[HALO - 1 : HALO, :] = jnp.where(tile % per_seq == 0, edge_ref[0], halo)
    inverses = unit_into(x_refs, unit_scr, rows, width)
    row_scr[...] = jnp.zeros_like(row_scr)

    def gather(at, value):
        total = value[0:8]
        for top in range(8, value.shape[0], 8):
            total = total + value[top : top + 8]
        return total

    def first_pass(lanes):
        gain, bias_term = norm_ref[0:1, lanes], norm_ref[1:2, lanes]
        mixers = [mix_ref[at : at + 1, lanes] for at in range(mixes)]
        totals = [jnp.zeros((8, PAIR), jnp.float32)] * mixes
        for block in row_blocks(rows):
            keep = keep_ref[block, 0:1]
            normed = unit_scr[block.start + HALO : block.stop + HALO, lanes] * gain + bias_term
            before = pltpu.roll(unit_scr[block.start : block.stop + HALO, lanes], 1, 0)[HALO:]
            delta = normed - (before * gain + bias_term) * keep
            d_norm, d_all = None, None
            for at in range(mixes):
                d_in = d_scr[at, block, lanes]
                totals[at] = totals[at] + gather(at, d_in * delta)
                share = d_in * mixers[at]
                d_norm = share if d_norm is None else d_norm + share
                d_all = d_in if d_all is None else d_all + d_in
            prev_scr[block, lanes] = (d_all - d_norm) * keep
            d_scr[0, block, lanes] = d_norm
        for at in range(mixes):
            sums[2 + at, :, lanes] += totals[at]

    lane_loop(width, first_pass)

    def second_pass(lanes):
        gain = norm_ref[0:1, lanes]
        totals = [jnp.zeros((8, PAIR), jnp.float32)] * 2
        for block in row_blocks(rows):
            size = block.stop - block.start
            later = pltpu.roll(
                prev_scr[block.start : block.stop + HALO, lanes], size + HALO - 1, 0
            )[:size]
            d_norm = d_scr[0, block, lanes] + later
            unit = unit_scr[block.start + HALO : block.stop + HALO, lanes]
            product = d_norm * unit
            totals[0] = totals[0] + gather(0, product)
            totals[1] = totals[1] + gather(1, d_norm)
            d_scr[0, block, lanes] = d_norm * gain
            row_scr[0, block, :] += d_norm * gain
            row_scr[1, block, :] += product * gain
        for at in range(2):
            sums[at, :, lanes] += totals[at]

    lane_loop(width, second_pass)
    means, tilts = [], []
    for block in row_blocks(rows):
        means.append(jnp.sum(row_scr[0, block, :], -1, keepdims=True) * (1.0 / width))
        tilts.append(jnp.sum(row_scr[1, block, :], -1, keepdims=True) * (1.0 / width))
    blocks = list(zip(row_blocks(rows), inverses, means, tilts))

    def last_pass(start, lanes):
        for block, inverse, mean, tilt in blocks:
            unit = unit_scr[block.start + HALO : block.stop + HALO, lanes]
            value = inverse * (d_scr[0, block, lanes] - mean - unit * tilt)
            if own:
                extra = own_refs[0][block, start].astype(jnp.float32)
                value = value + extra * own_refs[1][0:1, lanes]
            out_ref[block, lanes] = value.astype(jnp.bfloat16)

    def last_step(at, _):
        lanes = pl.ds(pl.multiple_of(at * PAIR, PAIR), PAIR)
        inner = None
        if own:
            count = own_refs[0].shape[1] // PAIR
            inner = pl.ds(pl.multiple_of((at % count) * PAIR, PAIR), PAIR)
        last_pass(inner, lanes)
        return 0

    lax.fori_loop(0, width // PAIR, last_step, 0)

    @pl.when(pl.program_id(0) == tiles - 1)
    def _():
        for at in range(2 + mixes):
            small_ref[at : at + 1, :] = jnp.sum(sums[at], 0, keepdims=True)


def blend_back(xs, grads, weights, keep, edge, back, norm, mixers, piece, own, name):
    tokens, width = xs[0].shape
    rows = min(piece, 256)
    mixes = mixers.shape[0]
    per_seq = piece // rows
    tiles = tokens // rows

    def reverse(i):
        return tiles - 1 - i

    def halo_at(i):
        return (jnp.maximum(reverse(i) * (rows // GROUP) - 1, 0), 0)

    wide = pl.BlockSpec((rows, width), lambda i: (reverse(i), 0))
    per = pl.BlockSpec((1, 1, width), lambda i: (reverse(i) // per_seq, 0, 0))
    weight_specs, weight_arrays = [], []
    for (array, at), grad in zip(weights, grads):
        weight_specs.append(
            pl.BlockSpec(
                (width, grad.shape[1]), partial(lambda at, i: (0, at), at),
                pipeline_mode=pl.Buffered(1),
            )
        )
        weight_arrays.append(array)
    return pl.pallas_call(
        partial(blend_back_kernel, len(xs), mixes, per_seq, int(own is not None)),
        grid=(tiles,),
        in_specs=[wide] * len(xs)
        + [pl.BlockSpec((GROUP, width), halo_at)] * len(xs)
        + [pl.BlockSpec((rows, grad.shape[1]), lambda i: (reverse(i), 0)) for grad in grads]
        + weight_specs
        + [
            pl.BlockSpec((rows, 1), lambda i: (reverse(i), 0)),
            per,
            per,
            pl.BlockSpec((2, width), lambda i: (0, 0)),
            pl.BlockSpec((mixes, width), lambda i: (0, 0)),
        ]
        + (
            [
                pl.BlockSpec((rows, own[0].shape[1]), lambda i: (reverse(i), 0)),
                pl.BlockSpec((1, width), lambda i: (0, 0)),
            ]
            if own is not None
            else []
        ),
        out_specs=[wide, pl.BlockSpec((8, width), lambda i: (0, 0))],
        out_shape=[
            jax.ShapeDtypeStruct((tokens, width), jnp.bfloat16),
            jax.ShapeDtypeStruct((8, width), jnp.float32),
        ],
        scratch_shapes=[
            pltpu.VMEM((mixes, rows, width), jnp.float32),
            pltpu.VMEM((rows + HALO, width), jnp.float32),
            pltpu.VMEM((rows + HALO, width), jnp.float32),
            pltpu.VMEM((2, rows, PAIR), jnp.float32),
            pltpu.VMEM((2 + mixes, 8, width), jnp.float32),
        ],
        cost_estimate=pl.CostEstimate(
            flops=2 * tokens * width * sum(grad.shape[1] for grad in grads),
            bytes_accessed=2 * tokens * width * 4,
            transcendentals=0,
        ),
        name=name,
    )(*xs, *xs, *grads, *weight_arrays, keep, edge, back, norm, mixers, *(own or ()))


def per_device(
    entering_activations,
    document_indices,
    acceptor_matrix,
    lookup_matrix,
    payload_matrix,
    valve_matrix,
    result_matrix,
    ffn_lookup_matrix,
    ffn_payload_matrix,
    ffn_acceptor_matrix,
    first_standardize_scaling,
    first_standardize_offset,
    acceptor_lerp_factor,
    lookup_lerp_factor,
    payload_lerp_factor,
    valve_lerp_factor,
    token_fading,
    diagonal_reward,
    subspace_standardize_scaling,
    subspace_standardize_offset,
    second_standardize_scaling,
    second_standardize_offset,
    ffn_lookup_lerp,
    ffn_acceptor_lerp,
    upstream_derivative,
):
    seqs_here, piece_len, embedding_extent = entering_activations.shape
    token_count = seqs_here * piece_len
    tp_count = lax.axis_size("tp")
    fourth_extent = embedding_extent // tp_count
    sharded_layout = lax.axis_index("tp") * fourth_extent
    ctx_place = lax.axis_index("ctx") * piece_len
    padded_seg = jnp.concatenate(
        [jnp.full((seqs_here, 1), -1, jnp.int32), document_indices], axis=1
    )
    segment_present = lax.dynamic_slice_in_dim(document_indices, ctx_place, piece_len, 1)
    seg_before = lax.dynamic_slice_in_dim(padded_seg, ctx_place, piece_len, 1)
    document_begins = seg_before[:, :1]
    pairs_here = fourth_extent // PAIR
    same_mask = segment_present == seg_before
    live_mask = segment_present == document_begins
    ending_mask = segment_present == segment_present[:, -1:]
    cols = jnp.stack([segment_present, live_mask, ending_mask, same_mask], axis=-1)
    cols = cols.astype(jnp.float32).reshape(token_count, 4)
    keep = same_mask.astype(jnp.float32).reshape(token_count, 1)
    keep_first = same_mask[:, :1].astype(jnp.float32)
    seg_row = segment_present.astype(jnp.float32)[:, None, :]
    owners = ("fsdp", "ctx")
    w_time = lax.all_gather(
        jnp.concatenate(
            [acceptor_matrix, lookup_matrix, payload_matrix, valve_matrix], axis=1
        ),
        owners,
        axis=0,
        tiled=True,
    )
    w_chan = lax.all_gather(
        jnp.concatenate([ffn_lookup_matrix, ffn_acceptor_matrix], axis=1),
        owners,
        axis=0,
        tiled=True,
    )
    units = ffn_lookup_matrix.shape[1]
    w_recept, w_key, w_value, w_gate = (
        w_time[:, at * fourth_extent : (at + 1) * fourth_extent] for at in range(4)
    )
    w_output_t = owner_gather(result_matrix.T)
    w_chankey = w_chan[:, :units]
    w_chanrecept = w_chan[:, units:]
    w_chanvalue_t = lax.all_gather(ffn_payload_matrix.T, owners, axis=0, tiled=True)
    x_low = entering_activations.reshape(token_count, embedding_extent)
    norm_one = jnp.stack([first_standardize_scaling, first_standardize_offset])
    norm_two = jnp.stack([second_standardize_scaling, second_standardize_offset])
    mix_one = jnp.stack(
        [acceptor_lerp_factor, lookup_lerp_factor, payload_lerp_factor, valve_lerp_factor]
    )
    mix_two = jnp.stack([ffn_lookup_lerp, ffn_acceptor_lerp])

    def edge_from(last_rows):
        return shifted(unit_rows(last_rows), "ctx", 1)[:, None]

    def back_from(grads, weights, mixers):
        first = jnp.zeros((seqs_here, embedding_extent), jnp.float32)
        for at, (grad_low, weight) in enumerate(zip(grads, weights)):
            rows = grad_low.reshape(seqs_here, piece_len, -1)[:, 0]
            first = first + matmul_nt(rows, weight) * (1.0 - mixers[at])
        return shifted(first * keep_first, "ctx", -1)[:, None]

    edge_one = edge_from(entering_activations[:, -1].astype(jnp.float32))
    x_first, w_output_t = after(x_low, w_output_t)
    mixed_in = blend((x_first,), keep, edge_one, norm_one, mix_one, piece_len, "blend_one")
    key_low = matmul(mixed_in[1], w_key).astype(jnp.bfloat16)
    value_low = matmul(mixed_in[2], w_value).astype(jnp.bfloat16)

    def own_share(vector):
        return lax.dynamic_slice_in_dim(vector, sharded_layout, fourth_extent, 0)[None]

    log_row = jnp.log(own_share(token_fading))
    vectors = jnp.concatenate(
        [own_share(diagonal_reward), own_share(subspace_standardize_scaling)]
        + [own_share(subspace_standardize_offset)] * 6
    )
    call = partial(pair_call, seqs=seqs_here, length=piece_len, width=fourth_extent)
    square = 2 * token_count * piece_len * fourth_extent
    (carry_sums,) = call(
        carry_kernel,
        operands=[("wide", key_low), ("wide", value_low), ("vector", log_row), ("cols", cols)],
        outs=[("state", jnp.float32)],
        name="carry",
        flops=square // 8,
    )
    alive_mask = (live_mask[:, -1]).astype(jnp.float32)[:, None, None, None]
    carry_mult = alive_mask * jnp.exp(float(piece_len) * log_row).reshape(1, pairs_here, 1, PAIR)
    incoming = carried(carry_mult, carry_sums, "ctx", 1)
    recept_low = matmul(mixed_in[0], w_recept).astype(jnp.bfloat16)
    gate_pre = matmul(mixed_in[3], w_gate)
    joined_low, attend = call(
        mix_kernel,
        operands=[
            ("wide", recept_low),
            ("wide", key_low),
            ("wide", value_low),
            ("wide", gate_pre),
            ("vector", log_row),
            ("vectors", vectors),
            ("cols", cols),
            ("row", seg_row),
            ("state", incoming),
        ],
        outs=[("wide", jnp.bfloat16), ("wide", jnp.float32)],
        name="mix",
        flops=2 * square,
    )
    mixed_out = tp_sum(matmul_nt(joined_low, w_output_t).astype(jnp.bfloat16))
    last_rows = entering_activations[:, -1].astype(jnp.float32) + mixed_out.reshape(
        seqs_here, piece_len, embedding_extent
    )[:, -1].astype(jnp.float32)
    edge_two = edge_from(last_rows)
    key_in, rec_in = blend(
        (x_low, mixed_out), keep, edge_two, norm_two, mix_two, piece_len, "blend_two"
    )
    rec_gate = jax.nn.sigmoid(matmul(rec_in, w_chanrecept))
    d_result_low = upstream_derivative.reshape(token_count, fourth_extent)
    d_result = d_result_low.astype(jnp.float32)
    d_chan = (d_result * rec_gate).astype(jnp.bfloat16)
    d_chan_full = tp_gather(d_chan)
    key_pre = matmul(key_in, w_chankey)
    hidden = jnp.square(jax.nn.relu(key_pre)).astype(jnp.bfloat16)
    grad_chanvalue = matmul_tn(hidden, d_chan_full).astype(jnp.bfloat16)
    g_chanvalue = lax.psum_scatter(grad_chanvalue, owners, scatter_dimension=1, tiled=True)
    hidden, grad_chanvalue = after(hidden, grad_chanvalue)
    chan_sum = tp_scatter(matmul_nt(hidden, w_chanvalue_t).astype(jnp.bfloat16)).astype(jnp.float32)
    middle_q = lax.dynamic_slice_in_dim(x_low, sharded_layout, fourth_extent, 1).astype(
        jnp.float32
    ) + lax.dynamic_slice_in_dim(mixed_out, sharded_layout, fourth_extent, 1).astype(jnp.float32)
    result = (
        (middle_q + rec_gate * chan_sum)
        .astype(jnp.bfloat16)
        .reshape(seqs_here, piece_len, fourth_extent)
    )
    d_rec_pre = (d_result * chan_sum * rec_gate * (1.0 - rec_gate)).astype(jnp.bfloat16)
    d_hidden = matmul(d_chan_full, w_chanvalue_t)
    d_key_pre = (d_hidden * 2.0 * jax.nn.relu(key_pre)).astype(jnp.bfloat16)
    full_shape = (seqs_here, piece_len, embedding_extent)
    own_mask = (jnp.arange(embedding_extent) // fourth_extent == lax.axis_index("tp")).astype(
        jnp.float32
    )[None]
    d_middle_part, chan_small = blend_back(
        (x_low, mixed_out),
        (d_key_pre, d_rec_pre),
        ((w_chan, 0), (w_chanrecept, 0)),
        keep,
        edge_two,
        back_from((d_key_pre, d_rec_pre), (w_chankey, w_chanrecept), mix_two),
        norm_two,
        mix_two,
        piece_len,
        (d_result_low, own_mask),
        "blend_two_back",
    )

    def chan_grads(token):
        d_key_late, d_rec_late, _ = after(d_key_pre, d_rec_pre, token)
        return jnp.concatenate(
            [
                matmul_tn(key_in, d_key_late).astype(jnp.bfloat16),
                matmul_tn(rec_in, d_rec_late).astype(jnp.bfloat16),
            ],
            axis=1,
        )

    d_mixed, grads_chan = tp_sum(d_middle_part, chan_grads)
    d_mixed, grads_chan, g_chanvalue = after(d_mixed, grads_chan, g_chanvalue)
    g_chan = lax.psum_scatter(grads_chan, owners, scatter_dimension=0, tiled=True)
    grad_output_t = matmul_tn(d_mixed, joined_low).astype(jnp.bfloat16)
    d_joined = matmul(d_mixed, w_output_t)
    d_gate_pre, d_attend, local_grad, group_small = call(
        gate_back_kernel,
        operands=[
            ("wide", d_joined),
            ("wide", attend),
            ("wide", gate_pre),
            ("wide", recept_low),
            ("vector", log_row),
            ("vectors", vectors),
            ("cols", cols),
        ],
        outs=[
            ("wide", jnp.bfloat16),
            ("wide", jnp.bfloat16),
            ("state", jnp.float32),
            ("vectors", jnp.float32),
        ],
        name="gate_back",
        flops=square // 8,
    )
    outgoing_state = carried(carry_mult, local_grad, "ctx", -1)
    d_recept, d_key, d_value, state_small = call(
        mix_back_kernel,
        operands=[
            ("wide", recept_low),
            ("wide", key_low),
            ("wide", value_low),
            ("wide", d_attend),
            ("vector", log_row),
            ("vectors", vectors),
            ("cols", cols),
            ("row", seg_row),
            ("state", incoming),
            ("state", outgoing_state),
            ("mult", carry_mult),
        ],
        outs=[("wide", jnp.bfloat16)] * 3 + [("vectors", jnp.float32)],
        name="mix_back",
        flops=6 * square,
    )
    d_lows = [d_recept, d_key, d_value, d_gate_pre]
    weights_time = (w_recept, w_key, w_value, w_gate)
    grads_time = jnp.concatenate(
        [grad_output_t]
        + [
            matmul_tn(mixed, grad_low).astype(jnp.bfloat16)
            for mixed, grad_low in zip(mixed_in, d_lows)
        ],
        axis=1,
    )
    *d_lows, _ = after(d_lows[0], *d_lows[1:], grads_time)
    g_time = lax.psum_scatter(grads_time, owners, scatter_dimension=0, tiled=True)
    d_input_part, time_small = blend_back(
        (x_low,),
        d_lows,
        [(w_time, at) for at in range(4)],
        keep,
        edge_one,
        back_from(d_lows, weights_time, mix_one),
        norm_one,
        mix_one,
        piece_len,
        None,
        "blend_one_back",
    )
    d_input_part, g_chan = after(d_input_part, g_chan)
    head_small = jnp.concatenate([state_small[:2], group_small[:2]])
    head_small = lax.dynamic_update_slice_in_dim(
        jnp.zeros((4, embedding_extent), jnp.float32), head_small, sharded_layout, 1
    )
    small_part = jnp.concatenate([time_small[:6], head_small, chan_small[:4]], axis=0)

    def small_total(token):
        return whole_sum(after(small_part, token)[0], ("tp", "fsdp", "ctx"))

    d_input_sum, small_sum = tp_sum(d_input_part, small_total)
    owned = embedding_extent // (lax.axis_size("fsdp") * lax.axis_size("ctx"))
    small_owned = lax.dynamic_slice_in_dim(
        small_sum,
        (lax.axis_index("fsdp") * lax.axis_size("ctx") + lax.axis_index("ctx")) * owned,
        owned,
        1,
    )
    grad_inputs = (d_mixed.astype(jnp.float32) + d_input_sum.astype(jnp.float32)).reshape(
        full_shape
    )
    g_chanvalue = g_chanvalue.astype(jnp.float32)
    g_chan = g_chan.astype(jnp.float32)
    g_time = g_time.astype(jnp.float32)
    g_output = g_time[:, :fourth_extent].T
    g_recept, g_key, g_value, g_gate = (
        g_time[:, at * fourth_extent : (at + 1) * fourth_extent] for at in range(1, 5)
    )
    g_chankey = g_chan[:, :units]
    g_chanrecept = g_chan[:, units:]
    return (
        result,
        grad_inputs,
        g_recept,
        g_key,
        g_value,
        g_gate,
        g_output,
        g_chankey,
        g_chanvalue,
        g_chanrecept,
    ) + tuple(small_owned[at] for at in range(14))


def solution(mesh):
    return jax.shard_map(
        per_device,
        mesh=mesh,
        in_specs=(
            P("fsdp", "ctx", None),
            P("fsdp", None),
            P(("fsdp", "ctx"), "tp"),
            P(("fsdp", "ctx"), "tp"),
            P(("fsdp", "ctx"), "tp"),
            P(("fsdp", "ctx"), "tp"),
            P("tp", ("fsdp", "ctx")),
            P(("fsdp", "ctx"), "tp"),
            P("tp", ("fsdp", "ctx")),
            P(("fsdp", "ctx"), "tp"),
            P(),
            P(),
            P(),
            P(),
            P(),
            P(),
            P(),
            P(),
            P(),
            P(),
            P(),
            P(),
            P(),
            P(),
            P("fsdp", "ctx", "tp"),
        ),
        out_specs=(
            P("fsdp", "ctx", "tp"),
            P("fsdp", "ctx", None),
            P(("fsdp", "ctx"), "tp"),
            P(("fsdp", "ctx"), "tp"),
            P(("fsdp", "ctx"), "tp"),
            P(("fsdp", "ctx"), "tp"),
            P("tp", ("fsdp", "ctx")),
            P(("fsdp", "ctx"), "tp"),
            P("tp", ("fsdp", "ctx")),
            P(("fsdp", "ctx"), "tp"),
            P(("fsdp", "ctx")),
            P(("fsdp", "ctx")),
            P(("fsdp", "ctx")),
            P(("fsdp", "ctx")),
            P(("fsdp", "ctx")),
            P(("fsdp", "ctx")),
            P(("fsdp", "ctx")),
            P(("fsdp", "ctx")),
            P(("fsdp", "ctx")),
            P(("fsdp", "ctx")),
            P(("fsdp", "ctx")),
            P(("fsdp", "ctx")),
            P(("fsdp", "ctx")),
            P(("fsdp", "ctx")),
        ),
        check_vma=False,
    )
```

```python
from functools import partial

import jax
import jax.numpy as jnp
from jax import lax
from jax.experimental import pallas as pl
from jax.experimental.pallas import tpu as pltpu
from jax.sharding import PartitionSpec as P

SUBSPACE_SIZE = 64
PAIR = 128
GROUP = 16
HALO = 8
SPAN = 64
TILE = 256


EPS = 1e-05
GROUP_EPS = 4.0


def shifted(x, axis, by):
    count = lax.axis_size(axis)
    pairs = [(i, i + by) for i in range(count) if 0 <= i + by < count]
    return lax.ppermute(x, axis, pairs)


def earlier_shift(x, axis, by):
    count = lax.axis_size(axis)
    return lax.ppermute(x, axis, [(i, i + by) for i in range(count) if 0 <= i + by < count])


def carried(mult, sums, axis, toward):
    count = lax.axis_size(axis)
    low = (mult.astype(jnp.bfloat16), sums.astype(jnp.bfloat16))
    arrived = [
        jax.tree.map(lambda part: earlier_shift(part, axis, toward * by), low)
        for by in range(1, count)
    ]
    state = jnp.zeros_like(sums)
    for far_mult, far_sums in reversed(arrived):
        state = far_mult.astype(jnp.float32) * state + far_sums.astype(jnp.float32)
    return state


def partner(x, bit):
    count = lax.axis_size("tp")
    return lax.ppermute(x, "tp", [(i, i ^ bit) for i in range(count)])


def halves(x, axis, bit):
    size = x.shape[axis] // 2
    mine = (lax.axis_index("tp") // bit) % 2
    return (
        lax.dynamic_slice_in_dim(x, mine * size, size, axis),
        lax.dynamic_slice_in_dim(x, (1 - mine) * size, size, axis),
    )


def add_low(left, right):
    return (left.astype(jnp.float32) + right.astype(jnp.float32)).astype(jnp.bfloat16)


def ordered(mine, other, axis, bit):
    first = (lax.axis_index("tp") // bit) % 2 == 0
    return jnp.where(
        first,
        jnp.concatenate([mine, other], axis),
        jnp.concatenate([other, mine], axis),
    )


def after(value, *earlier):
    return lax.optimization_barrier((value,) + earlier)


def tp_sum(x, work=None):
    mine, other = halves(x, 0, 1)
    part = add_low(mine, partner(other, 1))
    made = work(part) if work else None
    bit = 2
    while bit < lax.axis_size("tp"):
        arrived = partner(part, bit)
        if work and bit == 2:
            part = after(part, made)[0]
        part = add_low(part, arrived)
        bit *= 2
    whole = ordered(part, partner(part, 1), 0, 1)
    return (whole, made) if work else whole


def axis_bits(axis):
    bits, bit = [], 1
    while bit < lax.axis_size(axis):
        bits.append((axis, bit))
        bit *= 2
    return bits


def swap(x, axis, bit):
    return lax.ppermute(x, axis, [(i, i ^ bit) for i in range(lax.axis_size(axis))])


def split_kernel(x_ref, *outs):
    at = 0
    for out in outs:
        out[...] = x_ref[:, at : at + out.shape[1]].astype(jnp.float32)
        at += out.shape[1]


def split_columns(x, widths, name):
    count = x.shape[0]
    rows = min(count, 64)
    return pl.pallas_call(
        split_kernel,
        grid=(count // rows,),
        in_specs=[pl.BlockSpec((rows, x.shape[1]), lambda i: (i, 0))],
        out_specs=[pl.BlockSpec((rows, width), lambda i: (i, 0)) for width in widths],
        out_shape=[jax.ShapeDtypeStruct((count, width), jnp.float32) for width in widths],
        cost_estimate=pl.CostEstimate(flops=x.size, bytes_accessed=6 * x.size, transcendentals=0),
        name=name,
    )(x)


def owner_scatter_steps(x):
    fsdp_bits, ctx_bits = axis_bits("fsdp"), axis_bits("ctx")
    dims = list(reversed(fsdp_bits)) + list(reversed(ctx_bits))
    rows = x.shape[0] // 2 ** len(dims)
    part = x.reshape(*([2] * len(dims)), rows, x.shape[1])
    for axis, bit in fsdp_bits + ctx_bits:
        dim = dims.index((axis, bit))
        dims.pop(dim)
        mine = (lax.axis_index(axis) // bit) % 2
        own = lax.dynamic_index_in_dim(part, mine, dim, False)
        arrived = swap(lax.dynamic_index_in_dim(part, 1 - mine, dim, False), axis, bit)
        part = add_low(own, arrived)
        part = yield part
    yield None


def whole_sum(x, axes):
    for axis in axes:
        count = lax.axis_size(axis)
        bit = 1
        while bit < count:
            x = x + lax.ppermute(x, axis, [(i, i ^ bit) for i in range(count)])
            bit *= 2
    return x


def tp_scatter(x):
    count, place = lax.axis_size("tp"), lax.axis_index("tp")
    width = x.shape[1] // count
    parts = [
        lax.dynamic_slice_in_dim(x, (place ^ relative) * width, width, 1)
        for relative in range(count)
    ]
    bit = 1
    while bit < count:
        for relative in reversed(range(count)):
            if relative & bit and relative & (bit - 1) == 0:
                arrived = partner(parts[relative], bit)
                parts[relative ^ bit] = add_low(parts[relative ^ bit], arrived)
        bit *= 2
    return parts[0]


def tp_gather(x):
    count, place = lax.axis_size("tp"), lax.axis_index("tp")
    width = x.shape[1]
    parts = {0: x}
    bit = count // 2
    while bit:
        parts.update({relative ^ bit: partner(part, bit) for relative, part in parts.items()})
        bit //= 2
    whole = jnp.zeros((x.shape[0], width * count), x.dtype)
    for relative, part in parts.items():
        whole = lax.dynamic_update_slice_in_dim(whole, part, (place ^ relative) * width, 1)
    return whole


def matmul(left, right):
    return jnp.dot(left, right, preferred_element_type=jnp.float32)


def matmul_tn(left, right):
    return lax.dot_general(
        left, right, (((0,), (0,)), ((), ())), preferred_element_type=jnp.float32
    )


def matmul_nt(left, right):
    return lax.dot_general(
        left, right, (((1,), (1,)), ((), ())), preferred_element_type=jnp.float32
    )


def dot_nn(left, right):
    return lax.dot_general(
        left, right, (((1,), (0,)), ((), ())), preferred_element_type=jnp.float32
    )


def lanes_of(shape):
    return lax.broadcasted_iota(jnp.int32, shape, len(shape) - 1)


def low_head(shape):
    return lanes_of(shape) < SUBSPACE_SIZE


def head_sum(x):
    first = low_head(x.shape)
    low = jnp.sum(jnp.where(first, x, 0.0), -1, keepdims=True)
    high = jnp.sum(jnp.where(first, 0.0, x), -1, keepdims=True)
    return jnp.where(first, low, high)


def fold_pair(both):
    return jnp.where(
        low_head((SUBSPACE_SIZE, PAIR)), both[:SUBSPACE_SIZE], both[SUBSPACE_SIZE:]
    )


def spread_pair(folded):
    first = low_head((SUBSPACE_SIZE, PAIR))
    return jnp.concatenate(
        [jnp.where(first, folded, 0.0), jnp.where(first, 0.0, folded)], axis=0
    ).astype(jnp.bfloat16)


def head_parts(x):
    first = low_head(x.shape)
    zero = jnp.zeros_like(x)
    return jnp.where(first, x, zero), jnp.where(first, zero, x)


def places(length):
    return lax.broadcasted_iota(jnp.int32, (length, PAIR), 0).astype(jnp.float32)


def carry_kernel(k_ref, v_ref, log_ref, cols_ref, out_ref):
    length = k_ref.shape[0]
    closing = jnp.exp((length - 1.0 - places(length)) * log_ref[...])
    ending = cols_ref[:, 2:3]
    k_end = (k_ref[...].astype(jnp.float32) * closing * ending).astype(jnp.bfloat16)
    out_ref[0, 0] = fold_pair(matmul_tn(v_ref[...], k_end))


def group_norm(attend):
    centered = attend - head_sum(attend) * (1.0 / SUBSPACE_SIZE)
    inverse = lax.rsqrt(head_sum(centered * centered) * (1.0 / SUBSPACE_SIZE) + GROUP_EPS)
    return centered * inverse, inverse


def mix_kernel(
    r_ref, k_ref, v_ref, gate_ref, log_ref, rows_ref, cols_ref, seg_ref, state_ref,
    joined_ref, attend_ref,
):
    length = r_ref.shape[0]
    at = places(length)
    log = log_ref[...]
    r = r_ref[...].astype(jnp.float32)
    k = k_ref[...].astype(jnp.float32)
    v = v_ref[...]
    q_low = (r * jnp.exp(at * log)).astype(jnp.bfloat16)
    k_low = (k * jnp.exp(-(at + 1.0) * log)).astype(jnp.bfloat16)
    state = spread_pair(state_ref[0, 0])
    bonus = head_sum(r * rows_ref[0:1, :] * k)
    base = bonus * v.astype(jnp.float32) + cols_ref[:, 1:2] * matmul_nt(q_low, state)
    step = min(length, TILE)
    for top in range(0, length, step):
        reach = top + step
        rows = slice(top, reach)
        keep = pair_mask(cols_ref[rows, 0:1], seg_ref[0, :, :reach], top, step, reach)
        parts = []
        for q_part in head_parts(q_low[rows]):
            scores = matmul_nt(q_part, k_low[:reach])
            scores = jnp.where(keep, scores, 0.0).astype(jnp.bfloat16)
            parts.append(dot_nn(scores, v[:reach]))
        attend = base[rows] + jnp.where(low_head(parts[0].shape), parts[0], parts[1])
        unit, _ = group_norm(attend)
        grouped = unit * rows_ref[1:2, :] + rows_ref[2:3, :]
        gate = gate_ref[rows, :]
        attend_ref[rows, :] = attend
        joined_ref[rows, :] = (grouped * (gate * jax.nn.sigmoid(gate))).astype(jnp.bfloat16)


def pair_mask(seg_col, seg_row, top, count, reach):
    later = lax.broadcasted_iota(jnp.int32, (count, reach), 0) + top
    return (seg_col == seg_row) & (later > lanes_of((count, reach)))


def pair_mask_t(seg_col, seg_row, top, count, start):
    width = seg_row.shape[1]
    earlier = lax.broadcasted_iota(jnp.int32, (count, width), 0) + top
    return (seg_col == seg_row) & (lanes_of((count, width)) + start > earlier)


def gate_back_kernel(
    dj_ref, attend_ref, gate_ref, r_ref, log_ref, rows_ref, cols_ref,
    dgate_ref, dattend_ref, state_ref, small_ref,
):
    length = r_ref.shape[0]
    d_joined = dj_ref[...]
    gate = gate_ref[...]
    unit, inverse = group_norm(attend_ref[...])
    gain = rows_ref[1:2, :]
    grouped = unit * gain + rows_ref[2:3, :]
    sig = jax.nn.sigmoid(gate)
    dgate_ref[...] = (d_joined * grouped * sig * (1.0 + gate * (1.0 - sig))).astype(jnp.bfloat16)
    d_grouped = d_joined * gate * sig
    sums = [
        jnp.sum(d_grouped * unit, axis=0, keepdims=True),
        jnp.sum(d_grouped, axis=0, keepdims=True),
    ]
    scaled = d_grouped * gain
    share = 1.0 / SUBSPACE_SIZE
    d_attend = (
        inverse * (scaled - head_sum(scaled) * share - unit * (head_sum(scaled * unit) * share))
    ).astype(jnp.bfloat16)
    dattend_ref[...] = d_attend
    rising = jnp.exp(places(length) * log_ref[...])
    q_live = (r_ref[...].astype(jnp.float32) * rising * cols_ref[:, 1:2]).astype(jnp.bfloat16)
    state_ref[0, 0] = fold_pair(matmul_tn(d_attend, q_live))
    collect(small_ref, sums)


def collect(small_ref, sums):
    pad = jnp.zeros((small_ref.shape[0] - len(sums), sums[0].shape[1]), jnp.float32)
    total = jnp.concatenate(sums + [pad], axis=0)

    @pl.when(pl.program_id(1) == 0)
    def _():
        small_ref[...] = total

    @pl.when(pl.program_id(1) > 0)
    def _():
        small_ref[...] += total


def mix_back_kernel(
    r_ref, k_ref, v_ref, da_ref, log_ref, rows_ref, cols_ref, seg_ref, state_ref, gstate_ref,
    mult_ref, dr_ref, dk_ref, dv_ref, small_ref,
):
    length = r_ref.shape[0]
    at = places(length)
    log = log_ref[...]
    reward = rows_ref[0:1, :]
    r = r_ref[...].astype(jnp.float32)
    k = k_ref[...].astype(jnp.float32)
    v = v_ref[...]
    da = da_ref[...]
    rising = jnp.exp(at * log)
    falling = jnp.exp(-(at + 1.0) * log)
    closing = jnp.exp((length - 1.0 - at) * log) * cols_ref[:, 2:3]
    q_low = (r * rising).astype(jnp.bfloat16)
    k_low = (k * falling).astype(jnp.bfloat16)
    k_end = (k * closing).astype(jnp.bfloat16)
    state, gstate = state_ref[0, 0], gstate_ref[0, 0]
    state_low, gstate_low = spread_pair(state), spread_pair(gstate)
    v_f, da_f = v.astype(jnp.float32), da.astype(jnp.float32)
    dot_va = head_sum(v_f * da_f)
    dk_end = dot_nn(v, gstate_low)
    dq_base = cols_ref[:, 1:2] * dot_nn(da, state_low)
    dv_base = head_sum(r * reward * k) * da_f + matmul_nt(k_end, gstate_low)
    q_f, k_f = q_low.astype(jnp.float32), k_low.astype(jnp.float32)
    d_log = jnp.sum((length - 1.0 - at) * k_end.astype(jnp.float32) * dk_end, 0, keepdims=True)
    d_log += length * mult_ref[0, 0] * jnp.sum(
        state.astype(jnp.bfloat16).astype(jnp.float32)
        * gstate.astype(jnp.bfloat16).astype(jnp.float32),
        0,
        keepdims=True,
    )
    step = min(length, TILE)
    for top in range(0, length, step):
        rows = slice(top, top + step)
        reach = top + step
        keep = pair_mask(cols_ref[rows, 0:1], seg_ref[0, :, :reach], top, step, reach)
        dq = []
        for da_part in head_parts(da[rows]):
            pull = jnp.where(keep, matmul_nt(da_part, v[:reach]), 0.0).astype(jnp.bfloat16)
            dq.append(dot_nn(pull, k_low[:reach]))
        first = low_head(dq[0].shape)
        dq = jnp.where(first, dq[0], dq[1]) + dq_base[rows]
        d_log += jnp.sum(at[rows] * q_f[rows] * dq, 0, keepdims=True)
        dr_ref[rows, :] = (dq * rising[rows] + reward * k[rows] * dot_va[rows]).astype(jnp.bfloat16)
        keep = pair_mask_t(cols_ref[rows, 0:1], seg_ref[0, :, top:], top, step, top)
        dk, dv = [], []
        for v_part, k_part in zip(head_parts(v[rows]), head_parts(k_low[rows])):
            pull = jnp.where(keep, matmul_nt(v_part, da[top:]), 0.0).astype(jnp.bfloat16)
            dk.append(dot_nn(pull, q_low[top:]))
            scores = jnp.where(keep, matmul_nt(k_part, q_low[top:]), 0.0).astype(jnp.bfloat16)
            dv.append(dot_nn(scores, da[top:]))
        dk = jnp.where(first, dk[0], dk[1])
        d_log -= jnp.sum((at[rows] + 1.0) * k_f[rows] * dk, 0, keepdims=True)
        dk_ref[rows, :] = (
            dk * falling[rows]
            + dk_end[rows] * closing[rows]
            + reward * r[rows] * dot_va[rows]
        ).astype(jnp.bfloat16)
        dv_ref[rows, :] = (jnp.where(first, dv[0], dv[1]) + dv_base[rows]).astype(jnp.bfloat16)
    collect(small_ref, [d_log * jnp.exp(-log), jnp.sum(r * k * dot_va, 0, keepdims=True)])


def pair_call(kernel, seqs, length, width, operands, outs, name, flops):
    pairs = width // PAIR
    specs = {
        "wide": pl.BlockSpec((length, PAIR), lambda p, s: (s, p)),
        "vector": pl.BlockSpec((1, PAIR), lambda p, s: (0, p)),
        "vectors": pl.BlockSpec((8, PAIR), lambda p, s: (0, p)),
        "cols": pl.BlockSpec((length, 4), lambda p, s: (s, 0)),
        "row": pl.BlockSpec((1, 1, length), lambda p, s: (s, 0, 0)),
        "state": pl.BlockSpec((1, 1, SUBSPACE_SIZE, PAIR), lambda p, s: (s, p, 0, 0)),
        "mult": pl.BlockSpec((1, 1, 1, PAIR), lambda p, s: (s, p, 0, 0)),
    }
    shapes = {
        "wide": (seqs * length, width),
        "vectors": (8, width),
        "state": (seqs, pairs, SUBSPACE_SIZE, PAIR),
    }
    kinds, arrays = zip(*operands)
    size = sum(array.size * array.dtype.itemsize for array in arrays)
    return pl.pallas_call(
        kernel,
        grid=(pairs, seqs),
        in_specs=[specs[kind] for kind in kinds],
        out_specs=[specs[kind] for kind, _ in outs],
        out_shape=[jax.ShapeDtypeStruct(shapes[kind], dtype) for kind, dtype in outs],
        cost_estimate=pl.CostEstimate(flops=flops, bytes_accessed=2 * size, transcendentals=0),
        name=name,
    )(*arrays)


def unit_rows(x):
    centered = x - jnp.mean(x, -1, keepdims=True)
    return centered * lax.rsqrt(jnp.mean(centered * centered, -1, keepdims=True) + EPS)


def total_at(refs, rows, lanes):
    total = refs[0][rows, lanes].astype(jnp.float32)
    for ref in refs[1:]:
        total = total + ref[rows, lanes].astype(jnp.float32)
    return total


def lane_loop(width, body):
    def step(at, _):
        body(pl.ds(pl.multiple_of(at * PAIR, PAIR), PAIR))
        return 0

    lax.fori_loop(0, width // PAIR, step, 0)


def row_blocks(rows):
    return [slice(top, min(top + SPAN, rows)) for top in range(0, rows, SPAN)]


def unit_into(refs, unit_scr, rows, width):
    inverses = []
    for block in row_blocks(rows):
        inside = slice(block.start + HALO, block.stop + HALO)
        zero = jnp.zeros((block.stop - block.start, PAIR), jnp.float32)

        def load(at, total):
            lanes = pl.ds(pl.multiple_of(at * PAIR, PAIR), PAIR)
            value = total_at(refs, block, lanes)
            unit_scr[inside, lanes] = value
            return total + value

        total = lax.fori_loop(0, width // PAIR, load, zero, unroll=4)
        mean = jnp.sum(total, -1, keepdims=True) * (1.0 / width)

        def square(at, total):
            lanes = pl.ds(pl.multiple_of(at * PAIR, PAIR), PAIR)
            value = unit_scr[inside, lanes] - mean
            return total + value * value

        total = lax.fori_loop(0, width // PAIR, square, zero, unroll=4)
        inverse = lax.rsqrt(jnp.sum(total, -1, keepdims=True) * (1.0 / width) + EPS)

        def scale(at, _):
            lanes = pl.ds(pl.multiple_of(at * PAIR, PAIR), PAIR)
            unit_scr[inside, lanes] = (unit_scr[inside, lanes] - mean) * inverse
            return 0

        lax.fori_loop(0, width // PAIR, scale, 0, unroll=4)
        inverses.append(inverse)
    return inverses


def blend_kernel(parts, mixes, per_seq, *refs):
    x_refs, refs = refs[:parts], refs[parts:]
    keep_ref, edge_ref, norm_ref, mix_ref = refs[:4]
    outs, unit_scr = refs[4 : 4 + mixes], refs[4 + mixes]
    rows, width = x_refs[0].shape

    @pl.when(pl.program_id(0) % per_seq == 0)
    def _():
        unit_scr[HALO - 1 : HALO, :] = edge_ref[0]

    unit_into(x_refs, unit_scr, rows, width)

    def lane_block(lanes):
        gain, bias_term = norm_ref[0:1, lanes], norm_ref[1:2, lanes]
        mixers = [mix_ref[at : at + 1, lanes] for at in range(mixes)]
        for block in row_blocks(rows):
            normed = unit_scr[block.start + HALO : block.stop + HALO, lanes] * gain + bias_term
            before = pltpu.roll(unit_scr[block.start : block.stop + HALO, lanes], 1, 0)[HALO:]
            previous = (before * gain + bias_term) * keep_ref[block, 0:1]
            delta = normed - previous
            for mixer, out in zip(mixers, outs):
                out[block, lanes] = (previous + mixer * delta).astype(jnp.bfloat16)

    lane_loop(width, lane_block)
    unit_scr[HALO - 1 : HALO, :] = unit_scr[rows + HALO - 1 : rows + HALO, :]


def blend(xs, keep, edge, norm, mixers, piece, name):
    tokens, width = xs[0].shape
    rows = min(piece, 256)
    mixes = mixers.shape[0]
    per_seq = piece // rows
    wide = pl.BlockSpec((rows, width), lambda i: (i, 0))
    return pl.pallas_call(
        partial(blend_kernel, len(xs), mixes, per_seq),
        grid=(tokens // rows,),
        in_specs=[wide] * len(xs)
        + [
            pl.BlockSpec((rows, 1), lambda i: (i, 0)),
            pl.BlockSpec((1, 1, width), lambda i: (i // per_seq, 0, 0)),
            pl.BlockSpec((2, width), lambda i: (0, 0)),
            pl.BlockSpec((mixes, width), lambda i: (0, 0)),
        ],
        out_specs=[wide] * mixes,
        out_shape=[jax.ShapeDtypeStruct((tokens, width), jnp.bfloat16)] * mixes,
        scratch_shapes=[pltpu.VMEM((rows + HALO, width), jnp.float32)],
        cost_estimate=pl.CostEstimate(
            flops=20 * tokens * width,
            bytes_accessed=2 * tokens * width * (len(xs) + mixes),
            transcendentals=0,
        ),
        name=name,
    )(*xs, keep, edge, norm, mixers)


def blend_back_kernel(parts, mixes, per_seq, own, *refs):
    x_refs, refs = refs[:parts], refs[parts:]
    halo_refs, refs = refs[:parts], refs[parts:]
    grad_refs, refs = refs[:mixes], refs[mixes:]
    weight_refs, refs = refs[:mixes], refs[mixes:]
    keep_ref, edge_ref, back_ref, norm_ref, mix_ref = refs[:5]
    refs = refs[5:]
    own_refs, refs = refs[: 2 * own], refs[2 * own :]
    out_ref, small_ref, d_scr, unit_scr, prev_scr, row_scr, sums = refs
    rows, width = x_refs[0].shape
    tiles = pl.num_programs(0)
    tile = tiles - 1 - pl.program_id(0)

    @pl.when(pl.program_id(0) == 0)
    def _():
        sums[...] = jnp.zeros_like(sums)

    @pl.when(tile % per_seq == per_seq - 1)
    def _():
        prev_scr[rows : rows + 1, :] = back_ref[0]

    @pl.when(tile % per_seq < per_seq - 1)
    def _():
        prev_scr[rows : rows + 1, :] = prev_scr[0:1, :]

    for at in range(mixes):
        d_scr[at] = matmul_nt(grad_refs[at][...], weight_refs[at][...])

    halo = unit_rows(total_at(halo_refs, slice(None), slice(None)))[GROUP - 1 :, :]
    unit_scr[HALO - 1 : HALO, :] = jnp.where(tile % per_seq == 0, edge_ref[0], halo)
    inverses = unit_into(x_refs, unit_scr, rows, width)
    row_scr[...] = jnp.zeros_like(row_scr)

    def gather(at, value):
        total = value[0:8]
        for top in range(8, value.shape[0], 8):
            total = total + value[top : top + 8]
        return total

    def first_pass(lanes):
        gain, bias_term = norm_ref[0:1, lanes], norm_ref[1:2, lanes]
        mixers = [mix_ref[at : at + 1, lanes] for at in range(mixes)]
        totals = [jnp.zeros((8, PAIR), jnp.float32)] * mixes
        for block in row_blocks(rows):
            keep = keep_ref[block, 0:1]
            normed = unit_scr[block.start + HALO : block.stop + HALO, lanes] * gain + bias_term
            before = pltpu.roll(unit_scr[block.start : block.stop + HALO, lanes], 1, 0)[HALO:]
            delta = normed - (before * gain + bias_term) * keep
            d_norm, d_all = None, None
            for at in range(mixes):
                d_in = d_scr[at, block, lanes]
                totals[at] = totals[at] + gather(at, d_in * delta)
                share = d_in * mixers[at]
                d_norm = share if d_norm is None else d_norm + share
                d_all = d_in if d_all is None else d_all + d_in
            prev_scr[block, lanes] = (d_all - d_norm) * keep
            d_scr[0, block, lanes] = d_norm
        for at in range(mixes):
            sums[2 + at, :, lanes] += totals[at]

    lane_loop(width, first_pass)

    def second_pass(lanes):
        gain = norm_ref[0:1, lanes]
        totals = [jnp.zeros((8, PAIR), jnp.float32)] * 2
        for block in row_blocks(rows):
            size = block.stop - block.start
            later = pltpu.roll(
                prev_scr[block.start : block.stop + HALO, lanes], size + HALO - 1, 0
            )[:size]
            d_norm = d_scr[0, block, lanes] + later
            unit = unit_scr[block.start + HALO : block.stop + HALO, lanes]
            product = d_norm * unit
            totals[0] = totals[0] + gather(0, product)
            totals[1] = totals[1] + gather(1, d_norm)
            d_scr[0, block, lanes] = d_norm * gain
            row_scr[0, block, :] += d_norm * gain
            row_scr[1, block, :] += product * gain
        for at in range(2):
            sums[at, :, lanes] += totals[at]

    lane_loop(width, second_pass)
    means, tilts = [], []
    for block in row_blocks(rows):
        means.append(jnp.sum(row_scr[0, block, :], -1, keepdims=True) * (1.0 / width))
        tilts.append(jnp.sum(row_scr[1, block, :], -1, keepdims=True) * (1.0 / width))
    blocks = list(zip(row_blocks(rows), inverses, means, tilts))

    def last_pass(start, lanes):
        for block, inverse, mean, tilt in blocks:
            unit = unit_scr[block.start + HALO : block.stop + HALO, lanes]
            value = inverse * (d_scr[0, block, lanes] - mean - unit * tilt)
            if own:
                extra = own_refs[0][block, start].astype(jnp.float32)
                value = value + extra * own_refs[1][0:1, lanes]
            out_ref[block, lanes] = value.astype(jnp.bfloat16)

    def last_step(at, _):
        lanes = pl.ds(pl.multiple_of(at * PAIR, PAIR), PAIR)
        inner = None
        if own:
            count = own_refs[0].shape[1] // PAIR
            inner = pl.ds(pl.multiple_of((at % count) * PAIR, PAIR), PAIR)
        last_pass(inner, lanes)
        return 0

    lax.fori_loop(0, width // PAIR, last_step, 0)

    @pl.when(pl.program_id(0) == tiles - 1)
    def _():
        for at in range(2 + mixes):
            small_ref[at : at + 1, :] = jnp.sum(sums[at], 0, keepdims=True)


def blend_back(xs, grads, weights, keep, edge, back, norm, mixers, piece, own, name):
    tokens, width = xs[0].shape
    rows = min(piece, 256)
    mixes = mixers.shape[0]
    per_seq = piece // rows
    tiles = tokens // rows

    def reverse(i):
        return tiles - 1 - i

    def halo_at(i):
        return (jnp.maximum(reverse(i) * (rows // GROUP) - 1, 0), 0)

    wide = pl.BlockSpec((rows, width), lambda i: (reverse(i), 0))
    per = pl.BlockSpec((1, 1, width), lambda i: (reverse(i) // per_seq, 0, 0))
    weight_specs, weight_arrays = [], []
    for (array, at), grad in zip(weights, grads):
        weight_specs.append(
            pl.BlockSpec(
                (width, grad.shape[1]), partial(lambda at, i: (0, at), at),
                pipeline_mode=pl.Buffered(1),
            )
        )
        weight_arrays.append(array)
    return pl.pallas_call(
        partial(blend_back_kernel, len(xs), mixes, per_seq, int(own is not None)),
        grid=(tiles,),
        in_specs=[wide] * len(xs)
        + [pl.BlockSpec((GROUP, width), halo_at)] * len(xs)
        + [pl.BlockSpec((rows, grad.shape[1]), lambda i: (reverse(i), 0)) for grad in grads]
        + weight_specs
        + [
            pl.BlockSpec((rows, 1), lambda i: (reverse(i), 0)),
            per,
            per,
            pl.BlockSpec((2, width), lambda i: (0, 0)),
            pl.BlockSpec((mixes, width), lambda i: (0, 0)),
        ]
        + (
            [
                pl.BlockSpec((rows, own[0].shape[1]), lambda i: (reverse(i), 0)),
                pl.BlockSpec((1, width), lambda i: (0, 0)),
            ]
            if own is not None
            else []
        ),
        out_specs=[wide, pl.BlockSpec((8, width), lambda i: (0, 0))],
        out_shape=[
            jax.ShapeDtypeStruct((tokens, width), jnp.bfloat16),
            jax.ShapeDtypeStruct((8, width), jnp.float32),
        ],
        scratch_shapes=[
            pltpu.VMEM((mixes, rows, width), jnp.float32),
            pltpu.VMEM((rows + HALO, width), jnp.float32),
            pltpu.VMEM((rows + HALO, width), jnp.float32),
            pltpu.VMEM((2, rows, PAIR), jnp.float32),
            pltpu.VMEM((2 + mixes, 8, width), jnp.float32),
        ],
        cost_estimate=pl.CostEstimate(
            flops=2 * tokens * width * sum(grad.shape[1] for grad in grads),
            bytes_accessed=2 * tokens * width * 4,
            transcendentals=0,
        ),
        name=name,
    )(*xs, *xs, *grads, *weight_arrays, keep, edge, back, norm, mixers, *(own or ()))


def per_device(
    entering_activations,
    document_indices,
    acceptor_matrix,
    lookup_matrix,
    payload_matrix,
    valve_matrix,
    result_matrix,
    ffn_lookup_matrix,
    ffn_payload_matrix,
    ffn_acceptor_matrix,
    first_standardize_scaling,
    first_standardize_offset,
    acceptor_lerp_factor,
    lookup_lerp_factor,
    payload_lerp_factor,
    valve_lerp_factor,
    token_fading,
    diagonal_reward,
    subspace_standardize_scaling,
    subspace_standardize_offset,
    second_standardize_scaling,
    second_standardize_offset,
    ffn_lookup_lerp,
    ffn_acceptor_lerp,
    upstream_derivative,
):
    seqs_here, piece_len, embedding_extent = entering_activations.shape
    token_count = seqs_here * piece_len
    tp_count = lax.axis_size("tp")
    fourth_extent = embedding_extent // tp_count
    sharded_layout = lax.axis_index("tp") * fourth_extent
    ctx_place = lax.axis_index("ctx") * piece_len
    padded_seg = jnp.concatenate(
        [jnp.full((seqs_here, 1), -1, jnp.int32), document_indices], axis=1
    )
    segment_present = lax.dynamic_slice_in_dim(document_indices, ctx_place, piece_len, 1)
    seg_before = lax.dynamic_slice_in_dim(padded_seg, ctx_place, piece_len, 1)
    document_begins = seg_before[:, :1]
    pairs_here = fourth_extent // PAIR
    same_mask = segment_present == seg_before
    live_mask = segment_present == document_begins
    ending_mask = segment_present == segment_present[:, -1:]
    cols = jnp.stack([segment_present, live_mask, ending_mask, same_mask], axis=-1)
    cols = cols.astype(jnp.float32).reshape(token_count, 4)
    keep = same_mask.astype(jnp.float32).reshape(token_count, 1)
    keep_first = same_mask[:, :1].astype(jnp.float32)
    seg_row = segment_present.astype(jnp.float32)[:, None, :]
    owners = ("fsdp", "ctx")
    w_time = lax.all_gather(
        jnp.concatenate(
            [acceptor_matrix, lookup_matrix, payload_matrix, valve_matrix, result_matrix.T], axis=1
        ),
        owners,
        axis=0,
        tiled=True,
    )
    w_chan = lax.all_gather(
        jnp.concatenate([ffn_lookup_matrix, ffn_acceptor_matrix], axis=1),
        owners,
        axis=0,
        tiled=True,
    )
    units = ffn_lookup_matrix.shape[1]
    w_recept, w_key, w_value, w_gate, w_output_t = (
        w_time[:, at * fourth_extent : (at + 1) * fourth_extent] for at in range(5)
    )
    w_chankey = w_chan[:, :units]
    w_chanrecept = w_chan[:, units:]
    w_chanvalue_t = lax.all_gather(ffn_payload_matrix.T, owners, axis=0, tiled=True)
    x_low = entering_activations.reshape(token_count, embedding_extent)
    norm_one = jnp.stack([first_standardize_scaling, first_standardize_offset])
    norm_two = jnp.stack([second_standardize_scaling, second_standardize_offset])
    mix_one = jnp.stack(
        [acceptor_lerp_factor, lookup_lerp_factor, payload_lerp_factor, valve_lerp_factor]
    )
    mix_two = jnp.stack([ffn_lookup_lerp, ffn_acceptor_lerp])

    def edge_from(last_rows):
        return shifted(unit_rows(last_rows), "ctx", 1)[:, None]

    def back_from(grads, weights, mixers):
        first = jnp.zeros((seqs_here, embedding_extent), jnp.float32)
        for at, (grad_low, weight) in enumerate(zip(grads, weights)):
            rows = grad_low.reshape(seqs_here, piece_len, -1)[:, 0]
            first = first + matmul_nt(rows, weight) * (1.0 - mixers[at])
        return shifted(first * keep_first, "ctx", -1)[:, None]

    edge_one = edge_from(entering_activations[:, -1].astype(jnp.float32))
    mixed_in = blend((x_low,), keep, edge_one, norm_one, mix_one, piece_len, "blend_one")
    key_low = matmul(mixed_in[1], w_key).astype(jnp.bfloat16)
    value_low = matmul(mixed_in[2], w_value).astype(jnp.bfloat16)

    def own_share(vector):
        return lax.dynamic_slice_in_dim(vector, sharded_layout, fourth_extent, 0)[None]

    log_row = jnp.log(own_share(token_fading))
    vectors = jnp.concatenate(
        [own_share(diagonal_reward), own_share(subspace_standardize_scaling)]
        + [own_share(subspace_standardize_offset)] * 6
    )
    call = partial(pair_call, seqs=seqs_here, length=piece_len, width=fourth_extent)
    square = 2 * token_count * piece_len * fourth_extent
    (carry_sums,) = call(
        carry_kernel,
        operands=[("wide", key_low), ("wide", value_low), ("vector", log_row), ("cols", cols)],
        outs=[("state", jnp.float32)],
        name="carry",
        flops=square // 8,
    )
    alive_mask = (live_mask[:, -1]).astype(jnp.float32)[:, None, None, None]
    carry_mult = alive_mask * jnp.exp(float(piece_len) * log_row).reshape(1, pairs_here, 1, PAIR)
    incoming = carried(carry_mult, carry_sums, "ctx", 1)
    recept_low = matmul(mixed_in[0], w_recept).astype(jnp.bfloat16)
    gate_pre = matmul(mixed_in[3], w_gate)
    joined_low, attend = call(
        mix_kernel,
        operands=[
            ("wide", recept_low),
            ("wide", key_low),
            ("wide", value_low),
            ("wide", gate_pre),
            ("vector", log_row),
            ("vectors", vectors),
            ("cols", cols),
            ("row", seg_row),
            ("state", incoming),
        ],
        outs=[("wide", jnp.bfloat16), ("wide", jnp.float32)],
        name="mix",
        flops=2 * square,
    )
    mixed_out = tp_sum(matmul_nt(joined_low, w_output_t).astype(jnp.bfloat16))
    last_rows = entering_activations[:, -1].astype(jnp.float32) + mixed_out.reshape(
        seqs_here, piece_len, embedding_extent
    )[:, -1].astype(jnp.float32)
    edge_two = edge_from(last_rows)
    key_in, rec_in = blend(
        (x_low, mixed_out), keep, edge_two, norm_two, mix_two, piece_len, "blend_two"
    )
    rec_gate = jax.nn.sigmoid(matmul(rec_in, w_chanrecept))
    d_result_low = upstream_derivative.reshape(token_count, fourth_extent)
    d_result = d_result_low.astype(jnp.float32)
    d_chan = (d_result * rec_gate).astype(jnp.bfloat16)
    d_chan_full = tp_gather(d_chan)
    key_pre = matmul(key_in, w_chankey)
    hidden = jnp.square(jax.nn.relu(key_pre)).astype(jnp.bfloat16)
    grad_chanvalue = matmul_tn(hidden, d_chan_full).astype(jnp.bfloat16)
    g_chanvalue = lax.psum_scatter(grad_chanvalue, owners, scatter_dimension=1, tiled=True)
    hidden, grad_chanvalue = after(hidden, grad_chanvalue)
    chan_sum = tp_scatter(matmul_nt(hidden, w_chanvalue_t).astype(jnp.bfloat16)).astype(jnp.float32)
    middle_q = lax.dynamic_slice_in_dim(x_low, sharded_layout, fourth_extent, 1).astype(
        jnp.float32
    ) + lax.dynamic_slice_in_dim(mixed_out, sharded_layout, fourth_extent, 1).astype(jnp.float32)
    result = (
        (middle_q + rec_gate * chan_sum)
        .astype(jnp.bfloat16)
        .reshape(seqs_here, piece_len, fourth_extent)
    )
    d_rec_pre = (d_result * chan_sum * rec_gate * (1.0 - rec_gate)).astype(jnp.bfloat16)
    d_hidden = matmul(d_chan_full, w_chanvalue_t)
    d_key_pre = (d_hidden * 2.0 * jax.nn.relu(key_pre)).astype(jnp.bfloat16)
    full_shape = (seqs_here, piece_len, embedding_extent)
    own_mask = (jnp.arange(embedding_extent) // fourth_extent == lax.axis_index("tp")).astype(
        jnp.float32
    )[None]
    d_middle_part, chan_small = blend_back(
        (x_low, mixed_out),
        (d_key_pre, d_rec_pre),
        ((w_chan, 0), (w_chanrecept, 0)),
        keep,
        edge_two,
        back_from((d_key_pre, d_rec_pre), (w_chankey, w_chanrecept), mix_two),
        norm_two,
        mix_two,
        piece_len,
        (d_result_low, own_mask),
        "blend_two_back",
    )

    def chan_grads(token):
        d_key_late, d_rec_late, _ = after(d_key_pre, d_rec_pre, token)
        return jnp.concatenate(
            [
                matmul_tn(key_in, d_key_late).astype(jnp.bfloat16),
                matmul_tn(rec_in, d_rec_late).astype(jnp.bfloat16),
            ],
            axis=1,
        )

    d_mixed, grads_chan = tp_sum(d_middle_part, chan_grads)
    d_mixed, grads_chan, g_chanvalue = after(d_mixed, grads_chan, g_chanvalue)
    g_chan = lax.psum_scatter(grads_chan, owners, scatter_dimension=0, tiled=True)
    grad_output_t = matmul_tn(d_mixed, joined_low).astype(jnp.bfloat16)
    d_joined = matmul(d_mixed, w_output_t)
    d_gate_pre, d_attend, local_grad, group_small = call(
        gate_back_kernel,
        operands=[
            ("wide", d_joined),
            ("wide", attend),
            ("wide", gate_pre),
            ("wide", recept_low),
            ("vector", log_row),
            ("vectors", vectors),
            ("cols", cols),
        ],
        outs=[
            ("wide", jnp.bfloat16),
            ("wide", jnp.bfloat16),
            ("state", jnp.float32),
            ("vectors", jnp.float32),
        ],
        name="gate_back",
        flops=square // 8,
    )
    grads_early = jnp.concatenate(
        [grad_output_t, matmul_tn(mixed_in[3], d_gate_pre).astype(jnp.bfloat16)], axis=1
    )
    early = owner_scatter_steps(grads_early)
    g_early = next(early)
    outgoing_state = carried(carry_mult, local_grad, "ctx", -1)
    d_recept, d_key, d_value, state_small = call(
        mix_back_kernel,
        operands=[
            ("wide", recept_low),
            ("wide", key_low),
            ("wide", value_low),
            ("wide", d_attend),
            ("vector", log_row),
            ("vectors", vectors),
            ("cols", cols),
            ("row", seg_row),
            ("state", incoming),
            ("state", outgoing_state),
            ("mult", carry_mult),
        ],
        outs=[("wide", jnp.bfloat16)] * 3 + [("vectors", jnp.float32)],
        name="mix_back",
        flops=6 * square,
    )
    early_steps = len(axis_bits("fsdp")) + len(axis_bits("ctx"))
    d_recept, d_key, d_value, g_early = after(d_recept, d_key, d_value, g_early)
    for _ in range(early_steps - 3):
        g_early = early.send(g_early)
    d_lows = [d_recept, d_key, d_value, d_gate_pre]
    weights_time = (w_recept, w_key, w_value, w_gate)
    grads_time = jnp.concatenate(
        [
            matmul_tn(mixed, grad_low).astype(jnp.bfloat16)
            for mixed, grad_low in zip(mixed_in, d_lows[:3])
        ],
        axis=1,
    )
    *d_lows, _ = after(d_lows[0], *d_lows[1:], grads_time)
    g_time = lax.psum_scatter(grads_time, owners, scatter_dimension=0, tiled=True)
    back_one = back_from(d_lows, weights_time, mix_one)
    g_early = early.send(after(g_early, back_one)[0])
    d_input_part, time_small = blend_back(
        (x_low,),
        d_lows,
        [(w_time, at) for at in range(4)],
        keep,
        edge_one,
        back_one,
        norm_one,
        mix_one,
        piece_len,
        None,
        "blend_one_back",
    )
    d_input_part, g_early, g_chan = after(d_input_part, g_early, g_chan)
    head_small = jnp.concatenate([state_small[:2], group_small[:2]])
    head_small = lax.dynamic_update_slice_in_dim(
        jnp.zeros((4, embedding_extent), jnp.float32), head_small, sharded_layout, 1
    )
    small_part = jnp.concatenate([time_small[:6], head_small, chan_small[:4]], axis=0)

    def small_total(token):
        return whole_sum(after(small_part, token)[0], ("fsdp", "ctx", "tp"))

    d_input_sum, small_sum = tp_sum(d_input_part, small_total)
    g_early = early.send(after(g_early, small_sum)[0])
    owned = embedding_extent // (lax.axis_size("fsdp") * lax.axis_size("ctx"))
    small_owned = lax.dynamic_slice_in_dim(
        small_sum,
        (lax.axis_index("fsdp") * lax.axis_size("ctx") + lax.axis_index("ctx")) * owned,
        owned,
        1,
    )
    grad_inputs = (d_mixed.astype(jnp.float32) + d_input_sum.astype(jnp.float32)).reshape(
        full_shape
    )
    g_chanvalue = g_chanvalue.astype(jnp.float32)
    g_chankey, g_chanrecept = split_columns(g_chan, (units, fourth_extent), "split_chan")
    g_early = g_early.astype(jnp.float32)
    g_output = g_early[:, :fourth_extent].T
    g_gate = g_early[:, fourth_extent:]
    g_time = after(
        g_time, grad_inputs, result, g_chanvalue, g_chankey, g_chanrecept, g_output, g_gate
    )[0]
    g_recept, g_key, g_value = split_columns(g_time, (fourth_extent,) * 3, "split_time")
    return (
        result,
        grad_inputs,
        g_recept,
        g_key,
        g_value,
        g_gate,
        g_output,
        g_chankey,
        g_chanvalue,
        g_chanrecept,
    ) + tuple(small_owned[at] for at in range(14))


def solution(mesh):
    return jax.shard_map(
        per_device,
        mesh=mesh,
        in_specs=(
            P("fsdp", "ctx", None),
            P("fsdp", None),
            P(("fsdp", "ctx"), "tp"),
            P(("fsdp", "ctx"), "tp"),
            P(("fsdp", "ctx"), "tp"),
            P(("fsdp", "ctx"), "tp"),
            P("tp", ("fsdp", "ctx")),
            P(("fsdp", "ctx"), "tp"),
            P("tp", ("fsdp", "ctx")),
            P(("fsdp", "ctx"), "tp"),
            P(),
            P(),
            P(),
            P(),
            P(),
            P(),
            P(),
            P(),
            P(),
            P(),
            P(),
            P(),
            P(),
            P(),
            P("fsdp", "ctx", "tp"),
        ),
        out_specs=(
            P("fsdp", "ctx", "tp"),
            P("fsdp", "ctx", None),
            P(("fsdp", "ctx"), "tp"),
            P(("fsdp", "ctx"), "tp"),
            P(("fsdp", "ctx"), "tp"),
            P(("fsdp", "ctx"), "tp"),
            P("tp", ("fsdp", "ctx")),
            P(("fsdp", "ctx"), "tp"),
            P("tp", ("fsdp", "ctx")),
            P(("fsdp", "ctx"), "tp"),
            P(("fsdp", "ctx")),
            P(("fsdp", "ctx")),
            P(("fsdp", "ctx")),
            P(("fsdp", "ctx")),
            P(("fsdp", "ctx")),
            P(("fsdp", "ctx")),
            P(("fsdp", "ctx")),
            P(("fsdp", "ctx")),
            P(("fsdp", "ctx")),
            P(("fsdp", "ctx")),
            P(("fsdp", "ctx")),
            P(("fsdp", "ctx")),
            P(("fsdp", "ctx")),
            P(("fsdp", "ctx")),
        ),
        check_vma=False,
    )
```

```python
from functools import partial

import jax
import jax.numpy as jnp
from jax import lax
from jax.experimental import pallas as pl
from jax.experimental.pallas import tpu as pltpu
from jax.sharding import PartitionSpec as P

SUBSPACE_SIZE = 64
PAIR = 128
GROUP = 16
HALO = 8
SPAN = 64
TILE = 256


EPS = 1e-05
GROUP_EPS = 4.0


def shifted(x, axis, by):
    count = lax.axis_size(axis)
    pairs = [(i, i + by) for i in range(count) if 0 <= i + by < count]
    return lax.ppermute(x, axis, pairs)


def earlier_shift(x, axis, by):
    count = lax.axis_size(axis)
    return lax.ppermute(x, axis, [(i, i + by) for i in range(count) if 0 <= i + by < count])


def carried(mult, sums, axis, toward):
    count = lax.axis_size(axis)
    low = (mult.astype(jnp.bfloat16), sums.astype(jnp.bfloat16))
    arrived = [
        jax.tree.map(lambda part: earlier_shift(part, axis, toward * by), low)
        for by in range(1, count)
    ]
    state = jnp.zeros_like(sums)
    for far_mult, far_sums in reversed(arrived):
        state = far_mult.astype(jnp.float32) * state + far_sums.astype(jnp.float32)
    return state


def partner(x, bit):
    count = lax.axis_size("tp")
    return lax.ppermute(x, "tp", [(i, i ^ bit) for i in range(count)])


def halves(x, axis, bit):
    size = x.shape[axis] // 2
    mine = (lax.axis_index("tp") // bit) % 2
    return (
        lax.dynamic_slice_in_dim(x, mine * size, size, axis),
        lax.dynamic_slice_in_dim(x, (1 - mine) * size, size, axis),
    )


def add_low(left, right):
    return (left.astype(jnp.float32) + right.astype(jnp.float32)).astype(jnp.bfloat16)


def ordered(mine, other, axis, bit):
    first = (lax.axis_index("tp") // bit) % 2 == 0
    return jnp.where(
        first,
        jnp.concatenate([mine, other], axis),
        jnp.concatenate([other, mine], axis),
    )


def after(value, *earlier):
    return lax.optimization_barrier((value,) + earlier)


def tp_sum(x, work=None):
    mine, other = halves(x, 0, 1)
    part = add_low(mine, partner(other, 1))
    made = work(part) if work else None
    bit = 2
    while bit < lax.axis_size("tp"):
        arrived = partner(part, bit)
        if work and bit == 2:
            part = after(part, made)[0]
        part = add_low(part, arrived)
        bit *= 2
    whole = ordered(part, partner(part, 1), 0, 1)
    return (whole, made) if work else whole


def axis_bits(axis):
    bits, bit = [], 1
    while bit < lax.axis_size(axis):
        bits.append((axis, bit))
        bit *= 2
    return bits


def swap(x, axis, bit):
    return lax.ppermute(x, axis, [(i, i ^ bit) for i in range(lax.axis_size(axis))])


def split_kernel(x_ref, *outs):
    at = 0
    for out in outs:
        out[...] = x_ref[:, at : at + out.shape[1]].astype(jnp.float32)
        at += out.shape[1]


def split_columns(x, widths, name):
    count = x.shape[0]
    rows = min(count, 64)
    return pl.pallas_call(
        split_kernel,
        grid=(count // rows,),
        in_specs=[pl.BlockSpec((rows, x.shape[1]), lambda i: (i, 0))],
        out_specs=[pl.BlockSpec((rows, width), lambda i: (i, 0)) for width in widths],
        out_shape=[jax.ShapeDtypeStruct((count, width), jnp.float32) for width in widths],
        cost_estimate=pl.CostEstimate(flops=x.size, bytes_accessed=6 * x.size, transcendentals=0),
        name=name,
    )(x)


def owner_scatter_steps(x):
    fsdp_bits, ctx_bits = axis_bits("fsdp"), axis_bits("ctx")
    dims = list(reversed(fsdp_bits)) + list(reversed(ctx_bits))
    rows = x.shape[0] // 2 ** len(dims)
    part = x.reshape(*([2] * len(dims)), rows, x.shape[1])
    for axis, bit in fsdp_bits + ctx_bits:
        dim = dims.index((axis, bit))
        dims.pop(dim)
        mine = (lax.axis_index(axis) // bit) % 2
        own = lax.dynamic_index_in_dim(part, mine, dim, False)
        arrived = swap(lax.dynamic_index_in_dim(part, 1 - mine, dim, False), axis, bit)
        part = add_low(own, arrived)
        part = yield part
    yield None


def whole_sum(x, steps):
    for axis, bit in steps:
        x = x + swap(x, axis, bit)
    return x


def tp_scatter(x):
    count, place = lax.axis_size("tp"), lax.axis_index("tp")
    width = x.shape[1] // count
    parts = [
        lax.dynamic_slice_in_dim(x, (place ^ relative) * width, width, 1)
        for relative in range(count)
    ]
    bit = 1
    while bit < count:
        for relative in reversed(range(count)):
            if relative & bit and relative & (bit - 1) == 0:
                arrived = partner(parts[relative], bit)
                parts[relative ^ bit] = add_low(parts[relative ^ bit], arrived)
        bit *= 2
    return parts[0]


def tp_gather(x):
    count, place = lax.axis_size("tp"), lax.axis_index("tp")
    width = x.shape[1]
    parts = {0: x}
    bit = count // 2
    while bit:
        parts.update({relative ^ bit: partner(part, bit) for relative, part in parts.items()})
        bit //= 2
    whole = jnp.zeros((x.shape[0], width * count), x.dtype)
    for relative, part in parts.items():
        whole = lax.dynamic_update_slice_in_dim(whole, part, (place ^ relative) * width, 1)
    return whole


def matmul(left, right):
    return jnp.dot(left, right, preferred_element_type=jnp.float32)


def matmul_tn(left, right):
    return lax.dot_general(
        left, right, (((0,), (0,)), ((), ())), preferred_element_type=jnp.float32
    )


def matmul_nt(left, right):
    return lax.dot_general(
        left, right, (((1,), (1,)), ((), ())), preferred_element_type=jnp.float32
    )


def dot_nn(left, right):
    return lax.dot_general(
        left, right, (((1,), (0,)), ((), ())), preferred_element_type=jnp.float32
    )


def lanes_of(shape):
    return lax.broadcasted_iota(jnp.int32, shape, len(shape) - 1)


def low_head(shape):
    return lanes_of(shape) < SUBSPACE_SIZE


def head_sum(x):
    first = low_head(x.shape)
    low = jnp.sum(jnp.where(first, x, 0.0), -1, keepdims=True)
    high = jnp.sum(jnp.where(first, 0.0, x), -1, keepdims=True)
    return jnp.where(first, low, high)


def fold_pair(both):
    return jnp.where(
        low_head((SUBSPACE_SIZE, PAIR)), both[:SUBSPACE_SIZE], both[SUBSPACE_SIZE:]
    )


def spread_pair(folded):
    first = low_head((SUBSPACE_SIZE, PAIR))
    return jnp.concatenate(
        [jnp.where(first, folded, 0.0), jnp.where(first, 0.0, folded)], axis=0
    ).astype(jnp.bfloat16)


def head_parts(x):
    first = low_head(x.shape)
    zero = jnp.zeros_like(x)
    return jnp.where(first, x, zero), jnp.where(first, zero, x)


def places(length):
    return lax.broadcasted_iota(jnp.int32, (length, PAIR), 0).astype(jnp.float32)


def carry_kernel(k_ref, v_ref, log_ref, cols_ref, out_ref):
    length = k_ref.shape[0]
    closing = jnp.exp((length - 1.0 - places(length)) * log_ref[...])
    ending = cols_ref[:, 2:3]
    k_end = (k_ref[...].astype(jnp.float32) * closing * ending).astype(jnp.bfloat16)
    out_ref[0, 0] = fold_pair(matmul_tn(v_ref[...], k_end))


def group_norm(attend):
    centered = attend - head_sum(attend) * (1.0 / SUBSPACE_SIZE)
    inverse = lax.rsqrt(head_sum(centered * centered) * (1.0 / SUBSPACE_SIZE) + GROUP_EPS)
    return centered * inverse, inverse


def mix_kernel(
    r_ref, k_ref, v_ref, gate_ref, log_ref, rows_ref, cols_ref, seg_ref, state_ref,
    joined_ref, attend_ref,
):
    length = r_ref.shape[0]
    at = places(length)
    log = log_ref[...]
    r = r_ref[...].astype(jnp.float32)
    k = k_ref[...].astype(jnp.float32)
    v = v_ref[...]
    q_low = (r * jnp.exp(at * log)).astype(jnp.bfloat16)
    k_low = (k * jnp.exp(-(at + 1.0) * log)).astype(jnp.bfloat16)
    state = spread_pair(state_ref[0, 0])
    bonus = head_sum(r * rows_ref[0:1, :] * k)
    base = bonus * v.astype(jnp.float32) + cols_ref[:, 1:2] * matmul_nt(q_low, state)
    step = min(length, TILE)
    for top in range(0, length, step):
        reach = top + step
        rows = slice(top, reach)
        keep = pair_mask(cols_ref[rows, 0:1], seg_ref[0, :, :reach], top, step, reach)
        parts = []
        for q_part in head_parts(q_low[rows]):
            scores = matmul_nt(q_part, k_low[:reach])
            scores = jnp.where(keep, scores, 0.0).astype(jnp.bfloat16)
            parts.append(dot_nn(scores, v[:reach]))
        attend = base[rows] + jnp.where(low_head(parts[0].shape), parts[0], parts[1])
        unit, _ = group_norm(attend)
        grouped = unit * rows_ref[1:2, :] + rows_ref[2:3, :]
        gate = gate_ref[rows, :]
        attend_ref[rows, :] = attend
        joined_ref[rows, :] = (grouped * (gate * jax.nn.sigmoid(gate))).astype(jnp.bfloat16)


def pair_mask(seg_col, seg_row, top, count, reach):
    later = lax.broadcasted_iota(jnp.int32, (count, reach), 0) + top
    return (seg_col == seg_row) & (later > lanes_of((count, reach)))


def pair_mask_t(seg_col, seg_row, top, count, start):
    width = seg_row.shape[1]
    earlier = lax.broadcasted_iota(jnp.int32, (count, width), 0) + top
    return (seg_col == seg_row) & (lanes_of((count, width)) + start > earlier)


def gate_back_kernel(
    dj_ref, attend_ref, gate_ref, r_ref, log_ref, rows_ref, cols_ref,
    dgate_ref, dattend_ref, state_ref, small_ref,
):
    length = r_ref.shape[0]
    d_joined = dj_ref[...]
    gate = gate_ref[...]
    unit, inverse = group_norm(attend_ref[...])
    gain = rows_ref[1:2, :]
    grouped = unit * gain + rows_ref[2:3, :]
    sig = jax.nn.sigmoid(gate)
    dgate_ref[...] = (d_joined * grouped * sig * (1.0 + gate * (1.0 - sig))).astype(jnp.bfloat16)
    d_grouped = d_joined * gate * sig
    sums = [
        jnp.sum(d_grouped * unit, axis=0, keepdims=True),
        jnp.sum(d_grouped, axis=0, keepdims=True),
    ]
    scaled = d_grouped * gain
    share = 1.0 / SUBSPACE_SIZE
    d_attend = (
        inverse * (scaled - head_sum(scaled) * share - unit * (head_sum(scaled * unit) * share))
    ).astype(jnp.bfloat16)
    dattend_ref[...] = d_attend
    rising = jnp.exp(places(length) * log_ref[...])
    q_live = (r_ref[...].astype(jnp.float32) * rising * cols_ref[:, 1:2]).astype(jnp.bfloat16)
    state_ref[0, 0] = fold_pair(matmul_tn(d_attend, q_live))
    collect(small_ref, sums)


def collect(small_ref, sums):
    pad = jnp.zeros((small_ref.shape[0] - len(sums), sums[0].shape[1]), jnp.float32)
    total = jnp.concatenate(sums + [pad], axis=0)

    @pl.when(pl.program_id(1) == 0)
    def _():
        small_ref[...] = total

    @pl.when(pl.program_id(1) > 0)
    def _():
        small_ref[...] += total


def mix_back_kernel(
    r_ref, k_ref, v_ref, da_ref, log_ref, rows_ref, cols_ref, seg_ref, state_ref, gstate_ref,
    mult_ref, dr_ref, dk_ref, dv_ref, small_ref,
):
    length = r_ref.shape[0]
    at = places(length)
    log = log_ref[...]
    reward = rows_ref[0:1, :]
    r = r_ref[...].astype(jnp.float32)
    k = k_ref[...].astype(jnp.float32)
    v = v_ref[...]
    da = da_ref[...]
    rising = jnp.exp(at * log)
    falling = jnp.exp(-(at + 1.0) * log)
    closing = jnp.exp((length - 1.0 - at) * log) * cols_ref[:, 2:3]
    q_low = (r * rising).astype(jnp.bfloat16)
    k_low = (k * falling).astype(jnp.bfloat16)
    k_end = (k * closing).astype(jnp.bfloat16)
    state, gstate = state_ref[0, 0], gstate_ref[0, 0]
    state_low, gstate_low = spread_pair(state), spread_pair(gstate)
    v_f, da_f = v.astype(jnp.float32), da.astype(jnp.float32)
    dot_va = head_sum(v_f * da_f)
    dk_end = dot_nn(v, gstate_low)
    dq_base = cols_ref[:, 1:2] * dot_nn(da, state_low)
    dv_base = head_sum(r * reward * k) * da_f + matmul_nt(k_end, gstate_low)
    q_f, k_f = q_low.astype(jnp.float32), k_low.astype(jnp.float32)
    d_log = jnp.sum((length - 1.0 - at) * k_end.astype(jnp.float32) * dk_end, 0, keepdims=True)
    d_log += length * mult_ref[0, 0] * jnp.sum(
        state.astype(jnp.bfloat16).astype(jnp.float32)
        * gstate.astype(jnp.bfloat16).astype(jnp.float32),
        0,
        keepdims=True,
    )
    step = min(length, TILE)
    for top in range(0, length, step):
        rows = slice(top, top + step)
        reach = top + step
        keep = pair_mask(cols_ref[rows, 0:1], seg_ref[0, :, :reach], top, step, reach)
        dq = []
        for da_part in head_parts(da[rows]):
            pull = jnp.where(keep, matmul_nt(da_part, v[:reach]), 0.0).astype(jnp.bfloat16)
            dq.append(dot_nn(pull, k_low[:reach]))
        first = low_head(dq[0].shape)
        dq = jnp.where(first, dq[0], dq[1]) + dq_base[rows]
        d_log += jnp.sum(at[rows] * q_f[rows] * dq, 0, keepdims=True)
        dr_ref[rows, :] = (dq * rising[rows] + reward * k[rows] * dot_va[rows]).astype(jnp.bfloat16)
        keep = pair_mask_t(cols_ref[rows, 0:1], seg_ref[0, :, top:], top, step, top)
        dk, dv = [], []
        for v_part, k_part in zip(head_parts(v[rows]), head_parts(k_low[rows])):
            pull = jnp.where(keep, matmul_nt(v_part, da[top:]), 0.0).astype(jnp.bfloat16)
            dk.append(dot_nn(pull, q_low[top:]))
            scores = jnp.where(keep, matmul_nt(k_part, q_low[top:]), 0.0).astype(jnp.bfloat16)
            dv.append(dot_nn(scores, da[top:]))
        dk = jnp.where(first, dk[0], dk[1])
        d_log -= jnp.sum((at[rows] + 1.0) * k_f[rows] * dk, 0, keepdims=True)
        dk_ref[rows, :] = (
            dk * falling[rows]
            + dk_end[rows] * closing[rows]
            + reward * r[rows] * dot_va[rows]
        ).astype(jnp.bfloat16)
        dv_ref[rows, :] = (jnp.where(first, dv[0], dv[1]) + dv_base[rows]).astype(jnp.bfloat16)
    collect(small_ref, [d_log * jnp.exp(-log), jnp.sum(r * k * dot_va, 0, keepdims=True)])


def pair_call(kernel, seqs, length, width, operands, outs, name, flops):
    pairs = width // PAIR
    specs = {
        "wide": pl.BlockSpec((length, PAIR), lambda p, s: (s, p)),
        "vector": pl.BlockSpec((1, PAIR), lambda p, s: (0, p)),
        "vectors": pl.BlockSpec((8, PAIR), lambda p, s: (0, p)),
        "cols": pl.BlockSpec((length, 4), lambda p, s: (s, 0)),
        "row": pl.BlockSpec((1, 1, length), lambda p, s: (s, 0, 0)),
        "state": pl.BlockSpec((1, 1, SUBSPACE_SIZE, PAIR), lambda p, s: (s, p, 0, 0)),
        "mult": pl.BlockSpec((1, 1, 1, PAIR), lambda p, s: (s, p, 0, 0)),
    }
    shapes = {
        "wide": (seqs * length, width),
        "vectors": (8, width),
        "state": (seqs, pairs, SUBSPACE_SIZE, PAIR),
    }
    kinds, arrays = zip(*operands)
    size = sum(array.size * array.dtype.itemsize for array in arrays)
    return pl.pallas_call(
        kernel,
        grid=(pairs, seqs),
        in_specs=[specs[kind] for kind in kinds],
        out_specs=[specs[kind] for kind, _ in outs],
        out_shape=[jax.ShapeDtypeStruct(shapes[kind], dtype) for kind, dtype in outs],
        cost_estimate=pl.CostEstimate(flops=flops, bytes_accessed=2 * size, transcendentals=0),
        name=name,
    )(*arrays)


def unit_rows(x):
    centered = x - jnp.mean(x, -1, keepdims=True)
    return centered * lax.rsqrt(jnp.mean(centered * centered, -1, keepdims=True) + EPS)


def total_at(refs, rows, lanes):
    total = refs[0][rows, lanes].astype(jnp.float32)
    for ref in refs[1:]:
        total = total + ref[rows, lanes].astype(jnp.float32)
    return total


def lane_loop(width, body):
    def step(at, _):
        body(pl.ds(pl.multiple_of(at * PAIR, PAIR), PAIR))
        return 0

    lax.fori_loop(0, width // PAIR, step, 0)


def row_blocks(rows):
    return [slice(top, min(top + SPAN, rows)) for top in range(0, rows, SPAN)]


def unit_into(refs, unit_scr, rows, width):
    inverses = []
    for block in row_blocks(rows):
        inside = slice(block.start + HALO, block.stop + HALO)
        zero = jnp.zeros((block.stop - block.start, PAIR), jnp.float32)

        def load(at, total):
            lanes = pl.ds(pl.multiple_of(at * PAIR, PAIR), PAIR)
            value = total_at(refs, block, lanes)
            unit_scr[inside, lanes] = value
            return total + value

        total = lax.fori_loop(0, width // PAIR, load, zero, unroll=4)
        mean = jnp.sum(total, -1, keepdims=True) * (1.0 / width)

        def square(at, total):
            lanes = pl.ds(pl.multiple_of(at * PAIR, PAIR), PAIR)
            value = unit_scr[inside, lanes] - mean
            return total + value * value

        total = lax.fori_loop(0, width // PAIR, square, zero, unroll=4)
        inverse = lax.rsqrt(jnp.sum(total, -1, keepdims=True) * (1.0 / width) + EPS)

        def scale(at, _):
            lanes = pl.ds(pl.multiple_of(at * PAIR, PAIR), PAIR)
            unit_scr[inside, lanes] = (unit_scr[inside, lanes] - mean) * inverse
            return 0

        lax.fori_loop(0, width // PAIR, scale, 0, unroll=4)
        inverses.append(inverse)
    return inverses


def blend_kernel(parts, mixes, per_seq, *refs):
    x_refs, refs = refs[:parts], refs[parts:]
    keep_ref, edge_ref, norm_ref, mix_ref = refs[:4]
    outs, unit_scr = refs[4 : 4 + mixes], refs[4 + mixes]
    rows, width = x_refs[0].shape

    @pl.when(pl.program_id(0) % per_seq == 0)
    def _():
        unit_scr[HALO - 1 : HALO, :] = edge_ref[0]

    unit_into(x_refs, unit_scr, rows, width)

    def lane_block(lanes):
        gain, bias_term = norm_ref[0:1, lanes], norm_ref[1:2, lanes]
        mixers = [mix_ref[at : at + 1, lanes] for at in range(mixes)]
        for block in row_blocks(rows):
            normed = unit_scr[block.start + HALO : block.stop + HALO, lanes] * gain + bias_term
            before = pltpu.roll(unit_scr[block.start : block.stop + HALO, lanes], 1, 0)[HALO:]
            previous = (before * gain + bias_term) * keep_ref[block, 0:1]
            delta = normed - previous
            for mixer, out in zip(mixers, outs):
                out[block, lanes] = (previous + mixer * delta).astype(jnp.bfloat16)

    lane_loop(width, lane_block)
    unit_scr[HALO - 1 : HALO, :] = unit_scr[rows + HALO - 1 : rows + HALO, :]


def blend(xs, keep, edge, norm, mixers, piece, name):
    tokens, width = xs[0].shape
    rows = min(piece, 256)
    mixes = mixers.shape[0]
    per_seq = piece // rows
    wide = pl.BlockSpec((rows, width), lambda i: (i, 0))
    return pl.pallas_call(
        partial(blend_kernel, len(xs), mixes, per_seq),
        grid=(tokens // rows,),
        in_specs=[wide] * len(xs)
        + [
            pl.BlockSpec((rows, 1), lambda i: (i, 0)),
            pl.BlockSpec((1, 1, width), lambda i: (i // per_seq, 0, 0)),
            pl.BlockSpec((2, width), lambda i: (0, 0)),
            pl.BlockSpec((mixes, width), lambda i: (0, 0)),
        ],
        out_specs=[wide] * mixes,
        out_shape=[jax.ShapeDtypeStruct((tokens, width), jnp.bfloat16)] * mixes,
        scratch_shapes=[pltpu.VMEM((rows + HALO, width), jnp.float32)],
        cost_estimate=pl.CostEstimate(
            flops=20 * tokens * width,
            bytes_accessed=2 * tokens * width * (len(xs) + mixes),
            transcendentals=0,
        ),
        name=name,
    )(*xs, keep, edge, norm, mixers)


def blend_back_kernel(parts, mixes, per_seq, own, *refs):
    x_refs, refs = refs[:parts], refs[parts:]
    halo_refs, refs = refs[:parts], refs[parts:]
    grad_refs, refs = refs[:mixes], refs[mixes:]
    weight_refs, refs = refs[:mixes], refs[mixes:]
    keep_ref, edge_ref, back_ref, norm_ref, mix_ref = refs[:5]
    refs = refs[5:]
    own_refs, refs = refs[: 2 * own], refs[2 * own :]
    out_ref, small_ref, d_scr, unit_scr, prev_scr, row_scr, sums = refs
    rows, width = x_refs[0].shape
    tiles = pl.num_programs(0)
    tile = tiles - 1 - pl.program_id(0)

    @pl.when(pl.program_id(0) == 0)
    def _():
        sums[...] = jnp.zeros_like(sums)

    @pl.when(tile % per_seq == per_seq - 1)
    def _():
        prev_scr[rows : rows + 1, :] = back_ref[0]

    @pl.when(tile % per_seq < per_seq - 1)
    def _():
        prev_scr[rows : rows + 1, :] = prev_scr[0:1, :]

    for at in range(mixes):
        d_scr[at] = matmul_nt(grad_refs[at][...], weight_refs[at][...])

    halo = unit_rows(total_at(halo_refs, slice(None), slice(None)))[GROUP - 1 :, :]
    unit_scr[HALO - 1 : HALO, :] = jnp.where(tile % per_seq == 0, edge_ref[0], halo)
    inverses = unit_into(x_refs, unit_scr, rows, width)
    row_scr[...] = jnp.zeros_like(row_scr)

    def gather(at, value):
        total = value[0:8]
        for top in range(8, value.shape[0], 8):
            total = total + value[top : top + 8]
        return total

    def first_pass(lanes):
        gain, bias_term = norm_ref[0:1, lanes], norm_ref[1:2, lanes]
        mixers = [mix_ref[at : at + 1, lanes] for at in range(mixes)]
        totals = [jnp.zeros((8, PAIR), jnp.float32)] * mixes
        for block in row_blocks(rows):
            keep = keep_ref[block, 0:1]
            normed = unit_scr[block.start + HALO : block.stop + HALO, lanes] * gain + bias_term
            before = pltpu.roll(unit_scr[block.start : block.stop + HALO, lanes], 1, 0)[HALO:]
            delta = normed - (before * gain + bias_term) * keep
            d_norm, d_all = None, None
            for at in range(mixes):
                d_in = d_scr[at, block, lanes]
                totals[at] = totals[at] + gather(at, d_in * delta)
                share = d_in * mixers[at]
                d_norm = share if d_norm is None else d_norm + share
                d_all = d_in if d_all is None else d_all + d_in
            prev_scr[block, lanes] = (d_all - d_norm) * keep
            d_scr[0, block, lanes] = d_norm
        for at in range(mixes):
            sums[2 + at, :, lanes] += totals[at]

    lane_loop(width, first_pass)

    def second_pass(lanes):
        gain = norm_ref[0:1, lanes]
        totals = [jnp.zeros((8, PAIR), jnp.float32)] * 2
        for block in row_blocks(rows):
            size = block.stop - block.start
            later = pltpu.roll(
                prev_scr[block.start : block.stop + HALO, lanes], size + HALO - 1, 0
            )[:size]
            d_norm = d_scr[0, block, lanes] + later
            unit = unit_scr[block.start + HALO : block.stop + HALO, lanes]
            product = d_norm * unit
            totals[0] = totals[0] + gather(0, product)
            totals[1] = totals[1] + gather(1, d_norm)
            d_scr[0, block, lanes] = d_norm * gain
            row_scr[0, block, :] += d_norm * gain
            row_scr[1, block, :] += product * gain
        for at in range(2):
            sums[at, :, lanes] += totals[at]

    lane_loop(width, second_pass)
    means, tilts = [], []
    for block in row_blocks(rows):
        means.append(jnp.sum(row_scr[0, block, :], -1, keepdims=True) * (1.0 / width))
        tilts.append(jnp.sum(row_scr[1, block, :], -1, keepdims=True) * (1.0 / width))
    blocks = list(zip(row_blocks(rows), inverses, means, tilts))

    def last_pass(start, lanes):
        for block, inverse, mean, tilt in blocks:
            unit = unit_scr[block.start + HALO : block.stop + HALO, lanes]
            value = inverse * (d_scr[0, block, lanes] - mean - unit * tilt)
            if own:
                extra = own_refs[0][block, start].astype(jnp.float32)
                value = value + extra * own_refs[1][0:1, lanes]
            out_ref[block, lanes] = value.astype(jnp.bfloat16)

    def last_step(at, _):
        lanes = pl.ds(pl.multiple_of(at * PAIR, PAIR), PAIR)
        inner = None
        if own:
            count = own_refs[0].shape[1] // PAIR
            inner = pl.ds(pl.multiple_of((at % count) * PAIR, PAIR), PAIR)
        last_pass(inner, lanes)
        return 0

    lax.fori_loop(0, width // PAIR, last_step, 0)

    @pl.when(pl.program_id(0) == tiles - 1)
    def _():
        for at in range(2 + mixes):
            small_ref[at : at + 1, :] = jnp.sum(sums[at], 0, keepdims=True)


def blend_back(xs, grads, weights, keep, edge, back, norm, mixers, piece, own, name):
    tokens, width = xs[0].shape
    rows = min(piece, 256)
    mixes = mixers.shape[0]
    per_seq = piece // rows
    tiles = tokens // rows

    def reverse(i):
        return tiles - 1 - i

    def halo_at(i):
        return (jnp.maximum(reverse(i) * (rows // GROUP) - 1, 0), 0)

    wide = pl.BlockSpec((rows, width), lambda i: (reverse(i), 0))
    per = pl.BlockSpec((1, 1, width), lambda i: (reverse(i) // per_seq, 0, 0))
    weight_specs, weight_arrays = [], []
    for (array, at), grad in zip(weights, grads):
        weight_specs.append(
            pl.BlockSpec(
                (width, grad.shape[1]), partial(lambda at, i: (0, at), at),
                pipeline_mode=pl.Buffered(1),
            )
        )
        weight_arrays.append(array)
    return pl.pallas_call(
        partial(blend_back_kernel, len(xs), mixes, per_seq, int(own is not None)),
        grid=(tiles,),
        in_specs=[wide] * len(xs)
        + [pl.BlockSpec((GROUP, width), halo_at)] * len(xs)
        + [pl.BlockSpec((rows, grad.shape[1]), lambda i: (reverse(i), 0)) for grad in grads]
        + weight_specs
        + [
            pl.BlockSpec((rows, 1), lambda i: (reverse(i), 0)),
            per,
            per,
            pl.BlockSpec((2, width), lambda i: (0, 0)),
            pl.BlockSpec((mixes, width), lambda i: (0, 0)),
        ]
        + (
            [
                pl.BlockSpec((rows, own[0].shape[1]), lambda i: (reverse(i), 0)),
                pl.BlockSpec((1, width), lambda i: (0, 0)),
            ]
            if own is not None
            else []
        ),
        out_specs=[wide, pl.BlockSpec((8, width), lambda i: (0, 0))],
        out_shape=[
            jax.ShapeDtypeStruct((tokens, width), jnp.bfloat16),
            jax.ShapeDtypeStruct((8, width), jnp.float32),
        ],
        scratch_shapes=[
            pltpu.VMEM((mixes, rows, width), jnp.float32),
            pltpu.VMEM((rows + HALO, width), jnp.float32),
            pltpu.VMEM((rows + HALO, width), jnp.float32),
            pltpu.VMEM((2, rows, PAIR), jnp.float32),
            pltpu.VMEM((2 + mixes, 8, width), jnp.float32),
        ],
        cost_estimate=pl.CostEstimate(
            flops=2 * tokens * width * sum(grad.shape[1] for grad in grads),
            bytes_accessed=2 * tokens * width * 4,
            transcendentals=0,
        ),
        name=name,
    )(*xs, *xs, *grads, *weight_arrays, keep, edge, back, norm, mixers, *(own or ()))


def per_device(
    entering_activations,
    document_indices,
    acceptor_matrix,
    lookup_matrix,
    payload_matrix,
    valve_matrix,
    result_matrix,
    ffn_lookup_matrix,
    ffn_payload_matrix,
    ffn_acceptor_matrix,
    first_standardize_scaling,
    first_standardize_offset,
    acceptor_lerp_factor,
    lookup_lerp_factor,
    payload_lerp_factor,
    valve_lerp_factor,
    token_fading,
    diagonal_reward,
    subspace_standardize_scaling,
    subspace_standardize_offset,
    second_standardize_scaling,
    second_standardize_offset,
    ffn_lookup_lerp,
    ffn_acceptor_lerp,
    upstream_derivative,
):
    seqs_here, piece_len, embedding_extent = entering_activations.shape
    token_count = seqs_here * piece_len
    tp_count = lax.axis_size("tp")
    fourth_extent = embedding_extent // tp_count
    sharded_layout = lax.axis_index("tp") * fourth_extent
    ctx_place = lax.axis_index("ctx") * piece_len
    padded_seg = jnp.concatenate(
        [jnp.full((seqs_here, 1), -1, jnp.int32), document_indices], axis=1
    )
    segment_present = lax.dynamic_slice_in_dim(document_indices, ctx_place, piece_len, 1)
    seg_before = lax.dynamic_slice_in_dim(padded_seg, ctx_place, piece_len, 1)
    document_begins = seg_before[:, :1]
    pairs_here = fourth_extent // PAIR
    same_mask = segment_present == seg_before
    live_mask = segment_present == document_begins
    ending_mask = segment_present == segment_present[:, -1:]
    cols = jnp.stack([segment_present, live_mask, ending_mask, same_mask], axis=-1)
    cols = cols.astype(jnp.float32).reshape(token_count, 4)
    keep = same_mask.astype(jnp.float32).reshape(token_count, 1)
    keep_first = same_mask[:, :1].astype(jnp.float32)
    seg_row = segment_present.astype(jnp.float32)[:, None, :]
    owners = ("fsdp", "ctx")
    w_time = lax.all_gather(
        jnp.concatenate(
            [acceptor_matrix, lookup_matrix, payload_matrix, valve_matrix, result_matrix.T], axis=1
        ),
        owners,
        axis=0,
        tiled=True,
    )
    w_chan = lax.all_gather(
        jnp.concatenate([ffn_lookup_matrix, ffn_acceptor_matrix], axis=1),
        owners,
        axis=0,
        tiled=True,
    )
    units = ffn_lookup_matrix.shape[1]
    w_recept, w_key, w_value, w_gate, w_output_t = (
        w_time[:, at * fourth_extent : (at + 1) * fourth_extent] for at in range(5)
    )
    w_chankey = w_chan[:, :units]
    w_chanrecept = w_chan[:, units:]
    w_chanvalue_t = lax.all_gather(ffn_payload_matrix.T, owners, axis=0, tiled=True)
    x_low = entering_activations.reshape(token_count, embedding_extent)
    norm_one = jnp.stack([first_standardize_scaling, first_standardize_offset])
    norm_two = jnp.stack([second_standardize_scaling, second_standardize_offset])
    mix_one = jnp.stack(
        [acceptor_lerp_factor, lookup_lerp_factor, payload_lerp_factor, valve_lerp_factor]
    )
    mix_two = jnp.stack([ffn_lookup_lerp, ffn_acceptor_lerp])

    def edge_from(last_rows):
        return shifted(unit_rows(last_rows), "ctx", 1)[:, None]

    def back_from(grads, weights, mixers):
        first = jnp.zeros((seqs_here, embedding_extent), jnp.float32)
        for at, (grad_low, weight) in enumerate(zip(grads, weights)):
            rows = grad_low.reshape(seqs_here, piece_len, -1)[:, 0]
            first = first + matmul_nt(rows, weight) * (1.0 - mixers[at])
        return shifted(first * keep_first, "ctx", -1)[:, None]

    edge_one = edge_from(entering_activations[:, -1].astype(jnp.float32))
    mixed_in = blend((x_low,), keep, edge_one, norm_one, mix_one, piece_len, "blend_one")
    key_low = matmul(mixed_in[1], w_key).astype(jnp.bfloat16)
    value_low = matmul(mixed_in[2], w_value).astype(jnp.bfloat16)

    def own_share(vector):
        return lax.dynamic_slice_in_dim(vector, sharded_layout, fourth_extent, 0)[None]

    log_row = jnp.log(own_share(token_fading))
    vectors = jnp.concatenate(
        [own_share(diagonal_reward), own_share(subspace_standardize_scaling)]
        + [own_share(subspace_standardize_offset)] * 6
    )
    call = partial(pair_call, seqs=seqs_here, length=piece_len, width=fourth_extent)
    square = 2 * token_count * piece_len * fourth_extent
    (carry_sums,) = call(
        carry_kernel,
        operands=[("wide", key_low), ("wide", value_low), ("vector", log_row), ("cols", cols)],
        outs=[("state", jnp.float32)],
        name="carry",
        flops=square // 8,
    )
    alive_mask = (live_mask[:, -1]).astype(jnp.float32)[:, None, None, None]
    carry_mult = alive_mask * jnp.exp(float(piece_len) * log_row).reshape(1, pairs_here, 1, PAIR)
    incoming = carried(carry_mult, carry_sums, "ctx", 1)
    recept_low = matmul(mixed_in[0], w_recept).astype(jnp.bfloat16)
    gate_pre = matmul(mixed_in[3], w_gate)
    joined_low, attend = call(
        mix_kernel,
        operands=[
            ("wide", recept_low),
            ("wide", key_low),
            ("wide", value_low),
            ("wide", gate_pre),
            ("vector", log_row),
            ("vectors", vectors),
            ("cols", cols),
            ("row", seg_row),
            ("state", incoming),
        ],
        outs=[("wide", jnp.bfloat16), ("wide", jnp.float32)],
        name="mix",
        flops=2 * square,
    )
    mixed_out = tp_sum(matmul_nt(joined_low, w_output_t).astype(jnp.bfloat16))
    last_rows = entering_activations[:, -1].astype(jnp.float32) + mixed_out.reshape(
        seqs_here, piece_len, embedding_extent
    )[:, -1].astype(jnp.float32)
    edge_two = edge_from(last_rows)
    key_in, rec_in = blend(
        (x_low, mixed_out), keep, edge_two, norm_two, mix_two, piece_len, "blend_two"
    )
    rec_gate = jax.nn.sigmoid(matmul(rec_in, w_chanrecept))
    d_result_low = upstream_derivative.reshape(token_count, fourth_extent)
    d_result = d_result_low.astype(jnp.float32)
    d_chan = (d_result * rec_gate).astype(jnp.bfloat16)
    d_chan_full = tp_gather(d_chan)
    key_pre = matmul(key_in, w_chankey)
    hidden = jnp.square(jax.nn.relu(key_pre)).astype(jnp.bfloat16)
    grad_chanvalue = matmul_tn(hidden, d_chan_full).astype(jnp.bfloat16)
    g_chanvalue = lax.psum_scatter(grad_chanvalue, owners, scatter_dimension=1, tiled=True)
    hidden, grad_chanvalue = after(hidden, grad_chanvalue)
    chan_sum = tp_scatter(matmul_nt(hidden, w_chanvalue_t).astype(jnp.bfloat16)).astype(jnp.float32)
    middle_q = lax.dynamic_slice_in_dim(x_low, sharded_layout, fourth_extent, 1).astype(
        jnp.float32
    ) + lax.dynamic_slice_in_dim(mixed_out, sharded_layout, fourth_extent, 1).astype(jnp.float32)
    result = (
        (middle_q + rec_gate * chan_sum)
        .astype(jnp.bfloat16)
        .reshape(seqs_here, piece_len, fourth_extent)
    )
    d_rec_pre = (d_result * chan_sum * rec_gate * (1.0 - rec_gate)).astype(jnp.bfloat16)
    d_hidden = matmul(d_chan_full, w_chanvalue_t)
    d_key_pre = (d_hidden * 2.0 * jax.nn.relu(key_pre)).astype(jnp.bfloat16)
    full_shape = (seqs_here, piece_len, embedding_extent)
    own_mask = (jnp.arange(embedding_extent) // fourth_extent == lax.axis_index("tp")).astype(
        jnp.float32
    )[None]
    d_middle_part, chan_small = blend_back(
        (x_low, mixed_out),
        (d_key_pre, d_rec_pre),
        ((w_chan, 0), (w_chanrecept, 0)),
        keep,
        edge_two,
        back_from((d_key_pre, d_rec_pre), (w_chankey, w_chanrecept), mix_two),
        norm_two,
        mix_two,
        piece_len,
        (d_result_low, own_mask),
        "blend_two_back",
    )

    def chan_grads(token):
        d_key_late, d_rec_late, _ = after(d_key_pre, d_rec_pre, token)
        return jnp.concatenate(
            [
                matmul_tn(key_in, d_key_late).astype(jnp.bfloat16),
                matmul_tn(rec_in, d_rec_late).astype(jnp.bfloat16),
            ],
            axis=1,
        )

    d_mixed, grads_chan = tp_sum(d_middle_part, chan_grads)
    d_mixed, grads_chan, g_chanvalue = after(d_mixed, grads_chan, g_chanvalue)
    g_chan = lax.psum_scatter(grads_chan, owners, scatter_dimension=0, tiled=True)
    grad_output_t = matmul_tn(d_mixed, joined_low).astype(jnp.bfloat16)
    d_joined = matmul(d_mixed, w_output_t)
    d_gate_pre, d_attend, local_grad, group_small = call(
        gate_back_kernel,
        operands=[
            ("wide", d_joined),
            ("wide", attend),
            ("wide", gate_pre),
            ("wide", recept_low),
            ("vector", log_row),
            ("vectors", vectors),
            ("cols", cols),
        ],
        outs=[
            ("wide", jnp.bfloat16),
            ("wide", jnp.bfloat16),
            ("state", jnp.float32),
            ("vectors", jnp.float32),
        ],
        name="gate_back",
        flops=square // 8,
    )
    grads_early = jnp.concatenate(
        [grad_output_t, matmul_tn(mixed_in[3], d_gate_pre).astype(jnp.bfloat16)], axis=1
    )
    early = owner_scatter_steps(grads_early)
    g_early = next(early)
    outgoing_state = carried(carry_mult, local_grad, "ctx", -1)
    d_recept, d_key, d_value, state_small = call(
        mix_back_kernel,
        operands=[
            ("wide", recept_low),
            ("wide", key_low),
            ("wide", value_low),
            ("wide", d_attend),
            ("vector", log_row),
            ("vectors", vectors),
            ("cols", cols),
            ("row", seg_row),
            ("state", incoming),
            ("state", outgoing_state),
            ("mult", carry_mult),
        ],
        outs=[("wide", jnp.bfloat16)] * 3 + [("vectors", jnp.float32)],
        name="mix_back",
        flops=6 * square,
    )
    early_steps = len(axis_bits("fsdp")) + len(axis_bits("ctx"))
    d_recept, d_key, d_value, g_early = after(d_recept, d_key, d_value, g_early)
    for _ in range(early_steps - 3):
        g_early = early.send(g_early)
    d_lows = [d_recept, d_key, d_value, d_gate_pre]
    weights_time = (w_recept, w_key, w_value, w_gate)
    grads_time = jnp.concatenate(
        [
            matmul_tn(mixed, grad_low).astype(jnp.bfloat16)
            for mixed, grad_low in zip(mixed_in, d_lows[:2])
        ],
        axis=1,
    )
    value_steps = owner_scatter_steps(matmul_tn(mixed_in[2], d_value).astype(jnp.bfloat16))
    g_value = next(value_steps)
    for _ in range(early_steps - 3):
        g_value = value_steps.send(g_value)
    *d_lows, _ = after(d_lows[0], *d_lows[1:], grads_time)
    g_time = lax.psum_scatter(grads_time, owners, scatter_dimension=0, tiled=True)
    back_one = back_from(d_lows, weights_time, mix_one)
    g_early = early.send(after(g_early, back_one)[0])
    d_input_part, time_small = blend_back(
        (x_low,),
        d_lows,
        [(w_time, at) for at in range(4)],
        keep,
        edge_one,
        back_one,
        norm_one,
        mix_one,
        piece_len,
        None,
        "blend_one_back",
    )
    d_input_part, g_early, g_chan, g_value = after(d_input_part, g_early, g_chan, g_value)
    g_early = early.send(g_early)
    g_value = value_steps.send(g_value)
    head_small = jnp.concatenate([state_small[:2], group_small[:2]])
    head_small = lax.dynamic_update_slice_in_dim(
        jnp.zeros((4, embedding_extent), jnp.float32), head_small, sharded_layout, 1
    )
    small_part = jnp.concatenate([time_small[:6], head_small, chan_small[:4]], axis=0)

    def small_total(token):
        tp_bits = axis_bits("tp")
        total = whole_sum(
            after(small_part, token)[0],
            axis_bits("fsdp") + tp_bits[:1] + axis_bits("ctx") + tp_bits[1:],
        )
        return total, g_early, g_value

    d_input_sum, (small_sum, g_early, g_value) = tp_sum(d_input_part, small_total)
    g_value = value_steps.send(after(g_value, small_sum)[0])
    owned = embedding_extent // (lax.axis_size("fsdp") * lax.axis_size("ctx"))
    small_owned = lax.dynamic_slice_in_dim(
        small_sum,
        (lax.axis_index("fsdp") * lax.axis_size("ctx") + lax.axis_index("ctx")) * owned,
        owned,
        1,
    )
    grad_inputs = (d_mixed.astype(jnp.float32) + d_input_sum.astype(jnp.float32)).reshape(
        full_shape
    )
    g_chanvalue = g_chanvalue.astype(jnp.float32)
    g_chankey, g_chanrecept = split_columns(g_chan, (units, fourth_extent), "split_chan")
    g_early = g_early.astype(jnp.float32)
    g_value = g_value.astype(jnp.float32)
    g_output = g_early[:, :fourth_extent].T
    g_gate = g_early[:, fourth_extent:]
    g_time = after(
        g_time, grad_inputs, result, g_chanvalue, g_chankey, g_chanrecept, g_output, g_gate, g_value
    )[0]
    g_recept, g_key = split_columns(g_time, (fourth_extent,) * 2, "split_time")
    return (
        result,
        grad_inputs,
        g_recept,
        g_key,
        g_value,
        g_gate,
        g_output,
        g_chankey,
        g_chanvalue,
        g_chanrecept,
    ) + tuple(small_owned[at] for at in range(14))


def solution(mesh):
    return jax.shard_map(
        per_device,
        mesh=mesh,
        in_specs=(
            P("fsdp", "ctx", None),
            P("fsdp", None),
            P(("fsdp", "ctx"), "tp"),
            P(("fsdp", "ctx"), "tp"),
            P(("fsdp", "ctx"), "tp"),
            P(("fsdp", "ctx"), "tp"),
            P("tp", ("fsdp", "ctx")),
            P(("fsdp", "ctx"), "tp"),
            P("tp", ("fsdp", "ctx")),
            P(("fsdp", "ctx"), "tp"),
            P(),
            P(),
            P(),
            P(),
            P(),
            P(),
            P(),
            P(),
            P(),
            P(),
            P(),
            P(),
            P(),
            P(),
            P("fsdp", "ctx", "tp"),
        ),
        out_specs=(
            P("fsdp", "ctx", "tp"),
            P("fsdp", "ctx", None),
            P(("fsdp", "ctx"), "tp"),
            P(("fsdp", "ctx"), "tp"),
            P(("fsdp", "ctx"), "tp"),
            P(("fsdp", "ctx"), "tp"),
            P("tp", ("fsdp", "ctx")),
            P(("fsdp", "ctx"), "tp"),
            P("tp", ("fsdp", "ctx")),
            P(("fsdp", "ctx"), "tp"),
            P(("fsdp", "ctx")),
            P(("fsdp", "ctx")),
            P(("fsdp", "ctx")),
            P(("fsdp", "ctx")),
            P(("fsdp", "ctx")),
            P(("fsdp", "ctx")),
            P(("fsdp", "ctx")),
            P(("fsdp", "ctx")),
            P(("fsdp", "ctx")),
            P(("fsdp", "ctx")),
            P(("fsdp", "ctx")),
            P(("fsdp", "ctx")),
            P(("fsdp", "ctx")),
            P(("fsdp", "ctx")),
        ),
        check_vma=False,
    )
```

```python
from functools import partial

import jax
import jax.numpy as jnp
from jax import lax
from jax.experimental import pallas as pl
from jax.experimental.pallas import tpu as pltpu
from jax.sharding import PartitionSpec as P

SUBSPACE_SIZE = 64
PAIR = 128
GROUP = 16
HALO = 8
SPAN = 64
TILE = 256


EPS = 1e-05
GROUP_EPS = 4.0


def shifted(x, axis, by):
    count = lax.axis_size(axis)
    pairs = [(i, i + by) for i in range(count) if 0 <= i + by < count]
    return lax.ppermute(x, axis, pairs)


def earlier_shift(x, axis, by):
    count = lax.axis_size(axis)
    return lax.ppermute(x, axis, [(i, i + by) for i in range(count) if 0 <= i + by < count])


def carried(mult, sums, axis, toward):
    count = lax.axis_size(axis)
    low = (mult.astype(jnp.bfloat16), sums.astype(jnp.bfloat16))
    arrived = [
        jax.tree.map(lambda part: earlier_shift(part, axis, toward * by), low)
        for by in range(1, count)
    ]
    state = jnp.zeros_like(sums)
    for far_mult, far_sums in reversed(arrived):
        state = far_mult.astype(jnp.float32) * state + far_sums.astype(jnp.float32)
    return state


def partner(x, bit):
    count = lax.axis_size("tp")
    return lax.ppermute(x, "tp", [(i, i ^ bit) for i in range(count)])


def halves(x, axis, bit):
    size = x.shape[axis] // 2
    mine = (lax.axis_index("tp") // bit) % 2
    return (
        lax.dynamic_slice_in_dim(x, mine * size, size, axis),
        lax.dynamic_slice_in_dim(x, (1 - mine) * size, size, axis),
    )


def add_low(left, right):
    return (left.astype(jnp.float32) + right.astype(jnp.float32)).astype(jnp.bfloat16)


def ordered(mine, other, axis, bit):
    first = (lax.axis_index("tp") // bit) % 2 == 0
    return jnp.where(
        first,
        jnp.concatenate([mine, other], axis),
        jnp.concatenate([other, mine], axis),
    )


def after(value, *earlier):
    return lax.optimization_barrier((value,) + earlier)


def tp_sum(x, work=None):
    mine, other = halves(x, 0, 1)
    part = add_low(mine, partner(other, 1))
    made = work(part) if work else None
    bit = 2
    while bit < lax.axis_size("tp"):
        arrived = partner(part, bit)
        if work and bit == 2:
            part = after(part, made)[0]
        part = add_low(part, arrived)
        bit *= 2
    whole = ordered(part, partner(part, 1), 0, 1)
    return (whole, made) if work else whole


def axis_bits(axis):
    bits, bit = [], 1
    while bit < lax.axis_size(axis):
        bits.append((axis, bit))
        bit *= 2
    return bits


def swap(x, axis, bit):
    return lax.ppermute(x, axis, [(i, i ^ bit) for i in range(lax.axis_size(axis))])


def split_kernel(x_ref, *outs):
    at = 0
    for out in outs:
        out[...] = x_ref[:, at : at + out.shape[1]].astype(jnp.float32)
        at += out.shape[1]


def split_columns(x, widths, name):
    count = x.shape[0]
    rows = min(count, 64)
    return pl.pallas_call(
        split_kernel,
        grid=(count // rows,),
        in_specs=[pl.BlockSpec((rows, x.shape[1]), lambda i: (i, 0))],
        out_specs=[pl.BlockSpec((rows, width), lambda i: (i, 0)) for width in widths],
        out_shape=[jax.ShapeDtypeStruct((count, width), jnp.float32) for width in widths],
        cost_estimate=pl.CostEstimate(flops=x.size, bytes_accessed=6 * x.size, transcendentals=0),
        name=name,
    )(x)


def owner_scatter_steps(x):
    fsdp_bits, ctx_bits = axis_bits("fsdp"), axis_bits("ctx")
    dims = list(reversed(fsdp_bits)) + list(reversed(ctx_bits))
    rows = x.shape[0] // 2 ** len(dims)
    part = x.reshape(*([2] * len(dims)), rows, x.shape[1])
    hold = None
    for axis, bit in fsdp_bits + ctx_bits:
        dim = dims.index((axis, bit))
        dims.pop(dim)
        mine = (lax.axis_index(axis) // bit) % 2
        own = lax.dynamic_index_in_dim(part, mine, dim, False)
        arrived = swap(lax.dynamic_index_in_dim(part, 1 - mine, dim, False), axis, bit)
        if hold is not None:
            own = after(own, hold)[0]
        part = yield add_low(own, arrived)
        hold = None
        if isinstance(part, tuple):
            part, hold = part
    yield None


def whole_sum(x, steps):
    for axis, bit in steps:
        x = x + swap(x, axis, bit)
    return x


def tp_scatter(x):
    count, place = lax.axis_size("tp"), lax.axis_index("tp")
    width = x.shape[1] // count
    parts = [
        lax.dynamic_slice_in_dim(x, (place ^ relative) * width, width, 1)
        for relative in range(count)
    ]
    bit = 1
    while bit < count:
        for relative in reversed(range(count)):
            if relative & bit and relative & (bit - 1) == 0:
                arrived = partner(parts[relative], bit)
                parts[relative ^ bit] = add_low(parts[relative ^ bit], arrived)
        bit *= 2
    return parts[0]


def tp_gather(x):
    count, place = lax.axis_size("tp"), lax.axis_index("tp")
    width = x.shape[1]
    parts = {0: x}
    bit = count // 2
    while bit:
        parts.update({relative ^ bit: partner(part, bit) for relative, part in parts.items()})
        bit //= 2
    whole = jnp.zeros((x.shape[0], width * count), x.dtype)
    for relative, part in parts.items():
        whole = lax.dynamic_update_slice_in_dim(whole, part, (place ^ relative) * width, 1)
    return whole


def matmul(left, right):
    return jnp.dot(left, right, preferred_element_type=jnp.float32)


def matmul_tn(left, right):
    return lax.dot_general(
        left, right, (((0,), (0,)), ((), ())), preferred_element_type=jnp.float32
    )


def matmul_nt(left, right):
    return lax.dot_general(
        left, right, (((1,), (1,)), ((), ())), preferred_element_type=jnp.float32
    )


def dot_nn(left, right):
    return lax.dot_general(
        left, right, (((1,), (0,)), ((), ())), preferred_element_type=jnp.float32
    )


def lanes_of(shape):
    return lax.broadcasted_iota(jnp.int32, shape, len(shape) - 1)


def low_head(shape):
    return lanes_of(shape) < SUBSPACE_SIZE


def head_sum(x):
    first = low_head(x.shape)
    low = jnp.sum(jnp.where(first, x, 0.0), -1, keepdims=True)
    high = jnp.sum(jnp.where(first, 0.0, x), -1, keepdims=True)
    return jnp.where(first, low, high)


def fold_pair(both):
    return jnp.where(
        low_head((SUBSPACE_SIZE, PAIR)), both[:SUBSPACE_SIZE], both[SUBSPACE_SIZE:]
    )


def spread_pair(folded):
    first = low_head((SUBSPACE_SIZE, PAIR))
    return jnp.concatenate(
        [jnp.where(first, folded, 0.0), jnp.where(first, 0.0, folded)], axis=0
    ).astype(jnp.bfloat16)


def head_parts(x):
    first = low_head(x.shape)
    zero = jnp.zeros_like(x)
    return jnp.where(first, x, zero), jnp.where(first, zero, x)


def places(length):
    return lax.broadcasted_iota(jnp.int32, (length, PAIR), 0).astype(jnp.float32)


def carry_kernel(k_ref, v_ref, log_ref, cols_ref, out_ref):
    length = k_ref.shape[0]
    closing = jnp.exp((length - 1.0 - places(length)) * log_ref[...])
    ending = cols_ref[:, 2:3]
    k_end = (k_ref[...].astype(jnp.float32) * closing * ending).astype(jnp.bfloat16)
    out_ref[0, 0] = fold_pair(matmul_tn(v_ref[...], k_end))


def group_norm(attend):
    centered = attend - head_sum(attend) * (1.0 / SUBSPACE_SIZE)
    inverse = lax.rsqrt(head_sum(centered * centered) * (1.0 / SUBSPACE_SIZE) + GROUP_EPS)
    return centered * inverse, inverse


def mix_kernel(
    r_ref, k_ref, v_ref, gate_ref, log_ref, rows_ref, cols_ref, seg_ref, state_ref,
    joined_ref, attend_ref,
):
    length = r_ref.shape[0]
    at = places(length)
    log = log_ref[...]
    r = r_ref[...].astype(jnp.float32)
    k = k_ref[...].astype(jnp.float32)
    v = v_ref[...]
    q_low = (r * jnp.exp(at * log)).astype(jnp.bfloat16)
    k_low = (k * jnp.exp(-(at + 1.0) * log)).astype(jnp.bfloat16)
    state = spread_pair(state_ref[0, 0])
    bonus = head_sum(r * rows_ref[0:1, :] * k)
    base = bonus * v.astype(jnp.float32) + cols_ref[:, 1:2] * matmul_nt(q_low, state)
    step = min(length, TILE)
    for top in range(0, length, step):
        reach = top + step
        rows = slice(top, reach)
        keep = pair_mask(cols_ref[rows, 0:1], seg_ref[0, :, :reach], top, step, reach)
        parts = []
        for q_part in head_parts(q_low[rows]):
            scores = matmul_nt(q_part, k_low[:reach])
            scores = jnp.where(keep, scores, 0.0).astype(jnp.bfloat16)
            parts.append(dot_nn(scores, v[:reach]))
        attend = base[rows] + jnp.where(low_head(parts[0].shape), parts[0], parts[1])
        unit, _ = group_norm(attend)
        grouped = unit * rows_ref[1:2, :] + rows_ref[2:3, :]
        gate = gate_ref[rows, :]
        attend_ref[rows, :] = attend
        joined_ref[rows, :] = (grouped * (gate * jax.nn.sigmoid(gate))).astype(jnp.bfloat16)


def pair_mask(seg_col, seg_row, top, count, reach):
    later = lax.broadcasted_iota(jnp.int32, (count, reach), 0) + top
    return (seg_col == seg_row) & (later > lanes_of((count, reach)))


def pair_mask_t(seg_col, seg_row, top, count, start):
    width = seg_row.shape[1]
    earlier = lax.broadcasted_iota(jnp.int32, (count, width), 0) + top
    return (seg_col == seg_row) & (lanes_of((count, width)) + start > earlier)


def gate_back_kernel(
    dj_ref, attend_ref, gate_ref, r_ref, log_ref, rows_ref, cols_ref,
    dgate_ref, dattend_ref, state_ref, small_ref,
):
    length = r_ref.shape[0]
    d_joined = dj_ref[...]
    gate = gate_ref[...]
    unit, inverse = group_norm(attend_ref[...])
    gain = rows_ref[1:2, :]
    grouped = unit * gain + rows_ref[2:3, :]
    sig = jax.nn.sigmoid(gate)
    dgate_ref[...] = (d_joined * grouped * sig * (1.0 + gate * (1.0 - sig))).astype(jnp.bfloat16)
    d_grouped = d_joined * gate * sig
    sums = [
        jnp.sum(d_grouped * unit, axis=0, keepdims=True),
        jnp.sum(d_grouped, axis=0, keepdims=True),
    ]
    scaled = d_grouped * gain
    share = 1.0 / SUBSPACE_SIZE
    d_attend = (
        inverse * (scaled - head_sum(scaled) * share - unit * (head_sum(scaled * unit) * share))
    ).astype(jnp.bfloat16)
    dattend_ref[...] = d_attend
    rising = jnp.exp(places(length) * log_ref[...])
    q_live = (r_ref[...].astype(jnp.float32) * rising * cols_ref[:, 1:2]).astype(jnp.bfloat16)
    state_ref[0, 0] = fold_pair(matmul_tn(d_attend, q_live))
    collect(small_ref, sums)


def collect(small_ref, sums):
    pad = jnp.zeros((small_ref.shape[0] - len(sums), sums[0].shape[1]), jnp.float32)
    total = jnp.concatenate(sums + [pad], axis=0)

    @pl.when(pl.program_id(1) == 0)
    def _():
        small_ref[...] = total

    @pl.when(pl.program_id(1) > 0)
    def _():
        small_ref[...] += total


def mix_back_kernel(
    r_ref, k_ref, v_ref, da_ref, log_ref, rows_ref, cols_ref, seg_ref, state_ref, gstate_ref,
    mult_ref, dr_ref, dk_ref, dv_ref, small_ref,
):
    length = r_ref.shape[0]
    at = places(length)
    log = log_ref[...]
    reward = rows_ref[0:1, :]
    r = r_ref[...].astype(jnp.float32)
    k = k_ref[...].astype(jnp.float32)
    v = v_ref[...]
    da = da_ref[...]
    rising = jnp.exp(at * log)
    falling = jnp.exp(-(at + 1.0) * log)
    closing = jnp.exp((length - 1.0 - at) * log) * cols_ref[:, 2:3]
    q_low = (r * rising).astype(jnp.bfloat16)
    k_low = (k * falling).astype(jnp.bfloat16)
    k_end = (k * closing).astype(jnp.bfloat16)
    state, gstate = state_ref[0, 0], gstate_ref[0, 0]
    state_low, gstate_low = spread_pair(state), spread_pair(gstate)
    v_f, da_f = v.astype(jnp.float32), da.astype(jnp.float32)
    dot_va = head_sum(v_f * da_f)
    dk_end = dot_nn(v, gstate_low)
    dq_base = cols_ref[:, 1:2] * dot_nn(da, state_low)
    dv_base = head_sum(r * reward * k) * da_f + matmul_nt(k_end, gstate_low)
    q_f, k_f = q_low.astype(jnp.float32), k_low.astype(jnp.float32)
    d_log = jnp.sum((length - 1.0 - at) * k_end.astype(jnp.float32) * dk_end, 0, keepdims=True)
    d_log += length * mult_ref[0, 0] * jnp.sum(
        state.astype(jnp.bfloat16).astype(jnp.float32)
        * gstate.astype(jnp.bfloat16).astype(jnp.float32),
        0,
        keepdims=True,
    )
    step = min(length, TILE)
    for top in range(0, length, step):
        rows = slice(top, top + step)
        reach = top + step
        keep = pair_mask(cols_ref[rows, 0:1], seg_ref[0, :, :reach], top, step, reach)
        dq = []
        for da_part in head_parts(da[rows]):
            pull = jnp.where(keep, matmul_nt(da_part, v[:reach]), 0.0).astype(jnp.bfloat16)
            dq.append(dot_nn(pull, k_low[:reach]))
        first = low_head(dq[0].shape)
        dq = jnp.where(first, dq[0], dq[1]) + dq_base[rows]
        d_log += jnp.sum(at[rows] * q_f[rows] * dq, 0, keepdims=True)
        dr_ref[rows, :] = (dq * rising[rows] + reward * k[rows] * dot_va[rows]).astype(jnp.bfloat16)
        keep = pair_mask_t(cols_ref[rows, 0:1], seg_ref[0, :, top:], top, step, top)
        dk, dv = [], []
        for v_part, k_part in zip(head_parts(v[rows]), head_parts(k_low[rows])):
            pull = jnp.where(keep, matmul_nt(v_part, da[top:]), 0.0).astype(jnp.bfloat16)
            dk.append(dot_nn(pull, q_low[top:]))
            scores = jnp.where(keep, matmul_nt(k_part, q_low[top:]), 0.0).astype(jnp.bfloat16)
            dv.append(dot_nn(scores, da[top:]))
        dk = jnp.where(first, dk[0], dk[1])
        d_log -= jnp.sum((at[rows] + 1.0) * k_f[rows] * dk, 0, keepdims=True)
        dk_ref[rows, :] = (
            dk * falling[rows]
            + dk_end[rows] * closing[rows]
            + reward * r[rows] * dot_va[rows]
        ).astype(jnp.bfloat16)
        dv_ref[rows, :] = (jnp.where(first, dv[0], dv[1]) + dv_base[rows]).astype(jnp.bfloat16)
    collect(small_ref, [d_log * jnp.exp(-log), jnp.sum(r * k * dot_va, 0, keepdims=True)])


def pair_call(kernel, seqs, length, width, operands, outs, name, flops):
    pairs = width // PAIR
    specs = {
        "wide": pl.BlockSpec((length, PAIR), lambda p, s: (s, p)),
        "vector": pl.BlockSpec((1, PAIR), lambda p, s: (0, p)),
        "vectors": pl.BlockSpec((8, PAIR), lambda p, s: (0, p)),
        "cols": pl.BlockSpec((length, 4), lambda p, s: (s, 0)),
        "row": pl.BlockSpec((1, 1, length), lambda p, s: (s, 0, 0)),
        "state": pl.BlockSpec((1, 1, SUBSPACE_SIZE, PAIR), lambda p, s: (s, p, 0, 0)),
        "mult": pl.BlockSpec((1, 1, 1, PAIR), lambda p, s: (s, p, 0, 0)),
    }
    shapes = {
        "wide": (seqs * length, width),
        "vectors": (8, width),
        "state": (seqs, pairs, SUBSPACE_SIZE, PAIR),
    }
    kinds, arrays = zip(*operands)
    size = sum(array.size * array.dtype.itemsize for array in arrays)
    return pl.pallas_call(
        kernel,
        grid=(pairs, seqs),
        in_specs=[specs[kind] for kind in kinds],
        out_specs=[specs[kind] for kind, _ in outs],
        out_shape=[jax.ShapeDtypeStruct(shapes[kind], dtype) for kind, dtype in outs],
        cost_estimate=pl.CostEstimate(flops=flops, bytes_accessed=2 * size, transcendentals=0),
        name=name,
    )(*arrays)


def unit_rows(x):
    centered = x - jnp.mean(x, -1, keepdims=True)
    return centered * lax.rsqrt(jnp.mean(centered * centered, -1, keepdims=True) + EPS)


def total_at(refs, rows, lanes):
    total = refs[0][rows, lanes].astype(jnp.float32)
    for ref in refs[1:]:
        total = total + ref[rows, lanes].astype(jnp.float32)
    return total


def lane_loop(width, body):
    def step(at, _):
        body(pl.ds(pl.multiple_of(at * PAIR, PAIR), PAIR))
        return 0

    lax.fori_loop(0, width // PAIR, step, 0)


def row_blocks(rows):
    return [slice(top, min(top + SPAN, rows)) for top in range(0, rows, SPAN)]


def unit_into(refs, unit_scr, rows, width):
    inverses = []
    for block in row_blocks(rows):
        inside = slice(block.start + HALO, block.stop + HALO)
        zero = jnp.zeros((block.stop - block.start, PAIR), jnp.float32)

        def load(at, total):
            lanes = pl.ds(pl.multiple_of(at * PAIR, PAIR), PAIR)
            value = total_at(refs, block, lanes)
            unit_scr[inside, lanes] = value
            return total + value

        total = lax.fori_loop(0, width // PAIR, load, zero, unroll=4)
        mean = jnp.sum(total, -1, keepdims=True) * (1.0 / width)

        def square(at, total):
            lanes = pl.ds(pl.multiple_of(at * PAIR, PAIR), PAIR)
            value = unit_scr[inside, lanes] - mean
            return total + value * value

        total = lax.fori_loop(0, width // PAIR, square, zero, unroll=4)
        inverse = lax.rsqrt(jnp.sum(total, -1, keepdims=True) * (1.0 / width) + EPS)

        def scale(at, _):
            lanes = pl.ds(pl.multiple_of(at * PAIR, PAIR), PAIR)
            unit_scr[inside, lanes] = (unit_scr[inside, lanes] - mean) * inverse
            return 0

        lax.fori_loop(0, width // PAIR, scale, 0, unroll=4)
        inverses.append(inverse)
    return inverses


def blend_kernel(parts, mixes, per_seq, *refs):
    x_refs, refs = refs[:parts], refs[parts:]
    keep_ref, edge_ref, norm_ref, mix_ref = refs[:4]
    outs, unit_scr = refs[4 : 4 + mixes], refs[4 + mixes]
    rows, width = x_refs[0].shape

    @pl.when(pl.program_id(0) % per_seq == 0)
    def _():
        unit_scr[HALO - 1 : HALO, :] = edge_ref[0]

    unit_into(x_refs, unit_scr, rows, width)

    def lane_block(lanes):
        gain, bias_term = norm_ref[0:1, lanes], norm_ref[1:2, lanes]
        mixers = [mix_ref[at : at + 1, lanes] for at in range(mixes)]
        for block in row_blocks(rows):
            normed = unit_scr[block.start + HALO : block.stop + HALO, lanes] * gain + bias_term
            before = pltpu.roll(unit_scr[block.start : block.stop + HALO, lanes], 1, 0)[HALO:]
            previous = (before * gain + bias_term) * keep_ref[block, 0:1]
            delta = normed - previous
            for mixer, out in zip(mixers, outs):
                out[block, lanes] = (previous + mixer * delta).astype(jnp.bfloat16)

    lane_loop(width, lane_block)
    unit_scr[HALO - 1 : HALO, :] = unit_scr[rows + HALO - 1 : rows + HALO, :]


def blend(xs, keep, edge, norm, mixers, piece, name):
    tokens, width = xs[0].shape
    rows = min(piece, 256)
    mixes = mixers.shape[0]
    per_seq = piece // rows
    wide = pl.BlockSpec((rows, width), lambda i: (i, 0))
    return pl.pallas_call(
        partial(blend_kernel, len(xs), mixes, per_seq),
        grid=(tokens // rows,),
        in_specs=[wide] * len(xs)
        + [
            pl.BlockSpec((rows, 1), lambda i: (i, 0)),
            pl.BlockSpec((1, 1, width), lambda i: (i // per_seq, 0, 0)),
            pl.BlockSpec((2, width), lambda i: (0, 0)),
            pl.BlockSpec((mixes, width), lambda i: (0, 0)),
        ],
        out_specs=[wide] * mixes,
        out_shape=[jax.ShapeDtypeStruct((tokens, width), jnp.bfloat16)] * mixes,
        scratch_shapes=[pltpu.VMEM((rows + HALO, width), jnp.float32)],
        cost_estimate=pl.CostEstimate(
            flops=20 * tokens * width,
            bytes_accessed=2 * tokens * width * (len(xs) + mixes),
            transcendentals=0,
        ),
        name=name,
    )(*xs, keep, edge, norm, mixers)


def blend_back_kernel(parts, mixes, per_seq, own, *refs):
    x_refs, refs = refs[:parts], refs[parts:]
    halo_refs, refs = refs[:parts], refs[parts:]
    grad_refs, refs = refs[:mixes], refs[mixes:]
    weight_refs, refs = refs[:mixes], refs[mixes:]
    keep_ref, edge_ref, back_ref, norm_ref, mix_ref = refs[:5]
    refs = refs[5:]
    own_refs, refs = refs[: 2 * own], refs[2 * own :]
    out_ref, small_ref, d_scr, unit_scr, prev_scr, row_scr, sums = refs
    rows, width = x_refs[0].shape
    tiles = pl.num_programs(0)
    tile = tiles - 1 - pl.program_id(0)

    @pl.when(pl.program_id(0) == 0)
    def _():
        sums[...] = jnp.zeros_like(sums)

    @pl.when(tile % per_seq == per_seq - 1)
    def _():
        prev_scr[rows : rows + 1, :] = back_ref[0]

    @pl.when(tile % per_seq < per_seq - 1)
    def _():
        prev_scr[rows : rows + 1, :] = prev_scr[0:1, :]

    for at in range(mixes):
        d_scr[at] = matmul_nt(grad_refs[at][...], weight_refs[at][...])

    halo = unit_rows(total_at(halo_refs, slice(None), slice(None)))[GROUP - 1 :, :]
    unit_scr[HALO - 1 : HALO, :] = jnp.where(tile % per_seq == 0, edge_ref[0], halo)
    inverses = unit_into(x_refs, unit_scr, rows, width)
    row_scr[...] = jnp.zeros_like(row_scr)

    def gather(at, value):
        total = value[0:8]
        for top in range(8, value.shape[0], 8):
            total = total + value[top : top + 8]
        return total

    def first_pass(lanes):
        gain, bias_term = norm_ref[0:1, lanes], norm_ref[1:2, lanes]
        mixers = [mix_ref[at : at + 1, lanes] for at in range(mixes)]
        totals = [jnp.zeros((8, PAIR), jnp.float32)] * mixes
        for block in row_blocks(rows):
            keep = keep_ref[block, 0:1]
            normed = unit_scr[block.start + HALO : block.stop + HALO, lanes] * gain + bias_term
            before = pltpu.roll(unit_scr[block.start : block.stop + HALO, lanes], 1, 0)[HALO:]
            delta = normed - (before * gain + bias_term) * keep
            d_norm, d_all = None, None
            for at in range(mixes):
                d_in = d_scr[at, block, lanes]
                totals[at] = totals[at] + gather(at, d_in * delta)
                share = d_in * mixers[at]
                d_norm = share if d_norm is None else d_norm + share
                d_all = d_in if d_all is None else d_all + d_in
            prev_scr[block, lanes] = (d_all - d_norm) * keep
            d_scr[0, block, lanes] = d_norm
        for at in range(mixes):
            sums[2 + at, :, lanes] += totals[at]

    lane_loop(width, first_pass)

    def second_pass(lanes):
        gain = norm_ref[0:1, lanes]
        totals = [jnp.zeros((8, PAIR), jnp.float32)] * 2
        for block in row_blocks(rows):
            size = block.stop - block.start
            later = pltpu.roll(
                prev_scr[block.start : block.stop + HALO, lanes], size + HALO - 1, 0
            )[:size]
            d_norm = d_scr[0, block, lanes] + later
            unit = unit_scr[block.start + HALO : block.stop + HALO, lanes]
            product = d_norm * unit
            totals[0] = totals[0] + gather(0, product)
            totals[1] = totals[1] + gather(1, d_norm)
            d_scr[0, block, lanes] = d_norm * gain
            row_scr[0, block, :] += d_norm * gain
            row_scr[1, block, :] += product * gain
        for at in range(2):
            sums[at, :, lanes] += totals[at]

    lane_loop(width, second_pass)
    means, tilts = [], []
    for block in row_blocks(rows):
        means.append(jnp.sum(row_scr[0, block, :], -1, keepdims=True) * (1.0 / width))
        tilts.append(jnp.sum(row_scr[1, block, :], -1, keepdims=True) * (1.0 / width))
    blocks = list(zip(row_blocks(rows), inverses, means, tilts))

    def last_pass(start, lanes):
        for block, inverse, mean, tilt in blocks:
            unit = unit_scr[block.start + HALO : block.stop + HALO, lanes]
            value = inverse * (d_scr[0, block, lanes] - mean - unit * tilt)
            if own:
                extra = own_refs[0][block, start].astype(jnp.float32)
                value = value + extra * own_refs[1][0:1, lanes]
            out_ref[block, lanes] = value.astype(jnp.bfloat16)

    def last_step(at, _):
        lanes = pl.ds(pl.multiple_of(at * PAIR, PAIR), PAIR)
        inner = None
        if own:
            count = own_refs[0].shape[1] // PAIR
            inner = pl.ds(pl.multiple_of((at % count) * PAIR, PAIR), PAIR)
        last_pass(inner, lanes)
        return 0

    lax.fori_loop(0, width // PAIR, last_step, 0)

    @pl.when(pl.program_id(0) == tiles - 1)
    def _():
        for at in range(2 + mixes):
            small_ref[at : at + 1, :] = jnp.sum(sums[at], 0, keepdims=True)


def blend_back(xs, grads, weights, keep, edge, back, norm, mixers, piece, own, name):
    tokens, width = xs[0].shape
    rows = min(piece, 256)
    mixes = mixers.shape[0]
    per_seq = piece // rows
    tiles = tokens // rows

    def reverse(i):
        return tiles - 1 - i

    def halo_at(i):
        return (jnp.maximum(reverse(i) * (rows // GROUP) - 1, 0), 0)

    wide = pl.BlockSpec((rows, width), lambda i: (reverse(i), 0))
    per = pl.BlockSpec((1, 1, width), lambda i: (reverse(i) // per_seq, 0, 0))
    weight_specs, weight_arrays = [], []
    for (array, at), grad in zip(weights, grads):
        weight_specs.append(
            pl.BlockSpec(
                (width, grad.shape[1]), partial(lambda at, i: (0, at), at),
                pipeline_mode=pl.Buffered(1),
            )
        )
        weight_arrays.append(array)
    return pl.pallas_call(
        partial(blend_back_kernel, len(xs), mixes, per_seq, int(own is not None)),
        grid=(tiles,),
        in_specs=[wide] * len(xs)
        + [pl.BlockSpec((GROUP, width), halo_at)] * len(xs)
        + [pl.BlockSpec((rows, grad.shape[1]), lambda i: (reverse(i), 0)) for grad in grads]
        + weight_specs
        + [
            pl.BlockSpec((rows, 1), lambda i: (reverse(i), 0)),
            per,
            per,
            pl.BlockSpec((2, width), lambda i: (0, 0)),
            pl.BlockSpec((mixes, width), lambda i: (0, 0)),
        ]
        + (
            [
                pl.BlockSpec((rows, own[0].shape[1]), lambda i: (reverse(i), 0)),
                pl.BlockSpec((1, width), lambda i: (0, 0)),
            ]
            if own is not None
            else []
        ),
        out_specs=[wide, pl.BlockSpec((8, width), lambda i: (0, 0))],
        out_shape=[
            jax.ShapeDtypeStruct((tokens, width), jnp.bfloat16),
            jax.ShapeDtypeStruct((8, width), jnp.float32),
        ],
        scratch_shapes=[
            pltpu.VMEM((mixes, rows, width), jnp.float32),
            pltpu.VMEM((rows + HALO, width), jnp.float32),
            pltpu.VMEM((rows + HALO, width), jnp.float32),
            pltpu.VMEM((2, rows, PAIR), jnp.float32),
            pltpu.VMEM((2 + mixes, 8, width), jnp.float32),
        ],
        cost_estimate=pl.CostEstimate(
            flops=2 * tokens * width * sum(grad.shape[1] for grad in grads),
            bytes_accessed=2 * tokens * width * 4,
            transcendentals=0,
        ),
        name=name,
    )(*xs, *xs, *grads, *weight_arrays, keep, edge, back, norm, mixers, *(own or ()))


def per_device(
    entering_activations,
    document_indices,
    acceptor_matrix,
    lookup_matrix,
    payload_matrix,
    valve_matrix,
    result_matrix,
    ffn_lookup_matrix,
    ffn_payload_matrix,
    ffn_acceptor_matrix,
    first_standardize_scaling,
    first_standardize_offset,
    acceptor_lerp_factor,
    lookup_lerp_factor,
    payload_lerp_factor,
    valve_lerp_factor,
    token_fading,
    diagonal_reward,
    subspace_standardize_scaling,
    subspace_standardize_offset,
    second_standardize_scaling,
    second_standardize_offset,
    ffn_lookup_lerp,
    ffn_acceptor_lerp,
    upstream_derivative,
):
    seqs_here, piece_len, embedding_extent = entering_activations.shape
    token_count = seqs_here * piece_len
    tp_count = lax.axis_size("tp")
    fourth_extent = embedding_extent // tp_count
    sharded_layout = lax.axis_index("tp") * fourth_extent
    ctx_place = lax.axis_index("ctx") * piece_len
    padded_seg = jnp.concatenate(
        [jnp.full((seqs_here, 1), -1, jnp.int32), document_indices], axis=1
    )
    segment_present = lax.dynamic_slice_in_dim(document_indices, ctx_place, piece_len, 1)
    seg_before = lax.dynamic_slice_in_dim(padded_seg, ctx_place, piece_len, 1)
    document_begins = seg_before[:, :1]
    pairs_here = fourth_extent // PAIR
    same_mask = segment_present == seg_before
    live_mask = segment_present == document_begins
    ending_mask = segment_present == segment_present[:, -1:]
    cols = jnp.stack([segment_present, live_mask, ending_mask, same_mask], axis=-1)
    cols = cols.astype(jnp.float32).reshape(token_count, 4)
    keep = same_mask.astype(jnp.float32).reshape(token_count, 1)
    keep_first = same_mask[:, :1].astype(jnp.float32)
    seg_row = segment_present.astype(jnp.float32)[:, None, :]
    owners = ("fsdp", "ctx")
    w_time = lax.all_gather(
        jnp.concatenate(
            [acceptor_matrix, lookup_matrix, payload_matrix, valve_matrix, result_matrix.T], axis=1
        ),
        owners,
        axis=0,
        tiled=True,
    )
    w_chan = lax.all_gather(
        jnp.concatenate([ffn_lookup_matrix, ffn_acceptor_matrix], axis=1),
        owners,
        axis=0,
        tiled=True,
    )
    units = ffn_lookup_matrix.shape[1]
    w_recept, w_key, w_value, w_gate, w_output_t = (
        w_time[:, at * fourth_extent : (at + 1) * fourth_extent] for at in range(5)
    )
    w_chankey = w_chan[:, :units]
    w_chanrecept = w_chan[:, units:]
    w_chanvalue_t = lax.all_gather(ffn_payload_matrix.T, owners, axis=0, tiled=True)
    x_low = entering_activations.reshape(token_count, embedding_extent)
    norm_one = jnp.stack([first_standardize_scaling, first_standardize_offset])
    norm_two = jnp.stack([second_standardize_scaling, second_standardize_offset])
    mix_one = jnp.stack(
        [acceptor_lerp_factor, lookup_lerp_factor, payload_lerp_factor, valve_lerp_factor]
    )
    mix_two = jnp.stack([ffn_lookup_lerp, ffn_acceptor_lerp])

    def edge_from(last_rows):
        return shifted(unit_rows(last_rows), "ctx", 1)[:, None]

    def back_from(grads, weights, mixers):
        first = jnp.zeros((seqs_here, embedding_extent), jnp.float32)
        for at, (grad_low, weight) in enumerate(zip(grads, weights)):
            rows = grad_low.reshape(seqs_here, piece_len, -1)[:, 0]
            first = first + matmul_nt(rows, weight) * (1.0 - mixers[at])
        return shifted(first * keep_first, "ctx", -1)[:, None]

    edge_one = edge_from(entering_activations[:, -1].astype(jnp.float32))
    mixed_in = blend((x_low,), keep, edge_one, norm_one, mix_one, piece_len, "blend_one")
    key_low = matmul(mixed_in[1], w_key).astype(jnp.bfloat16)
    value_low = matmul(mixed_in[2], w_value).astype(jnp.bfloat16)

    def own_share(vector):
        return lax.dynamic_slice_in_dim(vector, sharded_layout, fourth_extent, 0)[None]

    log_row = jnp.log(own_share(token_fading))
    vectors = jnp.concatenate(
        [own_share(diagonal_reward), own_share(subspace_standardize_scaling)]
        + [own_share(subspace_standardize_offset)] * 6
    )
    call = partial(pair_call, seqs=seqs_here, length=piece_len, width=fourth_extent)
    square = 2 * token_count * piece_len * fourth_extent
    (carry_sums,) = call(
        carry_kernel,
        operands=[("wide", key_low), ("wide", value_low), ("vector", log_row), ("cols", cols)],
        outs=[("state", jnp.float32)],
        name="carry",
        flops=square // 8,
    )
    alive_mask = (live_mask[:, -1]).astype(jnp.float32)[:, None, None, None]
    carry_mult = alive_mask * jnp.exp(float(piece_len) * log_row).reshape(1, pairs_here, 1, PAIR)
    incoming = carried(carry_mult, carry_sums, "ctx", 1)
    recept_low = matmul(mixed_in[0], w_recept).astype(jnp.bfloat16)
    gate_pre = matmul(mixed_in[3], w_gate)
    joined_low, attend = call(
        mix_kernel,
        operands=[
            ("wide", recept_low),
            ("wide", key_low),
            ("wide", value_low),
            ("wide", gate_pre),
            ("vector", log_row),
            ("vectors", vectors),
            ("cols", cols),
            ("row", seg_row),
            ("state", incoming),
        ],
        outs=[("wide", jnp.bfloat16), ("wide", jnp.float32)],
        name="mix",
        flops=2 * square,
    )
    mixed_out = tp_sum(matmul_nt(joined_low, w_output_t).astype(jnp.bfloat16))
    last_rows = entering_activations[:, -1].astype(jnp.float32) + mixed_out.reshape(
        seqs_here, piece_len, embedding_extent
    )[:, -1].astype(jnp.float32)
    edge_two = edge_from(last_rows)
    key_in, rec_in = blend(
        (x_low, mixed_out), keep, edge_two, norm_two, mix_two, piece_len, "blend_two"
    )
    rec_gate = jax.nn.sigmoid(matmul(rec_in, w_chanrecept))
    d_result_low = upstream_derivative.reshape(token_count, fourth_extent)
    d_result = d_result_low.astype(jnp.float32)
    d_chan = (d_result * rec_gate).astype(jnp.bfloat16)
    d_chan_full = tp_gather(d_chan)
    key_pre = matmul(key_in, w_chankey)
    hidden = jnp.square(jax.nn.relu(key_pre)).astype(jnp.bfloat16)
    grad_chanvalue = matmul_tn(hidden, d_chan_full).astype(jnp.bfloat16)
    g_chanvalue = lax.psum_scatter(grad_chanvalue, owners, scatter_dimension=1, tiled=True)
    hidden, grad_chanvalue = after(hidden, grad_chanvalue)
    chan_sum = tp_scatter(matmul_nt(hidden, w_chanvalue_t).astype(jnp.bfloat16)).astype(jnp.float32)
    middle_q = lax.dynamic_slice_in_dim(x_low, sharded_layout, fourth_extent, 1).astype(
        jnp.float32
    ) + lax.dynamic_slice_in_dim(mixed_out, sharded_layout, fourth_extent, 1).astype(jnp.float32)
    result = (
        (middle_q + rec_gate * chan_sum)
        .astype(jnp.bfloat16)
        .reshape(seqs_here, piece_len, fourth_extent)
    )
    d_rec_pre = (d_result * chan_sum * rec_gate * (1.0 - rec_gate)).astype(jnp.bfloat16)
    d_hidden = matmul(d_chan_full, w_chanvalue_t)
    d_key_pre = (d_hidden * 2.0 * jax.nn.relu(key_pre)).astype(jnp.bfloat16)
    full_shape = (seqs_here, piece_len, embedding_extent)
    own_mask = (jnp.arange(embedding_extent) // fourth_extent == lax.axis_index("tp")).astype(
        jnp.float32
    )[None]
    d_middle_part, chan_small = blend_back(
        (x_low, mixed_out),
        (d_key_pre, d_rec_pre),
        ((w_chan, 0), (w_chanrecept, 0)),
        keep,
        edge_two,
        back_from((d_key_pre, d_rec_pre), (w_chankey, w_chanrecept), mix_two),
        norm_two,
        mix_two,
        piece_len,
        (d_result_low, own_mask),
        "blend_two_back",
    )

    def chan_grads(token):
        d_key_late, d_rec_late, _ = after(d_key_pre, d_rec_pre, token)
        return jnp.concatenate(
            [
                matmul_tn(key_in, d_key_late).astype(jnp.bfloat16),
                matmul_tn(rec_in, d_rec_late).astype(jnp.bfloat16),
            ],
            axis=1,
        )

    d_mixed, grads_chan = tp_sum(d_middle_part, chan_grads)
    d_mixed, grads_chan, g_chanvalue = after(d_mixed, grads_chan, g_chanvalue)
    g_chan = lax.psum_scatter(grads_chan, owners, scatter_dimension=0, tiled=True)
    grad_output_t = matmul_tn(d_mixed, joined_low).astype(jnp.bfloat16)
    d_joined = matmul(d_mixed, w_output_t)
    d_gate_pre, d_attend, local_grad, group_small = call(
        gate_back_kernel,
        operands=[
            ("wide", d_joined),
            ("wide", attend),
            ("wide", gate_pre),
            ("wide", recept_low),
            ("vector", log_row),
            ("vectors", vectors),
            ("cols", cols),
        ],
        outs=[
            ("wide", jnp.bfloat16),
            ("wide", jnp.bfloat16),
            ("state", jnp.float32),
            ("vectors", jnp.float32),
        ],
        name="gate_back",
        flops=square // 8,
    )
    grads_early = jnp.concatenate(
        [grad_output_t, matmul_tn(mixed_in[3], d_gate_pre).astype(jnp.bfloat16)], axis=1
    )
    early = owner_scatter_steps(grads_early)
    g_early = next(early)
    outgoing_state = carried(carry_mult, local_grad, "ctx", -1)
    d_recept, d_key, d_value, state_small = call(
        mix_back_kernel,
        operands=[
            ("wide", recept_low),
            ("wide", key_low),
            ("wide", value_low),
            ("wide", d_attend),
            ("vector", log_row),
            ("vectors", vectors),
            ("cols", cols),
            ("row", seg_row),
            ("state", incoming),
            ("state", outgoing_state),
            ("mult", carry_mult),
        ],
        outs=[("wide", jnp.bfloat16)] * 3 + [("vectors", jnp.float32)],
        name="mix_back",
        flops=6 * square,
    )
    early_steps = len(axis_bits("fsdp")) + len(axis_bits("ctx"))
    d_recept, d_key, d_value, g_early = after(d_recept, d_key, d_value, g_early)
    for _ in range(early_steps - 3):
        g_early = early.send(g_early)
    d_lows = [d_recept, d_key, d_value, d_gate_pre]
    weights_time = (w_recept, w_key, w_value, w_gate)
    grads_time = jnp.concatenate(
        [
            matmul_tn(mixed, grad_low).astype(jnp.bfloat16)
            for mixed, grad_low in zip(mixed_in, d_lows[:2])
        ],
        axis=1,
    )
    value_steps = owner_scatter_steps(matmul_tn(mixed_in[2], d_value).astype(jnp.bfloat16))
    g_value = next(value_steps)
    for _ in range(early_steps - 3):
        g_value = value_steps.send(g_value)
    *d_lows, _ = after(d_lows[0], *d_lows[1:], grads_time)
    g_time = lax.psum_scatter(grads_time, owners, scatter_dimension=0, tiled=True)
    back_one = back_from(d_lows, weights_time, mix_one)
    g_early = early.send(after(g_early, back_one)[0])
    d_input_part, time_small = blend_back(
        (x_low,),
        d_lows,
        [(w_time, at) for at in range(4)],
        keep,
        edge_one,
        back_one,
        norm_one,
        mix_one,
        piece_len,
        None,
        "blend_one_back",
    )
    d_input_part, g_early, g_chan, g_value = after(d_input_part, g_early, g_chan, g_value)
    g_early = early.send(g_early)
    g_value = value_steps.send(g_value)
    head_small = jnp.concatenate([state_small[:2], group_small[:2]])
    head_small = lax.dynamic_update_slice_in_dim(
        jnp.zeros((4, embedding_extent), jnp.float32), head_small, sharded_layout, 1
    )
    small_part = jnp.concatenate([time_small[:6], head_small, chan_small[:4]], axis=0)

    def small_total(token):
        tp_bits = axis_bits("tp")
        total = whole_sum(
            after(small_part, token)[0],
            axis_bits("fsdp") + tp_bits[:1] + axis_bits("ctx") + tp_bits[1:],
        )
        return total, g_early, g_value

    d_input_sum, (small_sum, g_early, g_value) = tp_sum(d_input_part, small_total)
    owned = embedding_extent // (lax.axis_size("fsdp") * lax.axis_size("ctx"))
    small_owned = lax.dynamic_slice_in_dim(
        small_sum,
        (lax.axis_index("fsdp") * lax.axis_size("ctx") + lax.axis_index("ctx")) * owned,
        owned,
        1,
    )
    grad_inputs = (d_mixed.astype(jnp.float32) + d_input_sum.astype(jnp.float32)).reshape(
        full_shape
    )
    g_chanvalue = g_chanvalue.astype(jnp.float32)
    g_chankey, g_chanrecept = split_columns(g_chan, (units, fourth_extent), "split_chan")
    g_early = g_early.astype(jnp.float32)
    g_value = value_steps.send((g_value, (grad_inputs, g_chankey, g_chanrecept)))
    g_value = g_value.astype(jnp.float32)
    g_output = g_early[:, :fourth_extent].T
    g_gate = g_early[:, fourth_extent:]
    g_time = after(
        g_time, grad_inputs, result, g_chanvalue, g_chankey, g_chanrecept, g_output, g_gate, g_value
    )[0]
    g_recept, g_key = split_columns(g_time, (fourth_extent,) * 2, "split_time")
    return (
        result,
        grad_inputs,
        g_recept,
        g_key,
        g_value,
        g_gate,
        g_output,
        g_chankey,
        g_chanvalue,
        g_chanrecept,
    ) + tuple(small_owned[at] for at in range(14))


def solution(mesh):
    return jax.shard_map(
        per_device,
        mesh=mesh,
        in_specs=(
            P("fsdp", "ctx", None),
            P("fsdp", None),
            P(("fsdp", "ctx"), "tp"),
            P(("fsdp", "ctx"), "tp"),
            P(("fsdp", "ctx"), "tp"),
            P(("fsdp", "ctx"), "tp"),
            P("tp", ("fsdp", "ctx")),
            P(("fsdp", "ctx"), "tp"),
            P("tp", ("fsdp", "ctx")),
            P(("fsdp", "ctx"), "tp"),
            P(),
            P(),
            P(),
            P(),
            P(),
            P(),
            P(),
            P(),
            P(),
            P(),
            P(),
            P(),
            P(),
            P(),
            P("fsdp", "ctx", "tp"),
        ),
        out_specs=(
            P("fsdp", "ctx", "tp"),
            P("fsdp", "ctx", None),
            P(("fsdp", "ctx"), "tp"),
            P(("fsdp", "ctx"), "tp"),
            P(("fsdp", "ctx"), "tp"),
            P(("fsdp", "ctx"), "tp"),
            P("tp", ("fsdp", "ctx")),
            P(("fsdp", "ctx"), "tp"),
            P("tp", ("fsdp", "ctx")),
            P(("fsdp", "ctx"), "tp"),
            P(("fsdp", "ctx")),
            P(("fsdp", "ctx")),
            P(("fsdp", "ctx")),
            P(("fsdp", "ctx")),
            P(("fsdp", "ctx")),
            P(("fsdp", "ctx")),
            P(("fsdp", "ctx")),
            P(("fsdp", "ctx")),
            P(("fsdp", "ctx")),
            P(("fsdp", "ctx")),
            P(("fsdp", "ctx")),
            P(("fsdp", "ctx")),
            P(("fsdp", "ctx")),
            P(("fsdp", "ctx")),
        ),
        check_vma=False,
    )
```

```python
from functools import partial

import jax
import jax.numpy as jnp
from jax import lax
from jax.experimental import pallas as pl
from jax.experimental.pallas import tpu as pltpu
from jax.sharding import PartitionSpec as P

SUBSPACE_SIZE = 64
PAIR = 128
GROUP = 16
HALO = 8
SPAN = 64
TILE = 256


EPS = 1e-05
GROUP_EPS = 4.0


def shifted(x, axis, by):
    count = lax.axis_size(axis)
    pairs = [(i, i + by) for i in range(count) if 0 <= i + by < count]
    return lax.ppermute(x, axis, pairs)


def earlier_shift(x, axis, by):
    count = lax.axis_size(axis)
    return lax.ppermute(x, axis, [(i, i + by) for i in range(count) if 0 <= i + by < count])


def carried(mult, sums, axis, toward):
    count = lax.axis_size(axis)
    low = (mult.astype(jnp.bfloat16), sums.astype(jnp.bfloat16))
    arrived = [
        jax.tree.map(lambda part: earlier_shift(part, axis, toward * by), low)
        for by in range(1, count)
    ]
    state = jnp.zeros_like(sums)
    for far_mult, far_sums in reversed(arrived):
        state = far_mult.astype(jnp.float32) * state + far_sums.astype(jnp.float32)
    return state


def partner(x, bit):
    count = lax.axis_size("tp")
    return lax.ppermute(x, "tp", [(i, i ^ bit) for i in range(count)])


def halves(x, axis, bit):
    size = x.shape[axis] // 2
    mine = (lax.axis_index("tp") // bit) % 2
    return (
        lax.dynamic_slice_in_dim(x, mine * size, size, axis),
        lax.dynamic_slice_in_dim(x, (1 - mine) * size, size, axis),
    )


def add_low(left, right):
    return (left.astype(jnp.float32) + right.astype(jnp.float32)).astype(jnp.bfloat16)


def ordered(mine, other, axis, bit):
    first = (lax.axis_index("tp") // bit) % 2 == 0
    return jnp.where(
        first,
        jnp.concatenate([mine, other], axis),
        jnp.concatenate([other, mine], axis),
    )


def after(value, *earlier):
    return lax.optimization_barrier((value,) + earlier)


def tp_sum(x, work=None):
    mine, other = halves(x, 0, 1)
    part = add_low(mine, partner(other, 1))
    made = work(part) if work else None
    bit = 2
    while bit < lax.axis_size("tp"):
        arrived = partner(part, bit)
        if work and bit == 2:
            part = after(part, made)[0]
        part = add_low(part, arrived)
        bit *= 2
    whole = ordered(part, partner(part, 1), 0, 1)
    return (whole, made, part) if work else whole


def axis_bits(axis):
    bits, bit = [], 1
    while bit < lax.axis_size(axis):
        bits.append((axis, bit))
        bit *= 2
    return bits


def swap(x, axis, bit):
    return lax.ppermute(x, axis, [(i, i ^ bit) for i in range(lax.axis_size(axis))])


def split_kernel(x_ref, *outs):
    at = 0
    for out in outs:
        out[...] = x_ref[:, at : at + out.shape[1]].astype(jnp.float32)
        at += out.shape[1]


def split_columns(x, widths, name):
    count = x.shape[0]
    rows = min(count, 64)
    return pl.pallas_call(
        split_kernel,
        grid=(count // rows,),
        in_specs=[pl.BlockSpec((rows, x.shape[1]), lambda i: (i, 0))],
        out_specs=[pl.BlockSpec((rows, width), lambda i: (i, 0)) for width in widths],
        out_shape=[jax.ShapeDtypeStruct((count, width), jnp.float32) for width in widths],
        cost_estimate=pl.CostEstimate(flops=x.size, bytes_accessed=6 * x.size, transcendentals=0),
        name=name,
    )(x)


def owner_scatter_steps(x):
    fsdp_bits, ctx_bits = axis_bits("fsdp"), axis_bits("ctx")
    dims = list(reversed(fsdp_bits)) + list(reversed(ctx_bits))
    rows = x.shape[0] // 2 ** len(dims)
    part = x.reshape(*([2] * len(dims)), rows, x.shape[1])
    hold = None
    for axis, bit in fsdp_bits + ctx_bits:
        dim = dims.index((axis, bit))
        dims.pop(dim)
        mine = (lax.axis_index(axis) // bit) % 2
        own = lax.dynamic_index_in_dim(part, mine, dim, False)
        arrived = swap(lax.dynamic_index_in_dim(part, 1 - mine, dim, False), axis, bit)
        if hold is not None:
            own = after(own, hold)[0]
        part = yield add_low(own, arrived)
        hold = None
        if isinstance(part, tuple):
            part, hold = part
    yield None


def whole_sum(x, steps):
    for axis, bit in steps:
        x = x + swap(x, axis, bit)
    return x


def tp_scatter(x):
    count, place = lax.axis_size("tp"), lax.axis_index("tp")
    width = x.shape[1] // count
    parts = [
        lax.dynamic_slice_in_dim(x, (place ^ relative) * width, width, 1)
        for relative in range(count)
    ]
    bit = 1
    while bit < count:
        for relative in reversed(range(count)):
            if relative & bit and relative & (bit - 1) == 0:
                arrived = partner(parts[relative], bit)
                parts[relative ^ bit] = add_low(parts[relative ^ bit], arrived)
        bit *= 2
    return parts[0]


def tp_gather(x):
    count, place = lax.axis_size("tp"), lax.axis_index("tp")
    width = x.shape[1]
    parts = {0: x}
    bit = count // 2
    while bit:
        parts.update({relative ^ bit: partner(part, bit) for relative, part in parts.items()})
        bit //= 2
    whole = jnp.zeros((x.shape[0], width * count), x.dtype)
    for relative, part in parts.items():
        whole = lax.dynamic_update_slice_in_dim(whole, part, (place ^ relative) * width, 1)
    return whole


def matmul(left, right):
    return jnp.dot(left, right, preferred_element_type=jnp.float32)


def matmul_tn(left, right):
    return lax.dot_general(
        left, right, (((0,), (0,)), ((), ())), preferred_element_type=jnp.float32
    )


def matmul_nt(left, right):
    return lax.dot_general(
        left, right, (((1,), (1,)), ((), ())), preferred_element_type=jnp.float32
    )


def dot_nn(left, right):
    return lax.dot_general(
        left, right, (((1,), (0,)), ((), ())), preferred_element_type=jnp.float32
    )


def lanes_of(shape):
    return lax.broadcasted_iota(jnp.int32, shape, len(shape) - 1)


def low_head(shape):
    return lanes_of(shape) < SUBSPACE_SIZE


def head_sum(x):
    first = low_head(x.shape)
    low = jnp.sum(jnp.where(first, x, 0.0), -1, keepdims=True)
    high = jnp.sum(jnp.where(first, 0.0, x), -1, keepdims=True)
    return jnp.where(first, low, high)


def fold_pair(both):
    return jnp.where(
        low_head((SUBSPACE_SIZE, PAIR)), both[:SUBSPACE_SIZE], both[SUBSPACE_SIZE:]
    )


def spread_pair(folded):
    first = low_head((SUBSPACE_SIZE, PAIR))
    return jnp.concatenate(
        [jnp.where(first, folded, 0.0), jnp.where(first, 0.0, folded)], axis=0
    ).astype(jnp.bfloat16)


def head_parts(x):
    first = low_head(x.shape)
    zero = jnp.zeros_like(x)
    return jnp.where(first, x, zero), jnp.where(first, zero, x)


def places(length):
    return lax.broadcasted_iota(jnp.int32, (length, PAIR), 0).astype(jnp.float32)


def carry_kernel(k_ref, v_ref, log_ref, cols_ref, out_ref):
    length = k_ref.shape[0]
    closing = jnp.exp((length - 1.0 - places(length)) * log_ref[...])
    ending = cols_ref[:, 2:3]
    k_end = (k_ref[...].astype(jnp.float32) * closing * ending).astype(jnp.bfloat16)
    out_ref[0, 0] = fold_pair(matmul_tn(v_ref[...], k_end))


def group_norm(attend):
    centered = attend - head_sum(attend) * (1.0 / SUBSPACE_SIZE)
    inverse = lax.rsqrt(head_sum(centered * centered) * (1.0 / SUBSPACE_SIZE) + GROUP_EPS)
    return centered * inverse, inverse


def mix_kernel(
    r_ref, k_ref, v_ref, gate_ref, log_ref, rows_ref, cols_ref, seg_ref, state_ref,
    joined_ref, attend_ref,
):
    length = r_ref.shape[0]
    at = places(length)
    log = log_ref[...]
    r = r_ref[...].astype(jnp.float32)
    k = k_ref[...].astype(jnp.float32)
    v = v_ref[...]
    q_low = (r * jnp.exp(at * log)).astype(jnp.bfloat16)
    k_low = (k * jnp.exp(-(at + 1.0) * log)).astype(jnp.bfloat16)
    state = spread_pair(state_ref[0, 0])
    bonus = head_sum(r * rows_ref[0:1, :] * k)
    base = bonus * v.astype(jnp.float32) + cols_ref[:, 1:2] * matmul_nt(q_low, state)
    step = min(length, TILE)
    for top in range(0, length, step):
        reach = top + step
        rows = slice(top, reach)
        keep = pair_mask(cols_ref[rows, 0:1], seg_ref[0, :, :reach], top, step, reach)
        parts = []
        for q_part in head_parts(q_low[rows]):
            scores = matmul_nt(q_part, k_low[:reach])
            scores = jnp.where(keep, scores, 0.0).astype(jnp.bfloat16)
            parts.append(dot_nn(scores, v[:reach]))
        attend = base[rows] + jnp.where(low_head(parts[0].shape), parts[0], parts[1])
        unit, _ = group_norm(attend)
        grouped = unit * rows_ref[1:2, :] + rows_ref[2:3, :]
        gate = gate_ref[rows, :]
        attend_ref[rows, :] = attend
        joined_ref[rows, :] = (grouped * (gate * jax.nn.sigmoid(gate))).astype(jnp.bfloat16)


def pair_mask(seg_col, seg_row, top, count, reach):
    later = lax.broadcasted_iota(jnp.int32, (count, reach), 0) + top
    return (seg_col == seg_row) & (later > lanes_of((count, reach)))


def pair_mask_t(seg_col, seg_row, top, count, start):
    width = seg_row.shape[1]
    earlier = lax.broadcasted_iota(jnp.int32, (count, width), 0) + top
    return (seg_col == seg_row) & (lanes_of((count, width)) + start > earlier)


def gate_back_kernel(
    dj_ref, attend_ref, gate_ref, r_ref, log_ref, rows_ref, cols_ref,
    dgate_ref, dattend_ref, state_ref, small_ref,
):
    length = r_ref.shape[0]
    d_joined = dj_ref[...]
    gate = gate_ref[...]
    unit, inverse = group_norm(attend_ref[...])
    gain = rows_ref[1:2, :]
    grouped = unit * gain + rows_ref[2:3, :]
    sig = jax.nn.sigmoid(gate)
    dgate_ref[...] = (d_joined * grouped * sig * (1.0 + gate * (1.0 - sig))).astype(jnp.bfloat16)
    d_grouped = d_joined * gate * sig
    sums = [
        jnp.sum(d_grouped * unit, axis=0, keepdims=True),
        jnp.sum(d_grouped, axis=0, keepdims=True),
    ]
    scaled = d_grouped * gain
    share = 1.0 / SUBSPACE_SIZE
    d_attend = (
        inverse * (scaled - head_sum(scaled) * share - unit * (head_sum(scaled * unit) * share))
    ).astype(jnp.bfloat16)
    dattend_ref[...] = d_attend
    rising = jnp.exp(places(length) * log_ref[...])
    q_live = (r_ref[...].astype(jnp.float32) * rising * cols_ref[:, 1:2]).astype(jnp.bfloat16)
    state_ref[0, 0] = fold_pair(matmul_tn(d_attend, q_live))
    collect(small_ref, sums)


def collect(small_ref, sums):
    pad = jnp.zeros((small_ref.shape[0] - len(sums), sums[0].shape[1]), jnp.float32)
    total = jnp.concatenate(sums + [pad], axis=0)

    @pl.when(pl.program_id(1) == 0)
    def _():
        small_ref[...] = total

    @pl.when(pl.program_id(1) > 0)
    def _():
        small_ref[...] += total


def mix_back_kernel(
    r_ref, k_ref, v_ref, da_ref, log_ref, rows_ref, cols_ref, seg_ref, state_ref, gstate_ref,
    mult_ref, dr_ref, dk_ref, dv_ref, small_ref,
):
    length = r_ref.shape[0]
    at = places(length)
    log = log_ref[...]
    reward = rows_ref[0:1, :]
    r = r_ref[...].astype(jnp.float32)
    k = k_ref[...].astype(jnp.float32)
    v = v_ref[...]
    da = da_ref[...]
    rising = jnp.exp(at * log)
    falling = jnp.exp(-(at + 1.0) * log)
    closing = jnp.exp((length - 1.0 - at) * log) * cols_ref[:, 2:3]
    q_low = (r * rising).astype(jnp.bfloat16)
    k_low = (k * falling).astype(jnp.bfloat16)
    k_end = (k * closing).astype(jnp.bfloat16)
    state, gstate = state_ref[0, 0], gstate_ref[0, 0]
    state_low, gstate_low = spread_pair(state), spread_pair(gstate)
    v_f, da_f = v.astype(jnp.float32), da.astype(jnp.float32)
    dot_va = head_sum(v_f * da_f)
    dk_end = dot_nn(v, gstate_low)
    dq_base = cols_ref[:, 1:2] * dot_nn(da, state_low)
    dv_base = head_sum(r * reward * k) * da_f + matmul_nt(k_end, gstate_low)
    q_f, k_f = q_low.astype(jnp.float32), k_low.astype(jnp.float32)
    d_log = jnp.sum((length - 1.0 - at) * k_end.astype(jnp.float32) * dk_end, 0, keepdims=True)
    d_log += length * mult_ref[0, 0] * jnp.sum(
        state.astype(jnp.bfloat16).astype(jnp.float32)
        * gstate.astype(jnp.bfloat16).astype(jnp.float32),
        0,
        keepdims=True,
    )
    step = min(length, TILE)
    for top in range(0, length, step):
        rows = slice(top, top + step)
        reach = top + step
        keep = pair_mask(cols_ref[rows, 0:1], seg_ref[0, :, :reach], top, step, reach)
        dq = []
        for da_part in head_parts(da[rows]):
            pull = jnp.where(keep, matmul_nt(da_part, v[:reach]), 0.0).astype(jnp.bfloat16)
            dq.append(dot_nn(pull, k_low[:reach]))
        first = low_head(dq[0].shape)
        dq = jnp.where(first, dq[0], dq[1]) + dq_base[rows]
        d_log += jnp.sum(at[rows] * q_f[rows] * dq, 0, keepdims=True)
        dr_ref[rows, :] = (dq * rising[rows] + reward * k[rows] * dot_va[rows]).astype(jnp.bfloat16)
        keep = pair_mask_t(cols_ref[rows, 0:1], seg_ref[0, :, top:], top, step, top)
        dk, dv = [], []
        for v_part, k_part in zip(head_parts(v[rows]), head_parts(k_low[rows])):
            pull = jnp.where(keep, matmul_nt(v_part, da[top:]), 0.0).astype(jnp.bfloat16)
            dk.append(dot_nn(pull, q_low[top:]))
            scores = jnp.where(keep, matmul_nt(k_part, q_low[top:]), 0.0).astype(jnp.bfloat16)
            dv.append(dot_nn(scores, da[top:]))
        dk = jnp.where(first, dk[0], dk[1])
        d_log -= jnp.sum((at[rows] + 1.0) * k_f[rows] * dk, 0, keepdims=True)
        dk_ref[rows, :] = (
            dk * falling[rows]
            + dk_end[rows] * closing[rows]
            + reward * r[rows] * dot_va[rows]
        ).astype(jnp.bfloat16)
        dv_ref[rows, :] = (jnp.where(first, dv[0], dv[1]) + dv_base[rows]).astype(jnp.bfloat16)
    collect(small_ref, [d_log * jnp.exp(-log), jnp.sum(r * k * dot_va, 0, keepdims=True)])


def pair_call(kernel, seqs, length, width, operands, outs, name, flops):
    pairs = width // PAIR
    specs = {
        "wide": pl.BlockSpec((length, PAIR), lambda p, s: (s, p)),
        "vector": pl.BlockSpec((1, PAIR), lambda p, s: (0, p)),
        "vectors": pl.BlockSpec((8, PAIR), lambda p, s: (0, p)),
        "cols": pl.BlockSpec((length, 4), lambda p, s: (s, 0)),
        "row": pl.BlockSpec((1, 1, length), lambda p, s: (s, 0, 0)),
        "state": pl.BlockSpec((1, 1, SUBSPACE_SIZE, PAIR), lambda p, s: (s, p, 0, 0)),
        "mult": pl.BlockSpec((1, 1, 1, PAIR), lambda p, s: (s, p, 0, 0)),
    }
    shapes = {
        "wide": (seqs * length, width),
        "vectors": (8, width),
        "state": (seqs, pairs, SUBSPACE_SIZE, PAIR),
    }
    kinds, arrays = zip(*operands)
    size = sum(array.size * array.dtype.itemsize for array in arrays)
    return pl.pallas_call(
        kernel,
        grid=(pairs, seqs),
        in_specs=[specs[kind] for kind in kinds],
        out_specs=[specs[kind] for kind, _ in outs],
        out_shape=[jax.ShapeDtypeStruct(shapes[kind], dtype) for kind, dtype in outs],
        cost_estimate=pl.CostEstimate(flops=flops, bytes_accessed=2 * size, transcendentals=0),
        name=name,
    )(*arrays)


def unit_rows(x):
    centered = x - jnp.mean(x, -1, keepdims=True)
    return centered * lax.rsqrt(jnp.mean(centered * centered, -1, keepdims=True) + EPS)


def total_at(refs, rows, lanes):
    total = refs[0][rows, lanes].astype(jnp.float32)
    for ref in refs[1:]:
        total = total + ref[rows, lanes].astype(jnp.float32)
    return total


def lane_loop(width, body):
    def step(at, _):
        body(pl.ds(pl.multiple_of(at * PAIR, PAIR), PAIR))
        return 0

    lax.fori_loop(0, width // PAIR, step, 0)


def row_blocks(rows):
    return [slice(top, min(top + SPAN, rows)) for top in range(0, rows, SPAN)]


def unit_into(refs, unit_scr, rows, width):
    inverses = []
    for block in row_blocks(rows):
        inside = slice(block.start + HALO, block.stop + HALO)
        zero = jnp.zeros((block.stop - block.start, PAIR), jnp.float32)

        def load(at, total):
            lanes = pl.ds(pl.multiple_of(at * PAIR, PAIR), PAIR)
            value = total_at(refs, block, lanes)
            unit_scr[inside, lanes] = value
            return total + value

        total = lax.fori_loop(0, width // PAIR, load, zero, unroll=4)
        mean = jnp.sum(total, -1, keepdims=True) * (1.0 / width)

        def square(at, total):
            lanes = pl.ds(pl.multiple_of(at * PAIR, PAIR), PAIR)
            value = unit_scr[inside, lanes] - mean
            return total + value * value

        total = lax.fori_loop(0, width // PAIR, square, zero, unroll=4)
        inverse = lax.rsqrt(jnp.sum(total, -1, keepdims=True) * (1.0 / width) + EPS)

        def scale(at, _):
            lanes = pl.ds(pl.multiple_of(at * PAIR, PAIR), PAIR)
            unit_scr[inside, lanes] = (unit_scr[inside, lanes] - mean) * inverse
            return 0

        lax.fori_loop(0, width // PAIR, scale, 0, unroll=4)
        inverses.append(inverse)
    return inverses


def blend_kernel(parts, mixes, per_seq, *refs):
    x_refs, refs = refs[:parts], refs[parts:]
    keep_ref, edge_ref, norm_ref, mix_ref = refs[:4]
    outs, unit_scr = refs[4 : 4 + mixes], refs[4 + mixes]
    rows, width = x_refs[0].shape

    @pl.when(pl.program_id(0) % per_seq == 0)
    def _():
        unit_scr[HALO - 1 : HALO, :] = edge_ref[0]

    unit_into(x_refs, unit_scr, rows, width)

    def lane_block(lanes):
        gain, bias_term = norm_ref[0:1, lanes], norm_ref[1:2, lanes]
        mixers = [mix_ref[at : at + 1, lanes] for at in range(mixes)]
        for block in row_blocks(rows):
            normed = unit_scr[block.start + HALO : block.stop + HALO, lanes] * gain + bias_term
            before = pltpu.roll(unit_scr[block.start : block.stop + HALO, lanes], 1, 0)[HALO:]
            previous = (before * gain + bias_term) * keep_ref[block, 0:1]
            delta = normed - previous
            for mixer, out in zip(mixers, outs):
                out[block, lanes] = (previous + mixer * delta).astype(jnp.bfloat16)

    lane_loop(width, lane_block)
    unit_scr[HALO - 1 : HALO, :] = unit_scr[rows + HALO - 1 : rows + HALO, :]


def blend(xs, keep, edge, norm, mixers, piece, name):
    tokens, width = xs[0].shape
    rows = min(piece, 256)
    mixes = mixers.shape[0]
    per_seq = piece // rows
    wide = pl.BlockSpec((rows, width), lambda i: (i, 0))
    return pl.pallas_call(
        partial(blend_kernel, len(xs), mixes, per_seq),
        grid=(tokens // rows,),
        in_specs=[wide] * len(xs)
        + [
            pl.BlockSpec((rows, 1), lambda i: (i, 0)),
            pl.BlockSpec((1, 1, width), lambda i: (i // per_seq, 0, 0)),
            pl.BlockSpec((2, width), lambda i: (0, 0)),
            pl.BlockSpec((mixes, width), lambda i: (0, 0)),
        ],
        out_specs=[wide] * mixes,
        out_shape=[jax.ShapeDtypeStruct((tokens, width), jnp.bfloat16)] * mixes,
        scratch_shapes=[pltpu.VMEM((rows + HALO, width), jnp.float32)],
        cost_estimate=pl.CostEstimate(
            flops=20 * tokens * width,
            bytes_accessed=2 * tokens * width * (len(xs) + mixes),
            transcendentals=0,
        ),
        name=name,
    )(*xs, keep, edge, norm, mixers)


def blend_back_kernel(parts, mixes, per_seq, own, *refs):
    x_refs, refs = refs[:parts], refs[parts:]
    halo_refs, refs = refs[:parts], refs[parts:]
    grad_refs, refs = refs[:mixes], refs[mixes:]
    weight_refs, refs = refs[:mixes], refs[mixes:]
    keep_ref, edge_ref, back_ref, norm_ref, mix_ref = refs[:5]
    refs = refs[5:]
    own_refs, refs = refs[: 2 * own], refs[2 * own :]
    out_ref, small_ref, d_scr, unit_scr, prev_scr, row_scr, sums = refs
    rows, width = x_refs[0].shape
    tiles = pl.num_programs(0)
    tile = tiles - 1 - pl.program_id(0)

    @pl.when(pl.program_id(0) == 0)
    def _():
        sums[...] = jnp.zeros_like(sums)

    @pl.when(tile % per_seq == per_seq - 1)
    def _():
        prev_scr[rows : rows + 1, :] = back_ref[0]

    @pl.when(tile % per_seq < per_seq - 1)
    def _():
        prev_scr[rows : rows + 1, :] = prev_scr[0:1, :]

    for at in range(mixes):
        d_scr[at] = matmul_nt(grad_refs[at][...], weight_refs[at][...])

    halo = unit_rows(total_at(halo_refs, slice(None), slice(None)))[GROUP - 1 :, :]
    unit_scr[HALO - 1 : HALO, :] = jnp.where(tile % per_seq == 0, edge_ref[0], halo)
    inverses = unit_into(x_refs, unit_scr, rows, width)
    row_scr[...] = jnp.zeros_like(row_scr)

    def gather(at, value):
        total = value[0:8]
        for top in range(8, value.shape[0], 8):
            total = total + value[top : top + 8]
        return total

    def first_pass(lanes):
        gain, bias_term = norm_ref[0:1, lanes], norm_ref[1:2, lanes]
        mixers = [mix_ref[at : at + 1, lanes] for at in range(mixes)]
        totals = [jnp.zeros((8, PAIR), jnp.float32)] * mixes
        for block in row_blocks(rows):
            keep = keep_ref[block, 0:1]
            normed = unit_scr[block.start + HALO : block.stop + HALO, lanes] * gain + bias_term
            before = pltpu.roll(unit_scr[block.start : block.stop + HALO, lanes], 1, 0)[HALO:]
            delta = normed - (before * gain + bias_term) * keep
            d_norm, d_all = None, None
            for at in range(mixes):
                d_in = d_scr[at, block, lanes]
                totals[at] = totals[at] + gather(at, d_in * delta)
                share = d_in * mixers[at]
                d_norm = share if d_norm is None else d_norm + share
                d_all = d_in if d_all is None else d_all + d_in
            prev_scr[block, lanes] = (d_all - d_norm) * keep
            d_scr[0, block, lanes] = d_norm
        for at in range(mixes):
            sums[2 + at, :, lanes] += totals[at]

    lane_loop(width, first_pass)

    def second_pass(lanes):
        gain = norm_ref[0:1, lanes]
        totals = [jnp.zeros((8, PAIR), jnp.float32)] * 2
        for block in row_blocks(rows):
            size = block.stop - block.start
            later = pltpu.roll(
                prev_scr[block.start : block.stop + HALO, lanes], size + HALO - 1, 0
            )[:size]
            d_norm = d_scr[0, block, lanes] + later
            unit = unit_scr[block.start + HALO : block.stop + HALO, lanes]
            product = d_norm * unit
            totals[0] = totals[0] + gather(0, product)
            totals[1] = totals[1] + gather(1, d_norm)
            d_scr[0, block, lanes] = d_norm * gain
            row_scr[0, block, :] += d_norm * gain
            row_scr[1, block, :] += product * gain
        for at in range(2):
            sums[at, :, lanes] += totals[at]

    lane_loop(width, second_pass)
    means, tilts = [], []
    for block in row_blocks(rows):
        means.append(jnp.sum(row_scr[0, block, :], -1, keepdims=True) * (1.0 / width))
        tilts.append(jnp.sum(row_scr[1, block, :], -1, keepdims=True) * (1.0 / width))
    blocks = list(zip(row_blocks(rows), inverses, means, tilts))

    def last_pass(start, lanes):
        for block, inverse, mean, tilt in blocks:
            unit = unit_scr[block.start + HALO : block.stop + HALO, lanes]
            value = inverse * (d_scr[0, block, lanes] - mean - unit * tilt)
            if own:
                extra = own_refs[0][block, start].astype(jnp.float32)
                value = value + extra * own_refs[1][0:1, lanes]
            out_ref[block, lanes] = value.astype(jnp.bfloat16)

    def last_step(at, _):
        lanes = pl.ds(pl.multiple_of(at * PAIR, PAIR), PAIR)
        inner = None
        if own:
            count = own_refs[0].shape[1] // PAIR
            inner = pl.ds(pl.multiple_of((at % count) * PAIR, PAIR), PAIR)
        last_pass(inner, lanes)
        return 0

    lax.fori_loop(0, width // PAIR, last_step, 0)

    @pl.when(pl.program_id(0) == tiles - 1)
    def _():
        for at in range(2 + mixes):
            small_ref[at : at + 1, :] = jnp.sum(sums[at], 0, keepdims=True)


def blend_back(xs, grads, weights, keep, edge, back, norm, mixers, piece, own, name):
    tokens, width = xs[0].shape
    rows = min(piece, 256)
    mixes = mixers.shape[0]
    per_seq = piece // rows
    tiles = tokens // rows

    def reverse(i):
        return tiles - 1 - i

    def halo_at(i):
        return (jnp.maximum(reverse(i) * (rows // GROUP) - 1, 0), 0)

    wide = pl.BlockSpec((rows, width), lambda i: (reverse(i), 0))
    per = pl.BlockSpec((1, 1, width), lambda i: (reverse(i) // per_seq, 0, 0))
    weight_specs, weight_arrays = [], []
    for (array, at), grad in zip(weights, grads):
        weight_specs.append(
            pl.BlockSpec(
                (width, grad.shape[1]), partial(lambda at, i: (0, at), at),
                pipeline_mode=pl.Buffered(1),
            )
        )
        weight_arrays.append(array)
    return pl.pallas_call(
        partial(blend_back_kernel, len(xs), mixes, per_seq, int(own is not None)),
        grid=(tiles,),
        in_specs=[wide] * len(xs)
        + [pl.BlockSpec((GROUP, width), halo_at)] * len(xs)
        + [pl.BlockSpec((rows, grad.shape[1]), lambda i: (reverse(i), 0)) for grad in grads]
        + weight_specs
        + [
            pl.BlockSpec((rows, 1), lambda i: (reverse(i), 0)),
            per,
            per,
            pl.BlockSpec((2, width), lambda i: (0, 0)),
            pl.BlockSpec((mixes, width), lambda i: (0, 0)),
        ]
        + (
            [
                pl.BlockSpec((rows, own[0].shape[1]), lambda i: (reverse(i), 0)),
                pl.BlockSpec((1, width), lambda i: (0, 0)),
            ]
            if own is not None
            else []
        ),
        out_specs=[wide, pl.BlockSpec((8, width), lambda i: (0, 0))],
        out_shape=[
            jax.ShapeDtypeStruct((tokens, width), jnp.bfloat16),
            jax.ShapeDtypeStruct((8, width), jnp.float32),
        ],
        scratch_shapes=[
            pltpu.VMEM((mixes, rows, width), jnp.float32),
            pltpu.VMEM((rows + HALO, width), jnp.float32),
            pltpu.VMEM((rows + HALO, width), jnp.float32),
            pltpu.VMEM((2, rows, PAIR), jnp.float32),
            pltpu.VMEM((2 + mixes, 8, width), jnp.float32),
        ],
        cost_estimate=pl.CostEstimate(
            flops=2 * tokens * width * sum(grad.shape[1] for grad in grads),
            bytes_accessed=2 * tokens * width * 4,
            transcendentals=0,
        ),
        name=name,
    )(*xs, *xs, *grads, *weight_arrays, keep, edge, back, norm, mixers, *(own or ()))


def per_device(
    entering_activations,
    document_indices,
    acceptor_matrix,
    lookup_matrix,
    payload_matrix,
    valve_matrix,
    result_matrix,
    ffn_lookup_matrix,
    ffn_payload_matrix,
    ffn_acceptor_matrix,
    first_standardize_scaling,
    first_standardize_offset,
    acceptor_lerp_factor,
    lookup_lerp_factor,
    payload_lerp_factor,
    valve_lerp_factor,
    token_fading,
    diagonal_reward,
    subspace_standardize_scaling,
    subspace_standardize_offset,
    second_standardize_scaling,
    second_standardize_offset,
    ffn_lookup_lerp,
    ffn_acceptor_lerp,
    upstream_derivative,
):
    seqs_here, piece_len, embedding_extent = entering_activations.shape
    token_count = seqs_here * piece_len
    tp_count = lax.axis_size("tp")
    fourth_extent = embedding_extent // tp_count
    sharded_layout = lax.axis_index("tp") * fourth_extent
    ctx_place = lax.axis_index("ctx") * piece_len
    padded_seg = jnp.concatenate(
        [jnp.full((seqs_here, 1), -1, jnp.int32), document_indices], axis=1
    )
    segment_present = lax.dynamic_slice_in_dim(document_indices, ctx_place, piece_len, 1)
    seg_before = lax.dynamic_slice_in_dim(padded_seg, ctx_place, piece_len, 1)
    document_begins = seg_before[:, :1]
    pairs_here = fourth_extent // PAIR
    same_mask = segment_present == seg_before
    live_mask = segment_present == document_begins
    ending_mask = segment_present == segment_present[:, -1:]
    cols = jnp.stack([segment_present, live_mask, ending_mask, same_mask], axis=-1)
    cols = cols.astype(jnp.float32).reshape(token_count, 4)
    keep = same_mask.astype(jnp.float32).reshape(token_count, 1)
    keep_first = same_mask[:, :1].astype(jnp.float32)
    seg_row = segment_present.astype(jnp.float32)[:, None, :]
    owners = ("fsdp", "ctx")
    w_time = lax.all_gather(
        jnp.concatenate(
            [acceptor_matrix, lookup_matrix, payload_matrix, valve_matrix, result_matrix.T], axis=1
        ),
        owners,
        axis=0,
        tiled=True,
    )
    w_chan = lax.all_gather(
        jnp.concatenate([ffn_lookup_matrix, ffn_acceptor_matrix], axis=1),
        owners,
        axis=0,
        tiled=True,
    )
    units = ffn_lookup_matrix.shape[1]
    w_recept, w_key, w_value, w_gate, w_output_t = (
        w_time[:, at * fourth_extent : (at + 1) * fourth_extent] for at in range(5)
    )
    w_chankey = w_chan[:, :units]
    w_chanrecept = w_chan[:, units:]
    w_chanvalue_t = lax.all_gather(ffn_payload_matrix.T, owners, axis=0, tiled=True)
    x_low = entering_activations.reshape(token_count, embedding_extent)
    norm_one = jnp.stack([first_standardize_scaling, first_standardize_offset])
    norm_two = jnp.stack([second_standardize_scaling, second_standardize_offset])
    mix_one = jnp.stack(
        [acceptor_lerp_factor, lookup_lerp_factor, payload_lerp_factor, valve_lerp_factor]
    )
    mix_two = jnp.stack([ffn_lookup_lerp, ffn_acceptor_lerp])

    def edge_from(last_rows):
        return shifted(unit_rows(last_rows), "ctx", 1)[:, None]

    def back_from(grads, weights, mixers):
        first = jnp.zeros((seqs_here, embedding_extent), jnp.float32)
        for at, (grad_low, weight) in enumerate(zip(grads, weights)):
            rows = grad_low.reshape(seqs_here, piece_len, -1)[:, 0]
            first = first + matmul_nt(rows, weight) * (1.0 - mixers[at])
        return shifted(first * keep_first, "ctx", -1)[:, None]

    edge_one = edge_from(entering_activations[:, -1].astype(jnp.float32))
    mixed_in = blend((x_low,), keep, edge_one, norm_one, mix_one, piece_len, "blend_one")
    key_low = matmul(mixed_in[1], w_key).astype(jnp.bfloat16)
    value_low = matmul(mixed_in[2], w_value).astype(jnp.bfloat16)

    def own_share(vector):
        return lax.dynamic_slice_in_dim(vector, sharded_layout, fourth_extent, 0)[None]

    log_row = jnp.log(own_share(token_fading))
    vectors = jnp.concatenate(
        [own_share(diagonal_reward), own_share(subspace_standardize_scaling)]
        + [own_share(subspace_standardize_offset)] * 6
    )
    call = partial(pair_call, seqs=seqs_here, length=piece_len, width=fourth_extent)
    square = 2 * token_count * piece_len * fourth_extent
    (carry_sums,) = call(
        carry_kernel,
        operands=[("wide", key_low), ("wide", value_low), ("vector", log_row), ("cols", cols)],
        outs=[("state", jnp.float32)],
        name="carry",
        flops=square // 8,
    )
    alive_mask = (live_mask[:, -1]).astype(jnp.float32)[:, None, None, None]
    carry_mult = alive_mask * jnp.exp(float(piece_len) * log_row).reshape(1, pairs_here, 1, PAIR)
    incoming = carried(carry_mult, carry_sums, "ctx", 1)
    recept_low = matmul(mixed_in[0], w_recept).astype(jnp.bfloat16)
    gate_pre = matmul(mixed_in[3], w_gate)
    joined_low, attend = call(
        mix_kernel,
        operands=[
            ("wide", recept_low),
            ("wide", key_low),
            ("wide", value_low),
            ("wide", gate_pre),
            ("vector", log_row),
            ("vectors", vectors),
            ("cols", cols),
            ("row", seg_row),
            ("state", incoming),
        ],
        outs=[("wide", jnp.bfloat16), ("wide", jnp.float32)],
        name="mix",
        flops=2 * square,
    )
    mixed_out = tp_sum(matmul_nt(joined_low, w_output_t).astype(jnp.bfloat16))
    last_rows = entering_activations[:, -1].astype(jnp.float32) + mixed_out.reshape(
        seqs_here, piece_len, embedding_extent
    )[:, -1].astype(jnp.float32)
    edge_two = edge_from(last_rows)
    key_in, rec_in = blend(
        (x_low, mixed_out), keep, edge_two, norm_two, mix_two, piece_len, "blend_two"
    )
    rec_gate = jax.nn.sigmoid(matmul(rec_in, w_chanrecept))
    d_result_low = upstream_derivative.reshape(token_count, fourth_extent)
    d_result = d_result_low.astype(jnp.float32)
    d_chan = (d_result * rec_gate).astype(jnp.bfloat16)
    d_chan_full = tp_gather(d_chan)
    key_pre = matmul(key_in, w_chankey)
    hidden = jnp.square(jax.nn.relu(key_pre)).astype(jnp.bfloat16)
    grad_chanvalue = matmul_tn(hidden, d_chan_full).astype(jnp.bfloat16)
    g_chanvalue = lax.psum_scatter(grad_chanvalue, owners, scatter_dimension=1, tiled=True)
    hidden, grad_chanvalue = after(hidden, grad_chanvalue)
    chan_sum = tp_scatter(matmul_nt(hidden, w_chanvalue_t).astype(jnp.bfloat16)).astype(jnp.float32)
    middle_q = lax.dynamic_slice_in_dim(x_low, sharded_layout, fourth_extent, 1).astype(
        jnp.float32
    ) + lax.dynamic_slice_in_dim(mixed_out, sharded_layout, fourth_extent, 1).astype(jnp.float32)
    result = (
        (middle_q + rec_gate * chan_sum)
        .astype(jnp.bfloat16)
        .reshape(seqs_here, piece_len, fourth_extent)
    )
    d_rec_pre = (d_result * chan_sum * rec_gate * (1.0 - rec_gate)).astype(jnp.bfloat16)
    d_hidden = matmul(d_chan_full, w_chanvalue_t)
    d_key_pre = (d_hidden * 2.0 * jax.nn.relu(key_pre)).astype(jnp.bfloat16)
    full_shape = (seqs_here, piece_len, embedding_extent)
    own_mask = (jnp.arange(embedding_extent) // fourth_extent == lax.axis_index("tp")).astype(
        jnp.float32
    )[None]
    d_middle_part, chan_small = blend_back(
        (x_low, mixed_out),
        (d_key_pre, d_rec_pre),
        ((w_chan, 0), (w_chanrecept, 0)),
        keep,
        edge_two,
        back_from((d_key_pre, d_rec_pre), (w_chankey, w_chanrecept), mix_two),
        norm_two,
        mix_two,
        piece_len,
        (d_result_low, own_mask),
        "blend_two_back",
    )

    def chan_grads(token):
        d_key_late, d_rec_late, _ = after(d_key_pre, d_rec_pre, token)
        return jnp.concatenate(
            [
                matmul_tn(key_in, d_key_late).astype(jnp.bfloat16),
                matmul_tn(rec_in, d_rec_late).astype(jnp.bfloat16),
            ],
            axis=1,
        )

    d_mixed, grads_chan, exchanged = tp_sum(d_middle_part, chan_grads)
    grads_chan, g_chanvalue, _ = after(grads_chan, g_chanvalue, exchanged)
    g_chan = lax.psum_scatter(grads_chan, owners, scatter_dimension=0, tiled=True)
    grad_output_t = matmul_tn(d_mixed, joined_low).astype(jnp.bfloat16)
    d_joined = matmul(d_mixed, w_output_t)
    d_gate_pre, d_attend, local_grad, group_small = call(
        gate_back_kernel,
        operands=[
            ("wide", d_joined),
            ("wide", attend),
            ("wide", gate_pre),
            ("wide", recept_low),
            ("vector", log_row),
            ("vectors", vectors),
            ("cols", cols),
        ],
        outs=[
            ("wide", jnp.bfloat16),
            ("wide", jnp.bfloat16),
            ("state", jnp.float32),
            ("vectors", jnp.float32),
        ],
        name="gate_back",
        flops=square // 8,
    )
    grads_early = jnp.concatenate(
        [grad_output_t, matmul_tn(mixed_in[3], d_gate_pre).astype(jnp.bfloat16)], axis=1
    )
    early = owner_scatter_steps(grads_early)
    g_early = next(early)
    outgoing_state = carried(carry_mult, local_grad, "ctx", -1)
    d_recept, d_key, d_value, state_small = call(
        mix_back_kernel,
        operands=[
            ("wide", recept_low),
            ("wide", key_low),
            ("wide", value_low),
            ("wide", d_attend),
            ("vector", log_row),
            ("vectors", vectors),
            ("cols", cols),
            ("row", seg_row),
            ("state", incoming),
            ("state", outgoing_state),
            ("mult", carry_mult),
        ],
        outs=[("wide", jnp.bfloat16)] * 3 + [("vectors", jnp.float32)],
        name="mix_back",
        flops=6 * square,
    )
    early_steps = len(axis_bits("fsdp")) + len(axis_bits("ctx"))
    d_recept, d_key, d_value, g_early = after(d_recept, d_key, d_value, g_early)
    for _ in range(early_steps - 3):
        g_early = early.send(g_early)
    d_lows = [d_recept, d_key, d_value, d_gate_pre]
    weights_time = (w_recept, w_key, w_value, w_gate)
    grads_time = jnp.concatenate(
        [
            matmul_tn(mixed, grad_low).astype(jnp.bfloat16)
            for mixed, grad_low in zip(mixed_in, d_lows[:2])
        ],
        axis=1,
    )
    value_steps = owner_scatter_steps(matmul_tn(mixed_in[2], d_value).astype(jnp.bfloat16))
    g_value = next(value_steps)
    for _ in range(early_steps - 3):
        g_value = value_steps.send(g_value)
    *d_lows, _ = after(d_lows[0], *d_lows[1:], grads_time)
    g_time = lax.psum_scatter(grads_time, owners, scatter_dimension=0, tiled=True)
    back_one = back_from(d_lows, weights_time, mix_one)
    g_early = early.send(after(g_early, back_one)[0])
    d_input_part, time_small = blend_back(
        (x_low,),
        d_lows,
        [(w_time, at) for at in range(4)],
        keep,
        edge_one,
        back_one,
        norm_one,
        mix_one,
        piece_len,
        None,
        "blend_one_back",
    )
    d_input_part, g_early, g_chan, g_value = after(d_input_part, g_early, g_chan, g_value)
    g_early = early.send(g_early)
    g_value = value_steps.send(g_value)
    head_small = jnp.concatenate([state_small[:2], group_small[:2]])
    head_small = lax.dynamic_update_slice_in_dim(
        jnp.zeros((4, embedding_extent), jnp.float32), head_small, sharded_layout, 1
    )
    small_part = jnp.concatenate([time_small[:6], head_small, chan_small[:4]], axis=0)

    def small_total(token):
        tp_bits = axis_bits("tp")
        total = whole_sum(
            after(small_part, token)[0],
            axis_bits("fsdp") + tp_bits[:1] + axis_bits("ctx") + tp_bits[1:],
        )
        return total, g_early, g_value

    d_input_sum, (small_sum, g_early, g_value), _ = tp_sum(d_input_part, small_total)
    owned = embedding_extent // (lax.axis_size("fsdp") * lax.axis_size("ctx"))
    small_owned = lax.dynamic_slice_in_dim(
        small_sum,
        (lax.axis_index("fsdp") * lax.axis_size("ctx") + lax.axis_index("ctx")) * owned,
        owned,
        1,
    )
    grad_inputs = (d_mixed.astype(jnp.float32) + d_input_sum.astype(jnp.float32)).reshape(
        full_shape
    )
    g_chanvalue = g_chanvalue.astype(jnp.float32)
    g_chankey, g_chanrecept = split_columns(g_chan, (units, fourth_extent), "split_chan")
    g_early = g_early.astype(jnp.float32)
    g_value = value_steps.send((g_value, (grad_inputs, g_chankey, g_chanrecept)))
    g_value = g_value.astype(jnp.float32)
    g_output = g_early[:, :fourth_extent].T
    g_gate = g_early[:, fourth_extent:]
    g_time = after(
        g_time, grad_inputs, result, g_chanvalue, g_chankey, g_chanrecept, g_output, g_gate, g_value
    )[0]
    g_recept, g_key = split_columns(g_time, (fourth_extent,) * 2, "split_time")
    return (
        result,
        grad_inputs,
        g_recept,
        g_key,
        g_value,
        g_gate,
        g_output,
        g_chankey,
        g_chanvalue,
        g_chanrecept,
    ) + tuple(small_owned[at] for at in range(14))


def solution(mesh):
    return jax.shard_map(
        per_device,
        mesh=mesh,
        in_specs=(
            P("fsdp", "ctx", None),
            P("fsdp", None),
            P(("fsdp", "ctx"), "tp"),
            P(("fsdp", "ctx"), "tp"),
            P(("fsdp", "ctx"), "tp"),
            P(("fsdp", "ctx"), "tp"),
            P("tp", ("fsdp", "ctx")),
            P(("fsdp", "ctx"), "tp"),
            P("tp", ("fsdp", "ctx")),
            P(("fsdp", "ctx"), "tp"),
            P(),
            P(),
            P(),
            P(),
            P(),
            P(),
            P(),
            P(),
            P(),
            P(),
            P(),
            P(),
            P(),
            P(),
            P("fsdp", "ctx", "tp"),
        ),
        out_specs=(
            P("fsdp", "ctx", "tp"),
            P("fsdp", "ctx", None),
            P(("fsdp", "ctx"), "tp"),
            P(("fsdp", "ctx"), "tp"),
            P(("fsdp", "ctx"), "tp"),
            P(("fsdp", "ctx"), "tp"),
            P("tp", ("fsdp", "ctx")),
            P(("fsdp", "ctx"), "tp"),
            P("tp", ("fsdp", "ctx")),
            P(("fsdp", "ctx"), "tp"),
            P(("fsdp", "ctx")),
            P(("fsdp", "ctx")),
            P(("fsdp", "ctx")),
            P(("fsdp", "ctx")),
            P(("fsdp", "ctx")),
            P(("fsdp", "ctx")),
            P(("fsdp", "ctx")),
            P(("fsdp", "ctx")),
            P(("fsdp", "ctx")),
            P(("fsdp", "ctx")),
            P(("fsdp", "ctx")),
            P(("fsdp", "ctx")),
            P(("fsdp", "ctx")),
            P(("fsdp", "ctx")),
        ),
        check_vma=False,
    )
```
